32 devices in a mesh: fsdp: 2 (over core), ctx: 4 (over y, x), tp: 4 (over z).
Axes of the slice: x: 2, y: 2, z: 4, core: 2. Of those that a mesh axis runs over, the one named last changes fastest.
Arguments:
- tokens: bfloat16 [8, 1024, 2048], P('fsdp', 'ctx'), may hold values from -6 to 6
- segment_ids: int32 [8, 1024], P('fsdp', 'ctx'), may hold values from 0 to 7, never falling along the last dimension, each value on 1 to 512 neighbouring positions
- w_in: float32 [3, 2048, 2048], P(None, 'fsdp', 'tp'), may hold values from -0.125 to 0.125
- w_out: float32 [2048, 2048], P('tp', 'fsdp'), may hold values from -0.125 to 0.125
- w_glu: float32 [2048, 2, 5632], P('fsdp', None, 'tp'), may hold values from -0.125 to 0.125
- w_down: float32 [5632, 2048], P('tp', 'fsdp'), may hold values from -0.078125 to 0.078125
- gain_one: float32 [2048], P('fsdp'), may hold values from 0.5 to 1.5
- gain_two: float32 [2048], P('fsdp'), may hold values from 0.5 to 1.5
- gate_gain: float32 [2048], P('tp'), may hold values from 0.5 to 1.5
- lower: float32 [2048], P('tp'), may hold values from 0.94 to 0.9995
- cotangent: bfloat16 [8, 1024, 2048], P('fsdp', 'ctx'), may hold values from -6 to 6
Outputs:
- output: bfloat16 [8, 1024, 2048], P('fsdp', 'ctx')
- grad_tokens: float32 [8, 1024, 2048], P('fsdp', 'ctx')
- grad_w_in: float32 [3, 2048, 2048], P(None, 'fsdp', 'tp')
- grad_w_out: float32 [2048, 2048], P('tp', 'fsdp')
- grad_w_glu: float32 [2048, 2, 5632], P('fsdp', None, 'tp')
- grad_w_down: float32 [5632, 2048], P('tp', 'fsdp')
- grad_gain_one: float32 [2048], P('fsdp')
- grad_gain_two: float32 [2048], P('fsdp')
- grad_gate_gain: float32 [2048], P('tp')
- grad_lower: float32 [2048], P('tp')
The draws below stay inside these ranges and needn't reach their ends.
Inputs may be any that keep to these rules, and one draw needn't show every extreme that they name: `segment_ids`: within each sequence the document numbers start at 0, never fall, and each document has 1 to 512 tokens, one of them exactly 512.
All inputs are finite; a program needn't handle non-finite values.
Results may differ from the reference program's by a relative error of at most 0.02.
Values may be sent and summed in bfloat16 or wider, within the bound.
A program may use at most 256 MiB of HBM per device.

```python
import math
import jax
import jax.numpy as jnp
import numpy as np
from jax import lax

D = 2048
FF = 5632
SEQ_DEV = 4
SEGS = 8
LEN = 1024
SEQS = 8
N_TP = 4


def draw_lower(key, part):
    uniform_part = jax.random.uniform(key, (D,), jnp.float32)
    low_end = math.log(0.001)
    high_end = math.log(0.06)
    return 1.0 - jnp.exp(low_end + (high_end - low_end) * uniform_part)


def block_scale(key, dims, pieces, least, largest):
    gain = 1.0
    for position, blocks in pieces:
        heights = jax.random.uniform(jax.random.fold_in(jax.random.fold_in(key, 6), position), (blocks,), jnp.float32, least / len(pieces), largest / len(pieces))
        gain = gain * jnp.repeat(jnp.exp(heights), dims[position] // blocks).reshape((-1,) + (1,) * (len(dims) - 1 - position))
    return gain


def split_up(count, total, most, lean):
    loads = [(1 << 20) // math.isqrt(standing ** lean) + 1 for standing in range(2, count + 1)]
    spare, counts = total - most - (count - 1), [1] * (count - 1)
    while spare > 0:
        movable = [i for i in range(count - 1) if counts[i] < most]
        pool, budget = sum([loads[i] for i in movable]), spare
        for i in movable:
            addition = min(most - counts[i], max(1, budget * loads[i] // pool), spare)
            counts[i] = counts[i] + addition
            spare = spare - addition
    return np.array([most] + counts)


def uneven(rng, number_of, total, most, lean):
    if number_of == 2:
        one = jax.random.randint(rng, (), max(1, total - most), min(most, total - 1) + 1)
        return jnp.stack([one, total - one])
    lengths = jnp.asarray(split_up(number_of, total, most, lean), jnp.int32)
    pairs = (number_of - 1) // 2
    giver, taker = lengths[1:1 + 2 * pairs:2], lengths[2:2 + 2 * pairs:2]
    room = jnp.minimum(giver - 1, most - taker)
    passed = jax.random.randint(jax.random.fold_in(rng, 1), (pairs,), 0, 1 << 20) % (room + 1)
    lengths = lengths.at[1:1 + 2 * pairs:2].set(giver - passed).at[2:2 + 2 * pairs:2].set(taker + passed)
    return lengths[jax.random.permutation(jax.random.fold_in(rng, 2), number_of)]


def noise(stream_key, shape, scale, most, shards=(), kind=jnp.bfloat16):
    entries = jax.random.normal(stream_key, shape, jnp.float32) * scale
    if len(shards) > 0:
        entries = block_scale(stream_key, shape, shards, -0.22, 0.18) * entries
    return jnp.clip(entries, min=-most, max=most).astype(kind)


def setup_inputs(seed: int = 0) -> dict:
    arg_keys = jax.random.split(jax.random.key(seed), 12)
    return {
        "tokens": noise(arg_keys[0], (SEQS, LEN, D), 1.0, 6.0, ((0, 2), (1, 4))),
        "segment_ids": jax.vmap(lambda own: jnp.searchsorted(jnp.cumsum(uneven(own, SEGS, LEN, LEN // 2, 2)), jnp.arange(LEN), side="right"))(jax.random.split(arg_keys[1], SEQS)).reshape((SEQS, LEN)).astype(jnp.int32),
        "w_in": noise(arg_keys[2], (3, D, D), D ** -0.5, 0.125, ((1, 2), (2, 4)), jnp.float32),
        "w_out": noise(arg_keys[3], (D, D), D ** -0.5, 0.125, ((0, 4), (1, 2)), jnp.float32),
        "w_glu": noise(arg_keys[4], (D, 2, FF), D ** -0.5, 0.125, ((0, 2), (2, 4)), jnp.float32),
        "w_down": noise(arg_keys[5], (FF, D), FF ** -0.5, 0.078125, ((0, 4), (1, 2)), jnp.float32),
        "gain_one": jnp.clip(1.0 + 0.1 * jax.random.normal(arg_keys[6], (D,), jnp.float32), 0.5, 1.5),
        "gain_two": jnp.clip(1.0 + 0.1 * jax.random.normal(arg_keys[7], (D,), jnp.float32), 0.5, 1.5),
        "gate_gain": jnp.clip(1.0 + 0.1 * jax.random.normal(arg_keys[8], (D,), jnp.float32), 0.5, 1.5),
        "lower": draw_lower(jax.random.fold_in(arg_keys[11], 71), 0),
        "cotangent": noise(arg_keys[10], (SEQS, LEN, D), 1.0, 6.0, ((0, 2), (1, 4))),
    }


EPS = 1e-06

@jax.custom_vjp
def low(v):
    return lax.optimization_barrier(v.astype(jnp.bfloat16)).astype(jnp.float32)

@jax.custom_vjp
def low_back(v):
    return v

def low_keep(v):
    return (low(v), None)

def low_pass(kept, grad):
    return (grad,)

def back_keep(v):
    return (v, None)

def back_low(kept, grad):
    return (low(grad),)
low.defvjp(low_keep, low_pass)
low_back.defvjp(back_keep, back_low)

def link(earlier, later):
    return (earlier[0] * later[0], later[0] * earlier[1] + later[1])

def rms_scale(values):
    return lax.rsqrt(lax.optimization_barrier(jnp.mean(values * values, -1, keepdims=True)) + EPS)

def layer_forward(tokens, seg, w_in, w_out, w_glu, w_down, gain_one, gain_two, gate_gain, lower):
    highest = lax.Precision.HIGHEST
    n_seq, length, width = tokens.shape
    rows = n_seq * length
    chan = width // N_TP
    units = w_glu.shape[2] // N_TP
    flat = tokens.reshape(rows, width)
    normed = low(flat * rms_scale(flat) * low(gain_one))
    copies = jnp.stack([low_back(normed) for block in range(N_TP)])
    proj = jnp.einsum('ktd,wdkc->wtkc', copies, low(w_in).reshape(3, width, N_TP, chan), precision=highest)
    proj = low_back(proj.reshape(3, n_seq, length, width))
    inp, forget, gate = (proj[0], proj[1], proj[2])
    fsig = jax.nn.sigmoid(forget)
    decay = lower + (1.0 - lower) * fsig
    update = jax.nn.silu(inp) * (1.0 - decay)
    same = (seg[:, 1:] == seg[:, :-1]).astype(jnp.float32)
    keep = jnp.concatenate([jnp.zeros((n_seq, 1), jnp.float32), same], 1)
    mult = decay * keep[:, :, None]
    reach, state = lax.associative_scan(link, (mult, update), axis=1)
    unit = state * rms_scale(state)
    gated = low(unit * gate_gain * jax.nn.silu(gate)).reshape(rows, N_TP, chan)
    parts = jnp.einsum('tkc,kce->kte', gated, low(w_out).reshape(N_TP, chan, width), precision=highest)
    mixed = low_back(lax.optimization_barrier(jnp.sum(low(parts), 0)))
    resid = flat + mixed
    normed_two = low(resid * rms_scale(resid) * low(gain_two))
    copies_two = jnp.stack([low_back(normed_two) for block in range(N_TP)])
    glu = jnp.einsum('ktd,dwkf->wtkf', copies_two, low(w_glu).reshape(width, 2, N_TP, units), precision=highest)
    glu = low_back(glu.reshape(2, rows, N_TP * units))
    act = low(jax.nn.silu(glu[0]) * glu[1]).reshape(rows, N_TP, units)
    parts_two = jnp.einsum('tkf,kfe->kte', act, low(w_down).reshape(N_TP, units, width), precision=highest)
    down = low_back(lax.optimization_barrier(jnp.sum(low(parts_two), 0)))
    return (resid + down).reshape(n_seq, length, width)

def reference(tokens, segment_ids, w_in, w_out, w_glu, w_down, gain_one, gain_two, gate_gain, lower, cotangent):
    params = (w_in, w_out, w_glu, w_down, gain_one, gain_two, gate_gain, lower)
    params = tuple((p.astype(jnp.float32) for p in params))
    groups = SEQS // SEQ_DEV
    width = tokens.shape[2]
    blocks = (tokens.reshape(groups, SEQ_DEV, LEN, width), segment_ids.reshape(groups, SEQ_DEV, LEN), cotangent.reshape(groups, SEQ_DEV, LEN, width))

    def one_group(totals, block):
        x_block, seg_block, cot_block = block

        def forward(x_value, *weights):
            return layer_forward(x_value, seg_block, *weights)
        result, pull = jax.vjp(forward, x_block.astype(jnp.float32), *params)
        grads = pull(cot_block.astype(jnp.float32))
        totals = tuple((t + g for t, g in zip(totals, grads[1:])))
        return (totals, (result.astype(jnp.bfloat16), grads[0]))
    zeros = tuple((jnp.zeros_like(p) for p in params))
    totals, (results, grad_x) = lax.scan(one_group, zeros, blocks)
    output = results.reshape(SEQS, LEN, width)
    grad_tokens = grad_x.reshape(SEQS, LEN, width)
    return (output, grad_tokens, totals[0], totals[1], totals[2], totals[3], totals[4], totals[5], totals[6], totals[7])
```

```python
import functools

import jax
import jax.numpy as jnp
from jax import lax
from jax.experimental import pallas as pl
from jax.experimental.pallas import tpu as pltpu
from jax.sharding import PartitionSpec as P

EPS = 1e-06
FLOAT = jnp.float32
HALF = jnp.bfloat16
MESH = pl.DeviceIdType.MESH
GROUP = 8
BLOCK = 128
MIB = 1 << 20


def rms_scale(values):
    return lax.rsqrt(jnp.mean(values * values, -1, keepdims=True) + EPS)


def silu_slope(values):
    sig = jax.nn.sigmoid(values)
    return sig * (1.0 + values * (1.0 - sig))


def greet(peers):
    barrier = pltpu.get_barrier_semaphore()
    for peer in peers:
        pl.semaphore_signal(barrier, inc=1, device_id=peer, device_id_type=MESH)
    pl.semaphore_wait(barrier, len(peers))


def others(axis, count):
    mine = lax.axis_index(axis)
    return [{axis: lax.rem(mine + step, count)} for step in range(1, count)]


def share(slots, axis, count, send, recv):
    mine = lax.axis_index(axis)
    copies = [
        pltpu.make_async_remote_copy(
            src_ref=slots.at[mine],
            dst_ref=slots.at[mine],
            send_sem=send.at[step],
            recv_sem=recv.at[step],
            device_id=peer,
            device_id_type=MESH,
        )
        for step, peer in enumerate(others(axis, count))
    ]
    for copy in copies:
        copy.start()
    for copy in copies:
        copy.wait()


def lane_sums(values):
    part = values[:, :BLOCK]
    for start in range(BLOCK, values.shape[1], BLOCK):
        part = part + values[:, start : start + BLOCK]
    return jnp.sum(part.T, 0, keepdims=True)


def columns(row):
    return jnp.broadcast_to(row, (BLOCK, BLOCK)).T


def widen(values, chan):
    return jnp.concatenate([values] * (chan // BLOCK), -1)


def scan_forward(
    n_ctx, n_tp, width,
    proj, keep, gain, lower,
    gated, state, scale, carry_out,
    local, reach, ends, squares, ctx_send, ctx_recv, tp_send, tp_recv,
):
    n_seq, length, chan = state.shape
    greet(others("ctx", n_ctx) + others("tp", n_tp))
    low = lower[...].reshape(1, 1, chan)
    row = lax.broadcasted_iota(jnp.int32, (n_seq, GROUP, chan), 1)

    def step(index, carry):
        prod, total = carry
        rows = pl.ds(pl.multiple_of(index * GROUP, GROUP), GROUP)
        inp = proj[0, :, rows, :]
        decay = low + (1.0 - low) * jax.nn.sigmoid(proj[1, :, rows, :])
        add = inp * jax.nn.sigmoid(inp) * (1.0 - decay)
        mult = decay * keep[:, rows, :]
        for hop in (1, 2, 4):
            inside = row >= hop
            add = jnp.where(inside, mult * pltpu.roll(add, hop, 1) + add, add)
            mult = jnp.where(inside, mult * pltpu.roll(mult, hop, 1), mult)
        add = add + mult * total
        mult = mult * prod
        local[:, rows, :] = add
        reach[:, rows, :] = mult
        return mult[:, GROUP - 1 :, :], add[:, GROUP - 1 :, :]

    start = (jnp.ones((n_seq, 1, chan), FLOAT), jnp.zeros((n_seq, 1, chan), FLOAT))
    prod, total = lax.fori_loop(0, length // GROUP, step, start)
    here = lax.axis_index("ctx")
    ends[here, 0] = prod.reshape(n_seq, chan)
    ends[here, 1] = total.reshape(n_seq, chan)
    share(ends, "ctx", n_ctx, ctx_send, ctx_recv)
    carry = jnp.zeros((n_seq, chan), FLOAT)
    for place in range(n_ctx - 1):
        carry = jnp.where(place < here, ends[place, 1] + ends[place, 0] * carry, carry)
    carry_out[...] = carry
    mine = lax.axis_index("tp")
    for seq in range(n_seq):
        for start in range(0, length, BLOCK):
            rows = slice(start, start + BLOCK)
            value = local[seq, rows, :] + reach[seq, rows, :] * carry[seq : seq + 1]
            state[seq, rows, :] = value
            squares[mine, seq : seq + 1, rows] = lane_sums(value * value)
    share(squares, "tp", n_tp, tp_send, tp_recv)
    total = squares[0]
    for place in range(1, n_tp):
        total = total + squares[place]
    rate = lax.rsqrt(total / width + EPS)
    scale[...] = rate
    for seq in range(n_seq):
        for start in range(0, length, BLOCK):
            rows = slice(start, start + BLOCK)
            gate = proj[2, seq, rows, :]
            unit = state[seq, rows, :] * widen(columns(rate[seq : seq + 1, rows]), chan)
            gated[seq, rows, :] = (unit * gain[...] * (gate * jax.nn.sigmoid(gate))).astype(HALF)


def run_scan_forward(proj, keep, gain, lower, n_ctx, n_tp, width):
    _, n_seq, length, chan = proj.shape
    vmem = pl.BlockSpec(memory_space=pltpu.VMEM)
    return pl.pallas_call(
        functools.partial(scan_forward, n_ctx, n_tp, width),
        name="scan_forward",
        out_shape=(
            jax.ShapeDtypeStruct((n_seq, length, chan), HALF),
            jax.ShapeDtypeStruct((n_seq, length, chan), FLOAT),
            jax.ShapeDtypeStruct((n_seq, length), FLOAT),
            jax.ShapeDtypeStruct((n_seq, chan), FLOAT),
        ),
        in_specs=[vmem] * 4,
        out_specs=[vmem] * 4,
        scratch_shapes=[
            pltpu.VMEM((n_seq, length, chan), FLOAT),
            pltpu.VMEM((n_seq, length, chan), FLOAT),
            pltpu.VMEM((n_ctx, 2, n_seq, chan), FLOAT),
            pltpu.VMEM((n_tp, n_seq, length), FLOAT),
            pltpu.SemaphoreType.DMA((n_ctx,)),
            pltpu.SemaphoreType.DMA((n_ctx,)),
            pltpu.SemaphoreType.DMA((n_tp,)),
            pltpu.SemaphoreType.DMA((n_tp,)),
        ],
        compiler_params=pltpu.CompilerParams(
            collective_id=0, has_side_effects=True, vmem_limit_bytes=40 * MIB
        ),
    )(proj, keep, gain, lower)


def scan_backward(
    n_ctx, n_tp, width,
    proj, keep, gain, lower, state, scale, carry_in, grad_gated,
    grad_proj, grad_gain, grad_lower,
    near, reach, rate_wide, cross_wide, ends, cross, ctx_send, ctx_recv, tp_send, tp_recv,
):
    n_seq, length, chan = state.shape
    greet(others("ctx", n_ctx) + others("tp", n_tp))
    low = lower[...].reshape(1, 1, chan)
    mine = lax.axis_index("tp")
    gain_total = jnp.zeros((8, chan), FLOAT)
    for seq in range(n_seq):
        for start in range(0, length, BLOCK):
            rows = slice(start, start + BLOCK)
            rate = columns(scale[seq : seq + 1, rows])
            rate_wide[seq, rows, :] = rate
            gate = proj[2, seq, rows, :]
            sig = jax.nn.sigmoid(gate)
            value = state[seq, rows, :]
            into = grad_gated[seq, rows, :]
            by_unit = into * value * widen(rate, chan)
            into_swish = into * (gate * sig)
            slope = sig * (1.0 + gate * (1.0 - sig))
            grad_proj[2, seq, rows, :] = (by_unit * gain[...] * slope).astype(HALF)
            gain_total = gain_total + jnp.sum((by_unit * (gate * sig)).reshape(-1, 8, chan), 0)
            grad_unit = into_swish * gain[...]
            near[seq, rows, :] = grad_unit
            cross[mine, seq : seq + 1, rows] = lane_sums(grad_unit * value)
    grad_gain[...] = jnp.sum(gain_total, 0, keepdims=True)
    share(cross, "tp", n_tp, tp_send, tp_recv)
    total = cross[0]
    for place in range(1, n_tp):
        total = total + cross[place]
    rate = scale[...]
    total = total * (rate * rate * rate) / width
    for seq in range(n_seq):
        for start in range(0, length, BLOCK):
            rows = slice(start, start + BLOCK)
            cross_wide[seq, rows, :] = columns(total[seq : seq + 1, rows])

    row = lax.broadcasted_iota(jnp.int32, (n_seq, GROUP, chan), 1)

    def back(index, carry):
        prod, above = carry
        rows = pl.ds(pl.multiple_of((length // GROUP - 1 - index) * GROUP, GROUP), GROUP)
        decay = low + (1.0 - low) * jax.nn.sigmoid(proj[1, :, rows, :])
        mult = decay * keep[:, rows, :]
        direct = (
            widen(rate_wide[:, rows, :], chan) * near[:, rows, :]
            - widen(cross_wide[:, rows, :], chan) * state[:, rows, :]
        )
        add = mult * direct
        for hop in (1, 2, 4):
            inside = row < GROUP - hop
            add = jnp.where(inside, mult * pltpu.roll(add, GROUP - hop, 1) + add, add)
            mult = jnp.where(inside, mult * pltpu.roll(mult, GROUP - hop, 1), mult)
        add = add + mult * above
        mult = mult * prod
        inside = row < GROUP - 1
        near[:, rows, :] = direct + jnp.where(inside, pltpu.roll(add, GROUP - 1, 1), above)
        reach[:, rows, :] = jnp.where(inside, pltpu.roll(mult, GROUP - 1, 1), prod)
        return mult[:, :1, :], add[:, :1, :]

    start = (jnp.ones((n_seq, 1, chan), FLOAT), jnp.zeros((n_seq, 1, chan), FLOAT))
    prod, total = lax.fori_loop(0, length // GROUP, back, start)
    here = lax.axis_index("ctx")
    ends[here, 0] = prod.reshape(n_seq, chan)
    ends[here, 1] = total.reshape(n_seq, chan)
    share(ends, "ctx", n_ctx, ctx_send, ctx_recv)
    carry = jnp.zeros((n_seq, chan), FLOAT)
    for place in range(n_ctx - 1, 0, -1):
        carry = jnp.where(place > here, ends[place, 1] + ends[place, 0] * carry, carry)
    carry = carry.reshape(n_seq, 1, chan)
    wide = 2 * GROUP
    first = lax.broadcasted_iota(jnp.int32, (n_seq, wide, chan), 1) == 0

    def finish(index, held):
        before, low_total = held
        rows = pl.ds(pl.multiple_of(index * wide, wide), wide)
        inp = proj[0, :, rows, :]
        sig = jax.nn.sigmoid(inp)
        silu = inp * sig
        fsig = jax.nn.sigmoid(proj[1, :, rows, :])
        rest = 1.0 - fsig
        decay = low + (1.0 - low) * fsig
        grad_state = near[:, rows, :] + reach[:, rows, :] * carry
        value = state[:, rows, :]
        prev = jnp.where(first, before, pltpu.roll(value, 1, 1))
        grad_decay = grad_state * (prev * keep[:, rows, :] - silu)
        grad_proj[0, :, rows, :] = (
            grad_state * (1.0 - decay) * (sig * (1.0 + inp * (1.0 - sig)))
        ).astype(HALF)
        grad_proj[1, :, rows, :] = (grad_decay * (1.0 - low) * fsig * rest).astype(HALF)
        return value[:, wide - 1 :, :], low_total + grad_decay * rest

    held = (carry_in[...].reshape(n_seq, 1, chan), jnp.zeros((n_seq, wide, chan), FLOAT))
    _, low_total = lax.fori_loop(0, length // wide, finish, held)
    grad_lower[...] = jnp.sum(jnp.sum(low_total, 0), 0, keepdims=True)


def run_scan_backward(
    proj, keep, gain, lower, state, scale, carry, grad_gated, n_ctx, n_tp, width
):
    _, n_seq, length, chan = proj.shape
    vmem = pl.BlockSpec(memory_space=pltpu.VMEM)
    return pl.pallas_call(
        functools.partial(scan_backward, n_ctx, n_tp, width),
        name="scan_backward",
        out_shape=(
            jax.ShapeDtypeStruct((3, n_seq, length, chan), HALF),
            jax.ShapeDtypeStruct((1, chan), FLOAT),
            jax.ShapeDtypeStruct((1, chan), FLOAT),
        ),
        in_specs=[vmem] * 8,
        out_specs=[vmem] * 3,
        scratch_shapes=[
            pltpu.VMEM((n_seq, length, chan), FLOAT),
            pltpu.VMEM((n_seq, length, chan), FLOAT),
            pltpu.VMEM((n_seq, length, BLOCK), FLOAT),
            pltpu.VMEM((n_seq, length, BLOCK), FLOAT),
            pltpu.VMEM((n_ctx, 2, n_seq, chan), FLOAT),
            pltpu.VMEM((n_tp, n_seq, length), FLOAT),
            pltpu.SemaphoreType.DMA((n_ctx,)),
            pltpu.SemaphoreType.DMA((n_ctx,)),
            pltpu.SemaphoreType.DMA((n_tp,)),
            pltpu.SemaphoreType.DMA((n_tp,)),
        ],
        compiler_params=pltpu.CompilerParams(
            collective_id=1, has_side_effects=True, vmem_limit_bytes=40 * MIB
        ),
    )(proj, keep, gain, lower, state, scale, carry, grad_gated)


def gather_fsdp(part, dim, count):
    if count != 2:
        return lax.all_gather(part, "fsdp", axis=dim, tiled=True)
    other = lax.ppermute(part, "fsdp", [(0, 1), (1, 0)])
    first = lax.axis_index("fsdp") == 0
    return jnp.concatenate(
        [jnp.where(first, part, other), jnp.where(first, other, part)], dim
    )


def keep_flags(segment_ids, count):
    last = lax.ppermute(
        segment_ids[:, -1:].astype(FLOAT), "ctx", [(place, place + 1) for place in range(count - 1)]
    )
    seg = segment_ids.astype(FLOAT)
    before = jnp.concatenate([last, seg[:, :-1]], 1)
    token = lax.broadcasted_iota(jnp.int32, seg.shape, 1)
    start = (token == 0) & (lax.axis_index("ctx") == 0)
    return jnp.where(start, 0.0, (seg == before).astype(FLOAT))


def local(
    sizes,
    tokens, segment_ids, w_in, w_out, w_glu, w_down, gain_one, gain_two, gate_gain, lower, cotangent,
):
    n_fsdp, n_ctx, n_tp = sizes
    n_seq, length, width = tokens.shape
    rows = n_seq * length
    chan = w_in.shape[2]
    gain_a = gather_fsdp(gain_one.astype(HALF)[None], 1, n_fsdp).astype(FLOAT)
    gain_b = gather_fsdp(gain_two.astype(HALF)[None], 1, n_fsdp).astype(FLOAT)
    w_in_all = gather_fsdp(w_in.astype(HALF), 1, n_fsdp)
    w_out_all = gather_fsdp(w_out.astype(HALF), 1, n_fsdp)
    w_glu_all = gather_fsdp(w_glu.astype(HALF), 0, n_fsdp)
    w_down_all = gather_fsdp(w_down.astype(HALF), 1, n_fsdp)
    keep = keep_flags(segment_ids, n_ctx)[..., None]
    gain_gate = gate_gain[None]
    low = lower[None]
    flat = tokens.reshape(rows, width).astype(FLOAT)
    scale_one = rms_scale(flat)
    normed = (flat * scale_one * gain_a).astype(HALF)
    proj = jnp.einsum("td,wdc->wtc", normed, w_in_all, preferred_element_type=FLOAT)
    proj = proj.reshape(3, n_seq, length, chan)
    gated, state, gate_scale, carry = run_scan_forward(
        proj, keep, gain_gate, low, n_ctx, n_tp, width
    )
    gated = gated.reshape(rows, chan)
    mixed = lax.psum(
        jnp.dot(gated, w_out_all, preferred_element_type=FLOAT).astype(HALF), "tp"
    ).astype(FLOAT)
    resid = flat + mixed
    scale_two = rms_scale(resid)
    normed_two = (resid * scale_two * gain_b).astype(HALF)
    glu = jnp.einsum("td,dwf->wtf", normed_two, w_glu_all, preferred_element_type=FLOAT)
    silu_glu = jax.nn.silu(glu[0])
    act = (silu_glu * glu[1]).astype(HALF)
    down = lax.psum(
        jnp.dot(act, w_down_all, preferred_element_type=FLOAT).astype(HALF), "tp"
    ).astype(FLOAT)
    output = (resid + down).astype(HALF).reshape(n_seq, length, width)
    grad_y_half = cotangent.reshape(rows, width)
    grad_y = grad_y_half.astype(FLOAT)
    grad_act = jnp.einsum("te,fe->tf", grad_y_half, w_down_all, preferred_element_type=FLOAT)
    grad_w_down = jnp.einsum("tf,te->fe", act, grad_y_half, preferred_element_type=FLOAT)
    grad_gate_pre = grad_act * glu[1] * silu_slope(glu[0])
    grad_up_pre = grad_act * silu_glu
    grad_glu = jnp.stack([grad_gate_pre, grad_up_pre]).astype(HALF)
    grad_normed_two = lax.psum(
        jnp.einsum("wtf,dwf->td", grad_glu, w_glu_all, preferred_element_type=FLOAT).astype(HALF),
        "tp",
    ).astype(FLOAT)
    grad_w_glu = jnp.einsum("td,wtf->dwf", normed_two, grad_glu, preferred_element_type=FLOAT)
    grad_gain_two = jnp.sum(grad_normed_two * resid * scale_two, 0)
    inner_two = gain_b * grad_normed_two
    grad_resid = (
        grad_y
        + scale_two * inner_two
        - resid * scale_two**3 * jnp.mean(inner_two * resid, -1, keepdims=True)
    )
    grad_mixed = grad_resid.astype(HALF)
    grad_gated = jnp.einsum(
        "te,ce->tc", grad_mixed, w_out_all, preferred_element_type=FLOAT
    ).reshape(n_seq, length, chan)
    grad_w_out = jnp.einsum("tc,te->ce", gated, grad_mixed, preferred_element_type=FLOAT)
    grad_proj, grad_gate_gain, grad_lower = run_scan_backward(
        proj, keep, gain_gate, low, state, gate_scale, carry, grad_gated, n_ctx, n_tp, width
    )
    grad_proj = grad_proj.reshape(3, rows, chan)
    grad_normed = lax.psum(
        jnp.einsum("wtc,wdc->td", grad_proj, w_in_all, preferred_element_type=FLOAT).astype(HALF),
        "tp",
    ).astype(FLOAT)
    grad_w_in = jnp.einsum("td,wtc->wdc", normed, grad_proj, preferred_element_type=FLOAT)
    grad_gain_one = jnp.sum(grad_normed * flat * scale_one, 0)
    inner_one = gain_a * grad_normed
    grad_tokens = (
        grad_resid
        + scale_one * inner_one
        - flat * scale_one**3 * jnp.mean(inner_one * flat, -1, keepdims=True)
    )
    pieces = [
        lax.psum(
            lax.psum_scatter(
                value.astype(HALF), "fsdp", scatter_dimension=dim, tiled=True
            ),
            "ctx",
        ).astype(FLOAT)
        for value, dim in (
            (grad_w_in, 1),
            (grad_w_out, 1),
            (grad_w_glu, 0),
            (grad_w_down, 1),
            (grad_gain_one, 0),
            (grad_gain_two, 0),
        )
    ]
    channel = lax.psum((grad_gate_gain[0], grad_lower[0]), ("fsdp", "ctx"))
    return (
        output,
        grad_tokens.reshape(n_seq, length, width),
        *pieces,
        channel[0],
        channel[1],
    )


def solution(mesh):
    sizes = tuple(mesh.shape[axis] for axis in ("fsdp", "ctx", "tp"))
    return jax.shard_map(
        functools.partial(local, sizes),
        mesh=mesh,
        in_specs=(
            P("fsdp", "ctx", None),
            P("fsdp", "ctx"),
            P(None, "fsdp", "tp"),
            P("tp", "fsdp"),
            P("fsdp", None, "tp"),
            P("tp", "fsdp"),
            P("fsdp"),
            P("fsdp"),
            P("tp"),
            P("tp"),
            P("fsdp", "ctx", None),
        ),
        out_specs=(
            P("fsdp", "ctx", None),
            P("fsdp", "ctx", None),
            P(None, "fsdp", "tp"),
            P("tp", "fsdp"),
            P("fsdp", None, "tp"),
            P("tp", "fsdp"),
            P("fsdp"),
            P("fsdp"),
            P("tp"),
            P("tp"),
        ),
        check_vma=False,
    )
```

```python
import functools

import jax
import jax.numpy as jnp
from jax import lax
from jax.experimental import pallas as pl
from jax.experimental.pallas import tpu as pltpu
from jax.sharding import PartitionSpec as P

EPS = 1e-06
FLOAT = jnp.float32
HALF = jnp.bfloat16
MESH = pl.DeviceIdType.MESH
GROUP = 8
BLOCK = 128
MIB = 1 << 20


def rms_scale(values):
    return lax.rsqrt(jnp.mean(values * values, -1, keepdims=True) + EPS)


def silu_slope(values):
    sig = jax.nn.sigmoid(values)
    return sig * (1.0 + values * (1.0 - sig))


def greet(peers):
    barrier = pltpu.get_barrier_semaphore()
    for peer in peers:
        pl.semaphore_signal(barrier, inc=1, device_id=peer, device_id_type=MESH)
    pl.semaphore_wait(barrier, len(peers))


def others(axis, count):
    mine = lax.axis_index(axis)
    return [{axis: lax.rem(mine + step, count)} for step in range(1, count)]


def share(slots, axis, count, send, recv):
    mine = lax.axis_index(axis)
    copies = [
        pltpu.make_async_remote_copy(
            src_ref=slots.at[mine],
            dst_ref=slots.at[mine],
            send_sem=send.at[step],
            recv_sem=recv.at[step],
            device_id=peer,
            device_id_type=MESH,
        )
        for step, peer in enumerate(others(axis, count))
    ]
    for copy in copies:
        copy.start()
    for copy in copies:
        copy.wait()


def lane_sums(values):
    part = values[:, :BLOCK]
    for start in range(BLOCK, values.shape[1], BLOCK):
        part = part + values[:, start : start + BLOCK]
    return jnp.sum(part.T, 0, keepdims=True)


def columns(row):
    return jnp.broadcast_to(row, (BLOCK, BLOCK)).T


def widen(values, chan):
    return jnp.concatenate([values] * (chan // BLOCK), -1)


def scan_forward(
    n_ctx, n_tp, width,
    proj, keep, gain, lower,
    gated, state, scale, carry_out,
    local, reach, ends, squares, ctx_send, ctx_recv, tp_send, tp_recv,
):
    n_seq, length, chan = state.shape
    greet(others("ctx", n_ctx) + others("tp", n_tp))
    low = lower[...].reshape(1, 1, chan)
    row = lax.broadcasted_iota(jnp.int32, (n_seq, GROUP, chan), 1)

    def step(index, carry):
        prod, total = carry
        rows = pl.ds(pl.multiple_of(index * GROUP, GROUP), GROUP)
        inp = proj[0, :, rows, :]
        decay = low + (1.0 - low) * jax.nn.sigmoid(proj[1, :, rows, :])
        add = inp * jax.nn.sigmoid(inp) * (1.0 - decay)
        mult = decay * keep[:, rows, :]
        for hop in (1, 2, 4):
            inside = row >= hop
            add = jnp.where(inside, mult * pltpu.roll(add, hop, 1) + add, add)
            mult = jnp.where(inside, mult * pltpu.roll(mult, hop, 1), mult)
        add = add + mult * total
        mult = mult * prod
        local[:, rows, :] = add
        reach[:, rows, :] = mult
        return mult[:, GROUP - 1 :, :], add[:, GROUP - 1 :, :]

    start = (jnp.ones((n_seq, 1, chan), FLOAT), jnp.zeros((n_seq, 1, chan), FLOAT))
    prod, total = lax.fori_loop(0, length // GROUP, step, start)
    here = lax.axis_index("ctx")
    ends[here, 0] = prod.reshape(n_seq, chan)
    ends[here, 1] = total.reshape(n_seq, chan)
    share(ends, "ctx", n_ctx, ctx_send, ctx_recv)
    carry = jnp.zeros((n_seq, chan), FLOAT)
    for place in range(n_ctx - 1):
        carry = jnp.where(place < here, ends[place, 1] + ends[place, 0] * carry, carry)
    carry_out[...] = carry
    mine = lax.axis_index("tp")
    for seq in range(n_seq):
        for start in range(0, length, BLOCK):
            rows = slice(start, start + BLOCK)
            value = local[seq, rows, :] + reach[seq, rows, :] * carry[seq : seq + 1]
            state[seq, rows, :] = value
            squares[mine, seq : seq + 1, rows] = lane_sums(value * value)
    share(squares, "tp", n_tp, tp_send, tp_recv)
    total = squares[0]
    for place in range(1, n_tp):
        total = total + squares[place]
    rate = lax.rsqrt(total / width + EPS)
    scale[...] = rate
    for seq in range(n_seq):
        for start in range(0, length, BLOCK):
            rows = slice(start, start + BLOCK)
            gate = proj[2, seq, rows, :]
            unit = state[seq, rows, :] * widen(columns(rate[seq : seq + 1, rows]), chan)
            gated[seq, rows, :] = (unit * gain[...] * (gate * jax.nn.sigmoid(gate))).astype(HALF)


def run_scan_forward(proj, keep, gain, lower, n_ctx, n_tp, width):
    _, n_seq, length, chan = proj.shape
    vmem = pl.BlockSpec(memory_space=pltpu.VMEM)
    return pl.pallas_call(
        functools.partial(scan_forward, n_ctx, n_tp, width),
        name="scan_forward",
        out_shape=(
            jax.ShapeDtypeStruct((n_seq, length, chan), HALF),
            jax.ShapeDtypeStruct((n_seq, length, chan), FLOAT),
            jax.ShapeDtypeStruct((n_seq, length), FLOAT),
            jax.ShapeDtypeStruct((n_seq, chan), FLOAT),
        ),
        in_specs=[vmem] * 4,
        out_specs=[vmem] * 4,
        scratch_shapes=[
            pltpu.VMEM((n_seq, length, chan), FLOAT),
            pltpu.VMEM((n_seq, length, chan), FLOAT),
            pltpu.VMEM((n_ctx, 2, n_seq, chan), FLOAT),
            pltpu.VMEM((n_tp, n_seq, length), FLOAT),
            pltpu.SemaphoreType.DMA((n_ctx,)),
            pltpu.SemaphoreType.DMA((n_ctx,)),
            pltpu.SemaphoreType.DMA((n_tp,)),
            pltpu.SemaphoreType.DMA((n_tp,)),
        ],
        compiler_params=pltpu.CompilerParams(
            collective_id=0, has_side_effects=True, vmem_limit_bytes=40 * MIB
        ),
    )(proj, keep, gain, lower)


def scan_backward(
    n_ctx, n_tp, width,
    proj, keep, gain, lower, state, scale, carry_in, grad_gated,
    grad_proj, grad_gain, grad_lower,
    near, reach, rate_wide, cross_wide, ends, cross, ctx_send, ctx_recv, tp_send, tp_recv,
):
    n_seq, length, chan = state.shape
    greet(others("ctx", n_ctx) + others("tp", n_tp))
    low = lower[...].reshape(1, 1, chan)
    mine = lax.axis_index("tp")
    gain_total = jnp.zeros((8, chan), FLOAT)
    for seq in range(n_seq):
        for start in range(0, length, BLOCK):
            rows = slice(start, start + BLOCK)
            rate = columns(scale[seq : seq + 1, rows])
            rate_wide[seq, rows, :] = rate
            gate = proj[2, seq, rows, :]
            sig = jax.nn.sigmoid(gate)
            value = state[seq, rows, :]
            into = grad_gated[seq, rows, :]
            by_unit = into * value * widen(rate, chan)
            into_swish = into * (gate * sig)
            slope = sig * (1.0 + gate * (1.0 - sig))
            grad_proj[2, seq, rows, :] = (by_unit * gain[...] * slope).astype(HALF)
            gain_total = gain_total + jnp.sum((by_unit * (gate * sig)).reshape(-1, 8, chan), 0)
            grad_unit = into_swish * gain[...]
            near[seq, rows, :] = grad_unit
            cross[mine, seq : seq + 1, rows] = lane_sums(grad_unit * value)
    grad_gain[...] = jnp.sum(gain_total, 0, keepdims=True)
    share(cross, "tp", n_tp, tp_send, tp_recv)
    total = cross[0]
    for place in range(1, n_tp):
        total = total + cross[place]
    rate = scale[...]
    total = total * (rate * rate * rate) / width
    for seq in range(n_seq):
        for start in range(0, length, BLOCK):
            rows = slice(start, start + BLOCK)
            cross_wide[seq, rows, :] = columns(total[seq : seq + 1, rows])

    row = lax.broadcasted_iota(jnp.int32, (n_seq, GROUP, chan), 1)

    def back(index, carry):
        prod, above = carry
        rows = pl.ds(pl.multiple_of((length // GROUP - 1 - index) * GROUP, GROUP), GROUP)
        decay = low + (1.0 - low) * jax.nn.sigmoid(proj[1, :, rows, :])
        mult = decay * keep[:, rows, :]
        direct = (
            widen(rate_wide[:, rows, :], chan) * near[:, rows, :]
            - widen(cross_wide[:, rows, :], chan) * state[:, rows, :]
        )
        add = mult * direct
        for hop in (1, 2, 4):
            inside = row < GROUP - hop
            add = jnp.where(inside, mult * pltpu.roll(add, GROUP - hop, 1) + add, add)
            mult = jnp.where(inside, mult * pltpu.roll(mult, GROUP - hop, 1), mult)
        add = add + mult * above
        mult = mult * prod
        inside = row < GROUP - 1
        near[:, rows, :] = direct + jnp.where(inside, pltpu.roll(add, GROUP - 1, 1), above)
        reach[:, rows, :] = jnp.where(inside, pltpu.roll(mult, GROUP - 1, 1), prod)
        return mult[:, :1, :], add[:, :1, :]

    start = (jnp.ones((n_seq, 1, chan), FLOAT), jnp.zeros((n_seq, 1, chan), FLOAT))
    prod, total = lax.fori_loop(0, length // GROUP, back, start)
    here = lax.axis_index("ctx")
    ends[here, 0] = prod.reshape(n_seq, chan)
    ends[here, 1] = total.reshape(n_seq, chan)
    share(ends, "ctx", n_ctx, ctx_send, ctx_recv)
    carry = jnp.zeros((n_seq, chan), FLOAT)
    for place in range(n_ctx - 1, 0, -1):
        carry = jnp.where(place > here, ends[place, 1] + ends[place, 0] * carry, carry)
    carry = carry.reshape(n_seq, 1, chan)
    wide = 2 * GROUP
    first = lax.broadcasted_iota(jnp.int32, (n_seq, wide, chan), 1) == 0

    def finish(index, held):
        before, low_total = held
        rows = pl.ds(pl.multiple_of(index * wide, wide), wide)
        inp = proj[0, :, rows, :]
        sig = jax.nn.sigmoid(inp)
        silu = inp * sig
        fsig = jax.nn.sigmoid(proj[1, :, rows, :])
        rest = 1.0 - fsig
        decay = low + (1.0 - low) * fsig
        grad_state = near[:, rows, :] + reach[:, rows, :] * carry
        value = state[:, rows, :]
        prev = jnp.where(first, before, pltpu.roll(value, 1, 1))
        grad_decay = grad_state * (prev * keep[:, rows, :] - silu)
        grad_proj[0, :, rows, :] = (
            grad_state * (1.0 - decay) * (sig * (1.0 + inp * (1.0 - sig)))
        ).astype(HALF)
        grad_proj[1, :, rows, :] = (grad_decay * (1.0 - low) * fsig * rest).astype(HALF)
        return value[:, wide - 1 :, :], low_total + grad_decay * rest

    held = (carry_in[...].reshape(n_seq, 1, chan), jnp.zeros((n_seq, wide, chan), FLOAT))
    _, low_total = lax.fori_loop(0, length // wide, finish, held)
    grad_lower[...] = jnp.sum(jnp.sum(low_total, 0), 0, keepdims=True)


def run_scan_backward(
    proj, keep, gain, lower, state, scale, carry, grad_gated, n_ctx, n_tp, width
):
    _, n_seq, length, chan = proj.shape
    vmem = pl.BlockSpec(memory_space=pltpu.VMEM)
    return pl.pallas_call(
        functools.partial(scan_backward, n_ctx, n_tp, width),
        name="scan_backward",
        out_shape=(
            jax.ShapeDtypeStruct((3, n_seq, length, chan), HALF),
            jax.ShapeDtypeStruct((1, chan), FLOAT),
            jax.ShapeDtypeStruct((1, chan), FLOAT),
        ),
        in_specs=[vmem] * 8,
        out_specs=[vmem] * 3,
        scratch_shapes=[
            pltpu.VMEM((n_seq, length, chan), FLOAT),
            pltpu.VMEM((n_seq, length, chan), FLOAT),
            pltpu.VMEM((n_seq, length, BLOCK), FLOAT),
            pltpu.VMEM((n_seq, length, BLOCK), FLOAT),
            pltpu.VMEM((n_ctx, 2, n_seq, chan), FLOAT),
            pltpu.VMEM((n_tp, n_seq, length), FLOAT),
            pltpu.SemaphoreType.DMA((n_ctx,)),
            pltpu.SemaphoreType.DMA((n_ctx,)),
            pltpu.SemaphoreType.DMA((n_tp,)),
            pltpu.SemaphoreType.DMA((n_tp,)),
        ],
        compiler_params=pltpu.CompilerParams(
            collective_id=1, has_side_effects=True, vmem_limit_bytes=40 * MIB
        ),
    )(proj, keep, gain, lower, state, scale, carry, grad_gated)


CHUNK = 256
PIECES = 4
TILE = 256


def dot(lhs, rhs):
    return jnp.dot(lhs, rhs, preferred_element_type=FLOAT)


def dot_nt(lhs, rhs):
    return lax.dot_general(lhs, rhs, (((1,), (1,)), ((), ())), preferred_element_type=FLOAT)


class Line:
    def __init__(self, held, cross, total, sems):
        self.held, self.cross, self.total, self.sems = held, cross, total, sems
        place = lax.axis_index("tp")
        self.inner = (place == 1) | (place == 2)
        self.side = place + 1 - 2 * lax.rem(place, 2)
        self.facing = 3 - place

    def slot(self, job):
        slots = self.held.shape[0]
        return job if slots == self.total.shape[0] else lax.rem(job, slots)

    def copy(self, source, target, send, recv, place):
        return pltpu.make_async_remote_copy(
            src_ref=source,
            dst_ref=target,
            send_sem=send,
            recv_sem=recv,
            device_id={"tp": place},
            device_id_type=MESH,
        )

    def inward(self, job, q):
        send, recv, _, _ = self.sems
        return self.copy(
            self.held.at[self.slot(job), q], self.total.at[job, q],
            send.at[job, q], recv.at[job, q], self.side,
        )

    def outward(self, job, q):
        send, recv, _, _ = self.sems
        return self.copy(
            self.total.at[job, q], self.total.at[job, q],
            send.at[job, q], recv.at[job, q], self.side,
        )

    def across(self, job, q):
        _, _, send, recv = self.sems
        return self.copy(
            self.held.at[self.slot(job), q], self.cross.at[self.slot(job), q],
            send.at[job, q], recv.at[job, q], self.facing,
        )

    def offer(self, job, q):
        @pl.when(jnp.logical_not(self.inner))
        def _():
            self.inward(job, q).start()

    def tick(self, job, step):
        slot = self.slot(job)

        @pl.when(self.inner)
        def _():
            if step < PIECES:
                self.inward(job, step).wait_recv()
                value = self.held[slot, step].astype(FLOAT) + self.total[job, step].astype(FLOAT)
                self.held[slot, step] = value.astype(HALF)
                self.across(job, step).start()
            if step > 0:
                q = step - 1
                self.across(job, q).wait_recv()
                value = self.held[slot, q].astype(FLOAT) + self.cross[slot, q].astype(FLOAT)
                self.total[job, q] = value.astype(HALF)
                self.outward(job, q).start()

    def relay(self, job):
        for step in range(PIECES + 1):
            self.tick(job, step)

    def arrive(self, job):
        @pl.when(jnp.logical_not(self.inner))
        def _():
            @pl.loop(0, PIECES)
            def _(q):
                self.outward(job, q).wait_recv()

    def release(self, job):
        @pl.when(self.inner)
        def _():
            @pl.loop(0, PIECES)
            def _(q):
                self.across(job, q).wait_send()

        @pl.when(jnp.logical_not(self.inner))
        def _():
            @pl.loop(0, PIECES)
            def _(q):
                self.inward(job, q).wait_send()

    def settle(self, job):
        @pl.when(self.inner)
        def _():
            @pl.loop(0, PIECES)
            def _(q):
                self.outward(job, q).wait_send()


def pull(parts, wholes, dims, n_fsdp, own_sem, send_sem, recv_sem):
    if n_fsdp != 2:
        copies = [
            pltpu.make_async_copy(part, whole, own_sem.at[index])
            for index, (part, whole) in enumerate(zip(parts, wholes))
        ]
        for copy in copies:
            copy.start()
        return lambda index: copies[index].wait()
    mine = lax.axis_index("fsdp")
    near, far = [], []
    for index, (part, whole, dim) in enumerate(zip(parts, wholes, dims)):
        size = part.shape[dim]
        at = pl.ds(pl.multiple_of(mine * size, size), size)
        place = whole.at[at] if dim == 0 else whole.at[:, at]
        near.append(pltpu.make_async_copy(part, place, own_sem.at[index]))
        far.append(
            pltpu.make_async_remote_copy(
                src_ref=part,
                dst_ref=place,
                send_sem=send_sem.at[index],
                recv_sem=recv_sem.at[index],
                device_id={"fsdp": 1 - mine},
                device_id_type=MESH,
            )
        )
    for one, two in zip(near, far):
        two.start()
        one.start()

    def wait(index):
        near[index].wait()
        far[index].wait()

    return wait


def row_blocks(count, size, body):
    @pl.loop(0, count // size)
    def _(index):
        body(pl.ds(pl.multiple_of(index * size, size), size))


def line_peers():
    place = lax.axis_index("tp")
    return [{"tp": place + 1 - 2 * lax.rem(place, 2)}, {"tp": 3 - place}]


def joined(ref, c, rows):
    return jnp.concatenate([ref[c, q, rows, :].astype(FLOAT) for q in range(PIECES)], -1)


def middle(
    n_fsdp,
    gated, tokens, cotangent, gain, wo_part, wg_part, wu_part, wd_part,
    mixed_out, normed_out, act_out, grad_glu_out, down_out, grad_resid_out, grad_mixed_out,
    grad_gated_out, grad_gain_out,
    wo, wg, wu, wd, x_all, dy_all, held, crossed, total, normed, act, grad_glu, down,
    grad_resid, grad_mixed, grad_gated, gain_total,
    own_sem, send_sem, recv_sem, load_sem, store_sem, *line_sems,
):
    n_chunks, _, _, piece = held.shape
    units = wd.shape[0]
    width = wd.shape[1]
    peers = line_peers()
    if n_fsdp == 2:
        peers.append({"fsdp": 1 - lax.axis_index("fsdp")})
    greet(peers)
    ready = pull(
        (wo_part, wg_part, wu_part, wd_part), (wo, wg, wu, wd), (1, 0, 0, 1),
        n_fsdp, own_sem, send_sem, recv_sem,
    )
    loads = [
        pltpu.make_async_copy(tokens, x_all, load_sem.at[0]),
        pltpu.make_async_copy(cotangent, dy_all, load_sem.at[1]),
    ]
    for load in loads:
        load.start()
    line = Line(held, crossed, total, line_sems)

    def chunk_rows(c):
        return pl.ds(pl.multiple_of(c * CHUNK, CHUNK), CHUNK)

    def stores(c, wanted=None):
        rows = chunk_rows(c)
        pairs = [
            (normed, normed_out.at[rows]),
            (act, act_out.at[rows]),
            (grad_glu.at[0], grad_glu_out.at[0, rows]),
            (grad_glu.at[1], grad_glu_out.at[1, rows]),
            (down, down_out.at[rows]),
            (grad_resid, grad_resid_out.at[rows]),
            (grad_mixed, grad_mixed_out.at[rows]),
            (grad_gated, grad_gated_out.at[rows]),
        ]
        pairs += [
            (total.at[c, q], mixed_out.at[rows, pl.ds(q * piece, piece)]) for q in range(PIECES)
        ]
        return [
            pltpu.make_async_copy(source, target, store_sem.at[index])
            for index, (source, target) in enumerate(pairs)
            if wanted is None or index in wanted
        ]

    FORWARD = (0, 1, 2, 3, 4, 8, 9, 10, 11)
    BACKWARD = (5, 6, 7)

    ready(0)

    @pl.loop(0, n_chunks)
    def _(c):
        lhs = gated[chunk_rows(c), :]

        @pl.loop(0, PIECES)
        def _(q):
            for half in range(piece // TILE):
                cols = pl.ds(pl.multiple_of(q * piece + half * TILE, TILE), TILE)
                held[c, q, :, half * TILE : (half + 1) * TILE] = dot(lhs, wo[:, cols]).astype(HALF)
            line.offer(c, q)

    for load in loads:
        load.wait()
    line.relay(0)
    for index in (1, 2, 3):
        ready(index)

    @pl.loop(0, n_chunks)
    def _(c):
        line.arrive(c)
        line.tick(c + 1, 0)

        @pl.when(c > 0)
        def _():
            for store in stores(c - 1, FORWARD):
                store.wait()

        def norm(rows):
            at = pl.ds(pl.multiple_of(c * CHUNK + rows.start, 16), rows.size)
            resid = x_all[at, :].astype(FLOAT) + joined(total, c, rows)
            normed[rows, :] = (resid * rms_scale(resid) * gain[...]).astype(HALF)

        row_blocks(CHUNK, 16, norm)

        def unit(cols):
            glu_gate = dot(normed[...], wg[:, cols])
            glu_up = dot(normed[...], wu[:, cols])
            grad_act = dot_nt(dy_all[chunk_rows(c), :], wd[cols, :])
            sig = jax.nn.sigmoid(glu_gate)
            silu = glu_gate * sig
            act[:, cols] = (silu * glu_up).astype(HALF)
            slope = sig * (1.0 + glu_gate * (1.0 - sig))
            grad_glu[0, :, cols] = (grad_act * glu_up * slope).astype(HALF)
            grad_glu[1, :, cols] = (grad_act * silu).astype(HALF)

        def units_from(start, stop):
            @pl.loop(start, stop)
            def _(index):
                unit(pl.ds(pl.multiple_of(index * TILE, TILE), TILE))

        half_way = units // TILE // 2
        units_from(0, half_way)
        line.tick(c + 1, 1)
        units_from(half_way, units // TILE)
        if units % TILE:
            unit(pl.ds(units - units % TILE, units % TILE))
        line.tick(c + 1, 2)
        line.release(c)

        @pl.loop(0, PIECES)
        def _(q):
            @pl.when(q == PIECES // 2)
            def _():
                line.tick(c + 1, 3)

            for half in range(piece // TILE):
                at = pl.ds(pl.multiple_of(q * piece + half * TILE, TILE), TILE)
                value = dot_nt(grad_glu[0], wg[at, :]) + dot_nt(grad_glu[1], wu[at, :])
                held[c, q, :, half * TILE : (half + 1) * TILE] = value.astype(HALF)
            line.offer(n_chunks + c, q)

        line.tick(c + 1, 4)

        @pl.loop(0, width // TILE)
        def _(index):
            cols = pl.ds(pl.multiple_of(index * TILE, TILE), TILE)
            down[:, cols] = dot(act[...], wd[:, cols]).astype(HALF)

        for store in stores(c, FORWARD):
            store.start()

    gain_total[...] = jnp.zeros_like(gain_total)

    @pl.loop(0, n_chunks)
    def _(c):
        @pl.when(c > 0)
        def _():
            line.relay(n_chunks + c)

        line.arrive(n_chunks + c)

        @pl.when(c > 0)
        def _():
            for store in stores(c - 1, BACKWARD):
                store.wait()

        def norm_back(rows):
            at = pl.ds(pl.multiple_of(c * CHUNK + rows.start, 16), rows.size)
            resid = x_all[at, :].astype(FLOAT) + joined(total, c, rows)
            rate = rms_scale(resid)
            grad = joined(total, n_chunks + c, rows)
            by_gain = grad * (resid * rate)
            gain_total[...] += by_gain[:8] + by_gain[8:]
            inner = gain[...] * grad
            mean = jnp.mean(inner * resid, -1, keepdims=True)
            value = dy_all[at, :].astype(FLOAT) + rate * inner - resid * (rate * rate * rate * mean)
            grad_resid[rows, :] = value
            grad_mixed[rows, :] = value.astype(HALF)

        row_blocks(CHUNK, 16, norm_back)
        for start in range(0, grad_gated.shape[1], TILE):
            grad_gated[:, start : start + TILE] = dot_nt(
                grad_mixed[...], wo[start : start + TILE, :]
            )
        for store in stores(c, BACKWARD):
            store.start()

    grad_gain_out[...] = jnp.sum(gain_total[...], 0, keepdims=True)
    for store in stores(n_chunks - 1):
        store.wait()

    @pl.loop(0, n_chunks)
    def _(c):
        line.settle(c)
        line.settle(n_chunks + c)
        line.release(n_chunks + c)


def run_middle(gated, tokens, cotangent, gain, parts, n_fsdp):
    rows, chan = gated.shape
    width = tokens.shape[1]
    wg = parts[1]
    units = wg.shape[1]
    n_chunks = rows // CHUNK
    piece = width // PIECES
    vmem = pl.BlockSpec(memory_space=pltpu.VMEM)
    hbm = pl.BlockSpec(memory_space=pl.ANY)
    sems = pltpu.SemaphoreType.DMA((2 * n_chunks, PIECES))
    return pl.pallas_call(
        functools.partial(middle, n_fsdp),
        name="middle",
        out_shape=(
            jax.ShapeDtypeStruct((rows, width), HALF),
            jax.ShapeDtypeStruct((rows, width), HALF),
            jax.ShapeDtypeStruct((rows, units), HALF),
            jax.ShapeDtypeStruct((2, rows, units), HALF),
            jax.ShapeDtypeStruct((rows, width), HALF),
            jax.ShapeDtypeStruct((rows, width), FLOAT),
            jax.ShapeDtypeStruct((rows, width), HALF),
            jax.ShapeDtypeStruct((rows, chan), FLOAT),
            jax.ShapeDtypeStruct((1, width), FLOAT),
        ),
        in_specs=[vmem, hbm, hbm, vmem, hbm, hbm, hbm, hbm],
        out_specs=[hbm] * 8 + [vmem],
        scratch_shapes=[
            pltpu.VMEM((chan, width), HALF),
            pltpu.VMEM((width, units), HALF),
            pltpu.VMEM((width, units), HALF),
            pltpu.VMEM((units, width), HALF),
            pltpu.VMEM((rows, width), HALF),
            pltpu.VMEM((rows, width), HALF),
            pltpu.VMEM((n_chunks, PIECES, CHUNK, piece), HALF),
            pltpu.VMEM((n_chunks, PIECES, CHUNK, piece), HALF),
            pltpu.VMEM((2 * n_chunks, PIECES, CHUNK, piece), HALF),
            pltpu.VMEM((CHUNK, width), HALF),
            pltpu.VMEM((CHUNK, units), HALF),
            pltpu.VMEM((2, CHUNK, units), HALF),
            pltpu.VMEM((CHUNK, width), HALF),
            pltpu.VMEM((CHUNK, width), FLOAT),
            pltpu.VMEM((CHUNK, width), HALF),
            pltpu.VMEM((CHUNK, chan), FLOAT),
            pltpu.VMEM((8, width), FLOAT),
            pltpu.SemaphoreType.DMA((4,)),
            pltpu.SemaphoreType.DMA((4,)),
            pltpu.SemaphoreType.DMA((4,)),
            pltpu.SemaphoreType.DMA((2,)),
            pltpu.SemaphoreType.DMA((12,)),
        ]
        + [sems] * 4,
        compiler_params=pltpu.CompilerParams(
            collective_id=2, has_side_effects=True, vmem_limit_bytes=63 * MIB
        ),
        cost_estimate=pl.CostEstimate(
            flops=16 * rows * width * units, bytes_accessed=400 * MIB, transcendentals=0
        ),
    )(gated, tokens, cotangent, gain, *parts)


def tail(
    n_fsdp, n_ctx,
    grad_proj, gain, vectors, w_in, down, grad_resid, tokens, mixed,
    grad_tokens_out, output_out, vectors_out,
    w_all, resid_all, x_all, mixed_all, held, crossed, total, gain_total, over_ctx, over_fsdp,
    load_sem, down_sem, store_sem, ctx_send, ctx_recv, fsdp_send, fsdp_recv, *line_sems,
):
    rows, width = x_all.shape
    n_chunks = rows // CHUNK
    piece = width // PIECES
    greet(line_peers() + others("ctx", n_ctx) + others("fsdp", n_fsdp))
    loads = [
        pltpu.make_async_copy(source, target, load_sem.at[index])
        for index, (source, target) in enumerate(
            [(w_in, w_all), (grad_resid, resid_all), (tokens, x_all), (mixed, mixed_all)]
        )
    ]
    for load in loads:
        load.start()

    def chunk_rows(c):
        return pl.ds(pl.multiple_of(c * CHUNK, CHUNK), CHUNK)

    def down_load(c, q):
        cols = pl.ds(pl.multiple_of(q * piece, piece), piece)
        return pltpu.make_async_copy(
            down.at[chunk_rows(c), cols], held.at[n_chunks + c, q], down_sem.at[c, q]
        )

    def every(body):
        @pl.loop(0, n_chunks)
        def _(c):
            @pl.loop(0, PIECES)
            def _(q):
                body(c, q)

    every(lambda c, q: down_load(c, q).start())
    line = Line(held, crossed, total, line_sems)
    loads[0].wait()

    def term(c, q):
        for half in range(piece // TILE):
            at = pl.ds(pl.multiple_of(q * piece + half * TILE, TILE), TILE)
            value = dot_nt(grad_proj[0, chunk_rows(c), :], w_all[0, at, :])
            for gate in (1, 2):
                value = value + dot_nt(grad_proj[gate, chunk_rows(c), :], w_all[gate, at, :])
            held[c, q, :, half * TILE : (half + 1) * TILE] = value.astype(HALF)
        line.offer(c, q)

    every(term)

    def hand_on(c, q):
        down_load(c, q).wait()
        line.offer(n_chunks + c, q)

    every(hand_on)
    for load in loads[1:]:
        load.wait()
    gain_total[...] = jnp.zeros_like(gain_total)
    line.relay(0)

    def token_store(c):
        at = chunk_rows(c)
        return pltpu.make_async_copy(resid_all.at[at], grad_tokens_out.at[at], store_sem.at[0, c])

    def output_store(c):
        at = chunk_rows(c)
        return pltpu.make_async_copy(mixed_all.at[at], output_out.at[at], store_sem.at[1, c])

    @pl.loop(0, n_chunks)
    def _(c):
        line.arrive(c)
        for quarter in range(PIECES):
            line.tick(c + 1, quarter)

            @pl.loop(0, CHUNK // PIECES // 16)
            def _(index):
                start = quarter * (CHUNK // PIECES) + index * 16
                rows = pl.ds(pl.multiple_of(start, 16), 16)
                at = pl.ds(pl.multiple_of(c * CHUNK + start, 16), 16)
                value = x_all[at, :].astype(FLOAT)
                rate = rms_scale(value)
                grad = joined(total, c, rows)
                by_gain = grad * (value * rate)
                gain_total[...] += by_gain[:8] + by_gain[8:]
                inner = gain[...] * grad
                mean = jnp.mean(inner * value, -1, keepdims=True)
                resid_all[at, :] = (
                    resid_all[at, :] + rate * inner - value * (rate * rate * rate * mean)
                )

        line.tick(c + 1, PIECES)
        token_store(c).start()

    here = lax.axis_index("ctx")
    over_ctx[here, :, width:] = vectors[...]
    over_ctx[here, :, :width] = jnp.sum(gain_total[...], 0, keepdims=True)
    share(over_ctx, "ctx", n_ctx, ctx_send, ctx_recv)
    value = over_ctx[0]
    for place in range(1, n_ctx):
        value = value + over_ctx[place]
    over_fsdp[lax.axis_index("fsdp")] = value
    share(over_fsdp, "fsdp", n_fsdp, fsdp_send, fsdp_recv)
    value = over_fsdp[0]
    for place in range(1, n_fsdp):
        value = value + over_fsdp[place]
    vectors_out[...] = value

    @pl.loop(0, n_chunks)
    def _(c):
        job = n_chunks + c
        line.arrive(job)

        @pl.when(c + 1 < n_chunks)
        def _():
            line.relay(job + 1)

        @pl.loop(0, CHUNK // 16)
        def _(index):
            rows = pl.ds(pl.multiple_of(index * 16, 16), 16)
            at = pl.ds(pl.multiple_of(c * CHUNK + index * 16, 16), 16)
            value = x_all[at, :].astype(FLOAT) + mixed_all[at, :].astype(FLOAT)
            mixed_all[at, :] = (value + joined(total, job, rows)).astype(HALF)

        output_store(c).start()

    for c in range(n_chunks):
        token_store(c).wait()
        output_store(c).wait()

    @pl.loop(0, 2 * n_chunks)
    def _(job):
        line.settle(job)
        line.release(job)


def run_tail(grad_proj, gain, vectors, w_in, down, grad_resid, tokens, mixed, n_fsdp, n_ctx):
    _, rows, chan = grad_proj.shape
    width = tokens.shape[1]
    n_chunks = rows // CHUNK
    piece = width // PIECES
    size = width + vectors.shape[1]
    vmem = pl.BlockSpec(memory_space=pltpu.VMEM)
    hbm = pl.BlockSpec(memory_space=pl.ANY)
    slots = pltpu.VMEM((2 * n_chunks, PIECES, CHUNK, piece), HALF)
    sems = pltpu.SemaphoreType.DMA((2 * n_chunks, PIECES))
    return pl.pallas_call(
        functools.partial(tail, n_fsdp, n_ctx),
        name="tail",
        out_shape=(
            jax.ShapeDtypeStruct((rows, width), FLOAT),
            jax.ShapeDtypeStruct((rows, width), HALF),
            jax.ShapeDtypeStruct((1, size), FLOAT),
        ),
        in_specs=[vmem] * 3 + [hbm] * 5,
        out_specs=[hbm, hbm, vmem],
        scratch_shapes=[
            pltpu.VMEM((3, width, chan), HALF),
            pltpu.VMEM((rows, width), FLOAT),
            pltpu.VMEM((rows, width), HALF),
            pltpu.VMEM((rows, width), HALF),
            slots,
            slots,
            slots,
            pltpu.VMEM((8, width), FLOAT),
            pltpu.VMEM((n_ctx, 1, size), FLOAT),
            pltpu.VMEM((n_fsdp, 1, size), FLOAT),
            pltpu.SemaphoreType.DMA((4,)),
            pltpu.SemaphoreType.DMA((n_chunks, PIECES)),
            pltpu.SemaphoreType.DMA((2, n_chunks)),
            pltpu.SemaphoreType.DMA((n_ctx,)),
            pltpu.SemaphoreType.DMA((n_ctx,)),
            pltpu.SemaphoreType.DMA((n_fsdp,)),
            pltpu.SemaphoreType.DMA((n_fsdp,)),
        ]
        + [sems] * 4,
        compiler_params=pltpu.CompilerParams(
            collective_id=3, has_side_effects=True, vmem_limit_bytes=63 * MIB
        ),
        cost_estimate=pl.CostEstimate(
            flops=6 * rows * width * chan, bytes_accessed=700 * MIB, transcendentals=0
        ),
    )(grad_proj, gain, vectors, w_in, down, grad_resid, tokens, mixed)


def gather_fsdp(part, dim, count):
    if count != 2:
        return lax.all_gather(part, "fsdp", axis=dim, tiled=True)
    other = lax.ppermute(part, "fsdp", [(0, 1), (1, 0)])
    first = lax.axis_index("fsdp") == 0
    return jnp.concatenate(
        [jnp.where(first, part, other), jnp.where(first, other, part)], dim
    )


def keep_flags(segment_ids, count):
    last = lax.ppermute(
        segment_ids[:, -1:].astype(FLOAT), "ctx", [(place, place + 1) for place in range(count - 1)]
    )
    seg = segment_ids.astype(FLOAT)
    before = jnp.concatenate([last, seg[:, :-1]], 1)
    token = lax.broadcasted_iota(jnp.int32, seg.shape, 1)
    start = (token == 0) & (lax.axis_index("ctx") == 0)
    return jnp.where(start, 0.0, (seg == before).astype(FLOAT))


def local(
    sizes,
    tokens, segment_ids, w_in, w_out, w_glu, w_down, gain_one, gain_two, gate_gain, lower, cotangent,
):
    n_fsdp, n_ctx, n_tp = sizes
    n_seq, length, width = tokens.shape
    rows = n_seq * length
    chan = w_in.shape[2]
    gain_a = gather_fsdp(gain_one.astype(HALF)[None], 1, n_fsdp).astype(FLOAT)
    gain_b = gather_fsdp(gain_two.astype(HALF)[None], 1, n_fsdp).astype(FLOAT)
    w_in_all = gather_fsdp(w_in.astype(HALF), 1, n_fsdp)
    parts = (w_out.astype(HALF), w_glu[:, 0].astype(HALF), w_glu[:, 1].astype(HALF), w_down.astype(HALF))
    if n_fsdp != 2:
        parts = tuple(gather_fsdp(part, dim, n_fsdp) for part, dim in zip(parts, (1, 0, 0, 1)))
    keep = keep_flags(segment_ids, n_ctx)[..., None]
    gain_gate = gate_gain[None]
    low = lower[None]
    flat = tokens.reshape(rows, width).astype(FLOAT)
    scale_one = rms_scale(flat)
    normed = (flat * scale_one * gain_a).astype(HALF)
    proj = jnp.einsum("td,wdc->wtc", normed, w_in_all, preferred_element_type=FLOAT)
    proj = proj.reshape(3, n_seq, length, chan)
    gated, state, gate_scale, carry = run_scan_forward(
        proj, keep, gain_gate, low, n_ctx, n_tp, width
    )
    gated = gated.reshape(rows, chan)
    grad_y_half = cotangent.reshape(rows, width)
    (
        mixed, normed_two, act, grad_glu, down, grad_resid, grad_mixed, grad_gated, grad_gain_two
    ) = run_middle(gated, tokens.reshape(rows, width), grad_y_half, gain_b, parts, n_fsdp)
    grad_w_down = jnp.einsum("tf,te->fe", act, grad_y_half, preferred_element_type=FLOAT)
    grad_w_glu = jnp.einsum("td,wtf->dwf", normed_two, grad_glu, preferred_element_type=FLOAT)
    grad_gated = grad_gated.reshape(n_seq, length, chan)
    grad_w_out = jnp.einsum("tc,te->ce", gated, grad_mixed, preferred_element_type=FLOAT)
    grad_proj, grad_gate_gain, grad_lower = run_scan_backward(
        proj, keep, gain_gate, low, state, gate_scale, carry, grad_gated, n_ctx, n_tp, width
    )
    grad_proj = grad_proj.reshape(3, rows, chan)
    vectors = jnp.concatenate([grad_gain_two, grad_gate_gain, grad_lower], 1)
    grad_tokens, output, vectors = run_tail(
        grad_proj, gain_a, vectors, w_in_all, down, grad_resid,
        tokens.reshape(rows, width), mixed, n_fsdp, n_ctx,
    )
    grad_w_in = jnp.einsum("td,wtc->wdc", normed, grad_proj, preferred_element_type=FLOAT)
    pieces = [
        lax.psum(
            lax.psum_scatter(
                value.astype(HALF), "fsdp", scatter_dimension=dim, tiled=True
            ),
            "ctx",
        ).astype(FLOAT)
        for value, dim in (
            (grad_w_in, 1),
            (grad_w_out, 1),
            (grad_w_glu, 0),
            (grad_w_down, 1),
        )
    ]
    part = gain_one.shape[0]
    begin = lax.axis_index("fsdp") * part
    return (
        output.reshape(n_seq, length, width),
        grad_tokens.reshape(n_seq, length, width),
        *pieces,
        lax.dynamic_slice(vectors[0], (begin,), (part,)),
        lax.dynamic_slice(vectors[0], (width + begin,), (part,)),
        vectors[0, 2 * width : 2 * width + chan],
        vectors[0, 2 * width + chan :],
    )


def solution(mesh):
    sizes = tuple(mesh.shape[axis] for axis in ("fsdp", "ctx", "tp"))
    return jax.shard_map(
        functools.partial(local, sizes),
        mesh=mesh,
        in_specs=(
            P("fsdp", "ctx", None),
            P("fsdp", "ctx"),
            P(None, "fsdp", "tp"),
            P("tp", "fsdp"),
            P("fsdp", None, "tp"),
            P("tp", "fsdp"),
            P("fsdp"),
            P("fsdp"),
            P("tp"),
            P("tp"),
            P("fsdp", "ctx", None),
        ),
        out_specs=(
            P("fsdp", "ctx", None),
            P("fsdp", "ctx", None),
            P(None, "fsdp", "tp"),
            P("tp", "fsdp"),
            P("fsdp", None, "tp"),
            P("tp", "fsdp"),
            P("fsdp"),
            P("fsdp"),
            P("tp"),
            P("tp"),
        ),
        check_vma=False,
    )
```

```python
import functools

import jax
import jax.numpy as jnp
from jax import lax
from jax.experimental import pallas as pl
from jax.experimental.pallas import tpu as pltpu
from jax.sharding import PartitionSpec as P

EPS = 1e-06
FLOAT = jnp.float32
HALF = jnp.bfloat16
MESH = pl.DeviceIdType.MESH
GROUP = 8
BLOCK = 128
MIB = 1 << 20


def rms_scale(values):
    return lax.rsqrt(jnp.mean(values * values, -1, keepdims=True) + EPS)


def silu_slope(values):
    sig = jax.nn.sigmoid(values)
    return sig * (1.0 + values * (1.0 - sig))


def greet(peers):
    barrier = pltpu.get_barrier_semaphore()
    for peer in peers:
        pl.semaphore_signal(barrier, inc=1, device_id=peer, device_id_type=MESH)
    pl.semaphore_wait(barrier, len(peers))


def others(axis, count):
    mine = lax.axis_index(axis)
    return [{axis: lax.rem(mine + step, count)} for step in range(1, count)]


def share(slots, axis, count, send, recv):
    mine = lax.axis_index(axis)
    copies = [
        pltpu.make_async_remote_copy(
            src_ref=slots.at[mine],
            dst_ref=slots.at[mine],
            send_sem=send.at[step],
            recv_sem=recv.at[step],
            device_id=peer,
            device_id_type=MESH,
        )
        for step, peer in enumerate(others(axis, count))
    ]
    for copy in copies:
        copy.start()
    for copy in copies:
        copy.wait()


def lane_sums(values):
    part = values[:, :BLOCK]
    for start in range(BLOCK, values.shape[1], BLOCK):
        part = part + values[:, start : start + BLOCK]
    return jnp.sum(part.T, 0, keepdims=True)


def columns(row):
    return jnp.broadcast_to(row, (BLOCK, BLOCK)).T


def widen(values, chan):
    return jnp.concatenate([values] * (chan // BLOCK), -1)


def scan_forward(
    n_ctx, n_tp, width,
    proj, keep, gain, lower,
    gated, state, scale, carry_out,
    local, reach, ends, squares, ctx_send, ctx_recv, tp_send, tp_recv,
):
    n_seq, length, chan = state.shape
    greet(others("ctx", n_ctx) + others("tp", n_tp))
    low = lower[...].reshape(1, 1, chan)
    row = lax.broadcasted_iota(jnp.int32, (n_seq, GROUP, chan), 1)

    def step(index, carry):
        prod, total = carry
        rows = pl.ds(pl.multiple_of(index * GROUP, GROUP), GROUP)
        inp = proj[0, :, rows, :]
        decay = low + (1.0 - low) * jax.nn.sigmoid(proj[1, :, rows, :])
        add = inp * jax.nn.sigmoid(inp) * (1.0 - decay)
        mult = decay * keep[:, rows, :]
        for hop in (1, 2, 4):
            inside = row >= hop
            add = jnp.where(inside, mult * pltpu.roll(add, hop, 1) + add, add)
            mult = jnp.where(inside, mult * pltpu.roll(mult, hop, 1), mult)
        add = add + mult * total
        mult = mult * prod
        local[:, rows, :] = add
        reach[:, rows, :] = mult
        return mult[:, GROUP - 1 :, :], add[:, GROUP - 1 :, :]

    start = (jnp.ones((n_seq, 1, chan), FLOAT), jnp.zeros((n_seq, 1, chan), FLOAT))
    prod, total = lax.fori_loop(0, length // GROUP, step, start)
    here = lax.axis_index("ctx")
    ends[here, 0] = prod.reshape(n_seq, chan)
    ends[here, 1] = total.reshape(n_seq, chan)
    share(ends, "ctx", n_ctx, ctx_send, ctx_recv)
    carry = jnp.zeros((n_seq, chan), FLOAT)
    for place in range(n_ctx - 1):
        carry = jnp.where(place < here, ends[place, 1] + ends[place, 0] * carry, carry)
    carry_out[...] = carry
    mine = lax.axis_index("tp")
    for seq in range(n_seq):
        for start in range(0, length, BLOCK):
            rows = slice(start, start + BLOCK)
            value = local[seq, rows, :] + reach[seq, rows, :] * carry[seq : seq + 1]
            state[seq, rows, :] = value
            squares[mine, seq : seq + 1, rows] = lane_sums(value * value)
    share(squares, "tp", n_tp, tp_send, tp_recv)
    total = squares[0]
    for place in range(1, n_tp):
        total = total + squares[place]
    rate = lax.rsqrt(total / width + EPS)
    scale[...] = rate
    for seq in range(n_seq):
        for start in range(0, length, BLOCK):
            rows = slice(start, start + BLOCK)
            gate = proj[2, seq, rows, :]
            unit = state[seq, rows, :] * widen(columns(rate[seq : seq + 1, rows]), chan)
            gated[seq, rows, :] = (unit * gain[...] * (gate * jax.nn.sigmoid(gate))).astype(HALF)


def run_scan_forward(proj, keep, gain, lower, n_ctx, n_tp, width):
    _, n_seq, length, chan = proj.shape
    vmem = pl.BlockSpec(memory_space=pltpu.VMEM)
    return pl.pallas_call(
        functools.partial(scan_forward, n_ctx, n_tp, width),
        name="scan_forward",
        out_shape=(
            jax.ShapeDtypeStruct((n_seq, length, chan), HALF),
            jax.ShapeDtypeStruct((n_seq, length, chan), FLOAT),
            jax.ShapeDtypeStruct((n_seq, length), FLOAT),
            jax.ShapeDtypeStruct((n_seq, chan), FLOAT),
        ),
        in_specs=[vmem] * 4,
        out_specs=[vmem] * 4,
        scratch_shapes=[
            pltpu.VMEM((n_seq, length, chan), FLOAT),
            pltpu.VMEM((n_seq, length, chan), FLOAT),
            pltpu.VMEM((n_ctx, 2, n_seq, chan), FLOAT),
            pltpu.VMEM((n_tp, n_seq, length), FLOAT),
            pltpu.SemaphoreType.DMA((n_ctx,)),
            pltpu.SemaphoreType.DMA((n_ctx,)),
            pltpu.SemaphoreType.DMA((n_tp,)),
            pltpu.SemaphoreType.DMA((n_tp,)),
        ],
        compiler_params=pltpu.CompilerParams(
            collective_id=0, has_side_effects=True, vmem_limit_bytes=40 * MIB
        ),
    )(proj, keep, gain, lower)


PIECES = 4
TILE = 256
WIDE = 512


def bands(count, size):
    return [(start, min(size, count - start)) for start in range(0, count, size)]


def dot(lhs, rhs):
    return jnp.dot(lhs, rhs, preferred_element_type=FLOAT)


def dot_nt(lhs, rhs):
    return lax.dot_general(lhs, rhs, (((1,), (1,)), ((), ())), preferred_element_type=FLOAT)


class Line:
    def __init__(self, held, cross, total, sems):
        self.held, self.cross, self.total, self.sems = held, cross, total, sems
        place = lax.axis_index("tp")
        self.inner = (place == 1) | (place == 2)
        self.side = place + 1 - 2 * lax.rem(place, 2)
        self.facing = 3 - place

    def slot(self, job, ref):
        slots = ref.shape[0]
        if slots == self.total.shape[0]:
            return job
        return job % slots if isinstance(job, int) else lax.rem(job, slots)

    def copy(self, source, target, send, recv, place):
        return pltpu.make_async_remote_copy(
            src_ref=source,
            dst_ref=target,
            send_sem=send,
            recv_sem=recv,
            device_id={"tp": place},
            device_id_type=MESH,
        )

    def inward(self, job, q):
        send, recv, _, _ = self.sems
        return self.copy(
            self.held.at[self.slot(job, self.held), q], self.total.at[job, q],
            send.at[job, q], recv.at[job, q], self.side,
        )

    def outward(self, job, q):
        send, recv, _, _ = self.sems
        return self.copy(
            self.total.at[job, q], self.total.at[job, q],
            send.at[job, q], recv.at[job, q], self.side,
        )

    def across(self, job, q):
        _, _, send, recv = self.sems
        return self.copy(
            self.held.at[self.slot(job, self.held), q], self.cross.at[self.slot(job, self.cross), q],
            send.at[job, q], recv.at[job, q], self.facing,
        )

    def offer(self, job, q):
        @pl.when(jnp.logical_not(self.inner))
        def _():
            self.inward(job, q).start()

    def tick(self, job, step):
        slot, cross_slot = self.slot(job, self.held), self.slot(job, self.cross)

        @pl.when(self.inner)
        def _():
            if step < PIECES:
                self.inward(job, step).wait_recv()
                value = self.held[slot, step].astype(FLOAT) + self.total[job, step].astype(FLOAT)
                self.held[slot, step] = value.astype(HALF)
                self.across(job, step).start()
            if step > 0:
                q = step - 1
                self.across(job, q).wait_recv()
                value = self.held[slot, q].astype(FLOAT) + self.cross[cross_slot, q].astype(FLOAT)
                self.total[job, q] = value.astype(HALF)
                self.outward(job, q).start()

    def relay(self, job):
        for step in range(PIECES + 1):
            self.tick(job, step)

    def arrive(self, job):
        @pl.when(jnp.logical_not(self.inner))
        def _():
            @pl.loop(0, PIECES)
            def _(q):
                self.outward(job, q).wait_recv()

    def release(self, job):
        @pl.when(self.inner)
        def _():
            @pl.loop(0, PIECES)
            def _(q):
                self.across(job, q).wait_send()

        @pl.when(jnp.logical_not(self.inner))
        def _():
            @pl.loop(0, PIECES)
            def _(q):
                self.inward(job, q).wait_send()

    def settle(self, job):
        @pl.when(self.inner)
        def _():
            @pl.loop(0, PIECES)
            def _(q):
                self.outward(job, q).wait_send()


def pull(parts, wholes, dims, n_fsdp, own_sem, send_sem, recv_sem):
    if n_fsdp != 2:
        copies = [
            pltpu.make_async_copy(part, whole, own_sem.at[index])
            for index, (part, whole) in enumerate(zip(parts, wholes))
        ]
        for copy in copies:
            copy.start()
        return lambda index: copies[index].wait()
    mine = lax.axis_index("fsdp")
    near, far = [], []
    for index, (part, whole, dim) in enumerate(zip(parts, wholes, dims)):
        size = part.shape[dim]
        at = pl.ds(pl.multiple_of(mine * size, size), size)
        place = whole.at[at] if dim == 0 else whole.at[:, at]
        near.append(pltpu.make_async_copy(part, place, own_sem.at[index]))
        far.append(
            pltpu.make_async_remote_copy(
                src_ref=part,
                dst_ref=place,
                send_sem=send_sem.at[index],
                recv_sem=recv_sem.at[index],
                device_id={"fsdp": 1 - mine},
                device_id_type=MESH,
            )
        )
    for one, two in zip(near, far):
        two.start()
        one.start()

    def wait(index):
        near[index].wait()
        far[index].wait()

    return wait


def span(start, size, unit):
    return pl.ds(pl.multiple_of(start, unit), size)


def row_blocks(count, size, body):
    @pl.loop(0, count // size)
    def _(index):
        body(pl.ds(pl.multiple_of(index * size, size), size))


def line_peers():
    place = lax.axis_index("tp")
    return [{"tp": place + 1 - 2 * lax.rem(place, 2)}, {"tp": 3 - place}]


def joined(ref, c, rows):
    return jnp.concatenate([ref[c, q, rows, :].astype(FLOAT) for q in range(PIECES)], -1)


def halves(n_fsdp, store_sem, send_sem, recv_sem, spare, inbox):
    mine = lax.axis_index("fsdp")
    pending = {}

    def send(index, view):
        slot = index % 2
        return pltpu.make_async_remote_copy(
            src_ref=view(spare.at[slot]),
            dst_ref=view(inbox.at[slot]),
            send_sem=send_sem.at[slot],
            recv_sem=recv_sem.at[slot],
            device_id={"fsdp": 1 - mine},
            device_id_type=MESH,
        )

    def item(index, view, compute_other, compute_own, other_place, target):
        slot = index % 2
        if index - 2 in pending:
            pending.pop(index - 2)()
        compute_other(view(spare.at[slot]))
        if n_fsdp == 2:
            copy = send(index, view)
            copy.start()
            pending[index] = lambda: send(index, view).wait_send()
        else:
            def store():
                return pltpu.make_async_copy(view(spare.at[slot]), other_place(), store_sem.at[slot])

            store().start()
            pending[index] = lambda: store().wait()
        compute_own(target)
        if n_fsdp == 2:
            send(index, view).wait_recv()
            extra = view(inbox.at[slot])

            def add(rows):
                value = target[rows, :].astype(FLOAT) + extra[rows, :].astype(FLOAT)
                target[rows, :] = value.astype(HALF)

            row_blocks(target.shape[0], 16, add)

    def finish():
        for wait in pending.values():
            wait()

    return item, finish


class Square:
    def __init__(self, index, buffers, at, place, send, recv, store_sem):
        self.buffers, self.at, self.place_of = buffers, at, place
        self.send, self.recv, self.index, self.store_sem = send, recv, index, store_sem

    @property
    def tile(self):
        return self.buffers[0].at[self.at]

    @property
    def half(self):
        return self.buffers[1].at[self.at]

    @property
    def quarter(self):
        return self.buffers[2].at[self.at]

    def geometry(self):
        here = lax.axis_index("ctx")
        low, high = lax.rem(here, 2), here // 2
        near, far = here + 1 - 2 * low, here + 2 - 4 * high
        bits = (low, high) if self.index % 2 == 0 else (high, low)
        peers = (near, far) if self.index % 2 == 0 else (far, near)
        wide, thin = self.half.shape[1], self.quarter.shape[1]
        begin = bits[0] * wide
        return (
            peers,
            span(begin, wide, BLOCK),
            span((1 - bits[0]) * wide, wide, BLOCK),
            span(begin + bits[1] * thin, thin, BLOCK),
            span(begin + (1 - bits[1]) * thin, thin, BLOCK),
        )

    def round(self, number):
        peers, mine, yours, my_part, your_part = self.geometry()
        source, target, peer = (
            (self.tile.at[:, yours], self.half, 0),
            (self.tile.at[:, your_part], self.quarter, 1),
            (self.tile.at[:, my_part], self.place_of().at[:, my_part], 1),
            (self.place_of().at[:, mine], self.place_of().at[:, mine], 0),
        )[number]
        return pltpu.make_async_remote_copy(
            src_ref=source,
            dst_ref=target,
            send_sem=self.send.at[self.index, number],
            recv_sem=self.recv.at[self.index, number],
            device_id={"ctx": peers[peer]},
            device_id_type=MESH,
        )

    def add(self, cols, extra):
        def body(rows):
            value = self.tile[rows, cols].astype(FLOAT) + extra[rows, :].astype(FLOAT)
            self.tile[rows, cols] = value.astype(HALF)

        row_blocks(self.tile.shape[0], 16, body)

    def store(self):
        return pltpu.make_async_copy(self.tile, self.place_of(), self.store_sem.at[self.index])

    def store_part(self):
        part = self.geometry()[3]
        return pltpu.make_async_copy(
            self.tile.at[:, part], self.place_of().at[:, part], self.store_sem.at[self.index]
        )

    def advance(self, number):
        if number > 0:
            self.round(number - 1).wait_recv()
        if number == 1:
            self.add(self.geometry()[1], self.half)
        if number == 2:
            self.add(self.geometry()[3], self.quarter)
            self.store_part().start()
        if number == 3:
            self.store_part().wait()
        if number < 4:
            self.round(number).start()

    def settle(self):
        for number in range(4):
            self.round(number).wait_send()


def fill(target, left, right, first):
    for start, size in bands(target.shape[1], WIDE):
        cols = pl.ds(pl.multiple_of(first + start, BLOCK), size)
        target[:, start : start + size] = dot(left, right[:, cols]).astype(HALF)


def middle(
    n_fsdp, CHUNK,
    gated, tokens, cotangent, gain, wo_part, wg_part, wu_part, wd_part,
    mixed_out, normed_out, act_out, grad_glu_out, grad_resid_out, grad_mixed_out,
    grad_gated_out, w_glu_out, w_down_out, grad_gain_out,
    wo, wg, wu, wd, x_all, dy_all, held, crossed, total, normed, act, grad_glu,
    grad_resid, grad_mixed, grad_gated, gain_total, spare, own, inbox,
    weight_sem, weight_send, weight_recv, again_sem, own_sem, send_sem, recv_sem, load_sem, store_sem, *line_sems,
):
    n_chunks, _, _, piece = held.shape
    units = wd.shape[0]
    width = wd.shape[1]
    peers = line_peers()
    if n_fsdp == 2:
        peers.append({"fsdp": 1 - lax.axis_index("fsdp")})
    greet(peers)
    ready = pull(
        (wo_part, wg_part, wu_part, wd_part), (wo, wg, wu, wd), (1, 0, 0, 1),
        n_fsdp, own_sem, send_sem, recv_sem,
    )
    loads = [
        pltpu.make_async_copy(tokens, x_all, load_sem.at[0]),
        pltpu.make_async_copy(cotangent, dy_all, load_sem.at[1]),
    ]
    for load in loads:
        load.start()
    line = Line(held, crossed, total, line_sems)

    def chunk_rows(c):
        return pl.ds(pl.multiple_of(c * CHUNK, CHUNK), CHUNK)

    def stores(c, wanted=None):
        rows = chunk_rows(c)
        pairs = [
            (normed, normed_out.at[rows]),
            (act, act_out.at[rows]),
            (grad_glu.at[0], grad_glu_out.at[0, rows]),
            (grad_glu.at[1], grad_glu_out.at[1, rows]),
            (grad_resid, grad_resid_out.at[rows]),
            (grad_mixed, grad_mixed_out.at[rows]),
            (grad_gated, grad_gated_out.at[rows]),
        ]
        pairs += [
            (total.at[c, q], mixed_out.at[rows, pl.ds(q * piece, piece)]) for q in range(PIECES)
        ]
        return [
            pltpu.make_async_copy(source, target, store_sem.at[index])
            for index, (source, target) in enumerate(pairs)
            if wanted is None or index in wanted
        ]

    FORWARD = (0, 1, 2, 3, 7, 8, 9, 10)
    BACKWARD = (4, 5, 6)

    ready(0)

    @pl.loop(0, n_chunks)
    def _(c):
        lhs = gated[chunk_rows(c), :]

        @pl.loop(0, PIECES)
        def _(q):
            cols = pl.ds(pl.multiple_of(q * piece, piece), piece)
            held[c, q] = dot(lhs, wo[:, cols]).astype(HALF)
            line.offer(c, q)

    for load in loads:
        load.wait()
    line.relay(0)
    for index in (1, 2, 3):
        ready(index)
    w_down_store = pltpu.make_async_copy(wd, w_down_out, again_sem.at[3])
    w_down_store.start()

    @pl.loop(0, n_chunks)
    def _(c):
        line.arrive(c)
        line.tick(c + 1, 0)

        @pl.when(c > 0)
        def _():
            for store in stores(c - 1, FORWARD):
                store.wait()

        def norm(rows):
            at = pl.ds(pl.multiple_of(c * CHUNK + rows.start, 16), rows.size)
            resid = x_all[at, :].astype(FLOAT) + joined(total, c, rows)
            normed[rows, :] = (resid * rms_scale(resid) * gain[...]).astype(HALF)

        row_blocks(CHUNK, 16, norm)

        def unit(cols):
            glu_gate = dot(normed[...], wg[:, cols])
            glu_up = dot(normed[...], wu[:, cols])
            grad_act = dot_nt(dy_all[chunk_rows(c), :], wd[cols, :])
            sig = jax.nn.sigmoid(glu_gate)
            silu = glu_gate * sig
            act[:, cols] = (silu * glu_up).astype(HALF)
            slope = sig * (1.0 + glu_gate * (1.0 - sig))
            grad_glu[0, :, cols] = (grad_act * glu_up * slope).astype(HALF)
            grad_glu[1, :, cols] = (grad_act * silu).astype(HALF)

        for index, (start, size) in enumerate(bands(units, WIDE)):
            unit(slice(start, start + size))
            if index == 0:
                line.tick(c + 1, 1)
        line.tick(c + 1, 2)
        line.release(c)

        @pl.loop(0, PIECES)
        def _(q):
            @pl.when(q == PIECES // 2)
            def _():
                line.tick(c + 1, 3)

            at = pl.ds(pl.multiple_of(q * piece, piece), piece)
            value = dot_nt(grad_glu[0], wg[at, :]) + dot_nt(grad_glu[1], wu[at, :])
            held[c, q] = value.astype(HALF)
            line.offer(n_chunks + c, q)

        line.tick(c + 1, 4)

        for store in stores(c, FORWARD):
            store.start()

    for store in stores(n_chunks - 1, FORWARD):
        store.wait()
    rows = n_chunks * CHUNK
    w_down_store.wait()
    kept = [
        (grad_glu_out.at[0], wg.at[:rows]),
        (grad_glu_out.at[1], wu.at[:rows]),
        (normed_out, wd.at[:rows]),
    ]
    again = [
        pltpu.make_async_copy(source, target, again_sem.at[index])
        for index, (source, target) in enumerate(kept)
    ]
    for copy in again:
        copy.start()
    gain_total[...] = jnp.zeros_like(gain_total)
    item, finish = halves(n_fsdp, weight_sem, weight_send, weight_recv, spare, inbox)
    mine = lax.axis_index("fsdp") if n_fsdp == 2 else 1
    depth = width // 2
    whole = n_fsdp != 2
    per_part = depth // TILE
    own_stores = {}

    def weight_item(index):
        if index >= 2 * per_part:
            return
        part, k = divmod(index, per_part)
        right = (wg, wu)[part].at[:rows]
        slot = index % 2
        if index > 1:
            own_stores.pop(slot).wait()

        def compute(side):
            at = pl.ds(pl.multiple_of(side * depth + k * TILE, TILE), TILE)
            return lambda target: fill(target, wd[:rows, at].T, right, 0)

        at = slice(k * TILE + whole * depth, (k + 1) * TILE + whole * depth)
        item(
            index, lambda ref: ref, compute(1 - mine), compute(mine),
            lambda: w_glu_out.at[part, k * TILE : (k + 1) * TILE], own.at[slot],
        )
        store = pltpu.make_async_copy(own.at[slot], w_glu_out.at[part, at], weight_sem.at[2 + slot])
        store.start()
        own_stores[slot] = store

    def backward(c):
        line.arrive(n_chunks + c)
        if c > 0:
            for store in stores(c - 1, BACKWARD):
                store.wait()

        def norm_back(rows):
            at = pl.ds(pl.multiple_of(c * CHUNK + rows.start, 16), rows.size)
            resid = x_all[at, :].astype(FLOAT) + joined(total, c, rows)
            rate = rms_scale(resid)
            grad = joined(total, n_chunks + c, rows)
            by_gain = grad * (resid * rate)
            gain_total[...] += by_gain[:8] + by_gain[8:]
            inner = gain[...] * grad
            mean = jnp.mean(inner * resid, -1, keepdims=True)
            value = dy_all[at, :].astype(FLOAT) + rate * inner - resid * (rate * rate * rate * mean)
            grad_resid[rows, :] = value
            grad_mixed[rows, :] = value.astype(HALF)

        row_blocks(CHUNK, 16, norm_back)
        for start, size in bands(grad_gated.shape[1], WIDE):
            grad_gated[:, start : start + size] = dot_nt(
                grad_mixed[...], wo[start : start + size, :]
            )
        for store in stores(c, BACKWARD):
            store.start()

    for copy in again:
        copy.wait()
    count = 0
    for c in range(n_chunks):
        if c == n_chunks - 1:
            while count < 2 * per_part:
                weight_item(count)
                count += 1
        backward(c)
        if c + 1 < n_chunks:
            for step in range(PIECES + 1):
                if step % 2 == 0:
                    weight_item(count)
                    count += 1
                line.tick(n_chunks + c + 1, step)
    finish()
    for store in own_stores.values():
        store.wait()

    grad_gain_out[...] = jnp.sum(gain_total[...], 0, keepdims=True)
    for store in stores(n_chunks - 1, BACKWARD):
        store.wait()

    @pl.loop(0, n_chunks)
    def _(c):
        line.settle(c)
        line.settle(n_chunks + c)
        line.release(n_chunks + c)


def run_middle(gated, tokens, cotangent, gain, parts, n_fsdp, length):
    rows, chan = gated.shape
    width = tokens.shape[1]
    wg = parts[1]
    units = wg.shape[1]
    n_chunks = rows // length
    piece = width // PIECES
    vmem = pl.BlockSpec(memory_space=pltpu.VMEM)
    hbm = pl.BlockSpec(memory_space=pl.ANY)
    sems = pltpu.SemaphoreType.DMA((2 * n_chunks, PIECES))
    return pl.pallas_call(
        functools.partial(middle, n_fsdp, length),
        name="middle",
        out_shape=(
            jax.ShapeDtypeStruct((rows, width), HALF),
            jax.ShapeDtypeStruct((rows, width), HALF),
            jax.ShapeDtypeStruct((rows, units), HALF),
            jax.ShapeDtypeStruct((2, rows, units), HALF),
            jax.ShapeDtypeStruct((rows, width), FLOAT),
            jax.ShapeDtypeStruct((rows, width), HALF),
            jax.ShapeDtypeStruct((rows, chan), FLOAT),
            jax.ShapeDtypeStruct((2, width if n_fsdp != 2 else width // 2, units), HALF),
            jax.ShapeDtypeStruct((units, width), HALF),
            jax.ShapeDtypeStruct((1, width), FLOAT),
        ),
        in_specs=[vmem, hbm, hbm, vmem, hbm, hbm, hbm, hbm],
        out_specs=[hbm] * 9 + [vmem],
        scratch_shapes=[
            pltpu.VMEM((chan, width), HALF),
            pltpu.VMEM((width, units), HALF),
            pltpu.VMEM((width, units), HALF),
            pltpu.VMEM((units, width), HALF),
            pltpu.VMEM((rows, width), HALF),
            pltpu.VMEM((rows, width), HALF),
            pltpu.VMEM((n_chunks, PIECES, length, piece), HALF),
            pltpu.VMEM((n_chunks, PIECES, length, piece), HALF),
            pltpu.VMEM((2 * n_chunks, PIECES, length, piece), HALF),
            pltpu.VMEM((length, width), HALF),
            pltpu.VMEM((length, units), HALF),
            pltpu.VMEM((2, length, units), HALF),
            pltpu.VMEM((length, width), FLOAT),
            pltpu.VMEM((length, width), HALF),
            pltpu.VMEM((length, chan), FLOAT),
            pltpu.VMEM((8, width), FLOAT),
            pltpu.VMEM((2, TILE, units), HALF),
            pltpu.VMEM((2, TILE, units), HALF),
            pltpu.VMEM((2, TILE, units), HALF),
            pltpu.SemaphoreType.DMA((4,)),
            pltpu.SemaphoreType.DMA((2,)),
            pltpu.SemaphoreType.DMA((2,)),
            pltpu.SemaphoreType.DMA((4,)),
            pltpu.SemaphoreType.DMA((4,)),
            pltpu.SemaphoreType.DMA((4,)),
            pltpu.SemaphoreType.DMA((4,)),
            pltpu.SemaphoreType.DMA((2,)),
            pltpu.SemaphoreType.DMA((12,)),
        ]
        + [sems] * 4,
        compiler_params=pltpu.CompilerParams(
            collective_id=2, has_side_effects=True, vmem_limit_bytes=63 * MIB
        ),
        cost_estimate=pl.CostEstimate(
            flops=16 * rows * width * units, bytes_accessed=400 * MIB, transcendentals=0
        ),
    )(gated, tokens, cotangent, gain, *parts)


def scan_back(
    n_ctx, n_tp, width, pump,
    proj, keep, gain, lower, state, scale, carry_in, near,
    grad_proj, gain_out, lower_out,
    reach, rate_wide, cross_wide, ends, cross, ctx_sems, tp_sems,
):
    n_seq, length, chan = state.shape
    low = lower[...].reshape(1, 1, chan)
    mine = lax.axis_index("tp")
    gain_total = jnp.zeros((8, chan), FLOAT)
    for seq in range(n_seq):
        for start in range(0, length, BLOCK):
            rows = slice(start, start + BLOCK)
            rate = columns(scale[seq : seq + 1, rows])
            rate_wide[seq, rows, :] = rate
            gate = proj[2, seq, rows, :]
            sig = jax.nn.sigmoid(gate)
            swish = gate * sig
            value = state[seq, rows, :]
            into = near[seq, rows, :]
            by_unit = into * value * widen(rate, chan)
            slope = sig * (1.0 + gate * (1.0 - sig))
            grad_proj[seq, rows, 2 * chan :] = (by_unit * gain[...] * slope).astype(HALF)
            gain_total = gain_total + jnp.sum((by_unit * swish).reshape(-1, 8, chan), 0)
            grad_unit = into * swish * gain[...]
            near[seq, rows, :] = grad_unit
            cross[mine, seq : seq + 1, rows] = lane_sums(grad_unit * value)
    gain_out[...] = jnp.sum(gain_total, 0, keepdims=True)
    share(cross, "tp", n_tp, *tp_sems)
    pump()
    total = cross[0]
    for place in range(1, n_tp):
        total = total + cross[place]
    rate = scale[...]
    total = total * (rate * rate * rate) / width
    for seq in range(n_seq):
        for start in range(0, length, BLOCK):
            rows = slice(start, start + BLOCK)
            cross_wide[seq, rows, :] = columns(total[seq : seq + 1, rows])

    row = lax.broadcasted_iota(jnp.int32, (n_seq, GROUP, chan), 1)

    def back(index, carry):
        prod, above = carry
        rows = pl.ds(pl.multiple_of((length // GROUP - 1 - index) * GROUP, GROUP), GROUP)
        decay = low + (1.0 - low) * jax.nn.sigmoid(proj[1, :, rows, :])
        mult = decay * keep[:, rows, :]
        direct = (
            widen(rate_wide[:, rows, :], chan) * near[:, rows, :]
            - widen(cross_wide[:, rows, :], chan) * state[:, rows, :]
        )
        add = mult * direct
        for hop in (1, 2, 4):
            inside = row < GROUP - hop
            add = jnp.where(inside, mult * pltpu.roll(add, GROUP - hop, 1) + add, add)
            mult = jnp.where(inside, mult * pltpu.roll(mult, GROUP - hop, 1), mult)
        add = add + mult * above
        mult = mult * prod
        inside = row < GROUP - 1
        near[:, rows, :] = direct + jnp.where(inside, pltpu.roll(add, GROUP - 1, 1), above)
        reach[:, rows, :] = jnp.where(inside, pltpu.roll(mult, GROUP - 1, 1), prod)
        return mult[:, :1, :], add[:, :1, :]

    held = (jnp.ones((n_seq, 1, chan), FLOAT), jnp.zeros((n_seq, 1, chan), FLOAT))
    held = lax.fori_loop(0, length // GROUP, back, held)
    prod, total = held
    here = lax.axis_index("ctx")
    ends[here, 0] = prod.reshape(n_seq, chan)
    ends[here, 1] = total.reshape(n_seq, chan)
    pump()
    share(ends, "ctx", n_ctx, *ctx_sems)
    carry = jnp.zeros((n_seq, chan), FLOAT)
    for place in range(n_ctx - 1, 0, -1):
        carry = jnp.where(place > here, ends[place, 1] + ends[place, 0] * carry, carry)
    carry = carry.reshape(n_seq, 1, chan)
    wide = 2 * GROUP
    first = lax.broadcasted_iota(jnp.int32, (n_seq, wide, chan), 1) == 0

    def finish(index, held):
        before, low_total = held
        rows = pl.ds(pl.multiple_of(index * wide, wide), wide)
        inp = proj[0, :, rows, :]
        sig = jax.nn.sigmoid(inp)
        silu = inp * sig
        fsig = jax.nn.sigmoid(proj[1, :, rows, :])
        rest = 1.0 - fsig
        decay = low + (1.0 - low) * fsig
        grad_state = near[:, rows, :] + reach[:, rows, :] * carry
        value = state[:, rows, :]
        prev = jnp.where(first, before, pltpu.roll(value, 1, 1))
        grad_decay = grad_state * (prev * keep[:, rows, :] - silu)
        grad_proj[:, rows, :chan] = (
            grad_state * (1.0 - decay) * (sig * (1.0 + inp * (1.0 - sig)))
        ).astype(HALF)
        grad_proj[:, rows, chan : 2 * chan] = (
            grad_decay * (1.0 - low) * fsig * rest
        ).astype(HALF)
        return value[:, wide - 1 :, :], low_total + grad_decay * rest

    held = (carry_in[...].reshape(n_seq, 1, chan), jnp.zeros((n_seq, wide, chan), FLOAT))
    _, low_total = lax.fori_loop(0, length // wide, finish, held)
    lower_out[...] = jnp.sum(jnp.sum(low_total, 0), 0, keepdims=True)
    pump()


def tail(
    n_fsdp, n_ctx, n_tp,
    keep, gate_gain, lower, scale, carry_in, gain, gain_two_grad,
    proj, state, grad_gated, w_in, w_down, act, normed, grad_mixed, gated, cotangent,
    grad_resid, tokens, mixed,
    grad_tokens_out, output_out, vectors_out, w_in_out, w_out_out, w_down_out,
    grad_proj, held, crossed, total, spare, inbox,
    in_tile, in_half, in_quarter, out_tile, out_half, out_quarter, down_tile, down_half, down_quarter,
    gain_total, ends, cross, over_ctx, over_fsdp,
    load_sem, store_sem, end_send, end_recv, cross_send, cross_recv, ctx_send, ctx_recv,
    fsdp_send, fsdp_recv, part_sem, part_send, part_recv, square_send, square_recv, square_store,
    *line_sems,
):
    n_seq, length, wide = grad_proj.shape
    chan = wide // 3
    rows = n_seq * length
    width = gain.shape[1]
    units = w_down.shape[0]
    piece = width // PIECES
    n_chunks = n_seq
    whole = n_fsdp != 2
    greet(others("ctx", n_ctx) + others("tp", n_tp) + others("fsdp", n_fsdp))
    line = Line(held, crossed, total, line_sems)
    ticks = [(job, step) for job in range(2 * n_chunks) for step in range(PIECES + 1)]
    squares = []
    turn = [0]
    SPACE = 3

    def pump(count=1):
        for _ in range(count):
            if ticks:
                line.tick(*ticks.pop(0))
            for index, square in enumerate(squares):
                if square[1] < 5 and turn[0] >= square[2] + SPACE * square[1]:
                    square[0].advance(square[1])
                    square[1] += 1
            turn[0] += 1

    def start_loads(pairs, first=0):
        copies = [
            pltpu.make_async_copy(source, target, load_sem.at[first + index])
            for index, (source, target) in enumerate(pairs)
        ]
        for copy in copies:
            copy.start()
        return copies

    def chunk_rows(c):
        return pl.ds(c * length, length) if isinstance(c, int) else span(c * length, length, length)

    def down_terms(w_all, act_all):
        for copy in start_loads([(w_down, w_all), (act, act_all)]):
            copy.wait()

        for c in range(n_chunks):
            @pl.loop(0, PIECES)
            def _(q):
                cols = pl.ds(pl.multiple_of(q * piece, piece), piece)
                held[c, q] = dot(act_all[chunk_rows(c), :], w_all[:, cols]).astype(HALF)
                line.offer(c, q)

            if c == n_chunks - 1:
                pump()

    pl.run_scoped(
        down_terms, pltpu.VMEM((units, width), HALF), pltpu.VMEM((rows, units), HALF)
    )

    def back(proj_all, state_all, near, reach, rate_wide, cross_wide):
        for copy in start_loads([(proj, proj_all), (state, state_all), (grad_gated, near)]):
            copy.wait()
        gain_at = over_ctx.at[lax.axis_index("ctx"), :, 2 * width : 2 * width + chan]
        lower_at = over_ctx.at[lax.axis_index("ctx"), :, 2 * width + chan :]
        scan_back(
            n_ctx, n_tp, width, pump,
            proj_all, keep, gate_gain, lower, state_all, scale, carry_in, near,
            grad_proj, gain_at, lower_at,
            reach, rate_wide, cross_wide, ends, cross, (end_send, end_recv), (cross_send, cross_recv),
        )

    shape = (n_seq, length, chan)
    pl.run_scoped(
        back,
        pltpu.VMEM((3, *shape), FLOAT),
        pltpu.VMEM(shape, FLOAT),
        pltpu.VMEM(shape, FLOAT),
        pltpu.VMEM(shape, FLOAT),
        pltpu.VMEM((n_seq, length, BLOCK), FLOAT),
        pltpu.VMEM((n_seq, length, BLOCK), FLOAT),
    )

    def back_terms(w_all):
        for copy in start_loads(
            [(w_in.at[gate], w_all.at[:, gate * chan : (gate + 1) * chan]) for gate in range(3)]
        ):
            copy.wait()

        for c in range(n_chunks):
            @pl.loop(0, PIECES)
            def _(q):
                at = pl.ds(pl.multiple_of(q * piece, piece), piece)
                held[n_chunks + c, q] = dot_nt(grad_proj[c], w_all[at, :]).astype(HALF)
                line.offer(n_chunks + c, q)

            if c % 2 == 1:
                pump()

    pl.run_scoped(back_terms, pltpu.VMEM((width, wide), HALF))

    item, finish = halves(n_fsdp, part_sem, part_send, part_recv, spare, inbox)
    mine = 1 if whole else lax.axis_index("fsdp")
    depth = width // 2
    skip = whole * depth
    stores = []

    def weights(act_all, dy_all, normed_all, mixed_all, gated_all):
        copies = start_loads(
            [(act, act_all), (cotangent, dy_all), (normed, normed_all), (grad_mixed, mixed_all),
             (gated, gated_all)]
        )
        count = [0]

        def tile(view, compute, other_place, own_place, buffers, at):
            index = count[0]
            count[0] += 1
            square = Square(
                index, buffers, at, own_place, square_send, square_recv, square_store
            )
            item(index, view, compute(1 - mine), compute(mine), other_place, square.tile)
            if whole:
                square.store().start()
                stores.append(square)
            else:
                squares.append([square, 0, turn[0]])
            pump()

        copies[0].wait()
        copies[1].wait()
        for start, size in bands(units, TILE):
            left = act_all[:, start : start + size].T
            at = slice(start, start + size)

            def compute(side):
                return lambda target: fill(target, left, dy_all, side * depth)

            tile(
                lambda ref, size=size: ref.at[:size, :depth], compute,
                lambda at=at: w_down_out.at[at, :depth], lambda at=at: w_down_out.at[at, skip:],
                (down_tile, down_half, down_quarter), at,
            )
        copies[2].wait()
        flat_proj = grad_proj.reshape(rows, wide)
        for k in range(depth // TILE):
            def compute(side):
                at = pl.ds(pl.multiple_of(side * depth + k * TILE, TILE), TILE)
                return lambda target: fill(target, normed_all[:, at].T, flat_proj, 0)

            at = slice(k * TILE, (k + 1) * TILE)
            tile(
                lambda ref: ref, compute,
                lambda at=at: w_in_out.at[at],
                lambda k=k: w_in_out.at[k * TILE + skip : (k + 1) * TILE + skip],
                (in_tile, in_half, in_quarter), k,
            )
        copies[3].wait()
        copies[4].wait()
        for k in range(chan // TILE):
            at = slice(k * TILE, (k + 1) * TILE)
            left = gated_all[:, at].T

            def compute(side):
                return lambda target: fill(target, left, mixed_all, side * depth)

            tile(
                lambda ref: ref.at[:, :depth], compute,
                lambda at=at: w_out_out.at[at, :depth], lambda at=at: w_out_out.at[at, skip:],
                (out_tile, out_half, out_quarter), k,
            )

    pl.run_scoped(
        weights,
        pltpu.VMEM((rows, units), HALF),
        pltpu.VMEM((rows, width), HALF),
        pltpu.VMEM((rows, width), HALF),
        pltpu.VMEM((rows, width), HALF),
        pltpu.VMEM((rows, chan), HALF),
    )
    finish()

    def ends_of(resid_all, x_all, mixed_all):
        for copy in start_loads([(tokens, x_all), (mixed, mixed_all), (grad_resid, resid_all)]):
            copy.wait()
        gain_total[...] = jnp.zeros_like(gain_total)

        def token_store(c):
            at = chunk_rows(c)
            return pltpu.make_async_copy(
                resid_all.at[at], grad_tokens_out.at[at], store_sem.at[0, c]
            )

        def output_store(c):
            at = chunk_rows(c)
            return pltpu.make_async_copy(mixed_all.at[at], output_out.at[at], store_sem.at[1, c])

        def until(job):
            while ticks and ticks[0][0] <= job:
                pump()

        for c in range(n_chunks):
            until(c)
            line.arrive(c)

            @pl.loop(0, length // 16)
            def _(index):
                at = pl.ds(pl.multiple_of(c * length + index * 16, 16), 16)
                rows = pl.ds(pl.multiple_of(index * 16, 16), 16)
                value = x_all[at, :].astype(FLOAT) + mixed_all[at, :].astype(FLOAT)
                mixed_all[at, :] = (value + joined(total, c, rows)).astype(HALF)

            output_store(c).start()

        for c in range(n_chunks):
            until(n_chunks + c)
            line.arrive(n_chunks + c)
            for quarter in range(PIECES):
                pump()

                @pl.loop(0, length // PIECES // 16)
                def _(index):
                    start = quarter * (length // PIECES) + index * 16
                    rows = pl.ds(pl.multiple_of(start, 16), 16)
                    at = pl.ds(pl.multiple_of(c * length + start, 16), 16)
                    value = x_all[at, :].astype(FLOAT)
                    rate = rms_scale(value)
                    grad = joined(total, n_chunks + c, rows)
                    by_gain = grad * (value * rate)
                    gain_total[...] += by_gain[:8] + by_gain[8:]
                    inner = gain[...] * grad
                    mean = jnp.mean(inner * value, -1, keepdims=True)
                    resid_all[at, :] = (
                        resid_all[at, :] + rate * inner - value * (rate * rate * rate * mean)
                    )

            token_store(c).start()

        here = lax.axis_index("ctx")
        over_ctx[here, :, :width] = jnp.sum(gain_total[...], 0, keepdims=True)
        over_ctx[here, :, width : 2 * width] = gain_two_grad[...]
        share(over_ctx, "ctx", n_ctx, ctx_send, ctx_recv)
        value = over_ctx[0]
        for place in range(1, n_ctx):
            value = value + over_ctx[place]
        over_fsdp[lax.axis_index("fsdp")] = value
        share(over_fsdp, "fsdp", n_fsdp, fsdp_send, fsdp_recv)
        value = over_fsdp[0]
        for place in range(1, n_fsdp):
            value = value + over_fsdp[place]
        vectors_out[...] = value
        while any(square[1] < 5 for square in squares):
            pump()
        for c in range(n_chunks):
            token_store(c).wait()
            output_store(c).wait()

    pl.run_scoped(
        ends_of,
        pltpu.VMEM((rows, width), FLOAT),
        pltpu.VMEM((rows, width), HALF),
        pltpu.VMEM((rows, width), HALF),
    )
    for square in squares:
        square[0].settle()
    for square in stores:
        square.store().wait()

    @pl.loop(0, 2 * n_chunks)
    def _(job):
        line.settle(job)
        line.release(job)


def run_tail(small, large, n_fsdp, n_ctx, n_tp):
    grad_gated, w_down, tokens = large[2], large[4], large[11]
    n_seq, length, chan = grad_gated.shape
    rows, width = tokens.shape
    units = w_down.shape[0]
    piece = width // PIECES
    size = 2 * width + 2 * chan
    depth = width // 2
    spread = width if n_fsdp != 2 else depth
    vmem = pl.BlockSpec(memory_space=pltpu.VMEM)
    hbm = pl.BlockSpec(memory_space=pl.ANY)
    slots = pltpu.VMEM((2 * n_seq, PIECES, length, piece), HALF)
    sems = pltpu.SemaphoreType.DMA((2 * n_seq, PIECES))
    n_in, n_out = depth // TILE, chan // TILE
    n_squares = n_in + n_out + len(bands(units, TILE))
    wide = max(3 * chan, depth)

    def tiles(*shape):
        return [pltpu.VMEM((*shape[:-1], shape[-1] // cut), HALF) for cut in (1, 2, 4)]

    return pl.pallas_call(
        functools.partial(tail, n_fsdp, n_ctx, n_tp),
        name="tail",
        out_shape=(
            jax.ShapeDtypeStruct((rows, width), FLOAT),
            jax.ShapeDtypeStruct((rows, width), HALF),
            jax.ShapeDtypeStruct((1, size), FLOAT),
            jax.ShapeDtypeStruct((spread, 3 * chan), HALF),
            jax.ShapeDtypeStruct((chan, spread), HALF),
            jax.ShapeDtypeStruct((units, spread), HALF),
        ),
        in_specs=[vmem] * len(small) + [hbm] * len(large),
        out_specs=[hbm, hbm, vmem, hbm, hbm, hbm],
        scratch_shapes=[
            pltpu.VMEM((n_seq, length, 3 * chan), HALF),
            slots,
            pltpu.VMEM((2 * n_seq, PIECES, length, piece), HALF),
            slots,
            pltpu.VMEM((2, TILE, wide), HALF),
            pltpu.VMEM((2, TILE, wide), HALF),
            *tiles(n_in, TILE, 3 * chan),
            *tiles(n_out, TILE, depth),
            *tiles(units, depth),
            pltpu.VMEM((8, width), FLOAT),
            pltpu.VMEM((n_ctx, 2, n_seq, chan), FLOAT),
            pltpu.VMEM((n_tp, n_seq, length), FLOAT),
            pltpu.VMEM((n_ctx, 1, size), FLOAT),
            pltpu.VMEM((n_fsdp, 1, size), FLOAT),
            pltpu.SemaphoreType.DMA((6,)),
            pltpu.SemaphoreType.DMA((2, n_seq)),
            pltpu.SemaphoreType.DMA((n_ctx,)),
            pltpu.SemaphoreType.DMA((n_ctx,)),
            pltpu.SemaphoreType.DMA((n_tp,)),
            pltpu.SemaphoreType.DMA((n_tp,)),
            pltpu.SemaphoreType.DMA((n_ctx,)),
            pltpu.SemaphoreType.DMA((n_ctx,)),
            pltpu.SemaphoreType.DMA((n_fsdp,)),
            pltpu.SemaphoreType.DMA((n_fsdp,)),
            pltpu.SemaphoreType.DMA((2,)),
            pltpu.SemaphoreType.DMA((2,)),
            pltpu.SemaphoreType.DMA((2,)),
            pltpu.SemaphoreType.DMA((n_squares, 4)),
            pltpu.SemaphoreType.DMA((n_squares, 4)),
            pltpu.SemaphoreType.DMA((n_squares,)),
        ]
        + [sems] * 4,
        compiler_params=pltpu.CompilerParams(
            collective_id=3, has_side_effects=True, vmem_limit_bytes=63 * MIB
        ),
        cost_estimate=pl.CostEstimate(
            flops=10 * rows * width * units, bytes_accessed=700 * MIB, transcendentals=0
        ),
    )(*small, *large)


def gather_fsdp(part, dim, count):
    if count != 2:
        return lax.all_gather(part, "fsdp", axis=dim, tiled=True)
    other = lax.ppermute(part, "fsdp", [(0, 1), (1, 0)])
    first = lax.axis_index("fsdp") == 0
    return jnp.concatenate(
        [jnp.where(first, part, other), jnp.where(first, other, part)], dim
    )


def keep_flags(segment_ids, count):
    last = lax.ppermute(
        segment_ids[:, -1:].astype(FLOAT), "ctx", [(place, place + 1) for place in range(count - 1)]
    )
    seg = segment_ids.astype(FLOAT)
    before = jnp.concatenate([last, seg[:, :-1]], 1)
    token = lax.broadcasted_iota(jnp.int32, seg.shape, 1)
    start = (token == 0) & (lax.axis_index("ctx") == 0)
    return jnp.where(start, 0.0, (seg == before).astype(FLOAT))


def local(
    sizes,
    tokens, segment_ids, w_in, w_out, w_glu, w_down, gain_one, gain_two, gate_gain, lower, cotangent,
):
    n_fsdp, n_ctx, n_tp = sizes
    n_seq, length, width = tokens.shape
    rows = n_seq * length
    chan = w_in.shape[2]
    gain_a = gather_fsdp(gain_one.astype(HALF)[None], 1, n_fsdp).astype(FLOAT)
    gain_b = gather_fsdp(gain_two.astype(HALF)[None], 1, n_fsdp).astype(FLOAT)
    w_in_all = gather_fsdp(w_in.astype(HALF), 1, n_fsdp)
    parts = (w_out.astype(HALF), w_glu[:, 0].astype(HALF), w_glu[:, 1].astype(HALF), w_down.astype(HALF))
    if n_fsdp != 2:
        parts = tuple(gather_fsdp(part, dim, n_fsdp) for part, dim in zip(parts, (1, 0, 0, 1)))
    keep = keep_flags(segment_ids, n_ctx)[..., None]
    gain_gate = gate_gain[None]
    low = lower[None]
    flat = tokens.reshape(rows, width).astype(FLOAT)
    scale_one = rms_scale(flat)
    normed = (flat * scale_one * gain_a).astype(HALF)
    proj = jnp.einsum("td,wdc->wtc", normed, w_in_all, preferred_element_type=FLOAT)
    proj = proj.reshape(3, n_seq, length, chan)
    gated, state, gate_scale, carry = run_scan_forward(
        proj, keep, gain_gate, low, n_ctx, n_tp, width
    )
    gated = gated.reshape(rows, chan)
    x_half = tokens.reshape(rows, width)
    grad_y_half = cotangent.reshape(rows, width)
    (
        mixed, _, act, _, grad_resid, grad_mixed, grad_gated, grad_w_glu, w_down_all, grad_gain_two
    ) = run_middle(gated, x_half, grad_y_half, gain_b, parts, n_fsdp, length)
    if n_fsdp != 2:
        grad_w_glu = lax.psum_scatter(grad_w_glu, "fsdp", scatter_dimension=1, tiled=True)
    grad_w_glu = lax.psum(grad_w_glu, "ctx")
    grad_tokens, output, vectors, grad_w_in, grad_w_out, grad_w_down = run_tail(
        (keep, gain_gate, low, gate_scale, carry, gain_a, grad_gain_two),
        (
            proj, state, grad_gated.reshape(n_seq, length, chan), w_in_all, w_down_all, act, normed,
            grad_mixed, gated, grad_y_half, grad_resid, x_half, mixed,
        ),
        n_fsdp, n_ctx, n_tp,
    )
    if n_fsdp == 2:
        grad_w_in = jnp.moveaxis(grad_w_in.reshape(width // 2, 3, chan), 1, 0)
    else:
        grad_w_in, grad_w_out, grad_w_down = (
            lax.psum(lax.psum_scatter(value, "fsdp", scatter_dimension=dim, tiled=True), "ctx")
            for value, dim in (
                (jnp.moveaxis(grad_w_in.reshape(width, 3, chan), 1, 0), 1),
                (grad_w_out, 1),
                (grad_w_down, 1),
            )
        )
    part = gain_one.shape[0]
    begin = lax.axis_index("fsdp") * part
    return (
        output.reshape(n_seq, length, width),
        grad_tokens.reshape(n_seq, length, width),
        grad_w_in.astype(FLOAT),
        grad_w_out.astype(FLOAT),
        jnp.moveaxis(grad_w_glu, 0, 1).astype(FLOAT),
        grad_w_down.astype(FLOAT),
        lax.dynamic_slice(vectors[0], (begin,), (part,)),
        lax.dynamic_slice(vectors[0], (width + begin,), (part,)),
        vectors[0, 2 * width : 2 * width + chan],
        vectors[0, 2 * width + chan :],
    )


def solution(mesh):
    sizes = tuple(mesh.shape[axis] for axis in ("fsdp", "ctx", "tp"))
    return jax.shard_map(
        functools.partial(local, sizes),
        mesh=mesh,
        in_specs=(
            P("fsdp", "ctx", None),
            P("fsdp", "ctx"),
            P(None, "fsdp", "tp"),
            P("tp", "fsdp"),
            P("fsdp", None, "tp"),
            P("tp", "fsdp"),
            P("fsdp"),
            P("fsdp"),
            P("tp"),
            P("tp"),
            P("fsdp", "ctx", None),
        ),
        out_specs=(
            P("fsdp", "ctx", None),
            P("fsdp", "ctx", None),
            P(None, "fsdp", "tp"),
            P("tp", "fsdp"),
            P("fsdp", None, "tp"),
            P("tp", "fsdp"),
            P("fsdp"),
            P("fsdp"),
            P("tp"),
            P("tp"),
        ),
        check_vma=False,
    )
```

```python
import functools

import jax
import jax.numpy as jnp
from jax import lax
from jax.experimental import pallas as pl
from jax.experimental.pallas import tpu as pltpu
from jax.sharding import PartitionSpec as P

EPS = 1e-06
FLOAT = jnp.float32
HALF = jnp.bfloat16
MESH = pl.DeviceIdType.MESH
GROUP = 8
BLOCK = 128
MIB = 1 << 20


def rms_scale(values):
    return lax.rsqrt(jnp.mean(values * values, -1, keepdims=True) + EPS)


def silu_slope(values):
    sig = jax.nn.sigmoid(values)
    return sig * (1.0 + values * (1.0 - sig))


def greet(peers):
    barrier = pltpu.get_barrier_semaphore()
    for peer in peers:
        pl.semaphore_signal(barrier, inc=1, device_id=peer, device_id_type=MESH)
    pl.semaphore_wait(barrier, len(peers))


def others(axis, count):
    mine = lax.axis_index(axis)
    return [{axis: lax.rem(mine + step, count)} for step in range(1, count)]


def shares(slots, axis, count, send, recv):
    mine = lax.axis_index(axis)
    return [
        pltpu.make_async_remote_copy(
            src_ref=slots.at[mine],
            dst_ref=slots.at[mine],
            send_sem=send.at[step],
            recv_sem=recv.at[step],
            device_id=peer,
            device_id_type=MESH,
        )
        for step, peer in enumerate(others(axis, count))
    ]


def share(slots, axis, count, send, recv):
    copies = shares(slots, axis, count, send, recv)
    for copy in copies:
        copy.start()
    for copy in copies:
        copy.wait()


def lane_sums(values):
    part = values[:, :BLOCK]
    for start in range(BLOCK, values.shape[1], BLOCK):
        part = part + values[:, start : start + BLOCK]
    return jnp.sum(part.T, 0, keepdims=True)


def columns(row):
    return jnp.broadcast_to(row, (BLOCK, BLOCK)).T


def widen(values, chan):
    return jnp.concatenate([values] * (chan // BLOCK), -1)


def scan_forward(
    n_ctx, n_tp, width,
    proj, keep, gain, lower,
    gated, state, scale, carry_out,
    local, reach, ends, squares, ctx_send, ctx_recv, tp_send, tp_recv,
):
    n_seq, length, chan = state.shape
    greet(others("ctx", n_ctx) + others("tp", n_tp))
    low = lower[...].reshape(1, 1, chan)
    row = lax.broadcasted_iota(jnp.int32, (n_seq, GROUP, chan), 1)

    def step(index, carry):
        prod, total = carry
        rows = pl.ds(pl.multiple_of(index * GROUP, GROUP), GROUP)
        inp = proj[0, :, rows, :]
        decay = low + (1.0 - low) * jax.nn.sigmoid(proj[1, :, rows, :])
        add = inp * jax.nn.sigmoid(inp) * (1.0 - decay)
        mult = decay * keep[:, rows, :]
        for hop in (1, 2, 4):
            inside = row >= hop
            add = jnp.where(inside, mult * pltpu.roll(add, hop, 1) + add, add)
            mult = jnp.where(inside, mult * pltpu.roll(mult, hop, 1), mult)
        add = add + mult * total
        mult = mult * prod
        local[:, rows, :] = add
        reach[:, rows, :] = mult
        return mult[:, GROUP - 1 :, :], add[:, GROUP - 1 :, :]

    start = (jnp.ones((n_seq, 1, chan), FLOAT), jnp.zeros((n_seq, 1, chan), FLOAT))
    prod, total = lax.fori_loop(0, length // GROUP, step, start)
    here = lax.axis_index("ctx")
    ends[here, 0] = prod.reshape(n_seq, chan)
    ends[here, 1] = total.reshape(n_seq, chan)
    share(ends, "ctx", n_ctx, ctx_send, ctx_recv)
    carry = jnp.zeros((n_seq, chan), FLOAT)
    for place in range(n_ctx - 1):
        carry = jnp.where(place < here, ends[place, 1] + ends[place, 0] * carry, carry)
    carry_out[...] = carry
    mine = lax.axis_index("tp")
    for seq in range(n_seq):
        for start in range(0, length, BLOCK):
            rows = slice(start, start + BLOCK)
            value = local[seq, rows, :] + reach[seq, rows, :] * carry[seq : seq + 1]
            state[seq, rows, :] = value
            squares[mine, seq : seq + 1, rows] = lane_sums(value * value)
    share(squares, "tp", n_tp, tp_send, tp_recv)
    total = squares[0]
    for place in range(1, n_tp):
        total = total + squares[place]
    rate = lax.rsqrt(total / width + EPS)
    scale[...] = rate
    for seq in range(n_seq):
        for start in range(0, length, BLOCK):
            rows = slice(start, start + BLOCK)
            gate = proj[2, seq, rows, :]
            unit = state[seq, rows, :] * widen(columns(rate[seq : seq + 1, rows]), chan)
            gated[seq, rows, :] = (unit * gain[...] * (gate * jax.nn.sigmoid(gate))).astype(HALF)


def run_scan_forward(proj, keep, gain, lower, n_ctx, n_tp, width):
    _, n_seq, length, chan = proj.shape
    vmem = pl.BlockSpec(memory_space=pltpu.VMEM)
    return pl.pallas_call(
        functools.partial(scan_forward, n_ctx, n_tp, width),
        name="scan_forward",
        out_shape=(
            jax.ShapeDtypeStruct((n_seq, length, chan), HALF),
            jax.ShapeDtypeStruct((n_seq, length, chan), FLOAT),
            jax.ShapeDtypeStruct((n_seq, length), FLOAT),
            jax.ShapeDtypeStruct((n_seq, chan), FLOAT),
        ),
        in_specs=[vmem] * 4,
        out_specs=[vmem] * 4,
        scratch_shapes=[
            pltpu.VMEM((n_seq, length, chan), FLOAT),
            pltpu.VMEM((n_seq, length, chan), FLOAT),
            pltpu.VMEM((n_ctx, 2, n_seq, chan), FLOAT),
            pltpu.VMEM((n_tp, n_seq, length), FLOAT),
            pltpu.SemaphoreType.DMA((n_ctx,)),
            pltpu.SemaphoreType.DMA((n_ctx,)),
            pltpu.SemaphoreType.DMA((n_tp,)),
            pltpu.SemaphoreType.DMA((n_tp,)),
        ],
        compiler_params=pltpu.CompilerParams(
            collective_id=0, has_side_effects=True, vmem_limit_bytes=40 * MIB
        ),
    )(proj, keep, gain, lower)


PIECES = 4
TILE = 256
WIDE = 512


def bands(count, size):
    return [(start, min(size, count - start)) for start in range(0, count, size)]


def dot(lhs, rhs):
    return jnp.dot(lhs, rhs, preferred_element_type=FLOAT)


def dot_nt(lhs, rhs):
    return lax.dot_general(lhs, rhs, (((1,), (1,)), ((), ())), preferred_element_type=FLOAT)


class Line:
    def __init__(self, held, cross, total, sems):
        self.held, self.cross, self.total, self.sems = held, cross, total, sems
        place = lax.axis_index("tp")
        self.inner = (place == 1) | (place == 2)
        self.side = place + 1 - 2 * lax.rem(place, 2)
        self.facing = 3 - place

    def slot(self, job, ref):
        slots = ref.shape[0]
        if slots == self.total.shape[0]:
            return job
        return job % slots if isinstance(job, int) else lax.rem(job, slots)

    def copy(self, source, target, send, recv, place):
        return pltpu.make_async_remote_copy(
            src_ref=source,
            dst_ref=target,
            send_sem=send,
            recv_sem=recv,
            device_id={"tp": place},
            device_id_type=MESH,
        )

    def inward(self, job, q):
        send, recv, _, _ = self.sems
        return self.copy(
            self.held.at[self.slot(job, self.held), q], self.total.at[job, q],
            send.at[job, q], recv.at[job, q], self.side,
        )

    def outward(self, job, q):
        send, recv, _, _ = self.sems
        return self.copy(
            self.total.at[job, q], self.total.at[job, q],
            send.at[job, q], recv.at[job, q], self.side,
        )

    def across(self, job, q):
        _, _, send, recv = self.sems
        return self.copy(
            self.held.at[self.slot(job, self.held), q], self.cross.at[self.slot(job, self.cross), q],
            send.at[job, q], recv.at[job, q], self.facing,
        )

    def offer(self, job, q):
        @pl.when(jnp.logical_not(self.inner))
        def _():
            self.inward(job, q).start()

    def forward(self, job, q):
        slot = self.slot(job, self.held)

        @pl.when(self.inner)
        def _():
            self.inward(job, q).wait_recv()
            self.held[slot, q] = self.held[slot, q] + self.total[job, q]
            self.across(job, q).start()

    def close(self, job, q):
        slot, cross_slot = self.slot(job, self.held), self.slot(job, self.cross)

        @pl.when(self.inner)
        def _():
            self.across(job, q).wait_recv()
            self.total[job, q] = self.held[slot, q] + self.cross[cross_slot, q]
            self.outward(job, q).start()

    def tick(self, base, step):
        if step > 0:
            self.close(base, step - 1)
        if step < PIECES:
            ahead = step + 1
            self.forward(base + ahead // PIECES, ahead % PIECES)

    def arrive(self, job):
        @pl.when(jnp.logical_not(self.inner))
        def _():
            @pl.loop(0, PIECES)
            def _(q):
                self.outward(job, q).wait_recv()

    def release(self, job):
        @pl.when(self.inner)
        def _():
            @pl.loop(0, PIECES)
            def _(q):
                self.across(job, q).wait_send()

        @pl.when(jnp.logical_not(self.inner))
        def _():
            @pl.loop(0, PIECES)
            def _(q):
                self.inward(job, q).wait_send()

    def settle(self, job):
        @pl.when(self.inner)
        def _():
            @pl.loop(0, PIECES)
            def _(q):
                self.outward(job, q).wait_send()


def pull(parts, wholes, dims, n_fsdp, own_sem, send_sem, recv_sem):
    if n_fsdp != 2:
        copies = [
            pltpu.make_async_copy(part, whole, own_sem.at[index])
            for index, (part, whole) in enumerate(zip(parts, wholes))
        ]
        for copy in copies:
            copy.start()
        return lambda index: copies[index].wait()
    mine = lax.axis_index("fsdp")
    near, far = [], []
    for index, (part, whole, dim) in enumerate(zip(parts, wholes, dims)):
        size = part.shape[dim]
        at = pl.ds(pl.multiple_of(mine * size, size), size)
        place = whole.at[at] if dim == 0 else whole.at[:, at]
        near.append(pltpu.make_async_copy(part, place, own_sem.at[index]))
        far.append(
            pltpu.make_async_remote_copy(
                src_ref=part,
                dst_ref=place,
                send_sem=send_sem.at[index],
                recv_sem=recv_sem.at[index],
                device_id={"fsdp": 1 - mine},
                device_id_type=MESH,
            )
        )
    for one, two in zip(near, far):
        two.start()
        one.start()

    def wait(index):
        near[index].wait()
        far[index].wait()

    return wait


def span(start, size, unit):
    return pl.ds(pl.multiple_of(start, unit), size)


def row_blocks(count, size, body):
    @pl.loop(0, count // size)
    def _(index):
        body(pl.ds(pl.multiple_of(index * size, size), size))


def line_peers():
    place = lax.axis_index("tp")
    return [{"tp": place + 1 - 2 * lax.rem(place, 2)}, {"tp": 3 - place}]


def joined(ref, c, rows):
    return jnp.concatenate([ref[c, q, rows, :].astype(FLOAT) for q in range(PIECES)], -1)


def add_to(target, extra, rows):
    target[rows, :] = target[rows, :] + extra[rows, :]


def halves(n_fsdp, store_sem, send_sem, recv_sem, spare, inbox):
    mine = lax.axis_index("fsdp")
    pending = {}

    def send(index, view):
        slot = index % 2
        return pltpu.make_async_remote_copy(
            src_ref=view(spare.at[slot]),
            dst_ref=view(inbox.at[slot]),
            send_sem=send_sem.at[slot],
            recv_sem=recv_sem.at[slot],
            device_id={"fsdp": 1 - mine},
            device_id_type=MESH,
        )

    def item(index, view, compute_other, compute_own, other_place, target):
        slot = index % 2
        if index - 2 in pending:
            pending.pop(index - 2)()
        compute_other(view(spare.at[slot]))
        if n_fsdp == 2:
            copy = send(index, view)
            copy.start()
            pending[index] = lambda: send(index, view).wait_send()
        else:
            def store():
                return pltpu.make_async_copy(view(spare.at[slot]), other_place(), store_sem.at[slot])

            store().start()
            pending[index] = lambda: store().wait()
        compute_own(target)
        if n_fsdp == 2:
            send(index, view).wait_recv()
            extra = view(inbox.at[slot])
            row_blocks(target.shape[0], 32, lambda rows: add_to(target, extra, rows))

    def finish():
        for wait in pending.values():
            wait()

    return item, finish


class Square:
    def __init__(self, index, buffers, at, place, send, recv, store_sem):
        self.buffers, self.at, self.place_of = buffers, at, place
        self.send, self.recv, self.index, self.store_sem = send, recv, index, store_sem

    @property
    def tile(self):
        return self.buffers[0].at[self.at]

    @property
    def half(self):
        return self.buffers[1].at[self.at]

    @property
    def quarter(self):
        return self.buffers[2].at[self.at]

    def geometry(self):
        here = lax.axis_index("ctx")
        low, high = lax.rem(here, 2), here // 2
        near, far = here + 1 - 2 * low, here + 2 - 4 * high
        bits = (low, high) if self.index % 2 == 0 else (high, low)
        peers = (near, far) if self.index % 2 == 0 else (far, near)
        wide, thin = self.half.shape[1], self.quarter.shape[1]
        begin = bits[0] * wide
        return (
            peers,
            span(begin, wide, BLOCK),
            span((1 - bits[0]) * wide, wide, BLOCK),
            span(begin + bits[1] * thin, thin, BLOCK),
            span(begin + (1 - bits[1]) * thin, thin, BLOCK),
        )

    def round(self, number):
        peers, mine, yours, my_part, your_part = self.geometry()
        source, target, peer = (
            (self.tile.at[:, yours], self.half, 0),
            (self.tile.at[:, your_part], self.quarter, 1),
            (self.tile.at[:, my_part], self.place_of().at[:, my_part], 1),
            (self.place_of().at[:, mine], self.place_of().at[:, mine], 0),
        )[number]
        return pltpu.make_async_remote_copy(
            src_ref=source,
            dst_ref=target,
            send_sem=self.send.at[self.index, number],
            recv_sem=self.recv.at[self.index, number],
            device_id={"ctx": peers[peer]},
            device_id_type=MESH,
        )

    def add(self, cols, extra):
        target = self.tile.at[:, cols]
        row_blocks(self.tile.shape[0], 32, lambda rows: add_to(target, extra, rows))

    def store(self):
        return pltpu.make_async_copy(self.tile, self.place_of(), self.store_sem.at[self.index])

    def store_part(self):
        part = self.geometry()[3]
        return pltpu.make_async_copy(
            self.tile.at[:, part], self.place_of().at[:, part], self.store_sem.at[self.index]
        )

    def advance(self, number):
        if number > 0:
            self.round(number - 1).wait_recv()
        if number == 1:
            self.add(self.geometry()[1], self.half)
        if number == 2:
            self.add(self.geometry()[3], self.quarter)
            self.store_part().start()
        if number == 3:
            self.store_part().wait()
        if number < 4:
            self.round(number).start()

    def settle(self):
        for number in range(4):
            self.round(number).wait_send()


def fill(target, left, right, first):
    for start, size in bands(target.shape[1], WIDE):
        cols = pl.ds(pl.multiple_of(first + start, BLOCK), size)
        target[:, start : start + size] = dot(left, right[:, cols]).astype(HALF)


def middle(
    n_fsdp, CHUNK,
    gated, tokens, cotangent, gain, wo_part, wg_part, wu_part, wd_part,
    mixed_out, normed_out, act_out, grad_glu_out, grad_resid_out, grad_mixed_out,
    grad_gated_out, w_glu_out, w_down_out, grad_gain_out,
    wo, wg, wu, wd, x_all, dy_all, held, crossed, total, normed, act, grad_glu,
    grad_resid, grad_mixed, grad_gated, gain_total, spare, own, inbox,
    weight_sem, weight_send, weight_recv, again_sem, own_sem, send_sem, recv_sem, load_sem, store_sem, *line_sems,
):
    n_chunks, _, _, piece = held.shape
    units = wd.shape[0]
    width = wd.shape[1]
    peers = line_peers()
    if n_fsdp == 2:
        peers.append({"fsdp": 1 - lax.axis_index("fsdp")})
    greet(peers)
    ready = pull(
        (wo_part, wg_part, wu_part, wd_part), (wo, wg, wu, wd), (1, 0, 0, 1),
        n_fsdp, own_sem, send_sem, recv_sem,
    )
    loads = [
        pltpu.make_async_copy(tokens, x_all, load_sem.at[0]),
        pltpu.make_async_copy(cotangent, dy_all, load_sem.at[1]),
    ]
    for load in loads:
        load.start()
    line = Line(held, crossed, total, line_sems)

    def chunk_rows(c):
        return pl.ds(pl.multiple_of(c * CHUNK, CHUNK), CHUNK)

    def stores(c, wanted=None):
        rows = chunk_rows(c)
        pairs = [
            (normed, normed_out.at[rows]),
            (act, act_out.at[rows]),
            (grad_glu.at[0], grad_glu_out.at[0, rows]),
            (grad_glu.at[1], grad_glu_out.at[1, rows]),
            (grad_resid, grad_resid_out.at[rows]),
            (grad_mixed, grad_mixed_out.at[rows]),
            (grad_gated, grad_gated_out.at[rows]),
        ]
        pairs += [
            (total.at[c, q], mixed_out.at[rows, pl.ds(q * piece, piece)]) for q in range(PIECES)
        ]
        return [
            pltpu.make_async_copy(source, target, store_sem.at[index])
            for index, (source, target) in enumerate(pairs)
            if wanted is None or index in wanted
        ]

    FORWARD = (0, 1, 2, 3, 7, 8, 9, 10)
    BACKWARD = (4, 5, 6)

    ready(0)

    @pl.loop(0, n_chunks)
    def _(c):
        lhs = gated[chunk_rows(c), :]

        @pl.loop(0, PIECES)
        def _(q):
            cols = pl.ds(pl.multiple_of(q * piece, piece), piece)
            held[c, q] = dot(lhs, wo[:, cols]).astype(HALF)
            line.offer(c, q)

    for load in loads:
        load.wait()
    line.forward(0, 0)
    for step in range(PIECES + 1):
        line.tick(0, step)
    for index in (1, 2, 3):
        ready(index)
    w_down_store = pltpu.make_async_copy(wd, w_down_out, again_sem.at[3])
    w_down_store.start()

    @pl.loop(0, n_chunks)
    def _(c):
        line.arrive(c)
        line.tick(c + 1, 0)

        @pl.when(c > 0)
        def _():
            for store in stores(c - 1, FORWARD):
                store.wait()

        def norm(rows):
            at = pl.ds(pl.multiple_of(c * CHUNK + rows.start, 16), rows.size)
            resid = x_all[at, :].astype(FLOAT) + joined(total, c, rows)
            normed[rows, :] = (resid * rms_scale(resid) * gain[...]).astype(HALF)

        row_blocks(CHUNK, 16, norm)

        def unit(cols):
            glu_gate = dot(normed[...], wg[:, cols])
            glu_up = dot(normed[...], wu[:, cols])
            grad_act = dot_nt(dy_all[chunk_rows(c), :], wd[cols, :])
            sig = jax.nn.sigmoid(glu_gate)
            silu = glu_gate * sig
            act[:, cols] = (silu * glu_up).astype(HALF)
            slope = sig * (1.0 + glu_gate * (1.0 - sig))
            grad_glu[0, :, cols] = (grad_act * glu_up * slope).astype(HALF)
            grad_glu[1, :, cols] = (grad_act * silu).astype(HALF)

        for index, (start, size) in enumerate(bands(units, WIDE)):
            unit(slice(start, start + size))
            if index == 0:
                line.tick(c + 1, 1)
        line.tick(c + 1, 2)
        line.release(c)

        @pl.loop(0, PIECES)
        def _(q):
            @pl.when(q == PIECES // 2)
            def _():
                line.tick(c + 1, 3)

            at = pl.ds(pl.multiple_of(q * piece, piece), piece)
            value = dot_nt(grad_glu[0], wg[at, :]) + dot_nt(grad_glu[1], wu[at, :])
            held[c, q] = value.astype(HALF)
            line.offer(n_chunks + c, q)

        line.tick(c + 1, 4)

        for store in stores(c, FORWARD):
            store.start()

    for store in stores(n_chunks - 1, FORWARD):
        store.wait()
    rows = n_chunks * CHUNK
    w_down_store.wait()
    kept = [
        (grad_glu_out.at[0], wg.at[:rows]),
        (grad_glu_out.at[1], wu.at[:rows]),
        (normed_out, wd.at[:rows]),
    ]
    again = [
        pltpu.make_async_copy(source, target, again_sem.at[index])
        for index, (source, target) in enumerate(kept)
    ]
    for copy in again:
        copy.start()
    gain_total[...] = jnp.zeros_like(gain_total)
    item, finish = halves(n_fsdp, weight_sem, weight_send, weight_recv, spare, inbox)
    mine = lax.axis_index("fsdp") if n_fsdp == 2 else 1
    depth = width // 2
    whole = n_fsdp != 2
    per_part = depth // TILE
    own_stores = {}

    def weight_item(index):
        if index >= 2 * per_part:
            return
        part, k = divmod(index, per_part)
        right = (wg, wu)[part].at[:rows]
        slot = index % 2
        if index > 1:
            own_stores.pop(slot).wait()

        def compute(side):
            at = pl.ds(pl.multiple_of(side * depth + k * TILE, TILE), TILE)
            return lambda target: fill(target, wd[:rows, at].T, right, 0)

        at = slice(k * TILE + whole * depth, (k + 1) * TILE + whole * depth)
        item(
            index, lambda ref: ref, compute(1 - mine), compute(mine),
            lambda: w_glu_out.at[part, k * TILE : (k + 1) * TILE], own.at[slot],
        )
        store = pltpu.make_async_copy(own.at[slot], w_glu_out.at[part, at], weight_sem.at[2 + slot])
        store.start()
        own_stores[slot] = store

    def backward(c):
        line.arrive(n_chunks + c)
        if c > 0:
            for store in stores(c - 1, BACKWARD):
                store.wait()

        def norm_back(rows):
            at = pl.ds(pl.multiple_of(c * CHUNK + rows.start, 16), rows.size)
            resid = x_all[at, :].astype(FLOAT) + joined(total, c, rows)
            rate = rms_scale(resid)
            grad = joined(total, n_chunks + c, rows)
            by_gain = grad * (resid * rate)
            gain_total[...] += by_gain[:8] + by_gain[8:]
            inner = gain[...] * grad
            mean = jnp.mean(inner * resid, -1, keepdims=True)
            value = dy_all[at, :].astype(FLOAT) + rate * inner - resid * (rate * rate * rate * mean)
            grad_resid[rows, :] = value
            grad_mixed[rows, :] = value.astype(HALF)

        row_blocks(CHUNK, 16, norm_back)
        for start, size in bands(grad_gated.shape[1], WIDE):
            grad_gated[:, start : start + size] = dot_nt(
                grad_mixed[...], wo[start : start + size, :]
            )
        for store in stores(c, BACKWARD):
            store.start()

    for copy in again:
        copy.wait()
    count = 0
    for c in range(n_chunks):
        if c == n_chunks - 1:
            while count < 2 * per_part:
                weight_item(count)
                count += 1
        backward(c)
        if c + 1 < n_chunks:
            for step in range(PIECES + 1):
                if step % 2 == 0:
                    weight_item(count)
                    count += 1
                if c + 2 == n_chunks and step == PIECES - 1:
                    line.close(2 * n_chunks - 1, step - 1)
                else:
                    line.tick(n_chunks + c + 1, step)
    finish()
    for store in own_stores.values():
        store.wait()

    grad_gain_out[...] = jnp.sum(gain_total[...], 0, keepdims=True)
    for store in stores(n_chunks - 1, BACKWARD):
        store.wait()

    @pl.loop(0, n_chunks)
    def _(c):
        line.settle(c)
        line.settle(n_chunks + c)
        line.release(n_chunks + c)


def run_middle(gated, tokens, cotangent, gain, parts, n_fsdp, length):
    rows, chan = gated.shape
    width = tokens.shape[1]
    wg = parts[1]
    units = wg.shape[1]
    n_chunks = rows // length
    piece = width // PIECES
    vmem = pl.BlockSpec(memory_space=pltpu.VMEM)
    hbm = pl.BlockSpec(memory_space=pl.ANY)
    sems = pltpu.SemaphoreType.DMA((2 * n_chunks, PIECES))
    return pl.pallas_call(
        functools.partial(middle, n_fsdp, length),
        name="middle",
        out_shape=(
            jax.ShapeDtypeStruct((rows, width), HALF),
            jax.ShapeDtypeStruct((rows, width), HALF),
            jax.ShapeDtypeStruct((rows, units), HALF),
            jax.ShapeDtypeStruct((2, rows, units), HALF),
            jax.ShapeDtypeStruct((rows, width), FLOAT),
            jax.ShapeDtypeStruct((rows, width), HALF),
            jax.ShapeDtypeStruct((rows, chan), FLOAT),
            jax.ShapeDtypeStruct((2, width if n_fsdp != 2 else width // 2, units), HALF),
            jax.ShapeDtypeStruct((units, width), HALF),
            jax.ShapeDtypeStruct((1, width), FLOAT),
        ),
        in_specs=[vmem, hbm, hbm, vmem, hbm, hbm, hbm, hbm],
        out_specs=[hbm] * 9 + [vmem],
        scratch_shapes=[
            pltpu.VMEM((chan, width), HALF),
            pltpu.VMEM((width, units), HALF),
            pltpu.VMEM((width, units), HALF),
            pltpu.VMEM((units, width), HALF),
            pltpu.VMEM((rows, width), HALF),
            pltpu.VMEM((rows, width), HALF),
            pltpu.VMEM((n_chunks, PIECES, length, piece), HALF),
            pltpu.VMEM((n_chunks, PIECES, length, piece), HALF),
            pltpu.VMEM((2 * n_chunks, PIECES, length, piece), HALF),
            pltpu.VMEM((length, width), HALF),
            pltpu.VMEM((length, units), HALF),
            pltpu.VMEM((2, length, units), HALF),
            pltpu.VMEM((length, width), FLOAT),
            pltpu.VMEM((length, width), HALF),
            pltpu.VMEM((length, chan), FLOAT),
            pltpu.VMEM((8, width), FLOAT),
            pltpu.VMEM((2, TILE, units), HALF),
            pltpu.VMEM((2, TILE, units), HALF),
            pltpu.VMEM((2, TILE, units), HALF),
            pltpu.SemaphoreType.DMA((4,)),
            pltpu.SemaphoreType.DMA((2,)),
            pltpu.SemaphoreType.DMA((2,)),
            pltpu.SemaphoreType.DMA((4,)),
            pltpu.SemaphoreType.DMA((4,)),
            pltpu.SemaphoreType.DMA((4,)),
            pltpu.SemaphoreType.DMA((4,)),
            pltpu.SemaphoreType.DMA((2,)),
            pltpu.SemaphoreType.DMA((12,)),
        ]
        + [sems] * 4,
        compiler_params=pltpu.CompilerParams(
            collective_id=2, has_side_effects=True, vmem_limit_bytes=63 * MIB
        ),
        cost_estimate=pl.CostEstimate(
            flops=16 * rows * width * units, bytes_accessed=400 * MIB, transcendentals=0
        ),
    )(gated, tokens, cotangent, gain, *parts)


def scan_cross(gate_all, state, scale, gain, near, grad_proj, gain_out, cross):
    n_seq, length, chan = state.shape
    mine = lax.axis_index("tp")
    gain_total = jnp.zeros((8, chan), FLOAT)
    for seq in range(n_seq):
        for start in range(0, length, BLOCK):
            rows = slice(start, start + BLOCK)
            rate = columns(scale[seq : seq + 1, rows])
            gate = gate_all[seq, rows, :]
            sig = jax.nn.sigmoid(gate)
            swish = gate * sig
            value = state[seq, rows, :]
            into = near[seq, rows, :]
            by_unit = into * value * widen(rate, chan)
            slope = sig * (1.0 + gate * (1.0 - sig))
            grad_proj[seq, rows, 2 * chan :] = (by_unit * gain[...] * slope).astype(HALF)
            gain_total = gain_total + jnp.sum((by_unit * swish).reshape(-1, 8, chan), 0)
            grad_unit = into * swish * gain[...]
            near[seq, rows, :] = grad_unit
            cross[mine, seq : seq + 1, rows] = lane_sums(grad_unit * value)
    gain_out[...] = jnp.sum(gain_total, 0, keepdims=True)


def scan_back(
    n_ctx, n_tp, width, pump,
    proj, keep, lower, state, scale, carry_in, near,
    grad_proj, lower_out,
    reach, rate_wide, cross_wide, ends, cross, ctx_sems,
):
    n_seq, length, chan = state.shape
    low = lower[...].reshape(1, 1, chan)
    total = cross[0]
    for place in range(1, n_tp):
        total = total + cross[place]
    rate = scale[...]
    total = total * (rate * rate * rate) / width
    for seq in range(n_seq):
        for start in range(0, length, BLOCK):
            rows = slice(start, start + BLOCK)
            rate_wide[seq, rows, :] = columns(rate[seq : seq + 1, rows])
            cross_wide[seq, rows, :] = columns(total[seq : seq + 1, rows])

    row = lax.broadcasted_iota(jnp.int32, (n_seq, GROUP, chan), 1)

    def back(index, carry):
        prod, above = carry
        rows = pl.ds(pl.multiple_of((length // GROUP - 1 - index) * GROUP, GROUP), GROUP)
        decay = low + (1.0 - low) * jax.nn.sigmoid(proj[1, :, rows, :])
        mult = decay * keep[:, rows, :]
        direct = (
            widen(rate_wide[:, rows, :], chan) * near[:, rows, :]
            - widen(cross_wide[:, rows, :], chan) * state[:, rows, :]
        )
        add = mult * direct
        for hop in (1, 2, 4):
            inside = row < GROUP - hop
            add = jnp.where(inside, mult * pltpu.roll(add, GROUP - hop, 1) + add, add)
            mult = jnp.where(inside, mult * pltpu.roll(mult, GROUP - hop, 1), mult)
        add = add + mult * above
        mult = mult * prod
        inside = row < GROUP - 1
        near[:, rows, :] = direct + jnp.where(inside, pltpu.roll(add, GROUP - 1, 1), above)
        reach[:, rows, :] = jnp.where(inside, pltpu.roll(mult, GROUP - 1, 1), prod)
        return mult[:, :1, :], add[:, :1, :]

    held = (jnp.ones((n_seq, 1, chan), FLOAT), jnp.zeros((n_seq, 1, chan), FLOAT))
    held = lax.fori_loop(0, length // GROUP, back, held)
    prod, total = held
    here = lax.axis_index("ctx")
    ends[here, 0] = prod.reshape(n_seq, chan)
    ends[here, 1] = total.reshape(n_seq, chan)
    pump()
    share(ends, "ctx", n_ctx, *ctx_sems)
    carry = jnp.zeros((n_seq, chan), FLOAT)
    for place in range(n_ctx - 1, 0, -1):
        carry = jnp.where(place > here, ends[place, 1] + ends[place, 0] * carry, carry)
    carry = carry.reshape(n_seq, 1, chan)
    wide = 2 * GROUP
    first = lax.broadcasted_iota(jnp.int32, (n_seq, wide, chan), 1) == 0

    def finish(index, held):
        before, low_total = held
        rows = pl.ds(pl.multiple_of(index * wide, wide), wide)
        inp = proj[0, :, rows, :]
        sig = jax.nn.sigmoid(inp)
        silu = inp * sig
        fsig = jax.nn.sigmoid(proj[1, :, rows, :])
        rest = 1.0 - fsig
        decay = low + (1.0 - low) * fsig
        grad_state = near[:, rows, :] + reach[:, rows, :] * carry
        value = state[:, rows, :]
        prev = jnp.where(first, before, pltpu.roll(value, 1, 1))
        grad_decay = grad_state * (prev * keep[:, rows, :] - silu)
        grad_proj[:, rows, :chan] = (
            grad_state * (1.0 - decay) * (sig * (1.0 + inp * (1.0 - sig)))
        ).astype(HALF)
        grad_proj[:, rows, chan : 2 * chan] = (
            grad_decay * (1.0 - low) * fsig * rest
        ).astype(HALF)
        return value[:, wide - 1 :, :], low_total + grad_decay * rest

    held = (carry_in[...].reshape(n_seq, 1, chan), jnp.zeros((n_seq, wide, chan), FLOAT))
    _, low_total = lax.fori_loop(0, length // wide, finish, held)
    lower_out[...] = jnp.sum(jnp.sum(low_total, 0), 0, keepdims=True)
    pump()


def tail(
    n_fsdp, n_ctx, n_tp,
    keep, gate_gain, lower, scale, carry_in, gain, gain_two_grad,
    proj, state, grad_gated, w_in, w_down, act, normed, grad_mixed, gated, cotangent,
    grad_resid, tokens, mixed,
    grad_tokens_out, output_out, vectors_out, w_in_out, w_out_out, w_down_out,
    grad_proj, held, crossed, total, spare, inbox,
    in_tile, in_half, in_quarter, out_tile, out_half, out_quarter, down_tile, down_half, down_quarter,
    gain_total, ends, cross, over_ctx, over_fsdp, near,
    load_sem, store_sem, end_send, end_recv, cross_send, cross_recv, ctx_send, ctx_recv,
    fsdp_send, fsdp_recv, part_sem, part_send, part_recv, square_send, square_recv, square_store,
    *line_sems,
):
    n_seq, length, wide = grad_proj.shape
    chan = wide // 3
    rows = n_seq * length
    width = gain.shape[1]
    units = w_down.shape[0]
    piece = width // PIECES
    n_chunks = n_seq
    whole = n_fsdp != 2
    greet(others("ctx", n_ctx) + others("tp", n_tp) + others("fsdp", n_fsdp))
    line = Line(held, crossed, total, line_sems)
    pieces = [(job, q) for job in range(2 * n_chunks) for q in range(PIECES)]
    relay = [(line.forward, spot) for spot in pieces[:2]]
    for index, spot in enumerate(pieces):
        relay.append((line.close, spot))
        relay += [(line.forward, ahead) for ahead in pieces[index + 2 : index + 3]]
    squares = []
    turn = [0]
    SPACE = 3

    def pump():
        while relay:
            action, spot = relay.pop(0)
            action(*spot)
            if action == line.forward:
                break
        for square in squares:
            if square[1] < 5 and turn[0] >= square[2] + SPACE * square[1]:
                square[0].advance(square[1])
                square[1] += 1
        turn[0] += 1

    def start_loads(pairs, first=0):
        copies = [
            pltpu.make_async_copy(source, target, load_sem.at[first + index])
            for index, (source, target) in enumerate(pairs)
        ]
        for copy in copies:
            copy.start()
        return copies

    def chunk_rows(c):
        return pl.ds(c * length, length) if isinstance(c, int) else span(c * length, length, length)

    shape = (n_seq, length, chan)

    crossing = shares(cross, "tp", n_tp, cross_send, cross_recv)

    def down_terms(w_all, act_all):
        copies = start_loads([(w_down, w_all), (act, act_all)], 3)

        def cross_terms(gate_all, state_all):
            for copy in start_loads(
                [(proj.at[2], gate_all), (state, state_all), (grad_gated, near)]
            ):
                copy.wait()
            gain_at = over_ctx.at[lax.axis_index("ctx"), :, 2 * width : 2 * width + chan]
            scan_cross(gate_all, state_all, scale, gate_gain, near, grad_proj, gain_at, cross)

        pl.run_scoped(cross_terms, pltpu.VMEM(shape, FLOAT), pltpu.VMEM(shape, FLOAT))
        for copy in crossing:
            copy.start()
        for copy in copies:
            copy.wait()

        for c in range(n_chunks):
            @pl.loop(0, PIECES)
            def _(q):
                cols = pl.ds(pl.multiple_of(q * piece, piece), piece)
                held[c, q] = dot(act_all[chunk_rows(c), :], w_all[:, cols]).astype(HALF)
                line.offer(c, q)

            if c >= n_chunks // 2:
                pump()

    pl.run_scoped(
        down_terms, pltpu.VMEM((units, width), HALF), pltpu.VMEM((rows, units), HALF)
    )

    for copy in crossing:
        copy.wait()

    def back(proj_all, state_all, reach, rate_wide, cross_wide):
        for copy in start_loads([(proj.at[:2], proj_all), (state, state_all)]):
            copy.wait()
        lower_at = over_ctx.at[lax.axis_index("ctx"), :, 2 * width + chan :]
        scan_back(
            n_ctx, n_tp, width, pump,
            proj_all, keep, lower, state_all, scale, carry_in, near,
            grad_proj, lower_at,
            reach, rate_wide, cross_wide, ends, cross, (end_send, end_recv),
        )

    pl.run_scoped(
        back,
        pltpu.VMEM((2, *shape), FLOAT),
        pltpu.VMEM(shape, FLOAT),
        pltpu.VMEM(shape, FLOAT),
        pltpu.VMEM((n_seq, length, BLOCK), FLOAT),
        pltpu.VMEM((n_seq, length, BLOCK), FLOAT),
    )

    def back_terms(w_all):
        for copy in start_loads(
            [(w_in.at[gate], w_all.at[:, gate * chan : (gate + 1) * chan]) for gate in range(3)]
        ):
            copy.wait()

        for c in range(n_chunks):
            @pl.loop(0, PIECES)
            def _(q):
                at = pl.ds(pl.multiple_of(q * piece, piece), piece)
                held[n_chunks + c, q] = dot_nt(grad_proj[c], w_all[at, :]).astype(HALF)
                line.offer(n_chunks + c, q)

            if c % 2 == 1:
                pump()

    pl.run_scoped(back_terms, pltpu.VMEM((width, wide), HALF))

    item, finish = halves(n_fsdp, part_sem, part_send, part_recv, spare, inbox)
    mine = 1 if whole else lax.axis_index("fsdp")
    depth = width // 2
    skip = whole * depth
    stores = []

    def weights(act_all, dy_all, normed_all, mixed_all, gated_all):
        copies = start_loads(
            [(act, act_all), (cotangent, dy_all), (normed, normed_all), (grad_mixed, mixed_all),
             (gated, gated_all)]
        )
        count = [0]

        def tile(view, compute, other_place, own_place, buffers, at):
            index = count[0]
            count[0] += 1
            square = Square(
                index, buffers, at, own_place, square_send, square_recv, square_store
            )
            item(index, view, compute(1 - mine), compute(mine), other_place, square.tile)
            if whole:
                square.store().start()
                stores.append(square)
            else:
                squares.append([square, 0, turn[0]])
            pump()

        copies[0].wait()
        copies[1].wait()
        for start, size in bands(units, TILE):
            left = act_all[:, start : start + size].T
            at = slice(start, start + size)

            def compute(side):
                return lambda target: fill(target, left, dy_all, side * depth)

            tile(
                lambda ref, size=size: ref.at[:size, :depth], compute,
                lambda at=at: w_down_out.at[at, :depth], lambda at=at: w_down_out.at[at, skip:],
                (down_tile, down_half, down_quarter), at,
            )
        copies[2].wait()
        flat_proj = grad_proj.reshape(rows, wide)
        for k in range(depth // TILE):
            def compute(side):
                at = pl.ds(pl.multiple_of(side * depth + k * TILE, TILE), TILE)
                return lambda target: fill(target, normed_all[:, at].T, flat_proj, 0)

            at = slice(k * TILE, (k + 1) * TILE)
            tile(
                lambda ref: ref, compute,
                lambda at=at: w_in_out.at[at],
                lambda k=k: w_in_out.at[k * TILE + skip : (k + 1) * TILE + skip],
                (in_tile, in_half, in_quarter), k,
            )
        copies[3].wait()
        copies[4].wait()
        for k in range(chan // TILE):
            at = slice(k * TILE, (k + 1) * TILE)
            left = gated_all[:, at].T

            def compute(side):
                return lambda target: fill(target, left, mixed_all, side * depth)

            tile(
                lambda ref: ref.at[:, :depth], compute,
                lambda at=at: w_out_out.at[at, :depth], lambda at=at: w_out_out.at[at, skip:],
                (out_tile, out_half, out_quarter), k,
            )

    pl.run_scoped(
        weights,
        pltpu.VMEM((rows, units), HALF),
        pltpu.VMEM((rows, width), HALF),
        pltpu.VMEM((rows, width), HALF),
        pltpu.VMEM((rows, width), HALF),
        pltpu.VMEM((rows, chan), HALF),
    )
    finish()

    def ends_of(resid_all, x_all, mixed_all):
        copies = start_loads([(tokens, x_all), (mixed, mixed_all), (grad_resid, resid_all)])
        copies[0].wait()
        copies[1].wait()
        gain_total[...] = jnp.zeros_like(gain_total)

        def token_store(c):
            at = chunk_rows(c)
            return pltpu.make_async_copy(
                resid_all.at[at], grad_tokens_out.at[at], store_sem.at[0, c]
            )

        def output_store(c):
            at = chunk_rows(c)
            return pltpu.make_async_copy(mixed_all.at[at], output_out.at[at], store_sem.at[1, c])

        def until(job):
            while (line.close, (job, PIECES - 1)) in relay:
                if relay[0] == (line.close, (job, PIECES - 1)):
                    action, spot = relay.pop(0)
                    action(*spot)
                else:
                    pump()

        for c in range(n_chunks):
            until(c)
            line.arrive(c)

            @pl.loop(0, length // 16)
            def _(index):
                at = pl.ds(pl.multiple_of(c * length + index * 16, 16), 16)
                rows = pl.ds(pl.multiple_of(index * 16, 16), 16)
                value = x_all[at, :].astype(FLOAT) + mixed_all[at, :].astype(FLOAT)
                mixed_all[at, :] = (value + joined(total, c, rows)).astype(HALF)

            output_store(c).start()

        copies[2].wait()
        for c in range(n_chunks):
            until(n_chunks + c)
            line.arrive(n_chunks + c)
            for quarter in range(PIECES):
                pump()

                @pl.loop(0, length // PIECES // 16)
                def _(index):
                    start = quarter * (length // PIECES) + index * 16
                    rows = pl.ds(pl.multiple_of(start, 16), 16)
                    at = pl.ds(pl.multiple_of(c * length + start, 16), 16)
                    value = x_all[at, :].astype(FLOAT)
                    rate = rms_scale(value)
                    grad = joined(total, n_chunks + c, rows)
                    by_gain = grad * (value * rate)
                    gain_total[...] += by_gain[:8] + by_gain[8:]
                    inner = gain[...] * grad
                    mean = jnp.mean(inner * value, -1, keepdims=True)
                    resid_all[at, :] = (
                        resid_all[at, :] + rate * inner - value * (rate * rate * rate * mean)
                    )

            token_store(c).start()

        here = lax.axis_index("ctx")
        over_ctx[here, :, :width] = jnp.sum(gain_total[...], 0, keepdims=True)
        over_ctx[here, :, width : 2 * width] = gain_two_grad[...]
        share(over_ctx, "ctx", n_ctx, ctx_send, ctx_recv)
        value = over_ctx[0]
        for place in range(1, n_ctx):
            value = value + over_ctx[place]
        over_fsdp[lax.axis_index("fsdp")] = value
        share(over_fsdp, "fsdp", n_fsdp, fsdp_send, fsdp_recv)
        value = over_fsdp[0]
        for place in range(1, n_fsdp):
            value = value + over_fsdp[place]
        vectors_out[...] = value
        while any(square[1] < 5 for square in squares):
            pump()
        for c in range(n_chunks):
            token_store(c).wait()
            output_store(c).wait()

    pl.run_scoped(
        ends_of,
        pltpu.VMEM((rows, width), FLOAT),
        pltpu.VMEM((rows, width), HALF),
        pltpu.VMEM((rows, width), HALF),
    )
    for square in squares:
        square[0].settle()
    for square in stores:
        square.store().wait()

    @pl.loop(0, 2 * n_chunks)
    def _(job):
        line.settle(job)
        line.release(job)


def run_tail(small, large, n_fsdp, n_ctx, n_tp):
    grad_gated, w_down, tokens = large[2], large[4], large[11]
    n_seq, length, chan = grad_gated.shape
    rows, width = tokens.shape
    units = w_down.shape[0]
    piece = width // PIECES
    size = 2 * width + 2 * chan
    depth = width // 2
    spread = width if n_fsdp != 2 else depth
    vmem = pl.BlockSpec(memory_space=pltpu.VMEM)
    hbm = pl.BlockSpec(memory_space=pl.ANY)
    slots = pltpu.VMEM((2 * n_seq, PIECES, length, piece), HALF)
    sems = pltpu.SemaphoreType.DMA((2 * n_seq, PIECES))
    n_in, n_out = depth // TILE, chan // TILE
    n_squares = n_in + n_out + len(bands(units, TILE))
    wide = max(3 * chan, depth)

    def tiles(*shape):
        return [pltpu.VMEM((*shape[:-1], shape[-1] // cut), HALF) for cut in (1, 2, 4)]

    return pl.pallas_call(
        functools.partial(tail, n_fsdp, n_ctx, n_tp),
        name="tail",
        out_shape=(
            jax.ShapeDtypeStruct((rows, width), FLOAT),
            jax.ShapeDtypeStruct((rows, width), HALF),
            jax.ShapeDtypeStruct((1, size), FLOAT),
            jax.ShapeDtypeStruct((spread, 3 * chan), HALF),
            jax.ShapeDtypeStruct((chan, spread), HALF),
            jax.ShapeDtypeStruct((units, spread), HALF),
        ),
        in_specs=[vmem] * len(small) + [hbm] * len(large),
        out_specs=[hbm, hbm, vmem, hbm, hbm, hbm],
        scratch_shapes=[
            pltpu.VMEM((n_seq, length, 3 * chan), HALF),
            slots,
            pltpu.VMEM((2 * n_seq, PIECES, length, piece), HALF),
            slots,
            pltpu.VMEM((2, TILE, wide), HALF),
            pltpu.VMEM((2, TILE, wide), HALF),
            *tiles(n_in, TILE, 3 * chan),
            *tiles(n_out, TILE, depth),
            *tiles(units, depth),
            pltpu.VMEM((8, width), FLOAT),
            pltpu.VMEM((n_ctx, 2, n_seq, chan), FLOAT),
            pltpu.VMEM((n_tp, n_seq, length), FLOAT),
            pltpu.VMEM((n_ctx, 1, size), FLOAT),
            pltpu.VMEM((n_fsdp, 1, size), FLOAT),
            pltpu.VMEM((n_seq, length, chan), FLOAT),
            pltpu.SemaphoreType.DMA((6,)),
            pltpu.SemaphoreType.DMA((2, n_seq)),
            pltpu.SemaphoreType.DMA((n_ctx,)),
            pltpu.SemaphoreType.DMA((n_ctx,)),
            pltpu.SemaphoreType.DMA((n_tp,)),
            pltpu.SemaphoreType.DMA((n_tp,)),
            pltpu.SemaphoreType.DMA((n_ctx,)),
            pltpu.SemaphoreType.DMA((n_ctx,)),
            pltpu.SemaphoreType.DMA((n_fsdp,)),
            pltpu.SemaphoreType.DMA((n_fsdp,)),
            pltpu.SemaphoreType.DMA((2,)),
            pltpu.SemaphoreType.DMA((2,)),
            pltpu.SemaphoreType.DMA((2,)),
            pltpu.SemaphoreType.DMA((n_squares, 4)),
            pltpu.SemaphoreType.DMA((n_squares, 4)),
            pltpu.SemaphoreType.DMA((n_squares,)),
        ]
        + [sems] * 4,
        compiler_params=pltpu.CompilerParams(
            collective_id=3, has_side_effects=True, vmem_limit_bytes=63 * MIB
        ),
        cost_estimate=pl.CostEstimate(
            flops=10 * rows * width * units, bytes_accessed=700 * MIB, transcendentals=0
        ),
    )(*small, *large)


def gather_fsdp(part, dim, count):
    if count != 2:
        return lax.all_gather(part, "fsdp", axis=dim, tiled=True)
    other = lax.ppermute(part, "fsdp", [(0, 1), (1, 0)])
    first = lax.axis_index("fsdp") == 0
    return jnp.concatenate(
        [jnp.where(first, part, other), jnp.where(first, other, part)], dim
    )


def keep_flags(segment_ids, count):
    last = lax.ppermute(
        segment_ids[:, -1:].astype(FLOAT), "ctx", [(place, place + 1) for place in range(count - 1)]
    )
    seg = segment_ids.astype(FLOAT)
    before = jnp.concatenate([last, seg[:, :-1]], 1)
    token = lax.broadcasted_iota(jnp.int32, seg.shape, 1)
    start = (token == 0) & (lax.axis_index("ctx") == 0)
    return jnp.where(start, 0.0, (seg == before).astype(FLOAT))


def local(
    sizes,
    tokens, segment_ids, w_in, w_out, w_glu, w_down, gain_one, gain_two, gate_gain, lower, cotangent,
):
    n_fsdp, n_ctx, n_tp = sizes
    n_seq, length, width = tokens.shape
    rows = n_seq * length
    chan = w_in.shape[2]
    gain_a = gather_fsdp(gain_one.astype(HALF)[None], 1, n_fsdp).astype(FLOAT)
    gain_b = gather_fsdp(gain_two.astype(HALF)[None], 1, n_fsdp).astype(FLOAT)
    w_in_all = gather_fsdp(w_in.astype(HALF), 1, n_fsdp)
    parts = (w_out.astype(HALF), w_glu[:, 0].astype(HALF), w_glu[:, 1].astype(HALF), w_down.astype(HALF))
    if n_fsdp != 2:
        parts = tuple(gather_fsdp(part, dim, n_fsdp) for part, dim in zip(parts, (1, 0, 0, 1)))
    keep = keep_flags(segment_ids, n_ctx)[..., None]
    gain_gate = gate_gain[None]
    low = lower[None]
    flat = tokens.reshape(rows, width).astype(FLOAT)
    scale_one = rms_scale(flat)
    normed = (flat * scale_one * gain_a).astype(HALF)
    proj = jnp.einsum("td,wdc->wtc", normed, w_in_all, preferred_element_type=FLOAT)
    proj = proj.reshape(3, n_seq, length, chan)
    gated, state, gate_scale, carry = run_scan_forward(
        proj, keep, gain_gate, low, n_ctx, n_tp, width
    )
    gated = gated.reshape(rows, chan)
    x_half = tokens.reshape(rows, width)
    grad_y_half = cotangent.reshape(rows, width)
    (
        mixed, _, act, _, grad_resid, grad_mixed, grad_gated, grad_w_glu, w_down_all, grad_gain_two
    ) = run_middle(gated, x_half, grad_y_half, gain_b, parts, n_fsdp, length)
    if n_fsdp != 2:
        grad_w_glu = lax.psum_scatter(grad_w_glu, "fsdp", scatter_dimension=1, tiled=True)
    grad_w_glu = lax.psum(grad_w_glu, "ctx")
    grad_tokens, output, vectors, grad_w_in, grad_w_out, grad_w_down = run_tail(
        (keep, gain_gate, low, gate_scale, carry, gain_a, grad_gain_two),
        (
            proj, state, grad_gated.reshape(n_seq, length, chan), w_in_all, w_down_all, act, normed,
            grad_mixed, gated, grad_y_half, grad_resid, x_half, mixed,
        ),
        n_fsdp, n_ctx, n_tp,
    )
    if n_fsdp == 2:
        grad_w_in = jnp.moveaxis(grad_w_in.reshape(width // 2, 3, chan), 1, 0)
    else:
        grad_w_in, grad_w_out, grad_w_down = (
            lax.psum(lax.psum_scatter(value, "fsdp", scatter_dimension=dim, tiled=True), "ctx")
            for value, dim in (
                (jnp.moveaxis(grad_w_in.reshape(width, 3, chan), 1, 0), 1),
                (grad_w_out, 1),
                (grad_w_down, 1),
            )
        )
    part = gain_one.shape[0]
    begin = lax.axis_index("fsdp") * part
    return (
        output.reshape(n_seq, length, width),
        grad_tokens.reshape(n_seq, length, width),
        grad_w_in.astype(FLOAT),
        grad_w_out.astype(FLOAT),
        jnp.moveaxis(grad_w_glu, 0, 1).astype(FLOAT),
        grad_w_down.astype(FLOAT),
        lax.dynamic_slice(vectors[0], (begin,), (part,)),
        lax.dynamic_slice(vectors[0], (width + begin,), (part,)),
        vectors[0, 2 * width : 2 * width + chan],
        vectors[0, 2 * width + chan :],
    )


def solution(mesh):
    sizes = tuple(mesh.shape[axis] for axis in ("fsdp", "ctx", "tp"))
    return jax.shard_map(
        functools.partial(local, sizes),
        mesh=mesh,
        in_specs=(
            P("fsdp", "ctx", None),
            P("fsdp", "ctx"),
            P(None, "fsdp", "tp"),
            P("tp", "fsdp"),
            P("fsdp", None, "tp"),
            P("tp", "fsdp"),
            P("fsdp"),
            P("fsdp"),
            P("tp"),
            P("tp"),
            P("fsdp", "ctx", None),
        ),
        out_specs=(
            P("fsdp", "ctx", None),
            P("fsdp", "ctx", None),
            P(None, "fsdp", "tp"),
            P("tp", "fsdp"),
            P("fsdp", None, "tp"),
            P("tp", "fsdp"),
            P("fsdp"),
            P("fsdp"),
            P("tp"),
            P("tp"),
        ),
        check_vma=False,
    )
```

```python
import functools

import jax
import jax.numpy as jnp
from jax import lax
from jax.experimental import pallas as pl
from jax.experimental.pallas import tpu as pltpu
from jax.sharding import PartitionSpec as P

EPS = 1e-06
FLOAT = jnp.float32
HALF = jnp.bfloat16
MESH = pl.DeviceIdType.MESH
GROUP = 8
BLOCK = 128
MIB = 1 << 20


def rms_scale(values):
    return lax.rsqrt(jnp.mean(values * values, -1, keepdims=True) + EPS)


def silu_slope(values):
    sig = jax.nn.sigmoid(values)
    return sig * (1.0 + values * (1.0 - sig))


def greet(peers):
    barrier = pltpu.get_barrier_semaphore()
    for peer in peers:
        pl.semaphore_signal(barrier, inc=1, device_id=peer, device_id_type=MESH)
    pl.semaphore_wait(barrier, len(peers))


def others(axis, count):
    mine = lax.axis_index(axis)
    return [{axis: lax.rem(mine + step, count)} for step in range(1, count)]


def shares(slots, axis, count, send, recv):
    mine = lax.axis_index(axis)
    return [
        pltpu.make_async_remote_copy(
            src_ref=slots.at[mine],
            dst_ref=slots.at[mine],
            send_sem=send.at[step],
            recv_sem=recv.at[step],
            device_id=peer,
            device_id_type=MESH,
        )
        for step, peer in enumerate(others(axis, count))
    ]


def share(slots, axis, count, send, recv):
    copies = shares(slots, axis, count, send, recv)
    for copy in copies:
        copy.start()
    for copy in copies:
        copy.wait()


def lane_sums(values):
    part = values[:, :BLOCK]
    for start in range(BLOCK, values.shape[1], BLOCK):
        part = part + values[:, start : start + BLOCK]
    return jnp.sum(part.T, 0, keepdims=True)


def columns(row):
    return jnp.broadcast_to(row, (BLOCK, BLOCK)).T


def widen(values, chan):
    return jnp.concatenate([values] * (chan // BLOCK), -1)


def scan_forward(
    n_ctx, n_tp, width,
    proj, keep, gain, lower,
    gated, state, scale, carry_out,
    local, reach, ends, squares, ctx_send, ctx_recv, tp_send, tp_recv,
):
    n_seq, length, chan = state.shape
    greet(others("ctx", n_ctx) + others("tp", n_tp))
    low = lower[...].reshape(1, 1, chan)
    row = lax.broadcasted_iota(jnp.int32, (n_seq, GROUP, chan), 1)

    def step(index, carry):
        prod, total = carry
        rows = pl.ds(pl.multiple_of(index * GROUP, GROUP), GROUP)
        inp = proj[0, :, rows, :]
        decay = low + (1.0 - low) * jax.nn.sigmoid(proj[1, :, rows, :])
        add = inp * jax.nn.sigmoid(inp) * (1.0 - decay)
        mult = decay * keep[:, rows, :]
        for hop in (1, 2, 4):
            inside = row >= hop
            add = jnp.where(inside, mult * pltpu.roll(add, hop, 1) + add, add)
            mult = jnp.where(inside, mult * pltpu.roll(mult, hop, 1), mult)
        add = add + mult * total
        mult = mult * prod
        local[:, rows, :] = add
        reach[:, rows, :] = mult
        return mult[:, GROUP - 1 :, :], add[:, GROUP - 1 :, :]

    start = (jnp.ones((n_seq, 1, chan), FLOAT), jnp.zeros((n_seq, 1, chan), FLOAT))
    prod, total = lax.fori_loop(0, length // GROUP, step, start)
    here = lax.axis_index("ctx")
    ends[here, 0] = prod.reshape(n_seq, chan)
    ends[here, 1] = total.reshape(n_seq, chan)
    share(ends, "ctx", n_ctx, ctx_send, ctx_recv)
    carry = jnp.zeros((n_seq, chan), FLOAT)
    for place in range(n_ctx - 1):
        carry = jnp.where(place < here, ends[place, 1] + ends[place, 0] * carry, carry)
    carry_out[...] = carry
    mine = lax.axis_index("tp")
    for seq in range(n_seq):
        for start in range(0, length, BLOCK):
            rows = slice(start, start + BLOCK)
            value = local[seq, rows, :] + reach[seq, rows, :] * carry[seq : seq + 1]
            state[seq, rows, :] = value
            squares[mine, seq : seq + 1, rows] = lane_sums(value * value)
    share(squares, "tp", n_tp, tp_send, tp_recv)
    total = squares[0]
    for place in range(1, n_tp):
        total = total + squares[place]
    rate = lax.rsqrt(total / width + EPS)
    scale[...] = rate
    for seq in range(n_seq):
        for start in range(0, length, BLOCK):
            rows = slice(start, start + BLOCK)
            gate = proj[2, seq, rows, :]
            unit = state[seq, rows, :] * widen(columns(rate[seq : seq + 1, rows]), chan)
            gated[seq, rows, :] = (unit * gain[...] * (gate * jax.nn.sigmoid(gate))).astype(HALF)


def run_scan_forward(proj, keep, gain, lower, n_ctx, n_tp, width):
    _, n_seq, length, chan = proj.shape
    vmem = pl.BlockSpec(memory_space=pltpu.VMEM)
    return pl.pallas_call(
        functools.partial(scan_forward, n_ctx, n_tp, width),
        name="scan_forward",
        out_shape=(
            jax.ShapeDtypeStruct((n_seq, length, chan), HALF),
            jax.ShapeDtypeStruct((n_seq, length, chan), FLOAT),
            jax.ShapeDtypeStruct((n_seq, length), FLOAT),
            jax.ShapeDtypeStruct((n_seq, chan), FLOAT),
        ),
        in_specs=[vmem] * 4,
        out_specs=[vmem] * 4,
        scratch_shapes=[
            pltpu.VMEM((n_seq, length, chan), FLOAT),
            pltpu.VMEM((n_seq, length, chan), FLOAT),
            pltpu.VMEM((n_ctx, 2, n_seq, chan), FLOAT),
            pltpu.VMEM((n_tp, n_seq, length), FLOAT),
            pltpu.SemaphoreType.DMA((n_ctx,)),
            pltpu.SemaphoreType.DMA((n_ctx,)),
            pltpu.SemaphoreType.DMA((n_tp,)),
            pltpu.SemaphoreType.DMA((n_tp,)),
        ],
        compiler_params=pltpu.CompilerParams(
            collective_id=0, has_side_effects=True, vmem_limit_bytes=40 * MIB
        ),
    )(proj, keep, gain, lower)


PIECES = 4
TILE = 256
WIDE = 512


def bands(count, size):
    return [(start, min(size, count - start)) for start in range(0, count, size)]


def dot(lhs, rhs):
    return jnp.dot(lhs, rhs, preferred_element_type=FLOAT)


def dot_nt(lhs, rhs):
    return lax.dot_general(lhs, rhs, (((1,), (1,)), ((), ())), preferred_element_type=FLOAT)


class Line:
    def __init__(self, held, cross, total, sems):
        self.held, self.cross, self.total, self.sems = held, cross, total, sems
        place = lax.axis_index("tp")
        self.inner = (place == 1) | (place == 2)
        self.side = place + 1 - 2 * lax.rem(place, 2)
        self.facing = 3 - place

    def slot(self, job, ref):
        slots = ref.shape[0]
        if slots == self.total.shape[0]:
            return job
        return job % slots if isinstance(job, int) else lax.rem(job, slots)

    def copy(self, source, target, send, recv, place):
        return pltpu.make_async_remote_copy(
            src_ref=source,
            dst_ref=target,
            send_sem=send,
            recv_sem=recv,
            device_id={"tp": place},
            device_id_type=MESH,
        )

    def inward(self, job, q):
        send, recv, _, _ = self.sems
        return self.copy(
            self.held.at[self.slot(job, self.held), q], self.total.at[job, q],
            send.at[job, q], recv.at[job, q], self.side,
        )

    def outward(self, job, q):
        send, recv, _, _ = self.sems
        return self.copy(
            self.total.at[job, q], self.total.at[job, q],
            send.at[job, q], recv.at[job, q], self.side,
        )

    def across(self, job, q):
        _, _, send, recv = self.sems
        return self.copy(
            self.held.at[self.slot(job, self.held), q], self.cross.at[self.slot(job, self.cross), q],
            send.at[job, q], recv.at[job, q], self.facing,
        )

    def offer(self, job, q):
        @pl.when(jnp.logical_not(self.inner))
        def _():
            self.inward(job, q).start()

    def forward(self, job, q):
        slot = self.slot(job, self.held)

        @pl.when(self.inner)
        def _():
            self.inward(job, q).wait_recv()
            self.held[slot, q] = self.held[slot, q] + self.total[job, q]
            self.across(job, q).start()

    def close(self, job, q):
        slot, cross_slot = self.slot(job, self.held), self.slot(job, self.cross)

        @pl.when(self.inner)
        def _():
            self.across(job, q).wait_recv()
            self.total[job, q] = self.held[slot, q] + self.cross[cross_slot, q]
            self.outward(job, q).start()

    def tick(self, base, step):
        if step > 0:
            self.close(base, step - 1)
        if step < PIECES:
            ahead = step + 1
            self.forward(base + ahead // PIECES, ahead % PIECES)

    def arrive(self, job):
        @pl.when(jnp.logical_not(self.inner))
        def _():
            @pl.loop(0, PIECES)
            def _(q):
                self.outward(job, q).wait_recv()

    def release(self, job):
        @pl.when(self.inner)
        def _():
            @pl.loop(0, PIECES)
            def _(q):
                self.across(job, q).wait_send()

        @pl.when(jnp.logical_not(self.inner))
        def _():
            @pl.loop(0, PIECES)
            def _(q):
                self.inward(job, q).wait_send()

    def settle(self, job):
        @pl.when(self.inner)
        def _():
            @pl.loop(0, PIECES)
            def _(q):
                self.outward(job, q).wait_send()


def pull(parts, wholes, dims, n_fsdp, own_sem, send_sem, recv_sem):
    if n_fsdp != 2:
        copies = [
            pltpu.make_async_copy(part, whole, own_sem.at[index])
            for index, (part, whole) in enumerate(zip(parts, wholes))
        ]
        for copy in copies:
            copy.start()
        return lambda index: copies[index].wait()
    mine = lax.axis_index("fsdp")
    near, far = [], []
    for index, (part, whole, dim) in enumerate(zip(parts, wholes, dims)):
        size = part.shape[dim]
        at = pl.ds(pl.multiple_of(mine * size, size), size)
        place = whole.at[at] if dim == 0 else whole.at[:, at]
        near.append(pltpu.make_async_copy(part, place, own_sem.at[index]))
        far.append(
            pltpu.make_async_remote_copy(
                src_ref=part,
                dst_ref=place,
                send_sem=send_sem.at[index],
                recv_sem=recv_sem.at[index],
                device_id={"fsdp": 1 - mine},
                device_id_type=MESH,
            )
        )
    for one, two in zip(near, far):
        two.start()
        one.start()

    def wait(index):
        near[index].wait()
        far[index].wait()

    return wait


def span(start, size, unit):
    return pl.ds(pl.multiple_of(start, unit), size)


def row_blocks(count, size, body):
    @pl.loop(0, count // size)
    def _(index):
        body(pl.ds(pl.multiple_of(index * size, size), size))


def line_peers():
    place = lax.axis_index("tp")
    return [{"tp": place + 1 - 2 * lax.rem(place, 2)}, {"tp": 3 - place}]


def joined(ref, c, rows):
    return jnp.concatenate([ref[c, q, rows, :].astype(FLOAT) for q in range(PIECES)], -1)


def add_to(target, extra, rows):
    target[rows, :] = target[rows, :] + extra[rows, :]


def halves(n_fsdp, store_sem, send_sem, recv_sem, spare, inbox):
    mine = lax.axis_index("fsdp")
    pending = {}

    def send(index, view):
        slot = index % 2
        return pltpu.make_async_remote_copy(
            src_ref=view(spare.at[slot]),
            dst_ref=view(inbox.at[slot]),
            send_sem=send_sem.at[slot],
            recv_sem=recv_sem.at[slot],
            device_id={"fsdp": 1 - mine},
            device_id_type=MESH,
        )

    def item(index, view, compute_other, compute_own, other_place, target):
        slot = index % 2
        if index - 2 in pending:
            pending.pop(index - 2)()
        compute_other(view(spare.at[slot]))
        if n_fsdp == 2:
            copy = send(index, view)
            copy.start()
            pending[index] = lambda: send(index, view).wait_send()
        else:
            def store():
                return pltpu.make_async_copy(view(spare.at[slot]), other_place(), store_sem.at[slot])

            store().start()
            pending[index] = lambda: store().wait()
        compute_own(target)
        if n_fsdp == 2:
            send(index, view).wait_recv()
            extra = view(inbox.at[slot])
            row_blocks(target.shape[0], 32, lambda rows: add_to(target, extra, rows))

    def finish():
        for wait in pending.values():
            wait()

    return item, finish


class Square:
    def __init__(self, index, buffers, at, place, send, recv, store_sem):
        self.buffers, self.at, self.place_of = buffers, at, place
        self.send, self.recv, self.index, self.store_sem = send, recv, index, store_sem

    @property
    def tile(self):
        return self.buffers[0].at[self.at[0]]

    @property
    def half(self):
        return self.buffers[1].at[self.at[1]]

    @property
    def quarter(self):
        return self.buffers[2].at[self.at[2]]

    def geometry(self):
        here = lax.axis_index("ctx")
        low, high = lax.rem(here, 2), here // 2
        near, far = here + 1 - 2 * low, here + 2 - 4 * high
        bits = (low, high) if self.index % 2 == 0 else (high, low)
        peers = (near, far) if self.index % 2 == 0 else (far, near)
        wide, thin = self.half.shape[0], self.quarter.shape[0]
        begin = bits[0] * wide
        return (
            peers,
            span(begin, wide, wide),
            span((1 - bits[0]) * wide, wide, wide),
            span(begin + bits[1] * thin, thin, thin),
            span(begin + (1 - bits[1]) * thin, thin, thin),
        )

    def round(self, number):
        peers, mine, yours, my_part, your_part = self.geometry()
        source, target, peer = (
            (self.tile.at[yours], self.half, 0),
            (self.tile.at[your_part], self.quarter, 1),
            (self.tile.at[my_part], self.place_of().at[my_part], 1),
            (self.place_of().at[mine], self.place_of().at[mine], 0),
        )[number]
        return pltpu.make_async_remote_copy(
            src_ref=source,
            dst_ref=target,
            send_sem=self.send.at[self.index, number],
            recv_sem=self.recv.at[self.index, number],
            device_id={"ctx": peers[peer]},
            device_id_type=MESH,
        )

    def add(self, part, extra):
        target = self.tile.at[part]
        row_blocks(extra.shape[0], 32, lambda rows: add_to(target, extra, rows))

    def store(self):
        return pltpu.make_async_copy(self.tile, self.place_of(), self.store_sem.at[self.index])

    def store_part(self):
        part = self.geometry()[3]
        return pltpu.make_async_copy(
            self.tile.at[part], self.place_of().at[part], self.store_sem.at[self.index]
        )

    def advance(self, number):
        if number > 0:
            self.round(number - 1).wait_recv()
        if number == 1:
            self.add(self.geometry()[1], self.half)
        if number == 2:
            self.add(self.geometry()[3], self.quarter)
            self.store_part().start()
        if number == 3:
            self.store_part().wait()
        if number < 4:
            self.round(number).start()

    def settle(self):
        for number in range(4):
            self.round(number).wait_send()


def fill(target, left, right, first):
    for start, size in bands(target.shape[1], WIDE):
        cols = pl.ds(pl.multiple_of(first + start, BLOCK), size)
        target[:, start : start + size] = dot(left, right[:, cols]).astype(HALF)


def middle(
    n_fsdp, n_ctx, CHUNK,
    gated, tokens, cotangent, gain, wo_part, wg_part, wu_part, wd_part,
    mixed_out, normed_out, act_out, grad_glu_out, grad_resid_out, grad_mixed_out,
    grad_gated_out, w_gate_out, w_up_out, w_down_out, grad_gain_out,
    wo, wg, wu, wd, x_all, dy_all, held, crossed, total, normed, act, grad_glu,
    grad_resid, grad_mixed, grad_gated, gain_total, spare, inbox, half, quarter,
    square_send, square_recv, square_store, weight_sem, weight_send, weight_recv, again_sem, own_sem, send_sem, recv_sem, load_sem, store_sem, *line_sems,
):
    n_chunks, _, _, piece = held.shape
    units = wd.shape[0]
    width = wd.shape[1]
    peers = line_peers() + others("ctx", n_ctx)
    if n_fsdp == 2:
        peers.append({"fsdp": 1 - lax.axis_index("fsdp")})
    greet(peers)
    ready = pull(
        (wo_part, wg_part, wu_part, wd_part), (wo, wg, wu, wd), (1, 0, 0, 1),
        n_fsdp, own_sem, send_sem, recv_sem,
    )
    loads = [
        pltpu.make_async_copy(tokens, x_all, load_sem.at[0]),
        pltpu.make_async_copy(cotangent, dy_all, load_sem.at[1]),
    ]
    for load in loads:
        load.start()
    line = Line(held, crossed, total, line_sems)

    def chunk_rows(c):
        return pl.ds(pl.multiple_of(c * CHUNK, CHUNK), CHUNK)

    def stores(c, wanted=None):
        rows = chunk_rows(c)
        pairs = [
            (normed, normed_out.at[rows]),
            (act, act_out.at[rows]),
            (grad_glu.at[0], grad_glu_out.at[0, rows]),
            (grad_glu.at[1], grad_glu_out.at[1, rows]),
            (grad_resid, grad_resid_out.at[rows]),
            (grad_mixed, grad_mixed_out.at[rows]),
            (grad_gated, grad_gated_out.at[rows]),
        ]
        pairs += [
            (total.at[c, q], mixed_out.at[rows, pl.ds(q * piece, piece)]) for q in range(PIECES)
        ]
        return [
            pltpu.make_async_copy(source, target, store_sem.at[index])
            for index, (source, target) in enumerate(pairs)
            if wanted is None or index in wanted
        ]

    FORWARD = (0, 1, 2, 3, 7, 8, 9, 10)
    BACKWARD = (4, 5, 6)

    ready(0)

    @pl.loop(0, n_chunks)
    def _(c):
        lhs = gated[chunk_rows(c), :]

        @pl.loop(0, PIECES)
        def _(q):
            cols = pl.ds(pl.multiple_of(q * piece, piece), piece)
            held[c, q] = dot(lhs, wo[:, cols]).astype(HALF)
            line.offer(c, q)

    for load in loads:
        load.wait()
    line.forward(0, 0)
    for step in range(PIECES + 1):
        line.tick(0, step)
    for index in (1, 2, 3):
        ready(index)
    w_down_store = pltpu.make_async_copy(wd, w_down_out, again_sem.at[3])
    w_down_store.start()

    @pl.loop(0, n_chunks)
    def _(c):
        line.arrive(c)
        line.tick(c + 1, 0)

        @pl.when(c > 0)
        def _():
            for store in stores(c - 1, FORWARD):
                store.wait()

        def norm(rows):
            at = pl.ds(pl.multiple_of(c * CHUNK + rows.start, 16), rows.size)
            resid = x_all[at, :].astype(FLOAT) + joined(total, c, rows)
            normed[rows, :] = (resid * rms_scale(resid) * gain[...]).astype(HALF)

        row_blocks(CHUNK, 16, norm)

        def unit(cols):
            glu_gate = dot(normed[...], wg[:, cols])
            glu_up = dot(normed[...], wu[:, cols])
            grad_act = dot_nt(dy_all[chunk_rows(c), :], wd[cols, :])
            sig = jax.nn.sigmoid(glu_gate)
            silu = glu_gate * sig
            act[:, cols] = (silu * glu_up).astype(HALF)
            slope = sig * (1.0 + glu_gate * (1.0 - sig))
            grad_glu[0, :, cols] = (grad_act * glu_up * slope).astype(HALF)
            grad_glu[1, :, cols] = (grad_act * silu).astype(HALF)

        for index, (start, size) in enumerate(bands(units, WIDE)):
            unit(slice(start, start + size))
            if index == 0:
                line.tick(c + 1, 1)
        line.tick(c + 1, 2)
        line.release(c)

        @pl.loop(0, PIECES)
        def _(q):
            @pl.when(q == PIECES // 2)
            def _():
                line.tick(c + 1, 3)

            at = pl.ds(pl.multiple_of(q * piece, piece), piece)
            value = dot_nt(grad_glu[0], wg[at, :]) + dot_nt(grad_glu[1], wu[at, :])
            held[c, q] = value.astype(HALF)
            line.offer(n_chunks + c, q)

        line.tick(c + 1, 4)

        for store in stores(c, FORWARD):
            store.start()

    for store in stores(n_chunks - 1, FORWARD):
        store.wait()
    rows = n_chunks * CHUNK
    w_down_store.wait()
    kept = [
        (grad_glu_out.at[0], wg.at[:rows]),
        (grad_glu_out.at[1], wu.at[:rows]),
        (normed_out, wd.at[:rows]),
    ]
    again = [
        pltpu.make_async_copy(source, target, again_sem.at[index])
        for index, (source, target) in enumerate(kept)
    ]
    for copy in again:
        copy.start()
    gain_total[...] = jnp.zeros_like(gain_total)
    item, finish = halves(n_fsdp, weight_sem, weight_send, weight_recv, spare, inbox)
    mine = lax.axis_index("fsdp") if n_fsdp == 2 else 1
    depth = width // 2
    whole = n_fsdp != 2
    per_part = depth // TILE
    squares, plain, turn = [], [], [0]

    def weight_item(index):
        if index >= 2 * per_part:
            return
        part, k = divmod(index, per_part)
        right = (wg, wu)[part].at[:rows]
        out = (w_gate_out, w_up_out)[part]

        def compute(side):
            at = pl.ds(pl.multiple_of(side * depth + k * TILE, TILE), TILE)
            return lambda target: fill(target, wd[:rows, at].T, right, 0)

        at = slice(k * TILE + whole * depth, (k + 1) * TILE + whole * depth)
        square = Square(
            index, ((wg, wu)[part], half, quarter),
            (slice(rows + k * TILE, rows + (k + 1) * TILE), k, k), lambda: out.at[at],
            square_send, square_recv, square_store,
        )
        item(
            index, lambda ref: ref, compute(1 - mine), compute(mine),
            lambda: out.at[k * TILE : (k + 1) * TILE], square.tile,
        )
        if whole or part == 1:
            square.store().start()
            plain.append(square)
        else:
            squares.append([square, 0, turn[0]])

    def pump():
        for square in squares:
            if square[1] < 5 and turn[0] >= square[2] + 2 * square[1]:
                square[0].advance(square[1])
                square[1] += 1
        turn[0] += 1

    def backward(c):
        line.arrive(n_chunks + c)
        if c > 0:
            for store in stores(c - 1, BACKWARD):
                store.wait()

        def norm_back(rows):
            at = pl.ds(pl.multiple_of(c * CHUNK + rows.start, 16), rows.size)
            resid = x_all[at, :].astype(FLOAT) + joined(total, c, rows)
            rate = rms_scale(resid)
            grad = joined(total, n_chunks + c, rows)
            by_gain = grad * (resid * rate)
            gain_total[...] += by_gain[:8] + by_gain[8:]
            inner = gain[...] * grad
            mean = jnp.mean(inner * resid, -1, keepdims=True)
            value = dy_all[at, :].astype(FLOAT) + rate * inner - resid * (rate * rate * rate * mean)
            grad_resid[rows, :] = value
            grad_mixed[rows, :] = value.astype(HALF)

        row_blocks(CHUNK, 16, norm_back)
        for start, size in bands(grad_gated.shape[1], WIDE):
            grad_gated[:, start : start + size] = dot_nt(
                grad_mixed[...], wo[start : start + size, :]
            )
        for store in stores(c, BACKWARD):
            store.start()

    for copy in again:
        copy.wait()
    count = 0
    for c in range(n_chunks):
        if c == n_chunks - 1:
            while count < 2 * per_part:
                weight_item(count)
                count += 1
        backward(c)
        if c + 1 < n_chunks:
            for step in range(PIECES + 1):
                weight_item(count)
                count += 1
                if c + 2 == n_chunks and step == PIECES - 1:
                    line.close(2 * n_chunks - 1, step - 1)
                else:
                    line.tick(n_chunks + c + 1, step)
                pump()
    while any(square[1] < 5 for square in squares):
        pump()
    finish()
    for square, _, _ in squares:
        square.settle()
    for square in plain:
        square.store().wait()

    grad_gain_out[...] = jnp.sum(gain_total[...], 0, keepdims=True)
    for store in stores(n_chunks - 1, BACKWARD):
        store.wait()

    @pl.loop(0, n_chunks)
    def _(c):
        line.settle(c)
        line.settle(n_chunks + c)
        line.release(n_chunks + c)


def run_middle(gated, tokens, cotangent, gain, parts, n_fsdp, n_ctx, length):
    rows, chan = gated.shape
    width = tokens.shape[1]
    wg = parts[1]
    units = wg.shape[1]
    n_chunks = rows // length
    piece = width // PIECES
    vmem = pl.BlockSpec(memory_space=pltpu.VMEM)
    hbm = pl.BlockSpec(memory_space=pl.ANY)
    sems = pltpu.SemaphoreType.DMA((2 * n_chunks, PIECES))
    return pl.pallas_call(
        functools.partial(middle, n_fsdp, n_ctx, length),
        name="middle",
        out_shape=(
            jax.ShapeDtypeStruct((rows, width), HALF),
            jax.ShapeDtypeStruct((rows, width), HALF),
            jax.ShapeDtypeStruct((rows, units), HALF),
            jax.ShapeDtypeStruct((2, rows, units), HALF),
            jax.ShapeDtypeStruct((rows, width), FLOAT),
            jax.ShapeDtypeStruct((rows, width), HALF),
            jax.ShapeDtypeStruct((rows, chan), FLOAT),
            jax.ShapeDtypeStruct((width if n_fsdp != 2 else width // 2, units), HALF),
            jax.ShapeDtypeStruct((width if n_fsdp != 2 else width // 2, units), HALF),
            jax.ShapeDtypeStruct((units, width), HALF),
            jax.ShapeDtypeStruct((1, width), FLOAT),
        ),
        in_specs=[vmem, hbm, hbm, vmem, hbm, hbm, hbm, hbm],
        out_specs=[hbm] * 10 + [vmem],
        scratch_shapes=[
            pltpu.VMEM((chan, width), HALF),
            pltpu.VMEM((width, units), HALF),
            pltpu.VMEM((width, units), HALF),
            pltpu.VMEM((units, width), HALF),
            pltpu.VMEM((rows, width), HALF),
            pltpu.VMEM((rows, width), HALF),
            pltpu.VMEM((n_chunks, PIECES, length, piece), HALF),
            pltpu.VMEM((n_chunks, PIECES, length, piece), HALF),
            pltpu.VMEM((2 * n_chunks, PIECES, length, piece), HALF),
            pltpu.VMEM((length, width), HALF),
            pltpu.VMEM((length, units), HALF),
            pltpu.VMEM((2, length, units), HALF),
            pltpu.VMEM((length, width), FLOAT),
            pltpu.VMEM((length, width), HALF),
            pltpu.VMEM((length, chan), FLOAT),
            pltpu.VMEM((8, width), FLOAT),
            pltpu.VMEM((2, TILE, units), HALF),
            pltpu.VMEM((2, TILE, units), HALF),
            pltpu.VMEM((width // 2 // TILE, TILE // 2, units), HALF),
            pltpu.VMEM((width // 2 // TILE, TILE // 4, units), HALF),
            pltpu.SemaphoreType.DMA((width // 2 // TILE, 4)),
            pltpu.SemaphoreType.DMA((width // 2 // TILE, 4)),
            pltpu.SemaphoreType.DMA((width // TILE,)),
            pltpu.SemaphoreType.DMA((4,)),
            pltpu.SemaphoreType.DMA((2,)),
            pltpu.SemaphoreType.DMA((2,)),
            pltpu.SemaphoreType.DMA((4,)),
            pltpu.SemaphoreType.DMA((4,)),
            pltpu.SemaphoreType.DMA((4,)),
            pltpu.SemaphoreType.DMA((4,)),
            pltpu.SemaphoreType.DMA((2,)),
            pltpu.SemaphoreType.DMA((12,)),
        ]
        + [sems] * 4,
        compiler_params=pltpu.CompilerParams(
            collective_id=2, has_side_effects=True, vmem_limit_bytes=63 * MIB
        ),
        cost_estimate=pl.CostEstimate(
            flops=16 * rows * width * units, bytes_accessed=400 * MIB, transcendentals=0
        ),
    )(gated, tokens, cotangent, gain, *parts)


def scan_cross(gate_all, state, scale, gain, near, grad_proj, gain_out, cross):
    n_seq, length, chan = state.shape
    mine = lax.axis_index("tp")
    gain_total = jnp.zeros((8, chan), FLOAT)
    for seq in range(n_seq):
        for start in range(0, length, BLOCK):
            rows = slice(start, start + BLOCK)
            rate = columns(scale[seq : seq + 1, rows])
            gate = gate_all[seq, rows, :]
            sig = jax.nn.sigmoid(gate)
            swish = gate * sig
            value = state[seq, rows, :]
            into = near[seq, rows, :]
            by_unit = into * value * widen(rate, chan)
            slope = sig * (1.0 + gate * (1.0 - sig))
            grad_proj[seq, rows, 2 * chan :] = (by_unit * gain[...] * slope).astype(HALF)
            gain_total = gain_total + jnp.sum((by_unit * swish).reshape(-1, 8, chan), 0)
            grad_unit = into * swish * gain[...]
            near[seq, rows, :] = grad_unit
            cross[mine, seq : seq + 1, rows] = lane_sums(grad_unit * value)
    gain_out[...] = jnp.sum(gain_total, 0, keepdims=True)


def scan_back(
    n_ctx, n_tp, width, pump,
    proj, keep, lower, state, scale, carry_in, near,
    grad_proj, lower_out,
    reach, rate_wide, cross_wide, ends, cross, ctx_sems,
):
    n_seq, length, chan = state.shape
    low = lower[...].reshape(1, 1, chan)
    total = cross[0]
    for place in range(1, n_tp):
        total = total + cross[place]
    rate = scale[...]
    total = total * (rate * rate * rate) / width
    for seq in range(n_seq):
        for start in range(0, length, BLOCK):
            rows = slice(start, start + BLOCK)
            rate_wide[seq, rows, :] = columns(rate[seq : seq + 1, rows])
            cross_wide[seq, rows, :] = columns(total[seq : seq + 1, rows])

    row = lax.broadcasted_iota(jnp.int32, (n_seq, GROUP, chan), 1)

    def back(index, carry):
        prod, above = carry
        rows = pl.ds(pl.multiple_of((length // GROUP - 1 - index) * GROUP, GROUP), GROUP)
        decay = low + (1.0 - low) * jax.nn.sigmoid(proj[1, :, rows, :])
        mult = decay * keep[:, rows, :]
        direct = (
            widen(rate_wide[:, rows, :], chan) * near[:, rows, :]
            - widen(cross_wide[:, rows, :], chan) * state[:, rows, :]
        )
        add = mult * direct
        for hop in (1, 2, 4):
            inside = row < GROUP - hop
            add = jnp.where(inside, mult * pltpu.roll(add, GROUP - hop, 1) + add, add)
            mult = jnp.where(inside, mult * pltpu.roll(mult, GROUP - hop, 1), mult)
        add = add + mult * above
        mult = mult * prod
        inside = row < GROUP - 1
        near[:, rows, :] = direct + jnp.where(inside, pltpu.roll(add, GROUP - 1, 1), above)
        reach[:, rows, :] = jnp.where(inside, pltpu.roll(mult, GROUP - 1, 1), prod)
        return mult[:, :1, :], add[:, :1, :]

    held = (jnp.ones((n_seq, 1, chan), FLOAT), jnp.zeros((n_seq, 1, chan), FLOAT))
    held = lax.fori_loop(0, length // GROUP, back, held)
    prod, total = held
    here = lax.axis_index("ctx")
    ends[here, 0] = prod.reshape(n_seq, chan)
    ends[here, 1] = total.reshape(n_seq, chan)
    pump()
    share(ends, "ctx", n_ctx, *ctx_sems)
    carry = jnp.zeros((n_seq, chan), FLOAT)
    for place in range(n_ctx - 1, 0, -1):
        carry = jnp.where(place > here, ends[place, 1] + ends[place, 0] * carry, carry)
    carry = carry.reshape(n_seq, 1, chan)
    wide = 2 * GROUP
    first = lax.broadcasted_iota(jnp.int32, (n_seq, wide, chan), 1) == 0

    def finish(index, held):
        before, low_total = held
        rows = pl.ds(pl.multiple_of(index * wide, wide), wide)
        inp = proj[0, :, rows, :]
        sig = jax.nn.sigmoid(inp)
        silu = inp * sig
        fsig = jax.nn.sigmoid(proj[1, :, rows, :])
        rest = 1.0 - fsig
        decay = low + (1.0 - low) * fsig
        grad_state = near[:, rows, :] + reach[:, rows, :] * carry
        value = state[:, rows, :]
        prev = jnp.where(first, before, pltpu.roll(value, 1, 1))
        grad_decay = grad_state * (prev * keep[:, rows, :] - silu)
        grad_proj[:, rows, :chan] = (
            grad_state * (1.0 - decay) * (sig * (1.0 + inp * (1.0 - sig)))
        ).astype(HALF)
        grad_proj[:, rows, chan : 2 * chan] = (
            grad_decay * (1.0 - low) * fsig * rest
        ).astype(HALF)
        return value[:, wide - 1 :, :], low_total + grad_decay * rest

    held = (carry_in[...].reshape(n_seq, 1, chan), jnp.zeros((n_seq, wide, chan), FLOAT))
    _, low_total = lax.fori_loop(0, length // wide, finish, held)
    lower_out[...] = jnp.sum(jnp.sum(low_total, 0), 0, keepdims=True)
    pump()


def tail(
    n_fsdp, n_ctx, n_tp,
    keep, gate_gain, lower, scale, carry_in, gain, gain_two_grad,
    proj, state, grad_gated, w_in, w_down, act, normed, grad_mixed, gated, cotangent,
    grad_resid, tokens, mixed,
    grad_tokens_out, output_out, vectors_out, w_in_out, w_out_out, w_down_out,
    grad_proj, held, crossed, total, spare, inbox,
    in_tile, in_half, in_quarter, out_tile, out_half, out_quarter, down_tile, down_half, down_quarter,
    gain_total, ends, cross, over_ctx, over_fsdp, near,
    load_sem, store_sem, end_send, end_recv, cross_send, cross_recv, ctx_send, ctx_recv,
    fsdp_send, fsdp_recv, part_sem, part_send, part_recv, square_send, square_recv, square_store,
    *line_sems,
):
    n_seq, length, wide = grad_proj.shape
    chan = wide // 3
    rows = n_seq * length
    width = gain.shape[1]
    units = w_down.shape[0]
    piece = width // PIECES
    n_chunks = n_seq
    whole = n_fsdp != 2
    greet(others("ctx", n_ctx) + others("tp", n_tp) + others("fsdp", n_fsdp))
    line = Line(held, crossed, total, line_sems)
    pieces = [(job, q) for job in range(2 * n_chunks) for q in range(PIECES)]
    relay = [(line.forward, spot) for spot in pieces[:2]]
    for index, spot in enumerate(pieces):
        relay.append((line.close, spot))
        relay += [(line.forward, ahead) for ahead in pieces[index + 2 : index + 3]]
    squares = []
    turn = [0]
    SPACE = 3

    def pump():
        while relay:
            action, spot = relay.pop(0)
            action(*spot)
            if action == line.forward:
                break
        for square in squares:
            if square[1] < 5 and turn[0] >= square[2] + SPACE * square[1]:
                square[0].advance(square[1])
                square[1] += 1
        turn[0] += 1

    def start_loads(pairs, first=0):
        copies = [
            pltpu.make_async_copy(source, target, load_sem.at[first + index])
            for index, (source, target) in enumerate(pairs)
        ]
        for copy in copies:
            copy.start()
        return copies

    def chunk_rows(c):
        return pl.ds(c * length, length) if isinstance(c, int) else span(c * length, length, length)

    shape = (n_seq, length, chan)

    crossing = shares(cross, "tp", n_tp, cross_send, cross_recv)

    def down_terms(w_all, act_all):
        copies = start_loads([(w_down, w_all), (act, act_all)], 3)

        def cross_terms(gate_all, state_all):
            for copy in start_loads(
                [(proj.at[2], gate_all), (state, state_all), (grad_gated, near)]
            ):
                copy.wait()
            gain_at = over_ctx.at[lax.axis_index("ctx"), :, 2 * width : 2 * width + chan]
            scan_cross(gate_all, state_all, scale, gate_gain, near, grad_proj, gain_at, cross)

        pl.run_scoped(cross_terms, pltpu.VMEM(shape, FLOAT), pltpu.VMEM(shape, FLOAT))
        for copy in crossing:
            copy.start()
        for copy in copies:
            copy.wait()

        for c in range(n_chunks):
            @pl.loop(0, PIECES)
            def _(q):
                cols = pl.ds(pl.multiple_of(q * piece, piece), piece)
                held[c, q] = dot(act_all[chunk_rows(c), :], w_all[:, cols]).astype(HALF)
                line.offer(c, q)

            if c >= n_chunks // 2:
                pump()

    pl.run_scoped(
        down_terms, pltpu.VMEM((units, width), HALF), pltpu.VMEM((rows, units), HALF)
    )

    for copy in crossing:
        copy.wait()

    def back(proj_all, state_all, reach, rate_wide, cross_wide):
        for copy in start_loads([(proj.at[:2], proj_all), (state, state_all)]):
            copy.wait()
        lower_at = over_ctx.at[lax.axis_index("ctx"), :, 2 * width + chan :]
        scan_back(
            n_ctx, n_tp, width, pump,
            proj_all, keep, lower, state_all, scale, carry_in, near,
            grad_proj, lower_at,
            reach, rate_wide, cross_wide, ends, cross, (end_send, end_recv),
        )

    pl.run_scoped(
        back,
        pltpu.VMEM((2, *shape), FLOAT),
        pltpu.VMEM(shape, FLOAT),
        pltpu.VMEM(shape, FLOAT),
        pltpu.VMEM((n_seq, length, BLOCK), FLOAT),
        pltpu.VMEM((n_seq, length, BLOCK), FLOAT),
    )

    def back_terms(w_all):
        for copy in start_loads(
            [(w_in.at[gate], w_all.at[:, gate * chan : (gate + 1) * chan]) for gate in range(3)]
        ):
            copy.wait()

        for c in range(n_chunks):
            @pl.loop(0, PIECES)
            def _(q):
                at = pl.ds(pl.multiple_of(q * piece, piece), piece)
                held[n_chunks + c, q] = dot_nt(grad_proj[c], w_all[at, :]).astype(HALF)
                line.offer(n_chunks + c, q)

            if c % 2 == 1:
                pump()

    pl.run_scoped(back_terms, pltpu.VMEM((width, wide), HALF))

    item, finish = halves(n_fsdp, part_sem, part_send, part_recv, spare, inbox)
    mine = 1 if whole else lax.axis_index("fsdp")
    depth = width // 2
    skip = whole * depth
    stores = []

    def weights(act_all, dy_all, normed_all, mixed_all, gated_all):
        copies = start_loads(
            [(act, act_all), (cotangent, dy_all), (normed, normed_all), (grad_mixed, mixed_all),
             (gated, gated_all)]
        )
        count = [0]

        def tile(view, compute, other_place, own_place, buffers, at):
            index = count[0]
            count[0] += 1
            square = Square(
                index, buffers, at, own_place, square_send, square_recv, square_store
            )
            item(index, view, compute(1 - mine), compute(mine), other_place, square.tile)
            if whole:
                square.store().start()
                stores.append(square)
            else:
                squares.append([square, 0, turn[0]])
            pump()

        copies[0].wait()
        copies[1].wait()
        for start, size in bands(units, TILE):
            left = act_all[:, start : start + size].T
            at = slice(start, start + size)

            def compute(side):
                return lambda target: fill(target, left, dy_all, side * depth)

            tile(
                lambda ref, size=size: ref.at[:size, :depth], compute,
                lambda at=at: w_down_out.at[at, :depth], lambda at=at: w_down_out.at[at, skip:],
                (down_tile, down_half, down_quarter),
                [slice(start // cut, (start + size) // cut) for cut in (1, 2, 4)],
            )
        copies[2].wait()
        flat_proj = grad_proj.reshape(rows, wide)
        for k in range(depth // TILE):
            def compute(side):
                at = pl.ds(pl.multiple_of(side * depth + k * TILE, TILE), TILE)
                return lambda target: fill(target, normed_all[:, at].T, flat_proj, 0)

            at = slice(k * TILE, (k + 1) * TILE)
            tile(
                lambda ref: ref, compute,
                lambda at=at: w_in_out.at[at],
                lambda k=k: w_in_out.at[k * TILE + skip : (k + 1) * TILE + skip],
                (in_tile, in_half, in_quarter), (k, k, k),
            )
        copies[3].wait()
        copies[4].wait()
        for k in range(chan // TILE):
            at = slice(k * TILE, (k + 1) * TILE)
            left = gated_all[:, at].T

            def compute(side):
                return lambda target: fill(target, left, mixed_all, side * depth)

            tile(
                lambda ref: ref.at[:, :depth], compute,
                lambda at=at: w_out_out.at[at, :depth], lambda at=at: w_out_out.at[at, skip:],
                (out_tile, out_half, out_quarter), (k, k, k),
            )

    pl.run_scoped(
        weights,
        pltpu.VMEM((rows, units), HALF),
        pltpu.VMEM((rows, width), HALF),
        pltpu.VMEM((rows, width), HALF),
        pltpu.VMEM((rows, width), HALF),
        pltpu.VMEM((rows, chan), HALF),
    )
    finish()

    def ends_of(resid_all, x_all, mixed_all):
        copies = start_loads([(tokens, x_all), (mixed, mixed_all), (grad_resid, resid_all)])
        copies[0].wait()
        copies[1].wait()
        gain_total[...] = jnp.zeros_like(gain_total)

        def token_store(c):
            at = chunk_rows(c)
            return pltpu.make_async_copy(
                x_all.at[at], grad_tokens_out.at[at], store_sem.at[0, c]
            )

        def output_store(c):
            at = chunk_rows(c)
            return pltpu.make_async_copy(mixed_all.at[at], output_out.at[at], store_sem.at[1, c])

        def until(job):
            while (line.close, (job, PIECES - 1)) in relay:
                if relay[0] == (line.close, (job, PIECES - 1)):
                    action, spot = relay.pop(0)
                    action(*spot)
                else:
                    pump()

        for c in range(n_chunks):
            until(c)
            line.arrive(c)

            @pl.loop(0, length // 16)
            def _(index):
                at = pl.ds(pl.multiple_of(c * length + index * 16, 16), 16)
                rows = pl.ds(pl.multiple_of(index * 16, 16), 16)
                value = x_all[at, :].astype(FLOAT) + mixed_all[at, :].astype(FLOAT)
                mixed_all[at, :] = (value + joined(total, c, rows)).astype(HALF)

            output_store(c).start()

        copies[2].wait()
        for c in range(n_chunks):
            until(n_chunks + c)
            line.arrive(n_chunks + c)
            for quarter in range(PIECES):
                pump()

                @pl.loop(0, length // PIECES // 16)
                def _(index):
                    start = quarter * (length // PIECES) + index * 16
                    rows = pl.ds(pl.multiple_of(start, 16), 16)
                    at = pl.ds(pl.multiple_of(c * length + start, 16), 16)
                    value = x_all[at, :].astype(FLOAT)
                    rate = rms_scale(value)
                    grad = joined(total, n_chunks + c, rows)
                    by_gain = grad * (value * rate)
                    gain_total[...] += by_gain[:8] + by_gain[8:]
                    inner = gain[...] * grad
                    mean = jnp.mean(inner * value, -1, keepdims=True)
                    result = resid_all[at, :] + rate * inner - value * (rate * rate * rate * mean)
                    x_all[at, :] = result.astype(HALF)

            token_store(c).start()

        here = lax.axis_index("ctx")
        over_ctx[here, :, :width] = jnp.sum(gain_total[...], 0, keepdims=True)
        over_ctx[here, :, width : 2 * width] = gain_two_grad[...]
        share(over_ctx, "ctx", n_ctx, ctx_send, ctx_recv)
        value = over_ctx[0]
        for place in range(1, n_ctx):
            value = value + over_ctx[place]
        over_fsdp[lax.axis_index("fsdp")] = value
        share(over_fsdp, "fsdp", n_fsdp, fsdp_send, fsdp_recv)
        value = over_fsdp[0]
        for place in range(1, n_fsdp):
            value = value + over_fsdp[place]
        vectors_out[...] = value
        while any(square[1] < 5 for square in squares):
            pump()
        for c in range(n_chunks):
            token_store(c).wait()
            output_store(c).wait()

    pl.run_scoped(
        ends_of,
        pltpu.VMEM((rows, width), FLOAT),
        pltpu.VMEM((rows, width), HALF),
        pltpu.VMEM((rows, width), HALF),
    )
    for square in squares:
        square[0].settle()
    for square in stores:
        square.store().wait()

    @pl.loop(0, 2 * n_chunks)
    def _(job):
        line.settle(job)
        line.release(job)


def run_tail(small, large, n_fsdp, n_ctx, n_tp):
    grad_gated, w_down, tokens = large[2], large[4], large[11]
    n_seq, length, chan = grad_gated.shape
    rows, width = tokens.shape
    units = w_down.shape[0]
    piece = width // PIECES
    size = 2 * width + 2 * chan
    depth = width // 2
    spread = width if n_fsdp != 2 else depth
    vmem = pl.BlockSpec(memory_space=pltpu.VMEM)
    hbm = pl.BlockSpec(memory_space=pl.ANY)
    slots = pltpu.VMEM((2 * n_seq, PIECES, length, piece), HALF)
    sems = pltpu.SemaphoreType.DMA((2 * n_seq, PIECES))
    n_in, n_out = depth // TILE, chan // TILE
    n_squares = n_in + n_out + len(bands(units, TILE))
    wide = max(3 * chan, depth)

    def tiles(*shape):
        return [
            pltpu.VMEM((*shape[:-2], shape[-2] // cut, shape[-1]), HALF) for cut in (1, 2, 4)
        ]

    return pl.pallas_call(
        functools.partial(tail, n_fsdp, n_ctx, n_tp),
        name="tail",
        out_shape=(
            jax.ShapeDtypeStruct((rows, width), HALF),
            jax.ShapeDtypeStruct((rows, width), HALF),
            jax.ShapeDtypeStruct((1, size), FLOAT),
            jax.ShapeDtypeStruct((spread, 3 * chan), HALF),
            jax.ShapeDtypeStruct((chan, spread), HALF),
            jax.ShapeDtypeStruct((units, spread), HALF),
        ),
        in_specs=[vmem] * len(small) + [hbm] * len(large),
        out_specs=[hbm, hbm, vmem, hbm, hbm, hbm],
        scratch_shapes=[
            pltpu.VMEM((n_seq, length, 3 * chan), HALF),
            slots,
            pltpu.VMEM((2 * n_seq, PIECES, length, piece), HALF),
            slots,
            pltpu.VMEM((2, TILE, wide), HALF),
            pltpu.VMEM((2, TILE, wide), HALF),
            *tiles(n_in, TILE, 3 * chan),
            *tiles(n_out, TILE, depth),
            *tiles(units, depth),
            pltpu.VMEM((8, width), FLOAT),
            pltpu.VMEM((n_ctx, 2, n_seq, chan), FLOAT),
            pltpu.VMEM((n_tp, n_seq, length), FLOAT),
            pltpu.VMEM((n_ctx, 1, size), FLOAT),
            pltpu.VMEM((n_fsdp, 1, size), FLOAT),
            pltpu.VMEM((n_seq, length, chan), FLOAT),
            pltpu.SemaphoreType.DMA((6,)),
            pltpu.SemaphoreType.DMA((2, n_seq)),
            pltpu.SemaphoreType.DMA((n_ctx,)),
            pltpu.SemaphoreType.DMA((n_ctx,)),
            pltpu.SemaphoreType.DMA((n_tp,)),
            pltpu.SemaphoreType.DMA((n_tp,)),
            pltpu.SemaphoreType.DMA((n_ctx,)),
            pltpu.SemaphoreType.DMA((n_ctx,)),
            pltpu.SemaphoreType.DMA((n_fsdp,)),
            pltpu.SemaphoreType.DMA((n_fsdp,)),
            pltpu.SemaphoreType.DMA((2,)),
            pltpu.SemaphoreType.DMA((2,)),
            pltpu.SemaphoreType.DMA((2,)),
            pltpu.SemaphoreType.DMA((n_squares, 4)),
            pltpu.SemaphoreType.DMA((n_squares, 4)),
            pltpu.SemaphoreType.DMA((n_squares,)),
        ]
        + [sems] * 4,
        compiler_params=pltpu.CompilerParams(
            collective_id=3, has_side_effects=True, vmem_limit_bytes=63 * MIB
        ),
        cost_estimate=pl.CostEstimate(
            flops=10 * rows * width * units, bytes_accessed=700 * MIB, transcendentals=0
        ),
    )(*small, *large)


def widen_outputs(w_in, w_out, w_gate, w_up, w_down, tokens, w_in_out, w_out_out, w_glu_out, w_down_out, tokens_out):
    chan = w_in_out.shape[2]
    for gate in range(3):
        w_in_out[gate] = w_in[:, gate * chan : (gate + 1) * chan].astype(FLOAT)
    w_out_out[...] = w_out[...].astype(FLOAT)
    w_glu_out[:, 0, :] = w_gate[...].astype(FLOAT)
    w_glu_out[:, 1, :] = w_up[...].astype(FLOAT)
    w_down_out[...] = w_down[...].astype(FLOAT)
    tokens_out[...] = tokens[...].astype(FLOAT)


def run_widen_outputs(w_in, w_out, w_gate, w_up, w_down, tokens):
    steps = 8
    arrays = (w_in, w_out, w_gate, w_up, w_down, tokens)

    def spec(array):
        return pl.BlockSpec((array.shape[0] // steps, array.shape[1]), lambda i: (i, 0))

    depth, wide = w_in.shape
    chan = wide // 3
    units = w_gate.shape[1]
    shapes = [
        jax.ShapeDtypeStruct((3, depth, chan), FLOAT),
        jax.ShapeDtypeStruct(w_out.shape, FLOAT),
        jax.ShapeDtypeStruct((depth, 2, units), FLOAT),
        jax.ShapeDtypeStruct(w_down.shape, FLOAT),
        jax.ShapeDtypeStruct(tokens.shape, FLOAT),
    ]
    specs = [
        pl.BlockSpec((3, depth // steps, chan), lambda i: (0, i, 0)),
        spec(w_out),
        pl.BlockSpec((depth // steps, 2, units), lambda i: (i, 0, 0)),
        spec(w_down),
        spec(tokens),
    ]
    return pl.pallas_call(
        widen_outputs,
        name="widen_outputs",
        grid=(steps,),
        out_shape=shapes,
        in_specs=[spec(array) for array in arrays],
        out_specs=specs,
        compiler_params=pltpu.CompilerParams(vmem_limit_bytes=48 * MIB),
    )(*arrays)


def gather_fsdp(part, dim, count):
    if count != 2:
        return lax.all_gather(part, "fsdp", axis=dim, tiled=True)
    other = lax.ppermute(part, "fsdp", [(0, 1), (1, 0)])
    first = lax.axis_index("fsdp") == 0
    return jnp.concatenate(
        [jnp.where(first, part, other), jnp.where(first, other, part)], dim
    )


def keep_flags(segment_ids, count):
    last = lax.ppermute(
        segment_ids[:, -1:].astype(FLOAT), "ctx", [(place, place + 1) for place in range(count - 1)]
    )
    seg = segment_ids.astype(FLOAT)
    before = jnp.concatenate([last, seg[:, :-1]], 1)
    token = lax.broadcasted_iota(jnp.int32, seg.shape, 1)
    start = (token == 0) & (lax.axis_index("ctx") == 0)
    return jnp.where(start, 0.0, (seg == before).astype(FLOAT))


def local(
    sizes,
    tokens, segment_ids, w_in, w_out, w_glu, w_down, gain_one, gain_two, gate_gain, lower, cotangent,
):
    n_fsdp, n_ctx, n_tp = sizes
    n_seq, length, width = tokens.shape
    rows = n_seq * length
    chan = w_in.shape[2]
    gain_a = gather_fsdp(gain_one.astype(HALF)[None], 1, n_fsdp).astype(FLOAT)
    gain_b = gather_fsdp(gain_two.astype(HALF)[None], 1, n_fsdp).astype(FLOAT)
    w_in_all = gather_fsdp(w_in.astype(HALF), 1, n_fsdp)
    parts = (w_out.astype(HALF), w_glu[:, 0].astype(HALF), w_glu[:, 1].astype(HALF), w_down.astype(HALF))
    if n_fsdp != 2:
        parts = tuple(gather_fsdp(part, dim, n_fsdp) for part, dim in zip(parts, (1, 0, 0, 1)))
    keep = keep_flags(segment_ids, n_ctx)[..., None]
    gain_gate = gate_gain[None]
    low = lower[None]
    flat = tokens.reshape(rows, width).astype(FLOAT)
    scale_one = rms_scale(flat)
    normed = (flat * scale_one * gain_a).astype(HALF)
    proj = jnp.einsum("td,wdc->wtc", normed, w_in_all, preferred_element_type=FLOAT)
    proj = proj.reshape(3, n_seq, length, chan)
    gated, state, gate_scale, carry = run_scan_forward(
        proj, keep, gain_gate, low, n_ctx, n_tp, width
    )
    gated = gated.reshape(rows, chan)
    x_half = tokens.reshape(rows, width)
    grad_y_half = cotangent.reshape(rows, width)
    (
        mixed, _, act, _, grad_resid, grad_mixed, grad_gated, grad_w_gate, grad_w_up, w_down_all,
        grad_gain_two,
    ) = run_middle(gated, x_half, grad_y_half, gain_b, parts, n_fsdp, n_ctx, length)
    if n_fsdp == 2:
        grad_w_up = lax.psum(grad_w_up, "ctx")
    grad_tokens, output, vectors, grad_w_in, grad_w_out, grad_w_down = run_tail(
        (keep, gain_gate, low, gate_scale, carry, gain_a, grad_gain_two),
        (
            proj, state, grad_gated.reshape(n_seq, length, chan), w_in_all, w_down_all, act, normed,
            grad_mixed, gated, grad_y_half, grad_resid, x_half, mixed,
        ),
        n_fsdp, n_ctx, n_tp,
    )
    grads = (grad_w_in, grad_w_out, grad_w_gate, grad_w_up, grad_w_down)
    if n_fsdp != 2:
        grads = tuple(
            lax.psum(lax.psum_scatter(value, "fsdp", scatter_dimension=dim, tiled=True), "ctx")
            for value, dim in zip(grads, (0, 1, 0, 0, 1))
        )
    grad_w_in, grad_w_out, grad_w_glu, grad_w_down, grad_tokens = run_widen_outputs(
        *grads, grad_tokens
    )
    part = gain_one.shape[0]
    begin = lax.axis_index("fsdp") * part
    return (
        output.reshape(n_seq, length, width),
        grad_tokens.reshape(n_seq, length, width),
        grad_w_in,
        grad_w_out,
        grad_w_glu,
        grad_w_down,
        lax.dynamic_slice(vectors[0], (begin,), (part,)),
        lax.dynamic_slice(vectors[0], (width + begin,), (part,)),
        vectors[0, 2 * width : 2 * width + chan],
        vectors[0, 2 * width + chan :],
    )


def solution(mesh):
    sizes = tuple(mesh.shape[axis] for axis in ("fsdp", "ctx", "tp"))
    return jax.shard_map(
        functools.partial(local, sizes),
        mesh=mesh,
        in_specs=(
            P("fsdp", "ctx", None),
            P("fsdp", "ctx"),
            P(None, "fsdp", "tp"),
            P("tp", "fsdp"),
            P("fsdp", None, "tp"),
            P("tp", "fsdp"),
            P("fsdp"),
            P("fsdp"),
            P("tp"),
            P("tp"),
            P("fsdp", "ctx", None),
        ),
        out_specs=(
            P("fsdp", "ctx", None),
            P("fsdp", "ctx", None),
            P(None, "fsdp", "tp"),
            P("tp", "fsdp"),
            P("fsdp", None, "tp"),
            P("tp", "fsdp"),
            P("fsdp"),
            P("fsdp"),
            P("tp"),
            P("tp"),
        ),
        check_vma=False,
    )
```

```python
import functools

import jax
import jax.numpy as jnp
from jax import lax
from jax.experimental import pallas as pl
from jax.experimental.pallas import tpu as pltpu
from jax.sharding import PartitionSpec as P

EPS = 1e-06
FLOAT = jnp.float32
HALF = jnp.bfloat16
MESH = pl.DeviceIdType.MESH
GROUP = 8
BLOCK = 128
MIB = 1 << 20


def rms_scale(values):
    return lax.rsqrt(jnp.mean(values * values, -1, keepdims=True) + EPS)


def silu_slope(values):
    sig = jax.nn.sigmoid(values)
    return sig * (1.0 + values * (1.0 - sig))


def greet(peers):
    barrier = pltpu.get_barrier_semaphore()
    for peer in peers:
        pl.semaphore_signal(barrier, inc=1, device_id=peer, device_id_type=MESH)
    pl.semaphore_wait(barrier, len(peers))


def others(axis, count):
    mine = lax.axis_index(axis)
    return [{axis: lax.rem(mine + step, count)} for step in range(1, count)]


def shares(slots, axis, count, send, recv):
    mine = lax.axis_index(axis)
    return [
        pltpu.make_async_remote_copy(
            src_ref=slots.at[mine],
            dst_ref=slots.at[mine],
            send_sem=send.at[step],
            recv_sem=recv.at[step],
            device_id=peer,
            device_id_type=MESH,
        )
        for step, peer in enumerate(others(axis, count))
    ]


def share(slots, axis, count, send, recv):
    copies = shares(slots, axis, count, send, recv)
    for copy in copies:
        copy.start()
    for copy in copies:
        copy.wait()


def lane_sums(values):
    part = values[:, :BLOCK]
    for start in range(BLOCK, values.shape[1], BLOCK):
        part = part + values[:, start : start + BLOCK]
    return jnp.sum(part.T, 0, keepdims=True)


def columns(row):
    return jnp.broadcast_to(row, (BLOCK, BLOCK)).T


def widen(values, chan):
    return jnp.concatenate([values] * (chan // BLOCK), -1)


PIECES = 4
TILE = 256
WIDE = 512


def bands(count, size):
    return [(start, min(size, count - start)) for start in range(0, count, size)]


def dot(lhs, rhs):
    return jnp.dot(lhs, rhs, preferred_element_type=FLOAT)


def dot_nt(lhs, rhs):
    return lax.dot_general(lhs, rhs, (((1,), (1,)), ((), ())), preferred_element_type=FLOAT)


class Line:
    def __init__(self, held, cross, total, sems):
        self.held, self.cross, self.total, self.sems = held, cross, total, sems
        place = lax.axis_index("tp")
        self.inner = (place == 1) | (place == 2)
        self.side = place + 1 - 2 * lax.rem(place, 2)
        self.facing = 3 - place

    def slot(self, job, ref):
        slots = ref.shape[0]
        if slots == self.total.shape[0]:
            return job
        return job % slots if isinstance(job, int) else lax.rem(job, slots)

    def copy(self, source, target, send, recv, place):
        return pltpu.make_async_remote_copy(
            src_ref=source,
            dst_ref=target,
            send_sem=send,
            recv_sem=recv,
            device_id={"tp": place},
            device_id_type=MESH,
        )

    def inward(self, job, q):
        send, recv, _, _ = self.sems
        return self.copy(
            self.held.at[self.slot(job, self.held), q], self.total.at[job, q],
            send.at[job, q], recv.at[job, q], self.side,
        )

    def outward(self, job, q):
        send, recv, _, _ = self.sems
        return self.copy(
            self.total.at[job, q], self.total.at[job, q],
            send.at[job, q], recv.at[job, q], self.side,
        )

    def across(self, job, q):
        _, _, send, recv = self.sems
        return self.copy(
            self.held.at[self.slot(job, self.held), q], self.cross.at[self.slot(job, self.cross), q],
            send.at[job, q], recv.at[job, q], self.facing,
        )

    def offer(self, job, q):
        @pl.when(jnp.logical_not(self.inner))
        def _():
            self.inward(job, q).start()

    def forward(self, job, q):
        slot = self.slot(job, self.held)

        @pl.when(self.inner)
        def _():
            self.inward(job, q).wait_recv()
            self.held[slot, q] = self.held[slot, q] + self.total[job, q]
            self.across(job, q).start()

    def close(self, job, q):
        slot, cross_slot = self.slot(job, self.held), self.slot(job, self.cross)

        @pl.when(self.inner)
        def _():
            self.across(job, q).wait_recv()
            self.total[job, q] = self.held[slot, q] + self.cross[cross_slot, q]
            self.outward(job, q).start()

    def tick(self, base, step):
        if step > 0:
            self.close(base, step - 1)
        if step < PIECES:
            ahead = step + 1
            self.forward(base + ahead // PIECES, ahead % PIECES)

    def arrive(self, job):
        @pl.when(jnp.logical_not(self.inner))
        def _():
            @pl.loop(0, PIECES)
            def _(q):
                self.outward(job, q).wait_recv()

    def release(self, job):
        @pl.when(self.inner)
        def _():
            @pl.loop(0, PIECES)
            def _(q):
                self.across(job, q).wait_send()

        @pl.when(jnp.logical_not(self.inner))
        def _():
            @pl.loop(0, PIECES)
            def _(q):
                self.inward(job, q).wait_send()

    def settle(self, job):
        @pl.when(self.inner)
        def _():
            @pl.loop(0, PIECES)
            def _(q):
                self.outward(job, q).wait_send()


def pull(parts, wholes, dims, n_fsdp, own_sem, send_sem, recv_sem):
    if n_fsdp != 2:
        copies = [
            pltpu.make_async_copy(part, whole, own_sem.at[index])
            for index, (part, whole) in enumerate(zip(parts, wholes))
        ]
        for copy in copies:
            copy.start()
        return lambda index: copies[index].wait()
    mine = lax.axis_index("fsdp")
    near, far = [], []
    for index, (part, whole, dim) in enumerate(zip(parts, wholes, dims)):
        size = part.shape[dim]
        at = pl.ds(pl.multiple_of(mine * size, size), size)
        place = whole.at[at] if dim == 0 else whole.at[:, at]
        near.append(pltpu.make_async_copy(part, place, own_sem.at[index]))
        far.append(
            pltpu.make_async_remote_copy(
                src_ref=part,
                dst_ref=place,
                send_sem=send_sem.at[index],
                recv_sem=recv_sem.at[index],
                device_id={"fsdp": 1 - mine},
                device_id_type=MESH,
            )
        )
    for one, two in zip(near, far):
        two.start()
        one.start()

    def wait(index):
        near[index].wait()
        far[index].wait()

    return wait


def span(start, size, unit):
    return pl.ds(pl.multiple_of(start, unit), size)


def row_blocks(count, size, body):
    @pl.loop(0, count // size)
    def _(index):
        body(pl.ds(pl.multiple_of(index * size, size), size))


def line_peers():
    place = lax.axis_index("tp")
    return [{"tp": place + 1 - 2 * lax.rem(place, 2)}, {"tp": 3 - place}]


def joined(ref, c, rows):
    return jnp.concatenate([ref[c, q, rows, :].astype(FLOAT) for q in range(PIECES)], -1)


def add_to(target, extra, rows):
    target[rows, :] = target[rows, :] + extra[rows, :]


def halves(n_fsdp, store_sem, send_sem, recv_sem, spare, inbox):
    mine = lax.axis_index("fsdp")
    pending = {}

    def send(index, view):
        slot = index % 2
        return pltpu.make_async_remote_copy(
            src_ref=view(spare.at[slot]),
            dst_ref=view(inbox.at[slot]),
            send_sem=send_sem.at[slot],
            recv_sem=recv_sem.at[slot],
            device_id={"fsdp": 1 - mine},
            device_id_type=MESH,
        )

    def item(index, view, compute_other, compute_own, other_place, target):
        slot = index % 2
        if index - 2 in pending:
            pending.pop(index - 2)()
        compute_other(view(spare.at[slot]))
        if n_fsdp == 2:
            copy = send(index, view)
            copy.start()
            pending[index] = lambda: send(index, view).wait_send()
        else:
            def store():
                return pltpu.make_async_copy(view(spare.at[slot]), other_place(), store_sem.at[slot])

            store().start()
            pending[index] = lambda: store().wait()
        compute_own(target)
        if n_fsdp == 2:
            send(index, view).wait_recv()
            extra = view(inbox.at[slot])
            row_blocks(target.shape[0], 32, lambda rows: add_to(target, extra, rows))

    def finish():
        for wait in pending.values():
            wait()

    return item, finish


class Square:
    def __init__(self, index, buffers, at, place, send, recv, store_sem):
        self.buffers, self.at, self.place_of = buffers, at, place
        self.send, self.recv, self.index, self.store_sem = send, recv, index, store_sem

    @property
    def tile(self):
        return self.buffers[0].at[self.at[0]]

    @property
    def half(self):
        return self.buffers[1].at[self.at[1]]

    @property
    def quarter(self):
        return self.buffers[2].at[self.at[2]]

    def geometry(self):
        here = lax.axis_index("ctx")
        low, high = lax.rem(here, 2), here // 2
        near, far = here + 1 - 2 * low, here + 2 - 4 * high
        bits = (low, high) if self.index % 2 == 0 else (high, low)
        peers = (near, far) if self.index % 2 == 0 else (far, near)
        wide, thin = self.half.shape[0], self.quarter.shape[0]
        begin = bits[0] * wide
        return (
            peers,
            span(begin, wide, wide),
            span((1 - bits[0]) * wide, wide, wide),
            span(begin + bits[1] * thin, thin, thin),
            span(begin + (1 - bits[1]) * thin, thin, thin),
        )

    def round(self, number):
        peers, mine, yours, my_part, your_part = self.geometry()
        source, target, peer = (
            (self.tile.at[yours], self.half, 0),
            (self.tile.at[your_part], self.quarter, 1),
            (self.tile.at[my_part], self.place_of().at[my_part], 1),
            (self.place_of().at[mine], self.place_of().at[mine], 0),
        )[number]
        return pltpu.make_async_remote_copy(
            src_ref=source,
            dst_ref=target,
            send_sem=self.send.at[self.index, number],
            recv_sem=self.recv.at[self.index, number],
            device_id={"ctx": peers[peer]},
            device_id_type=MESH,
        )

    def add(self, part, extra):
        target = self.tile.at[part]
        row_blocks(extra.shape[0], 32, lambda rows: add_to(target, extra, rows))

    def store(self):
        return pltpu.make_async_copy(self.tile, self.place_of(), self.store_sem.at[self.index])

    def store_part(self):
        part = self.geometry()[3]
        return pltpu.make_async_copy(
            self.tile.at[part], self.place_of().at[part], self.store_sem.at[self.index]
        )

    def advance(self, number):
        if number > 0:
            self.round(number - 1).wait_recv()
        if number == 1:
            self.add(self.geometry()[1], self.half)
        if number == 2:
            self.add(self.geometry()[3], self.quarter)
            self.store_part().start()
        if number == 3:
            self.store_part().wait()
        if number < 4:
            self.round(number).start()

    def settle(self):
        for number in range(4):
            self.round(number).wait_send()


def fill(target, left, right, first):
    for start, size in bands(target.shape[1], WIDE):
        cols = pl.ds(pl.multiple_of(first + start, BLOCK), size)
        target[:, start : start + size] = dot(left, right[:, cols]).astype(HALF)


def middle(
    n_fsdp, n_ctx, CHUNK,
    gated, tokens, cotangent, gain, wo_part, wg_part, wu_part, wd_part,
    mixed_out, normed_out, act_out, grad_glu_out, grad_resid_out, grad_mixed_out,
    grad_gated_out, w_gate_out, w_up_out, w_down_out, grad_gain_out,
    wo, wg, wu, wd, x_all, dy_all, held, crossed, total, normed, act, grad_glu,
    grad_resid, grad_mixed, grad_gated, gain_total, spare, inbox, half, quarter,
    square_send, square_recv, square_store, weight_sem, weight_send, weight_recv, again_sem, own_sem, send_sem, recv_sem, load_sem, store_sem, *line_sems,
):
    n_chunks, _, _, piece = held.shape
    units = wd.shape[0]
    width = wd.shape[1]
    peers = line_peers() + others("ctx", n_ctx)
    if n_fsdp == 2:
        peers.append({"fsdp": 1 - lax.axis_index("fsdp")})
    greet(peers)
    ready = pull(
        (wo_part, wg_part, wu_part, wd_part), (wo, wg, wu, wd), (1, 0, 0, 1),
        n_fsdp, own_sem, send_sem, recv_sem,
    )
    loads = [
        pltpu.make_async_copy(tokens, x_all, load_sem.at[0]),
        pltpu.make_async_copy(cotangent, dy_all, load_sem.at[1]),
    ]
    for load in loads:
        load.start()
    line = Line(held, crossed, total, line_sems)

    def chunk_rows(c):
        return pl.ds(pl.multiple_of(c * CHUNK, CHUNK), CHUNK)

    def stores(c, wanted=None):
        rows = chunk_rows(c)
        pairs = [
            (normed, normed_out.at[rows]),
            (act, act_out.at[rows]),
            (grad_glu.at[0], grad_glu_out.at[0, rows]),
            (grad_glu.at[1], grad_glu_out.at[1, rows]),
            (grad_resid, grad_resid_out.at[rows]),
            (grad_mixed, grad_mixed_out.at[rows]),
            (grad_gated, grad_gated_out.at[rows]),
        ]
        pairs += [
            (total.at[c, q], mixed_out.at[rows, pl.ds(q * piece, piece)]) for q in range(PIECES)
        ]
        return [
            pltpu.make_async_copy(source, target, store_sem.at[index])
            for index, (source, target) in enumerate(pairs)
            if wanted is None or index in wanted
        ]

    FORWARD = (0, 1, 2, 3, 7, 8, 9, 10)
    BACKWARD = (4, 5, 6)

    ready(0)

    @pl.loop(0, n_chunks)
    def _(c):
        lhs = gated[chunk_rows(c), :]

        @pl.loop(0, PIECES)
        def _(q):
            cols = pl.ds(pl.multiple_of(q * piece, piece), piece)
            held[c, q] = dot(lhs, wo[:, cols]).astype(HALF)
            line.offer(c, q)

    for load in loads:
        load.wait()
    line.forward(0, 0)
    for step in range(PIECES + 1):
        line.tick(0, step)
    for index in (1, 2, 3):
        ready(index)
    w_down_store = pltpu.make_async_copy(wd, w_down_out, again_sem.at[3])
    w_down_store.start()

    @pl.loop(0, n_chunks)
    def _(c):
        line.arrive(c)
        line.tick(c + 1, 0)

        @pl.when(c > 0)
        def _():
            for store in stores(c - 1, FORWARD):
                store.wait()

        def norm(rows):
            at = pl.ds(pl.multiple_of(c * CHUNK + rows.start, 16), rows.size)
            resid = x_all[at, :].astype(FLOAT) + joined(total, c, rows)
            normed[rows, :] = (resid * rms_scale(resid) * gain[...]).astype(HALF)

        row_blocks(CHUNK, 16, norm)

        def unit(cols):
            glu_gate = dot(normed[...], wg[:, cols])
            glu_up = dot(normed[...], wu[:, cols])
            grad_act = dot_nt(dy_all[chunk_rows(c), :], wd[cols, :])
            sig = jax.nn.sigmoid(glu_gate)
            silu = glu_gate * sig
            act[:, cols] = (silu * glu_up).astype(HALF)
            slope = sig * (1.0 + glu_gate * (1.0 - sig))
            grad_glu[0, :, cols] = (grad_act * glu_up * slope).astype(HALF)
            grad_glu[1, :, cols] = (grad_act * silu).astype(HALF)

        for index, (start, size) in enumerate(bands(units, WIDE)):
            unit(slice(start, start + size))
            if index == 0:
                line.tick(c + 1, 1)
        line.tick(c + 1, 2)
        line.release(c)

        @pl.loop(0, PIECES)
        def _(q):
            @pl.when(q == PIECES // 2)
            def _():
                line.tick(c + 1, 3)

            at = pl.ds(pl.multiple_of(q * piece, piece), piece)
            value = dot_nt(grad_glu[0], wg[at, :]) + dot_nt(grad_glu[1], wu[at, :])
            held[c, q] = value.astype(HALF)
            line.offer(n_chunks + c, q)

        line.tick(c + 1, 4)

        for store in stores(c, FORWARD):
            store.start()

    for store in stores(n_chunks - 1, FORWARD):
        store.wait()
    rows = n_chunks * CHUNK
    w_down_store.wait()
    kept = [
        (grad_glu_out.at[0], wg.at[:rows]),
        (grad_glu_out.at[1], wu.at[:rows]),
        (normed_out, wd.at[:rows]),
    ]
    again = [
        pltpu.make_async_copy(source, target, again_sem.at[index])
        for index, (source, target) in enumerate(kept)
    ]
    for copy in again:
        copy.start()
    gain_total[...] = jnp.zeros_like(gain_total)
    item, finish = halves(n_fsdp, weight_sem, weight_send, weight_recv, spare, inbox)
    mine = lax.axis_index("fsdp") if n_fsdp == 2 else 1
    depth = width // 2
    whole = n_fsdp != 2
    per_part = depth // TILE
    squares, plain, turn = [], [], [0]

    def weight_item(index):
        if index >= 2 * per_part:
            return
        part, k = divmod(index, per_part)
        right = (wg, wu)[part].at[:rows]
        out = (w_gate_out, w_up_out)[part]

        def compute(side):
            at = pl.ds(pl.multiple_of(side * depth + k * TILE, TILE), TILE)
            return lambda target: fill(target, wd[:rows, at].T, right, 0)

        at = slice(k * TILE + whole * depth, (k + 1) * TILE + whole * depth)
        square = Square(
            index, ((wg, wu)[part], half, quarter),
            (slice(rows + k * TILE, rows + (k + 1) * TILE), k, k), lambda: out.at[at],
            square_send, square_recv, square_store,
        )
        item(
            index, lambda ref: ref, compute(1 - mine), compute(mine),
            lambda: out.at[k * TILE : (k + 1) * TILE], square.tile,
        )
        if whole or part == 1:
            square.store().start()
            plain.append(square)
        else:
            squares.append([square, 0, turn[0]])

    def pump():
        for square in squares:
            if square[1] < 5 and turn[0] >= square[2] + 2 * square[1]:
                square[0].advance(square[1])
                square[1] += 1
        turn[0] += 1

    def backward(c):
        line.arrive(n_chunks + c)
        if c > 0:
            for store in stores(c - 1, BACKWARD):
                store.wait()

        def norm_back(rows):
            at = pl.ds(pl.multiple_of(c * CHUNK + rows.start, 16), rows.size)
            resid = x_all[at, :].astype(FLOAT) + joined(total, c, rows)
            rate = rms_scale(resid)
            grad = joined(total, n_chunks + c, rows)
            by_gain = grad * (resid * rate)
            gain_total[...] += by_gain[:8] + by_gain[8:]
            inner = gain[...] * grad
            mean = jnp.mean(inner * resid, -1, keepdims=True)
            value = dy_all[at, :].astype(FLOAT) + rate * inner - resid * (rate * rate * rate * mean)
            grad_resid[rows, :] = value
            grad_mixed[rows, :] = value.astype(HALF)

        row_blocks(CHUNK, 16, norm_back)
        for start, size in bands(grad_gated.shape[1], WIDE):
            grad_gated[:, start : start + size] = dot_nt(
                grad_mixed[...], wo[start : start + size, :]
            )
        for store in stores(c, BACKWARD):
            store.start()

    for copy in again:
        copy.wait()
    count = 0
    for c in range(n_chunks):
        if c == n_chunks - 1:
            while count < 2 * per_part:
                weight_item(count)
                count += 1
        backward(c)
        if c + 1 < n_chunks:
            for step in range(PIECES + 1):
                weight_item(count)
                count += 1
                if c + 2 == n_chunks and step == PIECES - 1:
                    line.close(2 * n_chunks - 1, step - 1)
                else:
                    line.tick(n_chunks + c + 1, step)
                pump()
    while any(square[1] < 5 for square in squares):
        pump()
    finish()
    for square, _, _ in squares:
        square.settle()
    for square in plain:
        square.store().wait()

    grad_gain_out[...] = jnp.sum(gain_total[...], 0, keepdims=True)
    for store in stores(n_chunks - 1, BACKWARD):
        store.wait()

    @pl.loop(0, n_chunks)
    def _(c):
        line.settle(c)
        line.settle(n_chunks + c)
        line.release(n_chunks + c)


def run_middle(gated, tokens, cotangent, gain, parts, n_fsdp, n_ctx, length):
    rows, chan = gated.shape
    width = tokens.shape[1]
    wg = parts[1]
    units = wg.shape[1]
    n_chunks = rows // length
    piece = width // PIECES
    vmem = pl.BlockSpec(memory_space=pltpu.VMEM)
    hbm = pl.BlockSpec(memory_space=pl.ANY)
    sems = pltpu.SemaphoreType.DMA((2 * n_chunks, PIECES))
    return pl.pallas_call(
        functools.partial(middle, n_fsdp, n_ctx, length),
        name="middle",
        out_shape=(
            jax.ShapeDtypeStruct((rows, width), HALF),
            jax.ShapeDtypeStruct((rows, width), HALF),
            jax.ShapeDtypeStruct((rows, units), HALF),
            jax.ShapeDtypeStruct((2, rows, units), HALF),
            jax.ShapeDtypeStruct((rows, width), FLOAT),
            jax.ShapeDtypeStruct((rows, width), HALF),
            jax.ShapeDtypeStruct((rows, chan), FLOAT),
            jax.ShapeDtypeStruct((width if n_fsdp != 2 else width // 2, units), HALF),
            jax.ShapeDtypeStruct((width if n_fsdp != 2 else width // 2, units), HALF),
            jax.ShapeDtypeStruct((units, width), HALF),
            jax.ShapeDtypeStruct((1, width), FLOAT),
        ),
        in_specs=[vmem, hbm, hbm, vmem, hbm, hbm, hbm, hbm],
        out_specs=[hbm] * 10 + [vmem],
        scratch_shapes=[
            pltpu.VMEM((chan, width), HALF),
            pltpu.VMEM((width, units), HALF),
            pltpu.VMEM((width, units), HALF),
            pltpu.VMEM((units, width), HALF),
            pltpu.VMEM((rows, width), HALF),
            pltpu.VMEM((rows, width), HALF),
            pltpu.VMEM((n_chunks, PIECES, length, piece), HALF),
            pltpu.VMEM((n_chunks, PIECES, length, piece), HALF),
            pltpu.VMEM((2 * n_chunks, PIECES, length, piece), HALF),
            pltpu.VMEM((length, width), HALF),
            pltpu.VMEM((length, units), HALF),
            pltpu.VMEM((2, length, units), HALF),
            pltpu.VMEM((length, width), FLOAT),
            pltpu.VMEM((length, width), HALF),
            pltpu.VMEM((length, chan), FLOAT),
            pltpu.VMEM((8, width), FLOAT),
            pltpu.VMEM((2, TILE, units), HALF),
            pltpu.VMEM((2, TILE, units), HALF),
            pltpu.VMEM((width // 2 // TILE, TILE // 2, units), HALF),
            pltpu.VMEM((width // 2 // TILE, TILE // 4, units), HALF),
            pltpu.SemaphoreType.DMA((width // 2 // TILE, 4)),
            pltpu.SemaphoreType.DMA((width // 2 // TILE, 4)),
            pltpu.SemaphoreType.DMA((width // TILE,)),
            pltpu.SemaphoreType.DMA((4,)),
            pltpu.SemaphoreType.DMA((2,)),
            pltpu.SemaphoreType.DMA((2,)),
            pltpu.SemaphoreType.DMA((4,)),
            pltpu.SemaphoreType.DMA((4,)),
            pltpu.SemaphoreType.DMA((4,)),
            pltpu.SemaphoreType.DMA((4,)),
            pltpu.SemaphoreType.DMA((2,)),
            pltpu.SemaphoreType.DMA((12,)),
        ]
        + [sems] * 4,
        compiler_params=pltpu.CompilerParams(
            collective_id=2, has_side_effects=True, vmem_limit_bytes=63 * MIB
        ),
        cost_estimate=pl.CostEstimate(
            flops=16 * rows * width * units, bytes_accessed=400 * MIB, transcendentals=0
        ),
    )(gated, tokens, cotangent, gain, *parts)


def scan_cross(gate_all, state, scale, gain, near, grad_proj, gain_out, cross):
    n_seq, length, chan = state.shape
    mine = lax.axis_index("tp")
    gain_total = jnp.zeros((8, chan), FLOAT)
    for seq in range(n_seq):
        for start in range(0, length, BLOCK):
            rows = slice(start, start + BLOCK)
            rate = columns(scale[seq : seq + 1, rows])
            gate = gate_all[seq, rows, :]
            sig = jax.nn.sigmoid(gate)
            swish = gate * sig
            value = state[seq, rows, :]
            into = near[seq, rows, :]
            by_unit = into * value * widen(rate, chan)
            slope = sig * (1.0 + gate * (1.0 - sig))
            grad_proj[seq, rows, 2 * chan :] = (by_unit * gain[...] * slope).astype(HALF)
            gain_total = gain_total + jnp.sum((by_unit * swish).reshape(-1, 8, chan), 0)
            grad_unit = into * swish * gain[...]
            near[seq, rows, :] = grad_unit
            cross[mine, seq : seq + 1, rows] = lane_sums(grad_unit * value)
    gain_out[...] = jnp.sum(gain_total, 0, keepdims=True)


def scan_back(
    n_ctx, n_tp, width, pump,
    proj, keep, lower, state, scale, carry_in, near,
    grad_proj, lower_out,
    reach, rate_wide, cross_wide, ends, cross, ctx_sems,
):
    n_seq, length, chan = state.shape
    low = lower[...].reshape(1, 1, chan)
    total = cross[0]
    for place in range(1, n_tp):
        total = total + cross[place]
    rate = scale[...]
    total = total * (rate * rate * rate) / width
    for seq in range(n_seq):
        for start in range(0, length, BLOCK):
            rows = slice(start, start + BLOCK)
            rate_wide[seq, rows, :] = columns(rate[seq : seq + 1, rows])
            cross_wide[seq, rows, :] = columns(total[seq : seq + 1, rows])

    row = lax.broadcasted_iota(jnp.int32, (n_seq, GROUP, chan), 1)

    def back(index, carry):
        prod, above = carry
        rows = pl.ds(pl.multiple_of((length // GROUP - 1 - index) * GROUP, GROUP), GROUP)
        decay = low + (1.0 - low) * jax.nn.sigmoid(proj[1, :, rows, :])
        mult = decay * keep[:, rows, :]
        direct = (
            widen(rate_wide[:, rows, :], chan) * near[:, rows, :]
            - widen(cross_wide[:, rows, :], chan) * state[:, rows, :]
        )
        add = mult * direct
        for hop in (1, 2, 4):
            inside = row < GROUP - hop
            add = jnp.where(inside, mult * pltpu.roll(add, GROUP - hop, 1) + add, add)
            mult = jnp.where(inside, mult * pltpu.roll(mult, GROUP - hop, 1), mult)
        add = add + mult * above
        mult = mult * prod
        inside = row < GROUP - 1
        near[:, rows, :] = direct + jnp.where(inside, pltpu.roll(add, GROUP - 1, 1), above)
        reach[:, rows, :] = jnp.where(inside, pltpu.roll(mult, GROUP - 1, 1), prod)
        return mult[:, :1, :], add[:, :1, :]

    held = (jnp.ones((n_seq, 1, chan), FLOAT), jnp.zeros((n_seq, 1, chan), FLOAT))
    held = lax.fori_loop(0, length // GROUP, back, held)
    prod, total = held
    here = lax.axis_index("ctx")
    ends[here, 0] = prod.reshape(n_seq, chan)
    ends[here, 1] = total.reshape(n_seq, chan)
    pump()
    share(ends, "ctx", n_ctx, *ctx_sems)
    carry = jnp.zeros((n_seq, chan), FLOAT)
    for place in range(n_ctx - 1, 0, -1):
        carry = jnp.where(place > here, ends[place, 1] + ends[place, 0] * carry, carry)
    carry = carry.reshape(n_seq, 1, chan)
    wide = 2 * GROUP
    first = lax.broadcasted_iota(jnp.int32, (n_seq, wide, chan), 1) == 0

    def finish(index, held):
        before, low_total = held
        rows = pl.ds(pl.multiple_of(index * wide, wide), wide)
        inp = proj[0, :, rows, :]
        sig = jax.nn.sigmoid(inp)
        silu = inp * sig
        fsig = jax.nn.sigmoid(proj[1, :, rows, :])
        rest = 1.0 - fsig
        decay = low + (1.0 - low) * fsig
        grad_state = near[:, rows, :] + reach[:, rows, :] * carry
        value = state[:, rows, :]
        prev = jnp.where(first, before, pltpu.roll(value, 1, 1))
        grad_decay = grad_state * (prev * keep[:, rows, :] - silu)
        grad_proj[:, rows, :chan] = (
            grad_state * (1.0 - decay) * (sig * (1.0 + inp * (1.0 - sig)))
        ).astype(HALF)
        grad_proj[:, rows, chan : 2 * chan] = (
            grad_decay * (1.0 - low) * fsig * rest
        ).astype(HALF)
        return value[:, wide - 1 :, :], low_total + grad_decay * rest

    held = (carry_in[...].reshape(n_seq, 1, chan), jnp.zeros((n_seq, wide, chan), FLOAT))
    _, low_total = lax.fori_loop(0, length // wide, finish, held)
    lower_out[...] = jnp.sum(jnp.sum(low_total, 0), 0, keepdims=True)
    pump()


def tail(
    n_fsdp, n_ctx, n_tp,
    keep, gate_gain, lower, scale, carry_in, gain, gain_two_grad,
    proj, state, grad_gated, w_in, w_down, act, normed, grad_mixed, gated, cotangent,
    grad_resid, tokens, mixed,
    grad_tokens_out, output_out, vectors_out, w_in_out, w_out_out, w_down_out,
    grad_proj, held, crossed, total, spare, inbox,
    in_tile, in_half, in_quarter, out_tile, out_half, out_quarter, down_tile, down_half, down_quarter,
    gain_total, ends, cross, over_ctx, over_fsdp, near,
    load_sem, store_sem, end_send, end_recv, cross_send, cross_recv, ctx_send, ctx_recv,
    fsdp_send, fsdp_recv, part_sem, part_send, part_recv, square_send, square_recv, square_store,
    *line_sems,
):
    n_seq, length, wide = grad_proj.shape
    chan = wide // 3
    rows = n_seq * length
    width = gain.shape[1]
    units = w_down.shape[0]
    piece = width // PIECES
    n_chunks = n_seq
    whole = n_fsdp != 2
    greet(others("ctx", n_ctx) + others("tp", n_tp) + others("fsdp", n_fsdp))
    line = Line(held, crossed, total, line_sems)
    pieces = [(job, q) for job in range(2 * n_chunks) for q in range(PIECES)]
    relay = [(line.forward, spot) for spot in pieces[:2]]
    for index, spot in enumerate(pieces):
        relay.append((line.close, spot))
        relay += [(line.forward, ahead) for ahead in pieces[index + 2 : index + 3]]
    squares = []
    turn = [0]
    SPACE = 3

    def pump():
        while relay:
            action, spot = relay.pop(0)
            action(*spot)
            if action == line.forward:
                break
        for square in squares:
            if square[1] < 5 and turn[0] >= square[2] + SPACE * square[1]:
                square[0].advance(square[1])
                square[1] += 1
        turn[0] += 1

    def start_loads(pairs, first=0):
        copies = [
            pltpu.make_async_copy(source, target, load_sem.at[first + index])
            for index, (source, target) in enumerate(pairs)
        ]
        for copy in copies:
            copy.start()
        return copies

    def chunk_rows(c):
        return pl.ds(c * length, length) if isinstance(c, int) else span(c * length, length, length)

    shape = (n_seq, length, chan)

    crossing = shares(cross, "tp", n_tp, cross_send, cross_recv)

    def down_terms(w_all, act_all):
        copies = start_loads([(w_down, w_all), (act, act_all)], 3)

        def cross_terms(gate_all, state_all):
            for copy in start_loads(
                [(proj.at[2], gate_all), (state, state_all), (grad_gated, near)]
            ):
                copy.wait()
            gain_at = over_ctx.at[lax.axis_index("ctx"), :, 2 * width : 2 * width + chan]
            scan_cross(gate_all, state_all, scale, gate_gain, near, grad_proj, gain_at, cross)

        pl.run_scoped(cross_terms, pltpu.VMEM(shape, FLOAT), pltpu.VMEM(shape, FLOAT))
        for copy in crossing:
            copy.start()
        for copy in copies:
            copy.wait()

        for c in range(n_chunks):
            @pl.loop(0, PIECES)
            def _(q):
                cols = pl.ds(pl.multiple_of(q * piece, piece), piece)
                held[c, q] = dot(act_all[chunk_rows(c), :], w_all[:, cols]).astype(HALF)
                line.offer(c, q)

            if c >= n_chunks // 2:
                pump()

    pl.run_scoped(
        down_terms, pltpu.VMEM((units, width), HALF), pltpu.VMEM((rows, units), HALF)
    )

    for copy in crossing:
        copy.wait()

    def back(proj_all, state_all, reach, rate_wide, cross_wide):
        for copy in start_loads([(proj.at[:2], proj_all), (state, state_all)]):
            copy.wait()
        lower_at = over_ctx.at[lax.axis_index("ctx"), :, 2 * width + chan :]
        scan_back(
            n_ctx, n_tp, width, pump,
            proj_all, keep, lower, state_all, scale, carry_in, near,
            grad_proj, lower_at,
            reach, rate_wide, cross_wide, ends, cross, (end_send, end_recv),
        )

    pl.run_scoped(
        back,
        pltpu.VMEM((2, *shape), FLOAT),
        pltpu.VMEM(shape, FLOAT),
        pltpu.VMEM(shape, FLOAT),
        pltpu.VMEM((n_seq, length, BLOCK), FLOAT),
        pltpu.VMEM((n_seq, length, BLOCK), FLOAT),
    )

    def back_terms(w_all):
        for copy in start_loads([(w_in, w_all)]):
            copy.wait()

        for c in range(n_chunks):
            @pl.loop(0, PIECES)
            def _(q):
                at = pl.ds(pl.multiple_of(q * piece, piece), piece)
                held[n_chunks + c, q] = dot_nt(grad_proj[c], w_all[at, :]).astype(HALF)
                line.offer(n_chunks + c, q)

            if c % 2 == 1:
                pump()

    pl.run_scoped(back_terms, pltpu.VMEM((width, wide), HALF))

    item, finish = halves(n_fsdp, part_sem, part_send, part_recv, spare, inbox)
    mine = 1 if whole else lax.axis_index("fsdp")
    depth = width // 2
    skip = whole * depth
    stores = []

    def weights(act_all, dy_all, normed_all, mixed_all, gated_all):
        copies = start_loads(
            [(act, act_all), (cotangent, dy_all), (normed, normed_all), (grad_mixed, mixed_all),
             (gated, gated_all)]
        )
        count = [0]

        def tile(view, compute, other_place, own_place, buffers, at):
            index = count[0]
            count[0] += 1
            square = Square(
                index, buffers, at, own_place, square_send, square_recv, square_store
            )
            item(index, view, compute(1 - mine), compute(mine), other_place, square.tile)
            if whole:
                square.store().start()
                stores.append(square)
            else:
                squares.append([square, 0, turn[0]])
            pump()

        copies[0].wait()
        copies[1].wait()
        for start, size in bands(units, TILE):
            left = act_all[:, start : start + size].T
            at = slice(start, start + size)

            def compute(side):
                return lambda target: fill(target, left, dy_all, side * depth)

            tile(
                lambda ref, size=size: ref.at[:size, :depth], compute,
                lambda at=at: w_down_out.at[at, :depth], lambda at=at: w_down_out.at[at, skip:],
                (down_tile, down_half, down_quarter),
                [slice(start // cut, (start + size) // cut) for cut in (1, 2, 4)],
            )
        copies[2].wait()
        flat_proj = grad_proj.reshape(rows, wide)
        for k in range(depth // TILE):
            def compute(side):
                at = pl.ds(pl.multiple_of(side * depth + k * TILE, TILE), TILE)
                return lambda target: fill(target, normed_all[:, at].T, flat_proj, 0)

            at = slice(k * TILE, (k + 1) * TILE)
            tile(
                lambda ref: ref, compute,
                lambda at=at: w_in_out.at[at],
                lambda k=k: w_in_out.at[k * TILE + skip : (k + 1) * TILE + skip],
                (in_tile, in_half, in_quarter), (k, k, k),
            )
        copies[3].wait()
        copies[4].wait()
        for k in range(chan // TILE):
            at = slice(k * TILE, (k + 1) * TILE)
            left = gated_all[:, at].T

            def compute(side):
                return lambda target: fill(target, left, mixed_all, side * depth)

            tile(
                lambda ref: ref.at[:, :depth], compute,
                lambda at=at: w_out_out.at[at, :depth], lambda at=at: w_out_out.at[at, skip:],
                (out_tile, out_half, out_quarter), (k, k, k),
            )

    pl.run_scoped(
        weights,
        pltpu.VMEM((rows, units), HALF),
        pltpu.VMEM((rows, width), HALF),
        pltpu.VMEM((rows, width), HALF),
        pltpu.VMEM((rows, width), HALF),
        pltpu.VMEM((rows, chan), HALF),
    )
    finish()

    def ends_of(resid_all, x_all, mixed_all):
        copies = start_loads([(tokens, x_all), (mixed, mixed_all), (grad_resid, resid_all)])
        copies[0].wait()
        copies[1].wait()
        gain_total[...] = jnp.zeros_like(gain_total)

        def token_store(c):
            at = chunk_rows(c)
            return pltpu.make_async_copy(
                x_all.at[at], grad_tokens_out.at[at], store_sem.at[0, c]
            )

        def output_store(c):
            at = chunk_rows(c)
            return pltpu.make_async_copy(mixed_all.at[at], output_out.at[at], store_sem.at[1, c])

        def until(job):
            while (line.close, (job, PIECES - 1)) in relay:
                if relay[0] == (line.close, (job, PIECES - 1)):
                    action, spot = relay.pop(0)
                    action(*spot)
                else:
                    pump()

        for c in range(n_chunks):
            until(c)
            line.arrive(c)

            @pl.loop(0, length // 16)
            def _(index):
                at = pl.ds(pl.multiple_of(c * length + index * 16, 16), 16)
                rows = pl.ds(pl.multiple_of(index * 16, 16), 16)
                value = x_all[at, :].astype(FLOAT) + mixed_all[at, :].astype(FLOAT)
                mixed_all[at, :] = (value + joined(total, c, rows)).astype(HALF)

            output_store(c).start()

        copies[2].wait()
        for c in range(n_chunks):
            until(n_chunks + c)
            line.arrive(n_chunks + c)
            for quarter in range(PIECES):
                pump()

                @pl.loop(0, length // PIECES // 16)
                def _(index):
                    start = quarter * (length // PIECES) + index * 16
                    rows = pl.ds(pl.multiple_of(start, 16), 16)
                    at = pl.ds(pl.multiple_of(c * length + start, 16), 16)
                    value = x_all[at, :].astype(FLOAT)
                    rate = rms_scale(value)
                    grad = joined(total, n_chunks + c, rows)
                    by_gain = grad * (value * rate)
                    gain_total[...] += by_gain[:8] + by_gain[8:]
                    inner = gain[...] * grad
                    mean = jnp.mean(inner * value, -1, keepdims=True)
                    result = resid_all[at, :] + rate * inner - value * (rate * rate * rate * mean)
                    x_all[at, :] = result.astype(HALF)

            token_store(c).start()

        here = lax.axis_index("ctx")
        over_ctx[here, :, :width] = jnp.sum(gain_total[...], 0, keepdims=True)
        over_ctx[here, :, width : 2 * width] = gain_two_grad[...]
        share(over_ctx, "ctx", n_ctx, ctx_send, ctx_recv)
        value = over_ctx[0]
        for place in range(1, n_ctx):
            value = value + over_ctx[place]
        over_fsdp[lax.axis_index("fsdp")] = value
        share(over_fsdp, "fsdp", n_fsdp, fsdp_send, fsdp_recv)
        value = over_fsdp[0]
        for place in range(1, n_fsdp):
            value = value + over_fsdp[place]
        vectors_out[...] = value
        while any(square[1] < 5 for square in squares):
            pump()
        for c in range(n_chunks):
            token_store(c).wait()
            output_store(c).wait()

    pl.run_scoped(
        ends_of,
        pltpu.VMEM((rows, width), FLOAT),
        pltpu.VMEM((rows, width), HALF),
        pltpu.VMEM((rows, width), HALF),
    )
    for square in squares:
        square[0].settle()
    for square in stores:
        square.store().wait()

    @pl.loop(0, 2 * n_chunks)
    def _(job):
        line.settle(job)
        line.release(job)


def run_tail(small, large, n_fsdp, n_ctx, n_tp):
    grad_gated, w_down, tokens = large[2], large[4], large[11]
    n_seq, length, chan = grad_gated.shape
    rows, width = tokens.shape
    units = w_down.shape[0]
    piece = width // PIECES
    size = 2 * width + 2 * chan
    depth = width // 2
    spread = width if n_fsdp != 2 else depth
    vmem = pl.BlockSpec(memory_space=pltpu.VMEM)
    hbm = pl.BlockSpec(memory_space=pl.ANY)
    slots = pltpu.VMEM((2 * n_seq, PIECES, length, piece), HALF)
    sems = pltpu.SemaphoreType.DMA((2 * n_seq, PIECES))
    n_in, n_out = depth // TILE, chan // TILE
    n_squares = n_in + n_out + len(bands(units, TILE))
    wide = max(3 * chan, depth)

    def tiles(*shape):
        return [
            pltpu.VMEM((*shape[:-2], shape[-2] // cut, shape[-1]), HALF) for cut in (1, 2, 4)
        ]

    return pl.pallas_call(
        functools.partial(tail, n_fsdp, n_ctx, n_tp),
        name="tail",
        out_shape=(
            jax.ShapeDtypeStruct((rows, width), HALF),
            jax.ShapeDtypeStruct((rows, width), HALF),
            jax.ShapeDtypeStruct((1, size), FLOAT),
            jax.ShapeDtypeStruct((spread, 3 * chan), HALF),
            jax.ShapeDtypeStruct((chan, spread), HALF),
            jax.ShapeDtypeStruct((units, spread), HALF),
        ),
        in_specs=[vmem] * len(small) + [hbm] * len(large),
        out_specs=[hbm, hbm, vmem, hbm, hbm, hbm],
        scratch_shapes=[
            pltpu.VMEM((n_seq, length, 3 * chan), HALF),
            slots,
            pltpu.VMEM((2 * n_seq, PIECES, length, piece), HALF),
            slots,
            pltpu.VMEM((2, TILE, wide), HALF),
            pltpu.VMEM((2, TILE, wide), HALF),
            *tiles(n_in, TILE, 3 * chan),
            *tiles(n_out, TILE, depth),
            *tiles(units, depth),
            pltpu.VMEM((8, width), FLOAT),
            pltpu.VMEM((n_ctx, 2, n_seq, chan), FLOAT),
            pltpu.VMEM((n_tp, n_seq, length), FLOAT),
            pltpu.VMEM((n_ctx, 1, size), FLOAT),
            pltpu.VMEM((n_fsdp, 1, size), FLOAT),
            pltpu.VMEM((n_seq, length, chan), FLOAT),
            pltpu.SemaphoreType.DMA((6,)),
            pltpu.SemaphoreType.DMA((2, n_seq)),
            pltpu.SemaphoreType.DMA((n_ctx,)),
            pltpu.SemaphoreType.DMA((n_ctx,)),
            pltpu.SemaphoreType.DMA((n_tp,)),
            pltpu.SemaphoreType.DMA((n_tp,)),
            pltpu.SemaphoreType.DMA((n_ctx,)),
            pltpu.SemaphoreType.DMA((n_ctx,)),
            pltpu.SemaphoreType.DMA((n_fsdp,)),
            pltpu.SemaphoreType.DMA((n_fsdp,)),
            pltpu.SemaphoreType.DMA((2,)),
            pltpu.SemaphoreType.DMA((2,)),
            pltpu.SemaphoreType.DMA((2,)),
            pltpu.SemaphoreType.DMA((n_squares, 4)),
            pltpu.SemaphoreType.DMA((n_squares, 4)),
            pltpu.SemaphoreType.DMA((n_squares,)),
        ]
        + [sems] * 4,
        compiler_params=pltpu.CompilerParams(
            collective_id=3, has_side_effects=True, vmem_limit_bytes=63 * MIB
        ),
        cost_estimate=pl.CostEstimate(
            flops=10 * rows * width * units, bytes_accessed=700 * MIB, transcendentals=0
        ),
    )(*small, *large)


def widen_outputs(w_in, w_out, w_gate, w_up, w_down, tokens, w_in_out, w_out_out, w_glu_out, w_down_out, tokens_out):
    chan = w_in_out.shape[2]
    for gate in range(3):
        w_in_out[gate] = w_in[:, gate * chan : (gate + 1) * chan].astype(FLOAT)
    w_out_out[...] = w_out[...].astype(FLOAT)
    w_glu_out[:, 0, :] = w_gate[...].astype(FLOAT)
    w_glu_out[:, 1, :] = w_up[...].astype(FLOAT)
    w_down_out[...] = w_down[...].astype(FLOAT)
    tokens_out[...] = tokens[...].astype(FLOAT)


def run_widen_outputs(w_in, w_out, w_gate, w_up, w_down, tokens):
    steps = 8
    arrays = (w_in, w_out, w_gate, w_up, w_down, tokens)

    def spec(array):
        return pl.BlockSpec((array.shape[0] // steps, array.shape[1]), lambda i: (i, 0))

    depth, wide = w_in.shape
    chan = wide // 3
    units = w_gate.shape[1]
    shapes = [
        jax.ShapeDtypeStruct((3, depth, chan), FLOAT),
        jax.ShapeDtypeStruct(w_out.shape, FLOAT),
        jax.ShapeDtypeStruct((depth, 2, units), FLOAT),
        jax.ShapeDtypeStruct(w_down.shape, FLOAT),
        jax.ShapeDtypeStruct(tokens.shape, FLOAT),
    ]
    specs = [
        pl.BlockSpec((3, depth // steps, chan), lambda i: (0, i, 0)),
        spec(w_out),
        pl.BlockSpec((depth // steps, 2, units), lambda i: (i, 0, 0)),
        spec(w_down),
        spec(tokens),
    ]
    return pl.pallas_call(
        widen_outputs,
        name="widen_outputs",
        grid=(steps,),
        out_shape=shapes,
        in_specs=[spec(array) for array in arrays],
        out_specs=specs,
        compiler_params=pltpu.CompilerParams(vmem_limit_bytes=48 * MIB),
    )(*arrays)


def head(
    n_fsdp, n_ctx, n_tp,
    gains, same, first, last, gate_gain, lower, w_in, tokens,
    gated, scale, carry_out, keep, gain_one, gain_two, proj_out, state_out, normed_out, w_out,
    staged, w_all, normed, proj, state, local, reach, ends, squares, gain_slots, edge_slots,
    load_sem, store_sem, half_send, half_recv, ctx_send, ctx_recv, tp_send, tp_recv,
    gain_send, gain_recv, edge_send, edge_recv,
):
    n_seq, length, chan = state.shape
    rows = n_seq * length
    depth = w_in.shape[1]
    width = w_all.shape[0]
    greet(others("ctx", n_ctx) + others("tp", n_tp) + others("fsdp", n_fsdp))
    core = lax.axis_index("fsdp")
    gate_cols = [slice(gate * chan, (gate + 1) * chan) for gate in range(3)]
    x_load = pltpu.make_async_copy(tokens, normed, load_sem.at[3])
    if n_fsdp == 2:
        w_loads = [
            pltpu.make_async_copy(w_in.at[gate], staged.at[gate], load_sem.at[gate])
            for gate in range(3)
        ]
    else:
        w_loads = [
            pltpu.make_async_copy(w_in.at[gate], w_all.at[:, gate_cols[gate]], load_sem.at[gate])
            for gate in range(3)
        ]
    for load in w_loads + [x_load]:
        load.start()
    gain_slots[core] = gains[...].astype(HALF).astype(FLOAT)
    edge_slots[lax.axis_index("ctx")] = last[...]
    small = shares(gain_slots, "fsdp", n_fsdp, gain_send, gain_recv)
    small += shares(edge_slots, "ctx", n_ctx, edge_send, edge_recv)
    for copy in small:
        copy.start()
    halves_sent = []
    if n_fsdp == 2:
        own = span(core * depth, depth, depth)
        for gate in range(3):
            w_loads[gate].wait()

            def cast(at):
                to = span(core * depth + at.start, at.size, at.size)
                w_all[to, gate_cols[gate]] = staged[gate, at, :].astype(HALF)

            row_blocks(depth, 32, cast)
            place = w_all.at[own, gate_cols[gate]]
            copy = pltpu.make_async_remote_copy(
                src_ref=place,
                dst_ref=place,
                send_sem=half_send.at[gate],
                recv_sem=half_recv.at[gate],
                device_id={"fsdp": 1 - core},
                device_id_type=MESH,
            )
            copy.start()
            halves_sent.append(copy)
    for copy in small:
        copy.wait()
    part = gains.shape[1]
    for place in range(n_fsdp):
        cols = slice(place * part, (place + 1) * part)
        gain_one[:, cols] = gain_slots[place, :1, :]
        gain_two[:, cols] = gain_slots[place, 1:2, :]
    here = lax.axis_index("ctx")
    keep[...] = same[...]
    before = edge_slots[0]
    for place in range(1, n_ctx):
        before = jnp.where(place == here - 1, edge_slots[place], before)
    joins = jnp.where((before == first[...]) & (here > 0), 1.0, 0.0)
    keep[:, :1, :] = joins[:, :1].reshape(n_seq, 1, 1)
    x_load.wait()

    def norm(at):
        value = normed[at, :].astype(FLOAT)
        normed[at, :] = (value * rms_scale(value) * gain_one[...]).astype(HALF)

    row_blocks(rows, 16, norm)
    normed_store = pltpu.make_async_copy(normed, normed_out, store_sem.at[0])
    normed_store.start()
    flat = proj.reshape(3, rows, chan)
    band = min(rows, WIDE)
    if n_fsdp == 2:
        for gate in range(3):
            @pl.loop(0, rows // band)
            def _(index):
                at = span(index * band, band, band)
                cols = span(core * depth, depth, depth)
                flat[gate, at, :] = dot(normed[at, cols], w_all[own, gate_cols[gate]])

        for gate in range(3):
            halves_sent[gate].wait_recv()

            @pl.loop(0, rows // band)
            def _(index):
                at = span(index * band, band, band)
                other = span((1 - core) * depth, depth, depth)
                flat[gate, at, :] += dot(normed[at, other], w_all[other, gate_cols[gate]])
    else:
        for gate in range(3):
            w_loads[gate].wait()

            @pl.loop(0, rows // band)
            def _(index):
                at = span(index * band, band, band)
                flat[gate, at, :] = dot(normed[at, :], w_all[:, gate_cols[gate]])

    stores = [
        pltpu.make_async_copy(proj, proj_out, store_sem.at[1]),
        pltpu.make_async_copy(w_all, w_out, store_sem.at[2]),
    ]
    for store in stores:
        store.start()
    low = lower[...].reshape(1, 1, chan)
    row = lax.broadcasted_iota(jnp.int32, (n_seq, GROUP, chan), 1)

    def step(index, carry):
        prod, total = carry
        rows = pl.ds(pl.multiple_of(index * GROUP, GROUP), GROUP)
        inp = proj[0, :, rows, :]
        decay = low + (1.0 - low) * jax.nn.sigmoid(proj[1, :, rows, :])
        add = inp * jax.nn.sigmoid(inp) * (1.0 - decay)
        mult = decay * keep[:, rows, :]
        for hop in (1, 2, 4):
            inside = row >= hop
            add = jnp.where(inside, mult * pltpu.roll(add, hop, 1) + add, add)
            mult = jnp.where(inside, mult * pltpu.roll(mult, hop, 1), mult)
        add = add + mult * total
        mult = mult * prod
        local[:, rows, :] = add
        reach[:, rows, :] = mult
        return mult[:, GROUP - 1 :, :], add[:, GROUP - 1 :, :]

    start = (jnp.ones((n_seq, 1, chan), FLOAT), jnp.zeros((n_seq, 1, chan), FLOAT))
    prod, total = lax.fori_loop(0, length // GROUP, step, start)
    ends[here, 0] = prod.reshape(n_seq, chan)
    ends[here, 1] = total.reshape(n_seq, chan)
    share(ends, "ctx", n_ctx, ctx_send, ctx_recv)
    carry = jnp.zeros((n_seq, chan), FLOAT)
    for place in range(n_ctx - 1):
        carry = jnp.where(place < here, ends[place, 1] + ends[place, 0] * carry, carry)
    carry_out[...] = carry
    mine = lax.axis_index("tp")
    for seq in range(n_seq):
        for start in range(0, length, BLOCK):
            rows = slice(start, start + BLOCK)
            value = local[seq, rows, :] + reach[seq, rows, :] * carry[seq : seq + 1]
            state[seq, rows, :] = value
            squares[mine, seq : seq + 1, rows] = lane_sums(value * value)
    state_store = pltpu.make_async_copy(state, state_out, store_sem.at[3])
    state_store.start()
    share(squares, "tp", n_tp, tp_send, tp_recv)
    total = squares[0]
    for place in range(1, n_tp):
        total = total + squares[place]
    rate = lax.rsqrt(total / width + EPS)
    scale[...] = rate
    for seq in range(n_seq):
        for start in range(0, length, BLOCK):
            rows = slice(start, start + BLOCK)
            gate = proj[2, seq, rows, :]
            unit = state[seq, rows, :] * widen(columns(rate[seq : seq + 1, rows]), chan)
            swish = gate * jax.nn.sigmoid(gate)
            gated[seq, rows, :] = (unit * gate_gain[...] * swish).astype(HALF)
    for copy in halves_sent:
        copy.wait_send()
    for store in stores + [normed_store, state_store]:
        store.wait()


def run_head(gains, same, first, last, gate_gain, lower, w_in, tokens, n_fsdp, n_ctx, n_tp):
    n_seq, length, _ = same.shape
    rows, width = tokens.shape
    chan = w_in.shape[2]
    shape = (n_seq, length, chan)
    vmem = pl.BlockSpec(memory_space=pltpu.VMEM)
    hbm = pl.BlockSpec(memory_space=pl.ANY)
    staged = w_in.shape if n_fsdp == 2 else (3, 8, BLOCK)
    dma = pltpu.SemaphoreType.DMA
    return pl.pallas_call(
        functools.partial(head, n_fsdp, n_ctx, n_tp),
        name="head",
        out_shape=(
            jax.ShapeDtypeStruct(shape, HALF),
            jax.ShapeDtypeStruct((n_seq, length), FLOAT),
            jax.ShapeDtypeStruct((n_seq, chan), FLOAT),
            jax.ShapeDtypeStruct((n_seq, length, 1), FLOAT),
            jax.ShapeDtypeStruct((1, width), FLOAT),
            jax.ShapeDtypeStruct((1, width), FLOAT),
            jax.ShapeDtypeStruct((3, *shape), FLOAT),
            jax.ShapeDtypeStruct(shape, FLOAT),
            jax.ShapeDtypeStruct((rows, width), HALF),
            jax.ShapeDtypeStruct((width, 3 * chan), HALF),
        ),
        in_specs=[vmem] * 6 + [hbm] * 2,
        out_specs=[vmem] * 6 + [hbm] * 4,
        scratch_shapes=[
            pltpu.VMEM(staged, FLOAT),
            pltpu.VMEM((width, 3 * chan), HALF),
            pltpu.VMEM((rows, width), HALF),
            pltpu.VMEM((3, *shape), FLOAT),
            pltpu.VMEM(shape, FLOAT),
            pltpu.VMEM(shape, FLOAT),
            pltpu.VMEM(shape, FLOAT),
            pltpu.VMEM((n_ctx, 2, n_seq, chan), FLOAT),
            pltpu.VMEM((n_tp, n_seq, length), FLOAT),
            pltpu.VMEM((n_fsdp, *gains.shape), FLOAT),
            pltpu.VMEM((n_ctx, *last.shape), FLOAT),
            dma((4,)), dma((4,)), dma((3,)), dma((3,)), dma((n_ctx,)), dma((n_ctx,)),
            dma((n_tp,)), dma((n_tp,)), dma((n_fsdp,)), dma((n_fsdp,)), dma((n_ctx,)), dma((n_ctx,)),
        ],
        compiler_params=pltpu.CompilerParams(
            collective_id=0, has_side_effects=True, vmem_limit_bytes=56 * MIB
        ),
    )(gains, same, first, last, gate_gain, lower, w_in, tokens)


def gather_fsdp(part, dim):
    return lax.all_gather(part, "fsdp", axis=dim, tiled=True)


def local(
    sizes,
    tokens, segment_ids, w_in, w_out, w_glu, w_down, gain_one, gain_two, gate_gain, lower, cotangent,
):
    n_fsdp, n_ctx, n_tp = sizes
    n_seq, length, width = tokens.shape
    rows = n_seq * length
    chan = w_in.shape[2]
    x_half = tokens.reshape(rows, width)
    parts = (w_out.astype(HALF), w_glu[:, 0].astype(HALF), w_glu[:, 1].astype(HALF), w_down.astype(HALF))
    if n_fsdp != 2:
        parts = tuple(gather_fsdp(part, dim) for part, dim in zip(parts, (1, 0, 0, 1)))
        w_in = gather_fsdp(w_in.astype(HALF), 1)
    gain_gate = gate_gain[None]
    low = lower[None]
    seg = segment_ids.astype(FLOAT)
    same = jnp.pad((seg[:, 1:] == seg[:, :-1]).astype(FLOAT), ((0, 0), (1, 0)))[..., None]
    first, last = (jnp.broadcast_to(seg[:, at], (n_seq, BLOCK)) for at in (slice(0, 1), slice(-1, None)))
    gated, gate_scale, carry, keep, gain_a, gain_b, proj, state, normed, w_in_all = run_head(
        jnp.stack([gain_one, gain_two]), same, first, last, gain_gate, low, w_in, x_half,
        n_fsdp, n_ctx, n_tp,
    )
    gated = gated.reshape(rows, chan)
    grad_y_half = cotangent.reshape(rows, width)
    (
        mixed, _, act, _, grad_resid, grad_mixed, grad_gated, grad_w_gate, grad_w_up, w_down_all,
        grad_gain_two,
    ) = run_middle(gated, x_half, grad_y_half, gain_b, parts, n_fsdp, n_ctx, length)
    if n_fsdp == 2:
        grad_w_up = lax.psum(grad_w_up, "ctx")
    grad_tokens, output, vectors, grad_w_in, grad_w_out, grad_w_down = run_tail(
        (keep, gain_gate, low, gate_scale, carry, gain_a, grad_gain_two),
        (
            proj, state, grad_gated.reshape(n_seq, length, chan), w_in_all, w_down_all, act, normed,
            grad_mixed, gated, grad_y_half, grad_resid, x_half, mixed,
        ),
        n_fsdp, n_ctx, n_tp,
    )
    grads = (grad_w_in, grad_w_out, grad_w_gate, grad_w_up, grad_w_down)
    if n_fsdp != 2:
        grads = tuple(
            lax.psum(lax.psum_scatter(value, "fsdp", scatter_dimension=dim, tiled=True), "ctx")
            for value, dim in zip(grads, (0, 1, 0, 0, 1))
        )
    grad_w_in, grad_w_out, grad_w_glu, grad_w_down, grad_tokens = run_widen_outputs(
        *grads, grad_tokens
    )
    part = gain_one.shape[0]
    begin = lax.axis_index("fsdp") * part
    return (
        output.reshape(n_seq, length, width),
        grad_tokens.reshape(n_seq, length, width),
        grad_w_in,
        grad_w_out,
        grad_w_glu,
        grad_w_down,
        lax.dynamic_slice(vectors[0], (begin,), (part,)),
        lax.dynamic_slice(vectors[0], (width + begin,), (part,)),
        vectors[0, 2 * width : 2 * width + chan],
        vectors[0, 2 * width + chan :],
    )


def solution(mesh):
    sizes = tuple(mesh.shape[axis] for axis in ("fsdp", "ctx", "tp"))
    return jax.shard_map(
        functools.partial(local, sizes),
        mesh=mesh,
        in_specs=(
            P("fsdp", "ctx", None),
            P("fsdp", "ctx"),
            P(None, "fsdp", "tp"),
            P("tp", "fsdp"),
            P("fsdp", None, "tp"),
            P("tp", "fsdp"),
            P("fsdp"),
            P("fsdp"),
            P("tp"),
            P("tp"),
            P("fsdp", "ctx", None),
        ),
        out_specs=(
            P("fsdp", "ctx", None),
            P("fsdp", "ctx", None),
            P(None, "fsdp", "tp"),
            P("tp", "fsdp"),
            P("fsdp", None, "tp"),
            P("tp", "fsdp"),
            P("fsdp"),
            P("fsdp"),
            P("tp"),
            P("tp"),
        ),
        check_vma=False,
    )
```

```python
import functools

import jax
import jax.numpy as jnp
from jax import lax
from jax.experimental import pallas as pl
from jax.experimental.pallas import tpu as pltpu
from jax.sharding import PartitionSpec as P

EPS = 1e-06
FLOAT = jnp.float32
HALF = jnp.bfloat16
MESH = pl.DeviceIdType.MESH
GROUP = 8
BLOCK = 128
MIB = 1 << 20


def rms_scale(values):
    return lax.rsqrt(jnp.mean(values * values, -1, keepdims=True) + EPS)


def silu_slope(values):
    sig = jax.nn.sigmoid(values)
    return sig * (1.0 + values * (1.0 - sig))


def greet(peers):
    barrier = pltpu.get_barrier_semaphore()
    for peer in peers:
        pl.semaphore_signal(barrier, inc=1, device_id=peer, device_id_type=MESH)
    pl.semaphore_wait(barrier, len(peers))


def others(axis, count):
    mine = lax.axis_index(axis)
    return [{axis: lax.rem(mine + step, count)} for step in range(1, count)]


def shares(slots, axis, count, send, recv):
    mine = lax.axis_index(axis)
    return [
        pltpu.make_async_remote_copy(
            src_ref=slots.at[mine],
            dst_ref=slots.at[mine],
            send_sem=send.at[step],
            recv_sem=recv.at[step],
            device_id=peer,
            device_id_type=MESH,
        )
        for step, peer in enumerate(others(axis, count))
    ]


def share(slots, axis, count, send, recv):
    copies = shares(slots, axis, count, send, recv)
    for copy in copies:
        copy.start()
    for copy in copies:
        copy.wait()


def lane_sums(values):
    part = values[:, :BLOCK]
    for start in range(BLOCK, values.shape[1], BLOCK):
        part = part + values[:, start : start + BLOCK]
    return jnp.sum(part.T, 0, keepdims=True)


def columns(row):
    return jnp.broadcast_to(row, (BLOCK, BLOCK)).T


def widen(values, chan):
    return jnp.concatenate([values] * (chan // BLOCK), -1)


PIECES = 4
TILE = 256
WIDE = 512


def bands(count, size):
    return [(start, min(size, count - start)) for start in range(0, count, size)]


def dot(lhs, rhs):
    return jnp.dot(lhs, rhs, preferred_element_type=FLOAT)


def dot_nt(lhs, rhs):
    return lax.dot_general(lhs, rhs, (((1,), (1,)), ((), ())), preferred_element_type=FLOAT)


class Line:
    def __init__(self, held, cross, total, sems):
        self.held, self.cross, self.total, self.sems = held, cross, total, sems
        place = lax.axis_index("tp")
        self.inner = (place == 1) | (place == 2)
        self.side = place + 1 - 2 * lax.rem(place, 2)
        self.facing = 3 - place

    def slot(self, job, ref):
        slots = ref.shape[0]
        if slots == self.total.shape[0]:
            return job
        return job % slots if isinstance(job, int) else lax.rem(job, slots)

    def copy(self, source, target, send, recv, place):
        return pltpu.make_async_remote_copy(
            src_ref=source,
            dst_ref=target,
            send_sem=send,
            recv_sem=recv,
            device_id={"tp": place},
            device_id_type=MESH,
        )

    def inward(self, job, q):
        send, recv, _, _ = self.sems
        return self.copy(
            self.held.at[self.slot(job, self.held), q], self.total.at[job, q],
            send.at[job, q], recv.at[job, q], self.side,
        )

    def outward(self, job, q):
        send, recv, _, _ = self.sems
        return self.copy(
            self.total.at[job, q], self.total.at[job, q],
            send.at[job, q], recv.at[job, q], self.side,
        )

    def across(self, job, q):
        _, _, send, recv = self.sems
        return self.copy(
            self.held.at[self.slot(job, self.held), q], self.cross.at[self.slot(job, self.cross), q],
            send.at[job, q], recv.at[job, q], self.facing,
        )

    def offer(self, job, q):
        @pl.when(jnp.logical_not(self.inner))
        def _():
            self.inward(job, q).start()

    def forward(self, job, q):
        slot = self.slot(job, self.held)

        @pl.when(self.inner)
        def _():
            self.inward(job, q).wait_recv()
            self.held[slot, q] = self.held[slot, q] + self.total[job, q]
            self.across(job, q).start()

    def close(self, job, q):
        slot, cross_slot = self.slot(job, self.held), self.slot(job, self.cross)

        @pl.when(self.inner)
        def _():
            self.across(job, q).wait_recv()
            self.total[job, q] = self.held[slot, q] + self.cross[cross_slot, q]
            self.outward(job, q).start()

    def tick(self, base, step):
        if step > 0:
            self.close(base, step - 1)
        if step < PIECES:
            ahead = step + 1
            self.forward(base + ahead // PIECES, ahead % PIECES)

    def arrive(self, job):
        @pl.when(jnp.logical_not(self.inner))
        def _():
            @pl.loop(0, PIECES)
            def _(q):
                self.outward(job, q).wait_recv()

    def release(self, job):
        @pl.when(self.inner)
        def _():
            @pl.loop(0, PIECES)
            def _(q):
                self.across(job, q).wait_send()

        @pl.when(jnp.logical_not(self.inner))
        def _():
            @pl.loop(0, PIECES)
            def _(q):
                self.inward(job, q).wait_send()

    def settle(self, job):
        @pl.when(self.inner)
        def _():
            @pl.loop(0, PIECES)
            def _(q):
                self.outward(job, q).wait_send()


def pull(parts, wholes, dims, n_fsdp, own_sem, send_sem, recv_sem):
    if n_fsdp != 2:
        copies = [
            pltpu.make_async_copy(part, whole, own_sem.at[index])
            for index, (part, whole) in enumerate(zip(parts, wholes))
        ]
        for copy in copies:
            copy.start()
        return lambda index: copies[index].wait()
    mine = lax.axis_index("fsdp")
    near, far = [], []
    for index, (part, whole, dim) in enumerate(zip(parts, wholes, dims)):
        size = part.shape[dim]
        at = pl.ds(pl.multiple_of(mine * size, size), size)
        place = whole.at[at] if dim == 0 else whole.at[:, at]
        near.append(pltpu.make_async_copy(part, place, own_sem.at[index]))
        far.append(
            pltpu.make_async_remote_copy(
                src_ref=part,
                dst_ref=place,
                send_sem=send_sem.at[index],
                recv_sem=recv_sem.at[index],
                device_id={"fsdp": 1 - mine},
                device_id_type=MESH,
            )
        )
    for one, two in zip(near, far):
        two.start()
        one.start()

    def wait(index):
        near[index].wait()
        far[index].wait()

    return wait


def span(start, size, unit):
    return pl.ds(pl.multiple_of(start, unit), size)


def row_blocks(count, size, body):
    @pl.loop(0, count // size)
    def _(index):
        body(pl.ds(pl.multiple_of(index * size, size), size))


def line_peers():
    place = lax.axis_index("tp")
    return [{"tp": place + 1 - 2 * lax.rem(place, 2)}, {"tp": 3 - place}]


def joined(ref, c, rows):
    return jnp.concatenate([ref[c, q, rows, :].astype(FLOAT) for q in range(PIECES)], -1)


def add_to(target, extra, rows):
    target[rows, :] = target[rows, :] + extra[rows, :]


def halves(n_fsdp, store_sem, send_sem, recv_sem, spare, inbox):
    mine = lax.axis_index("fsdp")
    pending = {}

    def send(index, view):
        slot = index % 2
        return pltpu.make_async_remote_copy(
            src_ref=view(spare.at[slot]),
            dst_ref=view(inbox.at[slot]),
            send_sem=send_sem.at[slot],
            recv_sem=recv_sem.at[slot],
            device_id={"fsdp": 1 - mine},
            device_id_type=MESH,
        )

    def item(index, view, compute_other, compute_own, other_place, target):
        slot = index % 2
        if index - 2 in pending:
            pending.pop(index - 2)()
        compute_other(view(spare.at[slot]))
        if n_fsdp == 2:
            copy = send(index, view)
            copy.start()
            pending[index] = lambda: send(index, view).wait_send()
        else:
            def store():
                return pltpu.make_async_copy(view(spare.at[slot]), other_place(), store_sem.at[slot])

            store().start()
            pending[index] = lambda: store().wait()
        compute_own(target)
        if n_fsdp == 2:
            send(index, view).wait_recv()
            extra = view(inbox.at[slot])
            row_blocks(target.shape[0], 32, lambda rows: add_to(target, extra, rows))

    def finish():
        for wait in pending.values():
            wait()

    return item, finish


class Square:
    def __init__(self, index, buffers, at, place, send, recv, store_sem):
        self.buffers, self.at, self.place_of = buffers, at, place
        self.send, self.recv, self.index, self.store_sem = send, recv, index, store_sem

    @property
    def tile(self):
        return self.buffers[0].at[self.at[0]]

    @property
    def half(self):
        return self.buffers[1].at[self.at[1]]

    @property
    def quarter(self):
        return self.buffers[2].at[self.at[2]]

    def geometry(self):
        here = lax.axis_index("ctx")
        low, high = lax.rem(here, 2), here // 2
        near, far = here + 1 - 2 * low, here + 2 - 4 * high
        bits = (low, high) if self.index % 2 == 0 else (high, low)
        peers = (near, far) if self.index % 2 == 0 else (far, near)
        wide, thin = self.half.shape[0], self.quarter.shape[0]
        begin = bits[0] * wide
        return (
            peers,
            span(begin, wide, wide),
            span((1 - bits[0]) * wide, wide, wide),
            span(begin + bits[1] * thin, thin, thin),
            span(begin + (1 - bits[1]) * thin, thin, thin),
        )

    def round(self, number):
        peers, mine, yours, my_part, your_part = self.geometry()
        source, target, peer = (
            (self.tile.at[yours], self.half, 0),
            (self.tile.at[your_part], self.quarter, 1),
            (self.tile.at[my_part], self.place_of().at[my_part], 1),
            (self.place_of().at[mine], self.place_of().at[mine], 0),
        )[number]
        return pltpu.make_async_remote_copy(
            src_ref=source,
            dst_ref=target,
            send_sem=self.send.at[self.index, number],
            recv_sem=self.recv.at[self.index, number],
            device_id={"ctx": peers[peer]},
            device_id_type=MESH,
        )

    def add(self, part, extra):
        target = self.tile.at[part]
        row_blocks(extra.shape[0], 32, lambda rows: add_to(target, extra, rows))

    def store(self):
        return pltpu.make_async_copy(self.tile, self.place_of(), self.store_sem.at[self.index])

    def store_part(self):
        part = self.geometry()[3]
        return pltpu.make_async_copy(
            self.tile.at[part], self.place_of().at[part], self.store_sem.at[self.index]
        )

    def advance(self, number):
        if number > 0:
            self.round(number - 1).wait_recv()
        if number == 1:
            self.add(self.geometry()[1], self.half)
        if number == 2:
            self.add(self.geometry()[3], self.quarter)
            self.store_part().start()
        if number == 3:
            self.store_part().wait()
        if number < 4:
            self.round(number).start()

    def settle(self):
        for number in range(4):
            self.round(number).wait_send()


def fill(target, left, right, first):
    for start, size in bands(target.shape[1], WIDE):
        cols = pl.ds(pl.multiple_of(first + start, BLOCK), size)
        target[:, start : start + size] = dot(left, right[:, cols]).astype(HALF)


def middle(
    n_fsdp, n_ctx, CHUNK,
    gated, tokens, cotangent, gain, wo_part, wg_part, wu_part, wd_part,
    mixed_out, normed_out, act_out, grad_glu_out, grad_resid_out, grad_mixed_out,
    grad_gated_out, w_gate_out, w_up_out, w_down_out, grad_gain_out,
    wo, wg, wu, wd, x_all, dy_all, held, crossed, total, normed, act, grad_glu,
    grad_resid, grad_mixed, grad_gated, gain_total, spare, inbox, half, quarter,
    square_send, square_recv, square_store, weight_sem, weight_send, weight_recv, again_sem, own_sem, send_sem, recv_sem, load_sem, store_sem, *line_sems,
):
    n_chunks, _, _, piece = held.shape
    units = wd.shape[0]
    width = wd.shape[1]
    peers = line_peers() + others("ctx", n_ctx)
    if n_fsdp == 2:
        peers.append({"fsdp": 1 - lax.axis_index("fsdp")})
    greet(peers)
    ready = pull(
        (wo_part, wg_part, wu_part, wd_part), (wo, wg, wu, wd), (1, 0, 0, 1),
        n_fsdp, own_sem, send_sem, recv_sem,
    )
    loads = [
        pltpu.make_async_copy(tokens, x_all, load_sem.at[0]),
        pltpu.make_async_copy(cotangent, dy_all, load_sem.at[1]),
    ]
    for load in loads:
        load.start()
    line = Line(held, crossed, total, line_sems)

    def chunk_rows(c):
        return pl.ds(pl.multiple_of(c * CHUNK, CHUNK), CHUNK)

    def stores(c, wanted=None):
        rows = chunk_rows(c)
        pairs = [
            (normed, normed_out.at[rows]),
            (act, act_out.at[rows]),
            (grad_glu.at[0], grad_glu_out.at[0, rows]),
            (grad_glu.at[1], grad_glu_out.at[1, rows]),
            (grad_resid, grad_resid_out.at[rows]),
            (grad_mixed, grad_mixed_out.at[rows]),
            (grad_gated, grad_gated_out.at[rows]),
        ]
        pairs += [
            (total.at[c, q], mixed_out.at[rows, pl.ds(q * piece, piece)]) for q in range(PIECES)
        ]
        return [
            pltpu.make_async_copy(source, target, store_sem.at[index])
            for index, (source, target) in enumerate(pairs)
            if wanted is None or index in wanted
        ]

    FORWARD = (0, 1, 2, 3, 7, 8, 9, 10)
    BACKWARD = (4, 5, 6)

    ready(0)

    @pl.loop(0, n_chunks)
    def _(c):
        lhs = gated[chunk_rows(c), :]

        @pl.loop(0, PIECES)
        def _(q):
            cols = pl.ds(pl.multiple_of(q * piece, piece), piece)
            held[c, q] = dot(lhs, wo[:, cols]).astype(HALF)
            line.offer(c, q)

    for load in loads:
        load.wait()
    line.forward(0, 0)
    for step in range(PIECES + 1):
        line.tick(0, step)
    for index in (1, 2, 3):
        ready(index)
    w_down_store = pltpu.make_async_copy(wd, w_down_out, again_sem.at[3])
    w_down_store.start()

    @pl.loop(0, n_chunks)
    def _(c):
        line.arrive(c)
        line.tick(c + 1, 0)

        @pl.when(c > 0)
        def _():
            for store in stores(c - 1, FORWARD):
                store.wait()

        def norm(rows):
            at = pl.ds(pl.multiple_of(c * CHUNK + rows.start, 16), rows.size)
            resid = x_all[at, :].astype(FLOAT) + joined(total, c, rows)
            normed[rows, :] = (resid * rms_scale(resid) * gain[...]).astype(HALF)

        row_blocks(CHUNK, 16, norm)

        def unit(cols):
            glu_gate = dot(normed[...], wg[:, cols])
            glu_up = dot(normed[...], wu[:, cols])
            grad_act = dot_nt(dy_all[chunk_rows(c), :], wd[cols, :])
            sig = jax.nn.sigmoid(glu_gate)
            silu = glu_gate * sig
            act[:, cols] = (silu * glu_up).astype(HALF)
            slope = sig * (1.0 + glu_gate * (1.0 - sig))
            grad_glu[0, :, cols] = (grad_act * glu_up * slope).astype(HALF)
            grad_glu[1, :, cols] = (grad_act * silu).astype(HALF)

        for index, (start, size) in enumerate(bands(units, WIDE)):
            unit(slice(start, start + size))
            if index == 0:
                line.tick(c + 1, 1)
        line.tick(c + 1, 2)
        line.release(c)

        @pl.loop(0, PIECES)
        def _(q):
            @pl.when(q == PIECES // 2)
            def _():
                line.tick(c + 1, 3)

            at = pl.ds(pl.multiple_of(q * piece, piece), piece)
            value = dot_nt(grad_glu[0], wg[at, :]) + dot_nt(grad_glu[1], wu[at, :])
            held[c, q] = value.astype(HALF)
            line.offer(n_chunks + c, q)

        line.tick(c + 1, 4)

        for store in stores(c, FORWARD):
            store.start()

    for store in stores(n_chunks - 1, FORWARD):
        store.wait()
    rows = n_chunks * CHUNK
    w_down_store.wait()
    kept = [
        (grad_glu_out.at[0], wg.at[:rows]),
        (grad_glu_out.at[1], wu.at[:rows]),
        (normed_out, wd.at[:rows]),
    ]
    again = [
        pltpu.make_async_copy(source, target, again_sem.at[index])
        for index, (source, target) in enumerate(kept)
    ]
    for copy in again:
        copy.start()
    gain_total[...] = jnp.zeros_like(gain_total)
    item, finish = halves(n_fsdp, weight_sem, weight_send, weight_recv, spare, inbox)
    mine = lax.axis_index("fsdp") if n_fsdp == 2 else 1
    depth = width // 2
    whole = n_fsdp != 2
    per_part = depth // TILE
    squares, plain, turn = [], [], [0]

    def weight_item(index):
        if index >= 2 * per_part:
            return
        part, k = divmod(index, per_part)
        right = (wg, wu)[part].at[:rows]
        out = (w_gate_out, w_up_out)[part]

        def compute(side):
            at = pl.ds(pl.multiple_of(side * depth + k * TILE, TILE), TILE)
            return lambda target: fill(target, wd[:rows, at].T, right, 0)

        at = slice(k * TILE + whole * depth, (k + 1) * TILE + whole * depth)
        square = Square(
            index, ((wg, wu)[part], half, quarter),
            (slice(rows + k * TILE, rows + (k + 1) * TILE), k, k), lambda: out.at[at],
            square_send, square_recv, square_store,
        )
        item(
            index, lambda ref: ref, compute(1 - mine), compute(mine),
            lambda: out.at[k * TILE : (k + 1) * TILE], square.tile,
        )
        if whole or part == 1:
            square.store().start()
            plain.append(square)
        else:
            squares.append([square, 0, turn[0]])

    def pump():
        for square in squares:
            if square[1] < 5 and turn[0] >= square[2] + 3 * square[1]:
                square[0].advance(square[1])
                square[1] += 1
        turn[0] += 1

    def backward(c, between):
        line.arrive(n_chunks + c)
        if c > 0:
            for store in stores(c - 1, BACKWARD):
                store.wait()

        def norm_back(rows):
            at = pl.ds(pl.multiple_of(c * CHUNK + rows.start, 16), rows.size)
            resid = x_all[at, :].astype(FLOAT) + joined(total, c, rows)
            rate = rms_scale(resid)
            grad = joined(total, n_chunks + c, rows)
            by_gain = grad * (resid * rate)
            gain_total[...] += by_gain[:8] + by_gain[8:]
            inner = gain[...] * grad
            mean = jnp.mean(inner * resid, -1, keepdims=True)
            value = dy_all[at, :].astype(FLOAT) + rate * inner - resid * (rate * rate * rate * mean)
            grad_resid[rows, :] = value
            grad_mixed[rows, :] = value.astype(HALF)

        row_blocks(CHUNK, 16, norm_back)
        between()
        for start, size in bands(grad_gated.shape[1], WIDE):
            grad_gated[:, start : start + size] = dot_nt(
                grad_mixed[...], wo[start : start + size, :]
            )
        for store in stores(c, BACKWARD):
            store.start()

    for copy in again:
        copy.wait()
    count = 0
    for c in range(n_chunks):
        if c == n_chunks - 1:
            while count < 2 * per_part:
                weight_item(count)
                count += 1
        if c + 1 == n_chunks:
            backward(c, lambda: None)
            continue

        def between():
            line.tick(n_chunks + c + 1, 0)
            pump()

        backward(c, between)
        for step in range(1, PIECES + 1):
            weight_item(count)
            count += 1
            if c + 2 == n_chunks and step == PIECES - 1:
                line.close(2 * n_chunks - 1, step - 1)
            else:
                line.tick(n_chunks + c + 1, step)
            pump()
    while any(square[1] < 5 for square in squares):
        pump()
    finish()
    for square, _, _ in squares:
        square.settle()
    for square in plain:
        square.store().wait()

    grad_gain_out[...] = jnp.sum(gain_total[...], 0, keepdims=True)
    for store in stores(n_chunks - 1, BACKWARD):
        store.wait()

    @pl.loop(0, n_chunks)
    def _(c):
        line.settle(c)
        line.settle(n_chunks + c)
        line.release(n_chunks + c)


def run_middle(gated, tokens, cotangent, gain, parts, n_fsdp, n_ctx, length):
    rows, chan = gated.shape
    width = tokens.shape[1]
    wg = parts[1]
    units = wg.shape[1]
    n_chunks = rows // length
    piece = width // PIECES
    vmem = pl.BlockSpec(memory_space=pltpu.VMEM)
    hbm = pl.BlockSpec(memory_space=pl.ANY)
    sems = pltpu.SemaphoreType.DMA((2 * n_chunks, PIECES))
    return pl.pallas_call(
        functools.partial(middle, n_fsdp, n_ctx, length),
        name="middle",
        out_shape=(
            jax.ShapeDtypeStruct((rows, width), HALF),
            jax.ShapeDtypeStruct((rows, width), HALF),
            jax.ShapeDtypeStruct((rows, units), HALF),
            jax.ShapeDtypeStruct((2, rows, units), HALF),
            jax.ShapeDtypeStruct((rows, width), FLOAT),
            jax.ShapeDtypeStruct((rows, width), HALF),
            jax.ShapeDtypeStruct((rows, chan), FLOAT),
            jax.ShapeDtypeStruct((width if n_fsdp != 2 else width // 2, units), HALF),
            jax.ShapeDtypeStruct((width if n_fsdp != 2 else width // 2, units), HALF),
            jax.ShapeDtypeStruct((units, width), HALF),
            jax.ShapeDtypeStruct((1, width), FLOAT),
        ),
        in_specs=[vmem, hbm, hbm, vmem, hbm, hbm, hbm, hbm],
        out_specs=[hbm] * 10 + [vmem],
        scratch_shapes=[
            pltpu.VMEM((chan, width), HALF),
            pltpu.VMEM((width, units), HALF),
            pltpu.VMEM((width, units), HALF),
            pltpu.VMEM((units, width), HALF),
            pltpu.VMEM((rows, width), HALF),
            pltpu.VMEM((rows, width), HALF),
            pltpu.VMEM((n_chunks, PIECES, length, piece), HALF),
            pltpu.VMEM((n_chunks, PIECES, length, piece), HALF),
            pltpu.VMEM((2 * n_chunks, PIECES, length, piece), HALF),
            pltpu.VMEM((length, width), HALF),
            pltpu.VMEM((length, units), HALF),
            pltpu.VMEM((2, length, units), HALF),
            pltpu.VMEM((length, width), FLOAT),
            pltpu.VMEM((length, width), HALF),
            pltpu.VMEM((length, chan), FLOAT),
            pltpu.VMEM((8, width), FLOAT),
            pltpu.VMEM((2, TILE, units), HALF),
            pltpu.VMEM((2, TILE, units), HALF),
            pltpu.VMEM((width // 2 // TILE, TILE // 2, units), HALF),
            pltpu.VMEM((width // 2 // TILE, TILE // 4, units), HALF),
            pltpu.SemaphoreType.DMA((width // 2 // TILE, 4)),
            pltpu.SemaphoreType.DMA((width // 2 // TILE, 4)),
            pltpu.SemaphoreType.DMA((width // TILE,)),
            pltpu.SemaphoreType.DMA((4,)),
            pltpu.SemaphoreType.DMA((2,)),
            pltpu.SemaphoreType.DMA((2,)),
            pltpu.SemaphoreType.DMA((4,)),
            pltpu.SemaphoreType.DMA((4,)),
            pltpu.SemaphoreType.DMA((4,)),
            pltpu.SemaphoreType.DMA((4,)),
            pltpu.SemaphoreType.DMA((2,)),
            pltpu.SemaphoreType.DMA((12,)),
        ]
        + [sems] * 4,
        compiler_params=pltpu.CompilerParams(
            collective_id=2, has_side_effects=True, vmem_limit_bytes=63 * MIB
        ),
        cost_estimate=pl.CostEstimate(
            flops=16 * rows * width * units, bytes_accessed=400 * MIB, transcendentals=0
        ),
    )(gated, tokens, cotangent, gain, *parts)


def scan_cross(gate_all, state, scale, gain, near, grad_proj, gain_out, cross):
    n_seq, length, chan = state.shape
    mine = lax.axis_index("tp")
    gain_total = jnp.zeros((8, chan), FLOAT)
    for seq in range(n_seq):
        for start in range(0, length, BLOCK):
            rows = slice(start, start + BLOCK)
            rate = columns(scale[seq : seq + 1, rows])
            gate = gate_all[seq, rows, :]
            sig = jax.nn.sigmoid(gate)
            swish = gate * sig
            value = state[seq, rows, :]
            into = near[seq, rows, :]
            by_unit = into * value * widen(rate, chan)
            slope = sig * (1.0 + gate * (1.0 - sig))
            grad_proj[seq, rows, 2 * chan :] = (by_unit * gain[...] * slope).astype(HALF)
            gain_total = gain_total + jnp.sum((by_unit * swish).reshape(-1, 8, chan), 0)
            grad_unit = into * swish * gain[...]
            near[seq, rows, :] = grad_unit
            cross[mine, seq : seq + 1, rows] = lane_sums(grad_unit * value)
    gain_out[...] = jnp.sum(gain_total, 0, keepdims=True)


def scan_back(
    n_ctx, n_tp, width, pump,
    proj, keep, lower, state, scale, carry_in, near,
    grad_proj, lower_out,
    reach, rate_wide, cross_wide, ends, cross, ctx_sems,
):
    n_seq, length, chan = state.shape
    low = lower[...].reshape(1, 1, chan)
    total = cross[0]
    for place in range(1, n_tp):
        total = total + cross[place]
    rate = scale[...]
    total = total * (rate * rate * rate) / width
    for seq in range(n_seq):
        for start in range(0, length, BLOCK):
            rows = slice(start, start + BLOCK)
            rate_wide[seq, rows, :] = columns(rate[seq : seq + 1, rows])
            cross_wide[seq, rows, :] = columns(total[seq : seq + 1, rows])

    row = lax.broadcasted_iota(jnp.int32, (n_seq, GROUP, chan), 1)

    def back(index, carry):
        prod, above = carry
        rows = pl.ds(pl.multiple_of((length // GROUP - 1 - index) * GROUP, GROUP), GROUP)
        decay = low + (1.0 - low) * jax.nn.sigmoid(proj[1, :, rows, :])
        mult = decay * keep[:, rows, :]
        direct = (
            widen(rate_wide[:, rows, :], chan) * near[:, rows, :]
            - widen(cross_wide[:, rows, :], chan) * state[:, rows, :]
        )
        add = mult * direct
        for hop in (1, 2, 4):
            inside = row < GROUP - hop
            add = jnp.where(inside, mult * pltpu.roll(add, GROUP - hop, 1) + add, add)
            mult = jnp.where(inside, mult * pltpu.roll(mult, GROUP - hop, 1), mult)
        add = add + mult * above
        mult = mult * prod
        inside = row < GROUP - 1
        near[:, rows, :] = direct + jnp.where(inside, pltpu.roll(add, GROUP - 1, 1), above)
        reach[:, rows, :] = jnp.where(inside, pltpu.roll(mult, GROUP - 1, 1), prod)
        return mult[:, :1, :], add[:, :1, :]

    held = (jnp.ones((n_seq, 1, chan), FLOAT), jnp.zeros((n_seq, 1, chan), FLOAT))
    middle_of = length // GROUP // 2
    held = lax.fori_loop(0, middle_of, back, held)
    pump()
    prod, total = lax.fori_loop(middle_of, length // GROUP, back, held)
    here = lax.axis_index("ctx")
    ends[here, 0] = prod.reshape(n_seq, chan)
    ends[here, 1] = total.reshape(n_seq, chan)
    pump()
    share(ends, "ctx", n_ctx, *ctx_sems)
    carry = jnp.zeros((n_seq, chan), FLOAT)
    for place in range(n_ctx - 1, 0, -1):
        carry = jnp.where(place > here, ends[place, 1] + ends[place, 0] * carry, carry)
    carry = carry.reshape(n_seq, 1, chan)
    wide = 2 * GROUP
    first = lax.broadcasted_iota(jnp.int32, (n_seq, wide, chan), 1) == 0

    def finish(index, held):
        before, low_total = held
        rows = pl.ds(pl.multiple_of(index * wide, wide), wide)
        inp = proj[0, :, rows, :]
        sig = jax.nn.sigmoid(inp)
        silu = inp * sig
        fsig = jax.nn.sigmoid(proj[1, :, rows, :])
        rest = 1.0 - fsig
        decay = low + (1.0 - low) * fsig
        grad_state = near[:, rows, :] + reach[:, rows, :] * carry
        value = state[:, rows, :]
        prev = jnp.where(first, before, pltpu.roll(value, 1, 1))
        grad_decay = grad_state * (prev * keep[:, rows, :] - silu)
        grad_proj[:, rows, :chan] = (
            grad_state * (1.0 - decay) * (sig * (1.0 + inp * (1.0 - sig)))
        ).astype(HALF)
        grad_proj[:, rows, chan : 2 * chan] = (
            grad_decay * (1.0 - low) * fsig * rest
        ).astype(HALF)
        return value[:, wide - 1 :, :], low_total + grad_decay * rest

    held = (carry_in[...].reshape(n_seq, 1, chan), jnp.zeros((n_seq, wide, chan), FLOAT))
    middle_of = length // wide // 2
    held = lax.fori_loop(0, middle_of, finish, held)
    pump()
    _, low_total = lax.fori_loop(middle_of, length // wide, finish, held)
    lower_out[...] = jnp.sum(jnp.sum(low_total, 0), 0, keepdims=True)
    pump()


def tail(
    n_fsdp, n_ctx, n_tp,
    keep, gate_gain, lower, scale, carry_in, gain, gain_two_grad,
    proj, state, grad_gated, w_in, w_down, act, normed, grad_mixed, gated, cotangent,
    grad_resid, tokens, mixed,
    grad_tokens_out, output_out, vectors_out, w_in_out, w_out_out, w_down_out,
    grad_proj, held, crossed, total, spare, inbox,
    in_tile, in_half, in_quarter, out_tile, out_half, out_quarter, down_tile, down_half, down_quarter,
    gain_total, ends, cross, over_ctx, over_fsdp, near,
    load_sem, store_sem, end_send, end_recv, cross_send, cross_recv, ctx_send, ctx_recv,
    fsdp_send, fsdp_recv, part_sem, part_send, part_recv, square_send, square_recv, square_store,
    *line_sems,
):
    n_seq, length, wide = grad_proj.shape
    chan = wide // 3
    rows = n_seq * length
    width = gain.shape[1]
    units = w_down.shape[0]
    piece = width // PIECES
    n_chunks = n_seq
    whole = n_fsdp != 2
    greet(others("ctx", n_ctx) + others("tp", n_tp) + others("fsdp", n_fsdp))
    line = Line(held, crossed, total, line_sems)
    pieces = [(job, q) for job in range(2 * n_chunks) for q in range(PIECES)]
    relay = [(line.forward, spot) for spot in pieces[:2]]
    for index, spot in enumerate(pieces):
        relay.append((line.close, spot))
        relay += [(line.forward, ahead) for ahead in pieces[index + 2 : index + 3]]
    squares = []
    turn = [0]
    SPACE = 4

    def pump():
        while relay:
            action, spot = relay.pop(0)
            action(*spot)
            if action == line.forward:
                break
        for square in squares:
            if square[1] < 5 and turn[0] >= square[2] + SPACE * square[1]:
                square[0].advance(square[1])
                square[1] += 1
        turn[0] += 1

    def start_loads(pairs, first=0):
        copies = [
            pltpu.make_async_copy(source, target, load_sem.at[first + index])
            for index, (source, target) in enumerate(pairs)
        ]
        for copy in copies:
            copy.start()
        return copies

    def chunk_rows(c):
        return pl.ds(c * length, length) if isinstance(c, int) else span(c * length, length, length)

    shape = (n_seq, length, chan)

    crossing = shares(cross, "tp", n_tp, cross_send, cross_recv)

    def down_terms(w_all, act_all):
        copies = start_loads([(w_down, w_all), (act, act_all)], 3)

        def cross_terms(gate_all, state_all):
            for copy in start_loads(
                [(proj.at[2], gate_all), (state, state_all), (grad_gated, near)]
            ):
                copy.wait()
            gain_at = over_ctx.at[lax.axis_index("ctx"), :, 2 * width : 2 * width + chan]
            scan_cross(gate_all, state_all, scale, gate_gain, near, grad_proj, gain_at, cross)

        pl.run_scoped(cross_terms, pltpu.VMEM(shape, FLOAT), pltpu.VMEM(shape, FLOAT))
        for copy in crossing:
            copy.start()
        for copy in copies:
            copy.wait()

        for c in range(n_chunks):
            @pl.loop(0, PIECES)
            def _(q):
                cols = pl.ds(pl.multiple_of(q * piece, piece), piece)
                held[c, q] = dot(act_all[chunk_rows(c), :], w_all[:, cols]).astype(HALF)
                line.offer(c, q)

            if c >= n_chunks // 2:
                pump()

    pl.run_scoped(
        down_terms, pltpu.VMEM((units, width), HALF), pltpu.VMEM((rows, units), HALF)
    )

    for copy in crossing:
        copy.wait()

    def back(proj_all, state_all, reach, rate_wide, cross_wide):
        for copy in start_loads([(proj.at[:2], proj_all), (state, state_all)]):
            copy.wait()
        lower_at = over_ctx.at[lax.axis_index("ctx"), :, 2 * width + chan :]
        scan_back(
            n_ctx, n_tp, width, pump,
            proj_all, keep, lower, state_all, scale, carry_in, near,
            grad_proj, lower_at,
            reach, rate_wide, cross_wide, ends, cross, (end_send, end_recv),
        )

    pl.run_scoped(
        back,
        pltpu.VMEM((2, *shape), FLOAT),
        pltpu.VMEM(shape, FLOAT),
        pltpu.VMEM(shape, FLOAT),
        pltpu.VMEM((n_seq, length, BLOCK), FLOAT),
        pltpu.VMEM((n_seq, length, BLOCK), FLOAT),
    )

    def back_terms(w_all):
        for copy in start_loads([(w_in, w_all)]):
            copy.wait()

        for c in range(n_chunks):
            @pl.loop(0, PIECES)
            def _(q):
                at = pl.ds(pl.multiple_of(q * piece, piece), piece)
                held[n_chunks + c, q] = dot_nt(grad_proj[c], w_all[at, :]).astype(HALF)
                line.offer(n_chunks + c, q)

            if c % 2 == 1:
                pump()

    pl.run_scoped(back_terms, pltpu.VMEM((width, wide), HALF))

    item, finish = halves(n_fsdp, part_sem, part_send, part_recv, spare, inbox)
    mine = 1 if whole else lax.axis_index("fsdp")
    depth = width // 2
    skip = whole * depth
    stores = []

    def weights(act_all, dy_all, normed_all, mixed_all, gated_all):
        copies = start_loads(
            [(act, act_all), (cotangent, dy_all), (normed, normed_all), (grad_mixed, mixed_all),
             (gated, gated_all)]
        )
        count = [0]

        def tile(view, compute, other_place, own_place, buffers, at):
            index = count[0]
            count[0] += 1
            square = Square(
                index, buffers, at, own_place, square_send, square_recv, square_store
            )
            item(index, view, compute(1 - mine), compute(mine), other_place, square.tile)
            if whole:
                square.store().start()
                stores.append(square)
            else:
                squares.append([square, 0, turn[0]])
            pump()

        copies[0].wait()
        copies[1].wait()
        for start, size in bands(units, TILE):
            left = act_all[:, start : start + size].T
            at = slice(start, start + size)

            def compute(side):
                return lambda target: fill(target, left, dy_all, side * depth)

            tile(
                lambda ref, size=size: ref.at[:size, :depth], compute,
                lambda at=at: w_down_out.at[at, :depth], lambda at=at: w_down_out.at[at, skip:],
                (down_tile, down_half, down_quarter),
                [slice(start // cut, (start + size) // cut) for cut in (1, 2, 4)],
            )
        copies[2].wait()
        flat_proj = grad_proj.reshape(rows, wide)
        for k in range(depth // TILE):
            def compute(side):
                at = pl.ds(pl.multiple_of(side * depth + k * TILE, TILE), TILE)
                return lambda target: fill(target, normed_all[:, at].T, flat_proj, 0)

            at = slice(k * TILE, (k + 1) * TILE)
            tile(
                lambda ref: ref, compute,
                lambda at=at: w_in_out.at[at],
                lambda k=k: w_in_out.at[k * TILE + skip : (k + 1) * TILE + skip],
                (in_tile, in_half, in_quarter), (k, k, k),
            )
        copies[3].wait()
        copies[4].wait()
        for k in range(chan // TILE):
            at = slice(k * TILE, (k + 1) * TILE)
            left = gated_all[:, at].T

            def compute(side):
                return lambda target: fill(target, left, mixed_all, side * depth)

            tile(
                lambda ref: ref.at[:, :depth], compute,
                lambda at=at: w_out_out.at[at, :depth], lambda at=at: w_out_out.at[at, skip:],
                (out_tile, out_half, out_quarter), (k, k, k),
            )

    pl.run_scoped(
        weights,
        pltpu.VMEM((rows, units), HALF),
        pltpu.VMEM((rows, width), HALF),
        pltpu.VMEM((rows, width), HALF),
        pltpu.VMEM((rows, width), HALF),
        pltpu.VMEM((rows, chan), HALF),
    )
    finish()

    def ends_of(resid_all, x_all, mixed_all):
        copies = start_loads([(tokens, x_all), (mixed, mixed_all), (grad_resid, resid_all)])
        copies[0].wait()
        copies[1].wait()
        gain_total[...] = jnp.zeros_like(gain_total)

        def token_store(c):
            at = chunk_rows(c)
            return pltpu.make_async_copy(
                x_all.at[at], grad_tokens_out.at[at], store_sem.at[0, c]
            )

        def output_store(c):
            at = chunk_rows(c)
            return pltpu.make_async_copy(mixed_all.at[at], output_out.at[at], store_sem.at[1, c])

        def until(job):
            while (line.close, (job, PIECES - 1)) in relay:
                if relay[0] == (line.close, (job, PIECES - 1)):
                    action, spot = relay.pop(0)
                    action(*spot)
                else:
                    pump()

        for c in range(n_chunks):
            until(c)
            line.arrive(c)

            @pl.loop(0, length // 16)
            def _(index):
                at = pl.ds(pl.multiple_of(c * length + index * 16, 16), 16)
                rows = pl.ds(pl.multiple_of(index * 16, 16), 16)
                value = x_all[at, :].astype(FLOAT) + mixed_all[at, :].astype(FLOAT)
                mixed_all[at, :] = (value + joined(total, c, rows)).astype(HALF)

            output_store(c).start()

        copies[2].wait()
        for c in range(n_chunks):
            until(n_chunks + c)
            line.arrive(n_chunks + c)
            for quarter in range(PIECES):
                pump()

                @pl.loop(0, length // PIECES // 16)
                def _(index):
                    start = quarter * (length // PIECES) + index * 16
                    rows = pl.ds(pl.multiple_of(start, 16), 16)
                    at = pl.ds(pl.multiple_of(c * length + start, 16), 16)
                    value = x_all[at, :].astype(FLOAT)
                    rate = rms_scale(value)
                    grad = joined(total, n_chunks + c, rows)
                    by_gain = grad * (value * rate)
                    gain_total[...] += by_gain[:8] + by_gain[8:]
                    inner = gain[...] * grad
                    mean = jnp.mean(inner * value, -1, keepdims=True)
                    result = resid_all[at, :] + rate * inner - value * (rate * rate * rate * mean)
                    x_all[at, :] = result.astype(HALF)

            token_store(c).start()

        here = lax.axis_index("ctx")
        over_ctx[here, :, :width] = jnp.sum(gain_total[...], 0, keepdims=True)
        over_ctx[here, :, width : 2 * width] = gain_two_grad[...]
        share(over_ctx, "ctx", n_ctx, ctx_send, ctx_recv)
        value = over_ctx[0]
        for place in range(1, n_ctx):
            value = value + over_ctx[place]
        over_fsdp[lax.axis_index("fsdp")] = value
        share(over_fsdp, "fsdp", n_fsdp, fsdp_send, fsdp_recv)
        value = over_fsdp[0]
        for place in range(1, n_fsdp):
            value = value + over_fsdp[place]
        vectors_out[...] = value
        while any(square[1] < 5 for square in squares):
            pump()
        for c in range(n_chunks):
            token_store(c).wait()
            output_store(c).wait()

    pl.run_scoped(
        ends_of,
        pltpu.VMEM((rows, width), FLOAT),
        pltpu.VMEM((rows, width), HALF),
        pltpu.VMEM((rows, width), HALF),
    )
    for square in squares:
        square[0].settle()
    for square in stores:
        square.store().wait()

    @pl.loop(0, 2 * n_chunks)
    def _(job):
        line.settle(job)
        line.release(job)


def run_tail(small, large, n_fsdp, n_ctx, n_tp):
    grad_gated, w_down, tokens = large[2], large[4], large[11]
    n_seq, length, chan = grad_gated.shape
    rows, width = tokens.shape
    units = w_down.shape[0]
    piece = width // PIECES
    size = 2 * width + 2 * chan
    depth = width // 2
    spread = width if n_fsdp != 2 else depth
    vmem = pl.BlockSpec(memory_space=pltpu.VMEM)
    hbm = pl.BlockSpec(memory_space=pl.ANY)
    slots = pltpu.VMEM((2 * n_seq, PIECES, length, piece), HALF)
    sems = pltpu.SemaphoreType.DMA((2 * n_seq, PIECES))
    n_in, n_out = depth // TILE, chan // TILE
    n_squares = n_in + n_out + len(bands(units, TILE))
    wide = max(3 * chan, depth)

    def tiles(*shape):
        return [
            pltpu.VMEM((*shape[:-2], shape[-2] // cut, shape[-1]), HALF) for cut in (1, 2, 4)
        ]

    return pl.pallas_call(
        functools.partial(tail, n_fsdp, n_ctx, n_tp),
        name="tail",
        out_shape=(
            jax.ShapeDtypeStruct((rows, width), HALF),
            jax.ShapeDtypeStruct((rows, width), HALF),
            jax.ShapeDtypeStruct((1, size), FLOAT),
            jax.ShapeDtypeStruct((spread, 3 * chan), HALF),
            jax.ShapeDtypeStruct((chan, spread), HALF),
            jax.ShapeDtypeStruct((units, spread), HALF),
        ),
        in_specs=[vmem] * len(small) + [hbm] * len(large),
        out_specs=[hbm, hbm, vmem, hbm, hbm, hbm],
        scratch_shapes=[
            pltpu.VMEM((n_seq, length, 3 * chan), HALF),
            slots,
            pltpu.VMEM((2 * n_seq, PIECES, length, piece), HALF),
            slots,
            pltpu.VMEM((2, TILE, wide), HALF),
            pltpu.VMEM((2, TILE, wide), HALF),
            *tiles(n_in, TILE, 3 * chan),
            *tiles(n_out, TILE, depth),
            *tiles(units, depth),
            pltpu.VMEM((8, width), FLOAT),
            pltpu.VMEM((n_ctx, 2, n_seq, chan), FLOAT),
            pltpu.VMEM((n_tp, n_seq, length), FLOAT),
            pltpu.VMEM((n_ctx, 1, size), FLOAT),
            pltpu.VMEM((n_fsdp, 1, size), FLOAT),
            pltpu.VMEM((n_seq, length, chan), FLOAT),
            pltpu.SemaphoreType.DMA((6,)),
            pltpu.SemaphoreType.DMA((2, n_seq)),
            pltpu.SemaphoreType.DMA((n_ctx,)),
            pltpu.SemaphoreType.DMA((n_ctx,)),
            pltpu.SemaphoreType.DMA((n_tp,)),
            pltpu.SemaphoreType.DMA((n_tp,)),
            pltpu.SemaphoreType.DMA((n_ctx,)),
            pltpu.SemaphoreType.DMA((n_ctx,)),
            pltpu.SemaphoreType.DMA((n_fsdp,)),
            pltpu.SemaphoreType.DMA((n_fsdp,)),
            pltpu.SemaphoreType.DMA((2,)),
            pltpu.SemaphoreType.DMA((2,)),
            pltpu.SemaphoreType.DMA((2,)),
            pltpu.SemaphoreType.DMA((n_squares, 4)),
            pltpu.SemaphoreType.DMA((n_squares, 4)),
            pltpu.SemaphoreType.DMA((n_squares,)),
        ]
        + [sems] * 4,
        compiler_params=pltpu.CompilerParams(
            collective_id=3, has_side_effects=True, vmem_limit_bytes=63 * MIB
        ),
        cost_estimate=pl.CostEstimate(
            flops=10 * rows * width * units, bytes_accessed=700 * MIB, transcendentals=0
        ),
    )(*small, *large)


def widen_outputs(
    w_in, w_out, w_gate, w_up, w_down, tokens, vectors,
    w_in_out, w_out_out, w_glu_out, w_down_out, tokens_out, one_out, two_out, gate_out, lower_out,
):
    chan = w_in_out.shape[2]
    for gate in range(3):
        w_in_out[gate] = w_in[:, gate * chan : (gate + 1) * chan].astype(FLOAT)
    w_out_out[...] = w_out[...].astype(FLOAT)
    w_glu_out[:, 0, :] = w_gate[...].astype(FLOAT)
    w_glu_out[:, 1, :] = w_up[...].astype(FLOAT)
    w_down_out[...] = w_down[...].astype(FLOAT)
    tokens_out[...] = tokens[...].astype(FLOAT)

    @pl.when(pl.program_id(0) == 0)
    def _():
        part = one_out.shape[1]
        width = (vectors.shape[1] - 2 * chan) // 2
        begin = lax.axis_index("fsdp") * part
        one_out[...] = vectors[:, span(begin, part, part)]
        two_out[...] = vectors[:, span(width + begin, part, part)]
        gate_out[...] = vectors[:, 2 * width : 2 * width + chan]
        lower_out[...] = vectors[:, 2 * width + chan :]


def run_widen_outputs(w_in, w_out, w_gate, w_up, w_down, tokens, vectors):
    steps = 8
    arrays = (w_in, w_out, w_gate, w_up, w_down, tokens)

    def spec(array):
        return pl.BlockSpec((array.shape[0] // steps, array.shape[1]), lambda i: (i, 0))

    depth, wide = w_in.shape
    chan = wide // 3
    units = w_gate.shape[1]
    whole = pl.BlockSpec(vectors.shape, lambda i: (0, 0))
    thin = [jax.ShapeDtypeStruct((1, size), FLOAT) for size in (depth, depth, chan, chan)]
    shapes = [
        jax.ShapeDtypeStruct((3, depth, chan), FLOAT),
        jax.ShapeDtypeStruct(w_out.shape, FLOAT),
        jax.ShapeDtypeStruct((depth, 2, units), FLOAT),
        jax.ShapeDtypeStruct(w_down.shape, FLOAT),
        jax.ShapeDtypeStruct(tokens.shape, FLOAT),
    ]
    in_specs = [spec(array) for array in arrays] + [whole]
    specs = [
        pl.BlockSpec((3, depth // steps, chan), lambda i: (0, i, 0)),
        spec(w_out),
        pl.BlockSpec((depth // steps, 2, units), lambda i: (i, 0, 0)),
        spec(w_down),
        spec(tokens),
    ] + [pl.BlockSpec(shape.shape, lambda i: (0, 0)) for shape in thin]
    return pl.pallas_call(
        widen_outputs,
        name="widen_outputs",
        grid=(steps,),
        out_shape=shapes + thin,
        in_specs=in_specs,
        out_specs=specs,
        compiler_params=pltpu.CompilerParams(vmem_limit_bytes=62 * MIB),
    )(*arrays, vectors)


def head(
    n_fsdp, n_ctx, n_tp,
    gains, same, first, last, gate_gain, lower, w_in, tokens,
    gated, scale, carry_out, keep, gain_one, gain_two, proj_out, state_out, normed_out, w_out,
    staged, w_all, normed, proj, state, local, reach, ends, squares, gain_slots, edge_slots,
    load_sem, store_sem, half_send, half_recv, ctx_send, ctx_recv, tp_send, tp_recv,
    gain_send, gain_recv, edge_send, edge_recv,
):
    n_seq, length, chan = state.shape
    rows = n_seq * length
    depth = w_in.shape[1]
    width = w_all.shape[0]
    greet(others("ctx", n_ctx) + others("tp", n_tp) + others("fsdp", n_fsdp))
    core = lax.axis_index("fsdp")
    gate_cols = [slice(gate * chan, (gate + 1) * chan) for gate in range(3)]
    x_load = pltpu.make_async_copy(tokens, normed, load_sem.at[3])
    if n_fsdp == 2:
        w_loads = [
            pltpu.make_async_copy(w_in.at[gate], staged.at[gate], load_sem.at[gate])
            for gate in range(3)
        ]
    else:
        w_loads = [
            pltpu.make_async_copy(w_in.at[gate], w_all.at[:, gate_cols[gate]], load_sem.at[gate])
            for gate in range(3)
        ]
    for load in w_loads + [x_load]:
        load.start()
    gain_slots[core] = gains[...].astype(HALF).astype(FLOAT)
    edge_slots[lax.axis_index("ctx")] = last[...]
    small = shares(gain_slots, "fsdp", n_fsdp, gain_send, gain_recv)
    small += shares(edge_slots, "ctx", n_ctx, edge_send, edge_recv)
    for copy in small:
        copy.start()
    halves_sent = []
    if n_fsdp == 2:
        own = span(core * depth, depth, depth)
        for gate in range(3):
            w_loads[gate].wait()

            def cast(at):
                to = span(core * depth + at.start, at.size, at.size)
                w_all[to, gate_cols[gate]] = staged[gate, at, :].astype(HALF)

            row_blocks(depth, 32, cast)
            place = w_all.at[own, gate_cols[gate]]
            copy = pltpu.make_async_remote_copy(
                src_ref=place,
                dst_ref=place,
                send_sem=half_send.at[gate],
                recv_sem=half_recv.at[gate],
                device_id={"fsdp": 1 - core},
                device_id_type=MESH,
            )
            copy.start()
            halves_sent.append(copy)
    for copy in small:
        copy.wait()
    part = gains.shape[1]
    for place in range(n_fsdp):
        cols = slice(place * part, (place + 1) * part)
        gain_one[:, cols] = gain_slots[place, :1, :]
        gain_two[:, cols] = gain_slots[place, 1:2, :]
    here = lax.axis_index("ctx")
    keep[...] = same[...]
    before = edge_slots[0]
    for place in range(1, n_ctx):
        before = jnp.where(place == here - 1, edge_slots[place], before)
    joins = jnp.where((before == first[...]) & (here > 0), 1.0, 0.0)
    keep[:, :1, :] = joins[:, :1].reshape(n_seq, 1, 1)
    x_load.wait()

    def norm(at):
        value = normed[at, :].astype(FLOAT)
        normed[at, :] = (value * rms_scale(value) * gain_one[...]).astype(HALF)

    row_blocks(rows, 16, norm)
    normed_store = pltpu.make_async_copy(normed, normed_out, store_sem.at[0])
    normed_store.start()
    flat = proj.reshape(3, rows, chan)
    band = rows
    if n_fsdp == 2:
        for gate in range(3):
            @pl.loop(0, rows // band)
            def _(index):
                at = span(index * band, band, band)
                cols = span(core * depth, depth, depth)
                flat[gate, at, :] = dot(normed[at, cols], w_all[own, gate_cols[gate]])

        for gate in range(3):
            halves_sent[gate].wait_recv()

            @pl.loop(0, rows // band)
            def _(index):
                at = span(index * band, band, band)
                other = span((1 - core) * depth, depth, depth)
                flat[gate, at, :] += dot(normed[at, other], w_all[other, gate_cols[gate]])
    else:
        for gate in range(3):
            w_loads[gate].wait()

            @pl.loop(0, rows // band)
            def _(index):
                at = span(index * band, band, band)
                flat[gate, at, :] = dot(normed[at, :], w_all[:, gate_cols[gate]])

    stores = [
        pltpu.make_async_copy(proj, proj_out, store_sem.at[1]),
        pltpu.make_async_copy(w_all, w_out, store_sem.at[2]),
    ]
    for store in stores:
        store.start()
    low = lower[...].reshape(1, 1, chan)
    row = lax.broadcasted_iota(jnp.int32, (n_seq, GROUP, chan), 1)

    def step(index, carry):
        prod, total = carry
        rows = pl.ds(pl.multiple_of(index * GROUP, GROUP), GROUP)
        inp = proj[0, :, rows, :]
        decay = low + (1.0 - low) * jax.nn.sigmoid(proj[1, :, rows, :])
        add = inp * jax.nn.sigmoid(inp) * (1.0 - decay)
        mult = decay * keep[:, rows, :]
        for hop in (1, 2, 4):
            inside = row >= hop
            add = jnp.where(inside, mult * pltpu.roll(add, hop, 1) + add, add)
            mult = jnp.where(inside, mult * pltpu.roll(mult, hop, 1), mult)
        add = add + mult * total
        mult = mult * prod
        local[:, rows, :] = add
        reach[:, rows, :] = mult
        return mult[:, GROUP - 1 :, :], add[:, GROUP - 1 :, :]

    start = (jnp.ones((n_seq, 1, chan), FLOAT), jnp.zeros((n_seq, 1, chan), FLOAT))
    prod, total = lax.fori_loop(0, length // GROUP, step, start)
    ends[here, 0] = prod.reshape(n_seq, chan)
    ends[here, 1] = total.reshape(n_seq, chan)
    share(ends, "ctx", n_ctx, ctx_send, ctx_recv)
    carry = jnp.zeros((n_seq, chan), FLOAT)
    for place in range(n_ctx - 1):
        carry = jnp.where(place < here, ends[place, 1] + ends[place, 0] * carry, carry)
    carry_out[...] = carry
    mine = lax.axis_index("tp")
    for seq in range(n_seq):
        for start in range(0, length, BLOCK):
            rows = slice(start, start + BLOCK)
            value = local[seq, rows, :] + reach[seq, rows, :] * carry[seq : seq + 1]
            state[seq, rows, :] = value
            squares[mine, seq : seq + 1, rows] = lane_sums(value * value)
    state_store = pltpu.make_async_copy(state, state_out, store_sem.at[3])
    state_store.start()
    share(squares, "tp", n_tp, tp_send, tp_recv)
    total = squares[0]
    for place in range(1, n_tp):
        total = total + squares[place]
    rate = lax.rsqrt(total / width + EPS)
    scale[...] = rate
    for seq in range(n_seq):
        for start in range(0, length, BLOCK):
            rows = slice(start, start + BLOCK)
            gate = proj[2, seq, rows, :]
            unit = state[seq, rows, :] * widen(columns(rate[seq : seq + 1, rows]), chan)
            swish = gate * jax.nn.sigmoid(gate)
            gated[seq, rows, :] = (unit * gate_gain[...] * swish).astype(HALF)
    for copy in halves_sent:
        copy.wait_send()
    for store in stores + [normed_store, state_store]:
        store.wait()


def run_head(gains, same, first, last, gate_gain, lower, w_in, tokens, n_fsdp, n_ctx, n_tp):
    n_seq, length, _ = same.shape
    rows, width = tokens.shape
    chan = w_in.shape[2]
    shape = (n_seq, length, chan)
    vmem = pl.BlockSpec(memory_space=pltpu.VMEM)
    hbm = pl.BlockSpec(memory_space=pl.ANY)
    staged = w_in.shape if n_fsdp == 2 else (3, 8, BLOCK)
    dma = pltpu.SemaphoreType.DMA
    return pl.pallas_call(
        functools.partial(head, n_fsdp, n_ctx, n_tp),
        name="head",
        out_shape=(
            jax.ShapeDtypeStruct(shape, HALF),
            jax.ShapeDtypeStruct((n_seq, length), FLOAT),
            jax.ShapeDtypeStruct((n_seq, chan), FLOAT),
            jax.ShapeDtypeStruct((n_seq, length, 1), FLOAT),
            jax.ShapeDtypeStruct((1, width), FLOAT),
            jax.ShapeDtypeStruct((1, width), FLOAT),
            jax.ShapeDtypeStruct((3, *shape), FLOAT),
            jax.ShapeDtypeStruct(shape, FLOAT),
            jax.ShapeDtypeStruct((rows, width), HALF),
            jax.ShapeDtypeStruct((width, 3 * chan), HALF),
        ),
        in_specs=[vmem] * 6 + [hbm] * 2,
        out_specs=[vmem] * 6 + [hbm] * 4,
        scratch_shapes=[
            pltpu.VMEM(staged, FLOAT),
            pltpu.VMEM((width, 3 * chan), HALF),
            pltpu.VMEM((rows, width), HALF),
            pltpu.VMEM((3, *shape), FLOAT),
            pltpu.VMEM(shape, FLOAT),
            pltpu.VMEM(shape, FLOAT),
            pltpu.VMEM(shape, FLOAT),
            pltpu.VMEM((n_ctx, 2, n_seq, chan), FLOAT),
            pltpu.VMEM((n_tp, n_seq, length), FLOAT),
            pltpu.VMEM((n_fsdp, *gains.shape), FLOAT),
            pltpu.VMEM((n_ctx, *last.shape), FLOAT),
            dma((4,)), dma((4,)), dma((3,)), dma((3,)), dma((n_ctx,)), dma((n_ctx,)),
            dma((n_tp,)), dma((n_tp,)), dma((n_fsdp,)), dma((n_fsdp,)), dma((n_ctx,)), dma((n_ctx,)),
        ],
        compiler_params=pltpu.CompilerParams(
            collective_id=0, has_side_effects=True, vmem_limit_bytes=63 * MIB
        ),
    )(gains, same, first, last, gate_gain, lower, w_in, tokens)


def gather_fsdp(part, dim):
    return lax.all_gather(part, "fsdp", axis=dim, tiled=True)


def local(
    sizes,
    tokens, segment_ids, w_in, w_out, w_glu, w_down, gain_one, gain_two, gate_gain, lower, cotangent,
):
    n_fsdp, n_ctx, n_tp = sizes
    n_seq, length, width = tokens.shape
    rows = n_seq * length
    chan = w_in.shape[2]
    x_half = tokens.reshape(rows, width)
    parts = (w_out.astype(HALF), w_glu[:, 0].astype(HALF), w_glu[:, 1].astype(HALF), w_down.astype(HALF))
    if n_fsdp != 2:
        parts = tuple(gather_fsdp(part, dim) for part, dim in zip(parts, (1, 0, 0, 1)))
        w_in = gather_fsdp(w_in.astype(HALF), 1)
    gain_gate = gate_gain[None]
    low = lower[None]
    seg = segment_ids.astype(FLOAT)
    same = jnp.pad((seg[:, 1:] == seg[:, :-1]).astype(FLOAT), ((0, 0), (1, 0)))[..., None]
    first, last = (jnp.broadcast_to(seg[:, at], (n_seq, BLOCK)) for at in (slice(0, 1), slice(-1, None)))
    gated, gate_scale, carry, keep, gain_a, gain_b, proj, state, normed, w_in_all = run_head(
        jnp.stack([gain_one, gain_two]), same, first, last, gain_gate, low, w_in, x_half,
        n_fsdp, n_ctx, n_tp,
    )
    gated = gated.reshape(rows, chan)
    grad_y_half = cotangent.reshape(rows, width)
    (
        mixed, _, act, _, grad_resid, grad_mixed, grad_gated, grad_w_gate, grad_w_up, w_down_all,
        grad_gain_two,
    ) = run_middle(gated, x_half, grad_y_half, gain_b, parts, n_fsdp, n_ctx, length)
    if n_fsdp == 2:
        grad_w_up = lax.psum(grad_w_up, "ctx")
    grad_tokens, output, vectors, grad_w_in, grad_w_out, grad_w_down = run_tail(
        (keep, gain_gate, low, gate_scale, carry, gain_a, grad_gain_two),
        (
            proj, state, grad_gated.reshape(n_seq, length, chan), w_in_all, w_down_all, act, normed,
            grad_mixed, gated, grad_y_half, grad_resid, x_half, mixed,
        ),
        n_fsdp, n_ctx, n_tp,
    )
    grads = (grad_w_in, grad_w_out, grad_w_gate, grad_w_up, grad_w_down)
    if n_fsdp != 2:
        grads = tuple(
            lax.psum(lax.psum_scatter(value, "fsdp", scatter_dimension=dim, tiled=True), "ctx")
            for value, dim in zip(grads, (0, 1, 0, 0, 1))
        )
    results = run_widen_outputs(*grads, grad_tokens, vectors)
    grad_w_in, grad_w_out, grad_w_glu, grad_w_down, grad_tokens = results[:5]
    return (
        output.reshape(n_seq, length, width),
        grad_tokens.reshape(n_seq, length, width),
        grad_w_in,
        grad_w_out,
        grad_w_glu,
        grad_w_down,
        *(vector[0] for vector in results[5:]),
    )


def solution(mesh):
    sizes = tuple(mesh.shape[axis] for axis in ("fsdp", "ctx", "tp"))
    return jax.shard_map(
        functools.partial(local, sizes),
        mesh=mesh,
        in_specs=(
            P("fsdp", "ctx", None),
            P("fsdp", "ctx"),
            P(None, "fsdp", "tp"),
            P("tp", "fsdp"),
            P("fsdp", None, "tp"),
            P("tp", "fsdp"),
            P("fsdp"),
            P("fsdp"),
            P("tp"),
            P("tp"),
            P("fsdp", "ctx", None),
        ),
        out_specs=(
            P("fsdp", "ctx", None),
            P("fsdp", "ctx", None),
            P(None, "fsdp", "tp"),
            P("tp", "fsdp"),
            P("fsdp", None, "tp"),
            P("tp", "fsdp"),
            P("fsdp"),
            P("fsdp"),
            P("tp"),
            P("tp"),
        ),
        check_vma=False,
    )
```

```python
import functools

import jax
import jax.numpy as jnp
from jax import lax
from jax.experimental import pallas as pl
from jax.experimental.pallas import tpu as pltpu
from jax.sharding import PartitionSpec as P

EPS = 1e-06
FLOAT = jnp.float32
HALF = jnp.bfloat16
MESH = pl.DeviceIdType.MESH
GROUP = 8
BLOCK = 128
MIB = 1 << 20


def rms_scale(values):
    return lax.rsqrt(jnp.mean(values * values, -1, keepdims=True) + EPS)


def silu_slope(values):
    sig = jax.nn.sigmoid(values)
    return sig * (1.0 + values * (1.0 - sig))


def greet(peers):
    barrier = pltpu.get_barrier_semaphore()
    for peer in peers:
        pl.semaphore_signal(barrier, inc=1, device_id=peer, device_id_type=MESH)
    pl.semaphore_wait(barrier, len(peers))


def others(axis, count):
    mine = lax.axis_index(axis)
    return [{axis: lax.rem(mine + step, count)} for step in range(1, count)]


def shares(slots, axis, count, send, recv):
    mine = lax.axis_index(axis)
    return [
        pltpu.make_async_remote_copy(
            src_ref=slots.at[mine],
            dst_ref=slots.at[mine],
            send_sem=send.at[step],
            recv_sem=recv.at[step],
            device_id=peer,
            device_id_type=MESH,
        )
        for step, peer in enumerate(others(axis, count))
    ]


def share(slots, axis, count, send, recv):
    copies = shares(slots, axis, count, send, recv)
    for copy in copies:
        copy.start()
    for copy in copies:
        copy.wait()


def lane_sums(values):
    part = values[:, :BLOCK]
    for start in range(BLOCK, values.shape[1], BLOCK):
        part = part + values[:, start : start + BLOCK]
    return jnp.sum(part.T, 0, keepdims=True)


def columns(row):
    return jnp.broadcast_to(row, (BLOCK, BLOCK)).T


def widen(values, chan):
    return jnp.concatenate([values] * (chan // BLOCK), -1)


PIECES = 4
TILE = 256
WIDE = 512


def bands(count, size):
    return [(start, min(size, count - start)) for start in range(0, count, size)]


def dot(lhs, rhs):
    return jnp.dot(lhs, rhs, preferred_element_type=FLOAT)


def dot_nt(lhs, rhs):
    return lax.dot_general(lhs, rhs, (((1,), (1,)), ((), ())), preferred_element_type=FLOAT)


class Line:
    def __init__(self, held, cross, total, sems):
        self.held, self.cross, self.total, self.sems = held, cross, total, sems
        place = lax.axis_index("tp")
        self.inner = (place == 1) | (place == 2)
        self.side = place + 1 - 2 * lax.rem(place, 2)
        self.facing = 3 - place

    def slot(self, job, ref):
        slots = ref.shape[0]
        if slots == self.total.shape[0]:
            return job
        return job % slots if isinstance(job, int) else lax.rem(job, slots)

    def copy(self, source, target, send, recv, place):
        return pltpu.make_async_remote_copy(
            src_ref=source,
            dst_ref=target,
            send_sem=send,
            recv_sem=recv,
            device_id={"tp": place},
            device_id_type=MESH,
        )

    def inward(self, job, q):
        send, recv, _, _ = self.sems
        return self.copy(
            self.held.at[self.slot(job, self.held), q], self.total.at[job, q],
            send.at[job, q], recv.at[job, q], self.side,
        )

    def outward(self, job, q):
        send, recv, _, _ = self.sems
        return self.copy(
            self.total.at[job, q], self.total.at[job, q],
            send.at[job, q], recv.at[job, q], self.side,
        )

    def across(self, job, q):
        _, _, send, recv = self.sems
        return self.copy(
            self.held.at[self.slot(job, self.held), q], self.cross.at[self.slot(job, self.cross), q],
            send.at[job, q], recv.at[job, q], self.facing,
        )

    def offer(self, job, q):
        @pl.when(jnp.logical_not(self.inner))
        def _():
            self.inward(job, q).start()

    def forward(self, job, q):
        slot = self.slot(job, self.held)

        @pl.when(self.inner)
        def _():
            self.inward(job, q).wait_recv()
            self.held[slot, q] = self.held[slot, q] + self.total[job, q]
            self.across(job, q).start()

    def close(self, job, q):
        slot, cross_slot = self.slot(job, self.held), self.slot(job, self.cross)

        @pl.when(self.inner)
        def _():
            self.across(job, q).wait_recv()
            self.total[job, q] = self.held[slot, q] + self.cross[cross_slot, q]
            self.outward(job, q).start()

    def tick(self, base, step):
        if step > 0:
            self.close(base, step - 1)
        if step < PIECES:
            ahead = step + 1
            self.forward(base + ahead // PIECES, ahead % PIECES)

    def arrive(self, job):
        @pl.when(jnp.logical_not(self.inner))
        def _():
            @pl.loop(0, PIECES)
            def _(q):
                self.outward(job, q).wait_recv()

    def release(self, job):
        @pl.when(self.inner)
        def _():
            @pl.loop(0, PIECES)
            def _(q):
                self.across(job, q).wait_send()

        @pl.when(jnp.logical_not(self.inner))
        def _():
            @pl.loop(0, PIECES)
            def _(q):
                self.inward(job, q).wait_send()

    def settle(self, job):
        @pl.when(self.inner)
        def _():
            @pl.loop(0, PIECES)
            def _(q):
                self.outward(job, q).wait_send()


def span(start, size, unit):
    return pl.ds(pl.multiple_of(start, unit), size)


def row_blocks(count, size, body):
    @pl.loop(0, count // size)
    def _(index):
        body(pl.ds(pl.multiple_of(index * size, size), size))


def line_peers():
    place = lax.axis_index("tp")
    return [{"tp": place + 1 - 2 * lax.rem(place, 2)}, {"tp": 3 - place}]


def joined(ref, c, rows):
    return jnp.concatenate([ref[c, q, rows, :].astype(FLOAT) for q in range(PIECES)], -1)


def add_to(target, extra, rows):
    target[rows, :] = target[rows, :] + extra[rows, :]


def halves(n_fsdp, store_sem, send_sem, recv_sem, spare, inbox):
    mine = lax.axis_index("fsdp")
    pending = {}

    def send(index, view):
        slot = index % 2
        return pltpu.make_async_remote_copy(
            src_ref=view(spare.at[slot]),
            dst_ref=view(inbox.at[slot]),
            send_sem=send_sem.at[slot],
            recv_sem=recv_sem.at[slot],
            device_id={"fsdp": 1 - mine},
            device_id_type=MESH,
        )

    def item(index, view, compute_other, compute_own, other_place, target):
        slot = index % 2
        if index - 2 in pending:
            pending.pop(index - 2)()
        compute_other(view(spare.at[slot]))
        if n_fsdp == 2:
            copy = send(index, view)
            copy.start()
            pending[index] = lambda: send(index, view).wait_send()
        else:
            def store():
                return pltpu.make_async_copy(view(spare.at[slot]), other_place(), store_sem.at[slot])

            store().start()
            pending[index] = lambda: store().wait()
        compute_own(target)
        if n_fsdp == 2:
            send(index, view).wait_recv()
            extra = view(inbox.at[slot])
            row_blocks(target.shape[0], 32, lambda rows: add_to(target, extra, rows))

    def finish():
        for wait in pending.values():
            wait()

    return item, finish


class Square:
    def __init__(self, index, buffers, at, place, send, recv, store_sem):
        self.buffers, self.at, self.place_of = buffers, at, place
        self.send, self.recv, self.index, self.store_sem = send, recv, index, store_sem

    @property
    def tile(self):
        return self.buffers[0].at[self.at[0]]

    @property
    def half(self):
        return self.buffers[1].at[self.at[1]]

    @property
    def quarter(self):
        return self.buffers[2].at[self.at[2]]

    def geometry(self):
        here = lax.axis_index("ctx")
        low, high = lax.rem(here, 2), here // 2
        near, far = here + 1 - 2 * low, here + 2 - 4 * high
        bits = (low, high) if self.index % 2 == 0 else (high, low)
        peers = (near, far) if self.index % 2 == 0 else (far, near)
        wide, thin = self.half.shape[0], self.quarter.shape[0]
        begin = bits[0] * wide
        return (
            peers,
            span(begin, wide, wide),
            span((1 - bits[0]) * wide, wide, wide),
            span(begin + bits[1] * thin, thin, thin),
            span(begin + (1 - bits[1]) * thin, thin, thin),
        )

    def round(self, number):
        peers, mine, yours, my_part, your_part = self.geometry()
        source, target, peer = (
            (self.tile.at[yours], self.half, 0),
            (self.tile.at[your_part], self.quarter, 1),
            (self.tile.at[my_part], self.place_of().at[my_part], 1),
            (self.place_of().at[mine], self.place_of().at[mine], 0),
        )[number]
        return pltpu.make_async_remote_copy(
            src_ref=source,
            dst_ref=target,
            send_sem=self.send.at[self.index, number],
            recv_sem=self.recv.at[self.index, number],
            device_id={"ctx": peers[peer]},
            device_id_type=MESH,
        )

    def add(self, part, extra):
        target = self.tile.at[part]
        row_blocks(extra.shape[0], 32, lambda rows: add_to(target, extra, rows))

    def store(self):
        return pltpu.make_async_copy(self.tile, self.place_of(), self.store_sem.at[self.index])

    def store_part(self):
        part = self.geometry()[3]
        return pltpu.make_async_copy(
            self.tile.at[part], self.place_of().at[part], self.store_sem.at[self.index]
        )

    def advance(self, number):
        if number > 0:
            self.round(number - 1).wait_recv()
        if number == 1:
            self.add(self.geometry()[1], self.half)
        if number == 2:
            self.add(self.geometry()[3], self.quarter)
            self.store_part().start()
        if number == 3:
            self.store_part().wait()
        if number < 4:
            self.round(number).start()

    def settle(self):
        for number in range(4):
            self.round(number).wait_send()


def fill(target, left, right, first):
    for start, size in bands(target.shape[1], WIDE):
        cols = pl.ds(pl.multiple_of(first + start, BLOCK), size)
        target[:, start : start + size] = dot(left, right[:, cols]).astype(HALF)


def middle(
    n_fsdp, n_ctx, CHUNK,
    gated, tokens, cotangent, gain, wo_part, wg_part, wu_part, wd_part,
    mixed_out, normed_out, act_out, grad_glu_out, grad_resid_out, grad_mixed_out,
    grad_gated_out, w_gate_out, w_up_out, w_down_out, grad_gain_out,
    wo, wg, wu, wd, x_all, dy_all, held, crossed, total, normed, act, grad_glu,
    grad_resid, grad_mixed, grad_gated, gain_total, spare, inbox, half, quarter,
    square_send, square_recv, square_store, weight_sem, weight_send, weight_recv, again_sem,
    own_sem, stage_sem, glu_send, glu_recv, down_send, down_recv,
    load_sem, store_sem, *line_sems,
):
    n_chunks, _, _, piece = held.shape
    units = wd.shape[0]
    width = wd.shape[1]
    peers = line_peers() + others("ctx", n_ctx)
    if n_fsdp == 2:
        peers.append({"fsdp": 1 - lax.axis_index("fsdp")})
    greet(peers)
    local_parts = [(wo_part, wo)]
    if n_fsdp != 2:
        local_parts += [(wg_part, wg), (wu_part, wu), (wd_part, wd)]
    ready = [
        pltpu.make_async_copy(part, whole, own_sem.at[index])
        for index, (part, whole) in enumerate(local_parts)
    ]
    for copy in ready:
        copy.start()
    core = lax.axis_index("fsdp")
    n_bands = units // BLOCK

    def to_sibling(place, send, recv):
        return pltpu.make_async_remote_copy(
            src_ref=place,
            dst_ref=place,
            send_sem=send,
            recv_sem=recv,
            device_id={"fsdp": 1 - core},
            device_id_type=MESH,
        )

    def glu_copies(number):
        part, whole = ((wg_part, wg), (wu_part, wu))[number]
        at = span(core * (width // 2), width // 2, width // 2)
        far = pltpu.make_async_remote_copy(
            src_ref=part,
            dst_ref=whole.at[at],
            send_sem=glu_send.at[number],
            recv_sem=glu_recv.at[number],
            device_id={"fsdp": 1 - core},
            device_id_type=MESH,
        )
        return far, pltpu.make_async_copy(part, whole.at[at], own_sem.at[1 + number])

    def down_stage(index):
        return grad_resid.at[span(lax.rem(index, 2) * BLOCK, BLOCK, BLOCK), : width // 2]

    def down_load(index):
        return pltpu.make_async_copy(
            wd_part.at[span(index * BLOCK, BLOCK, BLOCK)], down_stage(index),
            stage_sem.at[lax.rem(index, 2)],
        )

    def down_copy(index):
        cols = span(core * (width // 2), width // 2, width // 2)
        place = wd.at[span(index * BLOCK, BLOCK, BLOCK), cols]
        return to_sibling(place, down_send.at[index], down_recv.at[index])

    def down_band(index):
        down_load(index).wait()
        cols = span(core * (width // 2), width // 2, width // 2)
        wd[span(index * BLOCK, BLOCK, BLOCK), cols] = down_stage(index)[...].astype(HALF)

        @pl.when(index + 2 < n_bands)
        def _():
            down_load(index + 2).start()

        down_copy(index).start()

    if n_fsdp == 2:
        for first_load in (*glu_copies(0), *glu_copies(1), down_load(0), down_load(1)):
            first_load.start()
    loads = [
        pltpu.make_async_copy(tokens, x_all, load_sem.at[0]),
        pltpu.make_async_copy(cotangent, dy_all, load_sem.at[1]),
    ]
    for load in loads:
        load.start()
    line = Line(held, crossed, total, line_sems)

    def chunk_rows(c):
        return pl.ds(pl.multiple_of(c * CHUNK, CHUNK), CHUNK)

    def stores(c, wanted=None):
        rows = chunk_rows(c)
        pairs = [
            (normed, normed_out.at[rows]),
            (act, act_out.at[rows]),
            (grad_glu.at[0], grad_glu_out.at[0, rows]),
            (grad_glu.at[1], grad_glu_out.at[1, rows]),
            (grad_resid, grad_resid_out.at[rows]),
            (grad_mixed, grad_mixed_out.at[rows]),
            (grad_gated, grad_gated_out.at[rows]),
        ]
        pairs += [
            (total.at[c, q], mixed_out.at[rows, pl.ds(q * piece, piece)]) for q in range(PIECES)
        ]
        return [
            pltpu.make_async_copy(source, target, store_sem.at[index])
            for index, (source, target) in enumerate(pairs)
            if wanted is None or index in wanted
        ]

    FORWARD = (0, 1, 2, 3, 7, 8, 9, 10)
    BACKWARD = (4, 5, 6)

    ready[0].wait()

    @pl.loop(0, n_chunks)
    def _(c):
        lhs = gated[chunk_rows(c), :]

        @pl.loop(0, PIECES)
        def _(q):
            cols = pl.ds(pl.multiple_of(q * piece, piece), piece)
            held[c, q] = dot(lhs, wo[:, cols]).astype(HALF)
            line.offer(c, q)

    for load in loads:
        load.wait()
    def cast_down(part):
        pl.loop(part * n_bands // 4, (part + 1) * n_bands // 4)(down_band)

    for step in range(PIECES + 2):
        if n_fsdp == 2 and step < 4:
            cast_down(step)
        if step == 0:
            line.forward(0, 0)
        else:
            line.tick(0, step - 1)

    w_down_store = pltpu.make_async_copy(wd, w_down_out, again_sem.at[3])

    def weights_here():
        for copy in ready[1:]:
            copy.wait()
        if n_fsdp == 2:
            for copy in (*glu_copies(0), *glu_copies(1)):
                copy.wait()

            @pl.loop(0, n_bands)
            def _(index):
                down_copy(index).wait()

        w_down_store.start()

    @pl.loop(0, n_chunks)
    def _(c):
        line.arrive(c)
        line.tick(c + 1, 0)

        @pl.when(c > 0)
        def _():
            for store in stores(c - 1, FORWARD):
                store.wait()

        def norm(rows):
            at = pl.ds(pl.multiple_of(c * CHUNK + rows.start, 16), rows.size)
            resid = x_all[at, :].astype(FLOAT) + joined(total, c, rows)
            normed[rows, :] = (resid * rms_scale(resid) * gain[...]).astype(HALF)

        row_blocks(CHUNK, 16, norm)
        pl.when(c == 0)(weights_here)

        def unit(cols):
            glu_gate = dot(normed[...], wg[:, cols])
            glu_up = dot(normed[...], wu[:, cols])
            grad_act = dot_nt(dy_all[chunk_rows(c), :], wd[cols, :])
            sig = jax.nn.sigmoid(glu_gate)
            silu = glu_gate * sig
            act[:, cols] = (silu * glu_up).astype(HALF)
            slope = sig * (1.0 + glu_gate * (1.0 - sig))
            grad_glu[0, :, cols] = (grad_act * glu_up * slope).astype(HALF)
            grad_glu[1, :, cols] = (grad_act * silu).astype(HALF)

        for index, (start, size) in enumerate(bands(units, WIDE)):
            unit(slice(start, start + size))
            if index == 0:
                line.tick(c + 1, 1)
        line.tick(c + 1, 2)
        line.release(c)

        @pl.loop(0, PIECES)
        def _(q):
            @pl.when(q == PIECES // 2)
            def _():
                line.tick(c + 1, 3)

            at = pl.ds(pl.multiple_of(q * piece, piece), piece)
            value = dot_nt(grad_glu[0], wg[at, :]) + dot_nt(grad_glu[1], wu[at, :])
            held[c, q] = value.astype(HALF)
            line.offer(n_chunks + c, q)

        line.tick(c + 1, 4)

        for store in stores(c, FORWARD):
            store.start()

    for store in stores(n_chunks - 1, FORWARD):
        store.wait()
    rows = n_chunks * CHUNK
    w_down_store.wait()
    kept = [
        (grad_glu_out.at[0], wg.at[:rows]),
        (grad_glu_out.at[1], wu.at[:rows]),
        (normed_out, wd.at[:rows]),
    ]
    again = [
        pltpu.make_async_copy(source, target, again_sem.at[index])
        for index, (source, target) in enumerate(kept)
    ]
    for copy in again:
        copy.start()
    gain_total[...] = jnp.zeros_like(gain_total)
    item, finish = halves(n_fsdp, weight_sem, weight_send, weight_recv, spare, inbox)
    mine = lax.axis_index("fsdp") if n_fsdp == 2 else 1
    depth = width // 2
    whole = n_fsdp != 2
    per_part = depth // TILE
    squares, plain, turn = [], [], [0]

    def weight_item(index):
        if index >= 2 * per_part:
            return
        part, k = divmod(index, per_part)
        right = (wg, wu)[part].at[:rows]
        out = (w_gate_out, w_up_out)[part]

        def compute(side):
            at = pl.ds(pl.multiple_of(side * depth + k * TILE, TILE), TILE)
            return lambda target: fill(target, wd[:rows, at].T, right, 0)

        at = slice(k * TILE + whole * depth, (k + 1) * TILE + whole * depth)
        square = Square(
            index, ((wg, wu)[part], half, quarter),
            (slice(rows + k * TILE, rows + (k + 1) * TILE), k, k), lambda: out.at[at],
            square_send, square_recv, square_store,
        )
        item(
            index, lambda ref: ref, compute(1 - mine), compute(mine),
            lambda: out.at[k * TILE : (k + 1) * TILE], square.tile,
        )
        if whole or part == 1:
            square.store().start()
            plain.append(square)
        else:
            squares.append([square, 0, turn[0]])

    def pump():
        for square in squares:
            if square[1] < 5 and turn[0] >= square[2] + 3 * square[1]:
                square[0].advance(square[1])
                square[1] += 1
        turn[0] += 1

    def backward(c, between):
        line.arrive(n_chunks + c)
        if c > 0:
            for store in stores(c - 1, BACKWARD):
                store.wait()

        def norm_back(rows):
            at = pl.ds(pl.multiple_of(c * CHUNK + rows.start, 16), rows.size)
            resid = x_all[at, :].astype(FLOAT) + joined(total, c, rows)
            rate = rms_scale(resid)
            grad = joined(total, n_chunks + c, rows)
            by_gain = grad * (resid * rate)
            gain_total[...] += by_gain[:8] + by_gain[8:]
            inner = gain[...] * grad
            mean = jnp.mean(inner * resid, -1, keepdims=True)
            value = dy_all[at, :].astype(FLOAT) + rate * inner - resid * (rate * rate * rate * mean)
            grad_resid[rows, :] = value
            grad_mixed[rows, :] = value.astype(HALF)

        row_blocks(CHUNK, 16, norm_back)
        between()
        for start, size in bands(grad_gated.shape[1], WIDE):
            grad_gated[:, start : start + size] = dot_nt(
                grad_mixed[...], wo[start : start + size, :]
            )
        for store in stores(c, BACKWARD):
            store.start()

    for copy in again:
        copy.wait()
    count = 0
    for c in range(n_chunks):
        if c == n_chunks - 1:
            while count < 2 * per_part:
                weight_item(count)
                count += 1
        if c + 1 == n_chunks:
            backward(c, lambda: None)
            continue

        def between():
            line.tick(n_chunks + c + 1, 0)
            pump()

        backward(c, between)
        for step in range(1, PIECES + 1):
            weight_item(count)
            count += 1
            if c + 2 == n_chunks and step == PIECES - 1:
                line.close(2 * n_chunks - 1, step - 1)
            else:
                line.tick(n_chunks + c + 1, step)
            pump()
    while any(square[1] < 5 for square in squares):
        pump()
    finish()
    for square, _, _ in squares:
        square.settle()
    for square in plain:
        square.store().wait()

    grad_gain_out[...] = jnp.sum(gain_total[...], 0, keepdims=True)
    for store in stores(n_chunks - 1, BACKWARD):
        store.wait()

    @pl.loop(0, n_chunks)
    def _(c):
        line.settle(c)
        line.settle(n_chunks + c)
        line.release(n_chunks + c)


def run_middle(gated, tokens, cotangent, gain, parts, n_fsdp, n_ctx, length):
    rows, chan = gated.shape
    width = tokens.shape[1]
    units = parts[3].shape[0]
    n_chunks = rows // length
    piece = width // PIECES
    vmem = pl.BlockSpec(memory_space=pltpu.VMEM)
    hbm = pl.BlockSpec(memory_space=pl.ANY)
    sems = pltpu.SemaphoreType.DMA((2 * n_chunks, PIECES))
    return pl.pallas_call(
        functools.partial(middle, n_fsdp, n_ctx, length),
        name="middle",
        out_shape=(
            jax.ShapeDtypeStruct((rows, width), HALF),
            jax.ShapeDtypeStruct((rows, width), HALF),
            jax.ShapeDtypeStruct((rows, units), HALF),
            jax.ShapeDtypeStruct((2, rows, units), HALF),
            jax.ShapeDtypeStruct((rows, width), FLOAT),
            jax.ShapeDtypeStruct((rows, width), HALF),
            jax.ShapeDtypeStruct((rows, chan), FLOAT),
            jax.ShapeDtypeStruct((width if n_fsdp != 2 else width // 2, units), HALF),
            jax.ShapeDtypeStruct((width if n_fsdp != 2 else width // 2, units), HALF),
            jax.ShapeDtypeStruct((units, width), HALF),
            jax.ShapeDtypeStruct((1, width), FLOAT),
        ),
        in_specs=[vmem, hbm, hbm, vmem, hbm, hbm, hbm, hbm],
        out_specs=[hbm] * 10 + [vmem],
        scratch_shapes=[
            pltpu.VMEM((chan, width), HALF),
            pltpu.VMEM((width, units), HALF),
            pltpu.VMEM((width, units), HALF),
            pltpu.VMEM((units, width), HALF),
            pltpu.VMEM((rows, width), HALF),
            pltpu.VMEM((rows, width), HALF),
            pltpu.VMEM((n_chunks, PIECES, length, piece), HALF),
            pltpu.VMEM((n_chunks, PIECES, length, piece), HALF),
            pltpu.VMEM((2 * n_chunks, PIECES, length, piece), HALF),
            pltpu.VMEM((length, width), HALF),
            pltpu.VMEM((length, units), HALF),
            pltpu.VMEM((2, length, units), HALF),
            pltpu.VMEM((length, width), FLOAT),
            pltpu.VMEM((length, width), HALF),
            pltpu.VMEM((length, chan), FLOAT),
            pltpu.VMEM((8, width), FLOAT),
            pltpu.VMEM((2, TILE, units), HALF),
            pltpu.VMEM((2, TILE, units), HALF),
            pltpu.VMEM((width // 2 // TILE, TILE // 2, units), HALF),
            pltpu.VMEM((width // 2 // TILE, TILE // 4, units), HALF),
            pltpu.SemaphoreType.DMA((width // 2 // TILE, 4)),
            pltpu.SemaphoreType.DMA((width // 2 // TILE, 4)),
            pltpu.SemaphoreType.DMA((width // TILE,)),
            pltpu.SemaphoreType.DMA((4,)),
            pltpu.SemaphoreType.DMA((2,)),
            pltpu.SemaphoreType.DMA((2,)),
            pltpu.SemaphoreType.DMA((4,)),
            pltpu.SemaphoreType.DMA((4,)),
            pltpu.SemaphoreType.DMA((2,)),
            pltpu.SemaphoreType.DMA((2,)),
            pltpu.SemaphoreType.DMA((2,)),
            pltpu.SemaphoreType.DMA((units // BLOCK,)),
            pltpu.SemaphoreType.DMA((units // BLOCK,)),
            pltpu.SemaphoreType.DMA((2,)),
            pltpu.SemaphoreType.DMA((12,)),
        ]
        + [sems] * 4,
        compiler_params=pltpu.CompilerParams(
            collective_id=2, has_side_effects=True, vmem_limit_bytes=63 * MIB
        ),
        cost_estimate=pl.CostEstimate(
            flops=16 * rows * width * units, bytes_accessed=400 * MIB, transcendentals=0
        ),
    )(gated, tokens, cotangent, gain, *parts)


def scan_cross(gate_all, state, scale, gain, near, grad_proj, gain_out, cross):
    n_seq, length, chan = state.shape
    mine = lax.axis_index("tp")
    gain_total = jnp.zeros((8, chan), FLOAT)
    for seq in range(n_seq):
        for start in range(0, length, BLOCK):
            rows = slice(start, start + BLOCK)
            rate = columns(scale[seq : seq + 1, rows])
            gate = gate_all[seq, rows, :]
            sig = jax.nn.sigmoid(gate)
            swish = gate * sig
            value = state[seq, rows, :]
            into = near[seq, rows, :]
            by_unit = into * value * widen(rate, chan)
            slope = sig * (1.0 + gate * (1.0 - sig))
            grad_proj[seq, rows, 2 * chan :] = (by_unit * gain[...] * slope).astype(HALF)
            gain_total = gain_total + jnp.sum((by_unit * swish).reshape(-1, 8, chan), 0)
            grad_unit = into * swish * gain[...]
            near[seq, rows, :] = grad_unit
            cross[mine, seq : seq + 1, rows] = lane_sums(grad_unit * value)
    gain_out[...] = jnp.sum(gain_total, 0, keepdims=True)


def scan_back(
    n_ctx, n_tp, width, pump,
    proj, keep, lower, state, scale, carry_in, near,
    grad_proj, lower_out,
    reach, rate_wide, cross_wide, ends, cross, ctx_sems,
):
    n_seq, length, chan = state.shape
    low = lower[...].reshape(1, 1, chan)
    total = cross[0]
    for place in range(1, n_tp):
        total = total + cross[place]
    rate = scale[...]
    total = total * (rate * rate * rate) / width
    for seq in range(n_seq):
        for start in range(0, length, BLOCK):
            rows = slice(start, start + BLOCK)
            rate_wide[seq, rows, :] = columns(rate[seq : seq + 1, rows])
            cross_wide[seq, rows, :] = columns(total[seq : seq + 1, rows])

    row = lax.broadcasted_iota(jnp.int32, (n_seq, GROUP, chan), 1)

    def back(index, carry):
        prod, above = carry
        rows = pl.ds(pl.multiple_of((length // GROUP - 1 - index) * GROUP, GROUP), GROUP)
        decay = low + (1.0 - low) * jax.nn.sigmoid(proj[1, :, rows, :])
        mult = decay * keep[:, rows, :]
        direct = (
            widen(rate_wide[:, rows, :], chan) * near[:, rows, :]
            - widen(cross_wide[:, rows, :], chan) * state[:, rows, :]
        )
        add = mult * direct
        for hop in (1, 2, 4):
            inside = row < GROUP - hop
            add = jnp.where(inside, mult * pltpu.roll(add, GROUP - hop, 1) + add, add)
            mult = jnp.where(inside, mult * pltpu.roll(mult, GROUP - hop, 1), mult)
        add = add + mult * above
        mult = mult * prod
        inside = row < GROUP - 1
        near[:, rows, :] = direct + jnp.where(inside, pltpu.roll(add, GROUP - 1, 1), above)
        reach[:, rows, :] = jnp.where(inside, pltpu.roll(mult, GROUP - 1, 1), prod)
        return mult[:, :1, :], add[:, :1, :]

    held = (jnp.ones((n_seq, 1, chan), FLOAT), jnp.zeros((n_seq, 1, chan), FLOAT))
    middle_of = length // GROUP // 2
    held = lax.fori_loop(0, middle_of, back, held)
    pump()
    prod, total = lax.fori_loop(middle_of, length // GROUP, back, held)
    here = lax.axis_index("ctx")
    ends[here, 0] = prod.reshape(n_seq, chan)
    ends[here, 1] = total.reshape(n_seq, chan)
    pump()
    share(ends, "ctx", n_ctx, *ctx_sems)
    carry = jnp.zeros((n_seq, chan), FLOAT)
    for place in range(n_ctx - 1, 0, -1):
        carry = jnp.where(place > here, ends[place, 1] + ends[place, 0] * carry, carry)
    carry = carry.reshape(n_seq, 1, chan)
    wide = 2 * GROUP
    first = lax.broadcasted_iota(jnp.int32, (n_seq, wide, chan), 1) == 0

    def finish(index, held):
        before, low_total = held
        rows = pl.ds(pl.multiple_of(index * wide, wide), wide)
        inp = proj[0, :, rows, :]
        sig = jax.nn.sigmoid(inp)
        silu = inp * sig
        fsig = jax.nn.sigmoid(proj[1, :, rows, :])
        rest = 1.0 - fsig
        decay = low + (1.0 - low) * fsig
        grad_state = near[:, rows, :] + reach[:, rows, :] * carry
        value = state[:, rows, :]
        prev = jnp.where(first, before, pltpu.roll(value, 1, 1))
        grad_decay = grad_state * (prev * keep[:, rows, :] - silu)
        grad_proj[:, rows, :chan] = (
            grad_state * (1.0 - decay) * (sig * (1.0 + inp * (1.0 - sig)))
        ).astype(HALF)
        grad_proj[:, rows, chan : 2 * chan] = (
            grad_decay * (1.0 - low) * fsig * rest
        ).astype(HALF)
        return value[:, wide - 1 :, :], low_total + grad_decay * rest

    held = (carry_in[...].reshape(n_seq, 1, chan), jnp.zeros((n_seq, wide, chan), FLOAT))
    middle_of = length // wide // 2
    held = lax.fori_loop(0, middle_of, finish, held)
    pump()
    _, low_total = lax.fori_loop(middle_of, length // wide, finish, held)
    lower_out[...] = jnp.sum(jnp.sum(low_total, 0), 0, keepdims=True)
    pump()


def tail(
    n_fsdp, n_ctx, n_tp,
    keep, gate_gain, lower, scale, carry_in, gain, gain_two_grad,
    proj, state, grad_gated, w_in, w_down, act, normed, grad_mixed, gated, cotangent,
    grad_resid, tokens, mixed,
    grad_tokens_out, output_out, vectors_out, w_in_out, w_out_out, w_down_out,
    grad_proj, held, crossed, total, spare, inbox,
    in_tile, in_half, in_quarter, out_tile, out_half, out_quarter, down_tile, down_half, down_quarter,
    gain_total, ends, cross, over_ctx, over_fsdp, near,
    load_sem, store_sem, end_send, end_recv, cross_send, cross_recv, ctx_send, ctx_recv,
    fsdp_send, fsdp_recv, part_sem, part_send, part_recv, square_send, square_recv, square_store,
    *line_sems,
):
    n_seq, length, wide = grad_proj.shape
    chan = wide // 3
    rows = n_seq * length
    width = gain.shape[1]
    units = w_down.shape[0]
    piece = width // PIECES
    n_chunks = n_seq
    whole = n_fsdp != 2
    greet(others("ctx", n_ctx) + others("tp", n_tp) + others("fsdp", n_fsdp))
    line = Line(held, crossed, total, line_sems)
    pieces = [(job, q) for job in range(2 * n_chunks) for q in range(PIECES)]
    relay = [(line.forward, spot) for spot in pieces[:2]]
    for index, spot in enumerate(pieces):
        relay.append((line.close, spot))
        relay += [(line.forward, ahead) for ahead in pieces[index + 2 : index + 3]]
    squares = []
    turn = [0]
    SPACE = 4

    def pump():
        while relay:
            action, spot = relay.pop(0)
            action(*spot)
            if action == line.forward:
                break
        for square in squares:
            if square[1] < 5 and turn[0] >= square[2] + SPACE * square[1]:
                square[0].advance(square[1])
                square[1] += 1
        turn[0] += 1

    def start_loads(pairs, first=0):
        copies = [
            pltpu.make_async_copy(source, target, load_sem.at[first + index])
            for index, (source, target) in enumerate(pairs)
        ]
        for copy in copies:
            copy.start()
        return copies

    def chunk_rows(c):
        return pl.ds(c * length, length) if isinstance(c, int) else span(c * length, length, length)

    shape = (n_seq, length, chan)

    crossing = shares(cross, "tp", n_tp, cross_send, cross_recv)

    def down_terms(w_all, act_all):
        copies = start_loads([(w_down, w_all), (act, act_all)], 3)

        def cross_terms(gate_all, state_all):
            for copy in start_loads(
                [(proj.at[2], gate_all), (state, state_all), (grad_gated, near)]
            ):
                copy.wait()
            gain_at = over_ctx.at[lax.axis_index("ctx"), :, 2 * width : 2 * width + chan]
            scan_cross(gate_all, state_all, scale, gate_gain, near, grad_proj, gain_at, cross)

        def down_term(c, first, stop):
            @pl.loop(first, stop)
            def _(q):
                cols = pl.ds(pl.multiple_of(q * piece, piece), piece)
                held[c, q] = dot(act_all[chunk_rows(c), :], w_all[:, cols]).astype(HALF)
                line.offer(c, q)

        for copy in copies:
            copy.wait()
        down_term(0, 0, 2)
        pl.run_scoped(cross_terms, pltpu.VMEM(shape, FLOAT), pltpu.VMEM(shape, FLOAT))
        for copy in crossing:
            copy.start()

        for c in range(n_chunks):
            down_term(c, 0 if c else 2, PIECES)

            if c >= n_chunks // 2:
                pump()

    pl.run_scoped(
        down_terms, pltpu.VMEM((units, width), HALF), pltpu.VMEM((rows, units), HALF)
    )

    for copy in crossing:
        copy.wait()

    def back(proj_all, state_all, reach, rate_wide, cross_wide):
        for copy in start_loads([(proj.at[:2], proj_all), (state, state_all)]):
            copy.wait()
        lower_at = over_ctx.at[lax.axis_index("ctx"), :, 2 * width + chan :]
        scan_back(
            n_ctx, n_tp, width, pump,
            proj_all, keep, lower, state_all, scale, carry_in, near,
            grad_proj, lower_at,
            reach, rate_wide, cross_wide, ends, cross, (end_send, end_recv),
        )

    pl.run_scoped(
        back,
        pltpu.VMEM((2, *shape), FLOAT),
        pltpu.VMEM(shape, FLOAT),
        pltpu.VMEM(shape, FLOAT),
        pltpu.VMEM((n_seq, length, BLOCK), FLOAT),
        pltpu.VMEM((n_seq, length, BLOCK), FLOAT),
    )

    def back_terms(w_all):
        for copy in start_loads([(w_in, w_all)]):
            copy.wait()

        for c in range(n_chunks):
            @pl.loop(0, PIECES)
            def _(q):
                at = pl.ds(pl.multiple_of(q * piece, piece), piece)
                held[n_chunks + c, q] = dot_nt(grad_proj[c], w_all[at, :]).astype(HALF)
                line.offer(n_chunks + c, q)

            if c % 2 == 1:
                pump()

    pl.run_scoped(back_terms, pltpu.VMEM((width, wide), HALF))

    item, finish = halves(n_fsdp, part_sem, part_send, part_recv, spare, inbox)
    mine = 1 if whole else lax.axis_index("fsdp")
    depth = width // 2
    skip = whole * depth
    stores = []

    def weights(act_all, dy_all, normed_all, mixed_all, gated_all):
        copies = start_loads(
            [(act, act_all), (cotangent, dy_all), (normed, normed_all), (grad_mixed, mixed_all),
             (gated, gated_all)]
        )
        count = [0]

        def tile(view, compute, other_place, own_place, buffers, at):
            index = count[0]
            count[0] += 1
            square = Square(
                index, buffers, at, own_place, square_send, square_recv, square_store
            )
            item(index, view, compute(1 - mine), compute(mine), other_place, square.tile)
            if whole:
                square.store().start()
                stores.append(square)
            else:
                squares.append([square, 0, turn[0]])
            pump()

        copies[0].wait()
        copies[1].wait()
        for start, size in bands(units, TILE):
            left = act_all[:, start : start + size].T
            at = slice(start, start + size)

            def compute(side):
                return lambda target: fill(target, left, dy_all, side * depth)

            tile(
                lambda ref, size=size: ref.at[:size, :depth], compute,
                lambda at=at: w_down_out.at[at, :depth], lambda at=at: w_down_out.at[at, skip:],
                (down_tile, down_half, down_quarter),
                [slice(start // cut, (start + size) // cut) for cut in (1, 2, 4)],
            )
        copies[2].wait()
        flat_proj = grad_proj.reshape(rows, wide)
        for k in range(depth // TILE):
            def compute(side):
                at = pl.ds(pl.multiple_of(side * depth + k * TILE, TILE), TILE)
                return lambda target: fill(target, normed_all[:, at].T, flat_proj, 0)

            at = slice(k * TILE, (k + 1) * TILE)
            tile(
                lambda ref: ref, compute,
                lambda at=at: w_in_out.at[at],
                lambda k=k: w_in_out.at[k * TILE + skip : (k + 1) * TILE + skip],
                (in_tile, in_half, in_quarter), (k, k, k),
            )
        copies[3].wait()
        copies[4].wait()
        for k in range(chan // TILE):
            at = slice(k * TILE, (k + 1) * TILE)
            left = gated_all[:, at].T

            def compute(side):
                return lambda target: fill(target, left, mixed_all, side * depth)

            tile(
                lambda ref: ref.at[:, :depth], compute,
                lambda at=at: w_out_out.at[at, :depth], lambda at=at: w_out_out.at[at, skip:],
                (out_tile, out_half, out_quarter), (k, k, k),
            )

    pl.run_scoped(
        weights,
        pltpu.VMEM((rows, units), HALF),
        pltpu.VMEM((rows, width), HALF),
        pltpu.VMEM((rows, width), HALF),
        pltpu.VMEM((rows, width), HALF),
        pltpu.VMEM((rows, chan), HALF),
    )
    finish()

    def ends_of(resid_all, x_all, mixed_all):
        copies = start_loads([(tokens, x_all), (mixed, mixed_all), (grad_resid, resid_all)])
        copies[0].wait()
        copies[1].wait()
        gain_total[...] = jnp.zeros_like(gain_total)

        def token_store(c):
            at = chunk_rows(c)
            return pltpu.make_async_copy(
                x_all.at[at], grad_tokens_out.at[at], store_sem.at[0, c]
            )

        def output_store(c):
            at = chunk_rows(c)
            return pltpu.make_async_copy(mixed_all.at[at], output_out.at[at], store_sem.at[1, c])

        def until(job):
            while (line.close, (job, PIECES - 1)) in relay:
                if relay[0] == (line.close, (job, PIECES - 1)):
                    action, spot = relay.pop(0)
                    action(*spot)
                else:
                    pump()

        for c in range(n_chunks):
            until(c)
            line.arrive(c)

            @pl.loop(0, length // 16)
            def _(index):
                at = pl.ds(pl.multiple_of(c * length + index * 16, 16), 16)
                rows = pl.ds(pl.multiple_of(index * 16, 16), 16)
                value = x_all[at, :].astype(FLOAT) + mixed_all[at, :].astype(FLOAT)
                mixed_all[at, :] = (value + joined(total, c, rows)).astype(HALF)

            output_store(c).start()

        copies[2].wait()
        for c in range(n_chunks):
            until(n_chunks + c)
            line.arrive(n_chunks + c)
            for quarter in range(PIECES):
                pump()

                @pl.loop(0, length // PIECES // 16)
                def _(index):
                    start = quarter * (length // PIECES) + index * 16
                    rows = pl.ds(pl.multiple_of(start, 16), 16)
                    at = pl.ds(pl.multiple_of(c * length + start, 16), 16)
                    value = x_all[at, :].astype(FLOAT)
                    rate = rms_scale(value)
                    grad = joined(total, n_chunks + c, rows)
                    by_gain = grad * (value * rate)
                    gain_total[...] += by_gain[:8] + by_gain[8:]
                    inner = gain[...] * grad
                    mean = jnp.mean(inner * value, -1, keepdims=True)
                    result = resid_all[at, :] + rate * inner - value * (rate * rate * rate * mean)
                    x_all[at, :] = result.astype(HALF)

            token_store(c).start()

        here = lax.axis_index("ctx")
        over_ctx[here, :, :width] = jnp.sum(gain_total[...], 0, keepdims=True)
        over_ctx[here, :, width : 2 * width] = gain_two_grad[...]
        share(over_ctx, "ctx", n_ctx, ctx_send, ctx_recv)
        value = over_ctx[0]
        for place in range(1, n_ctx):
            value = value + over_ctx[place]
        over_fsdp[lax.axis_index("fsdp")] = value
        share(over_fsdp, "fsdp", n_fsdp, fsdp_send, fsdp_recv)
        value = over_fsdp[0]
        for place in range(1, n_fsdp):
            value = value + over_fsdp[place]
        vectors_out[...] = value
        while any(square[1] < 5 for square in squares):
            pump()
        for c in range(n_chunks):
            token_store(c).wait()
            output_store(c).wait()

    pl.run_scoped(
        ends_of,
        pltpu.VMEM((rows, width), FLOAT),
        pltpu.VMEM((rows, width), HALF),
        pltpu.VMEM((rows, width), HALF),
    )
    for square in squares:
        square[0].settle()
    for square in stores:
        square.store().wait()

    @pl.loop(0, 2 * n_chunks)
    def _(job):
        line.settle(job)
        line.release(job)


def run_tail(small, large, n_fsdp, n_ctx, n_tp):
    grad_gated, w_down, tokens = large[2], large[4], large[11]
    n_seq, length, chan = grad_gated.shape
    rows, width = tokens.shape
    units = w_down.shape[0]
    piece = width // PIECES
    size = 2 * width + 2 * chan
    depth = width // 2
    spread = width if n_fsdp != 2 else depth
    vmem = pl.BlockSpec(memory_space=pltpu.VMEM)
    hbm = pl.BlockSpec(memory_space=pl.ANY)
    slots = pltpu.VMEM((2 * n_seq, PIECES, length, piece), HALF)
    sems = pltpu.SemaphoreType.DMA((2 * n_seq, PIECES))
    n_in, n_out = depth // TILE, chan // TILE
    n_squares = n_in + n_out + len(bands(units, TILE))
    wide = max(3 * chan, depth)

    def tiles(*shape):
        return [
            pltpu.VMEM((*shape[:-2], shape[-2] // cut, shape[-1]), HALF) for cut in (1, 2, 4)
        ]

    return pl.pallas_call(
        functools.partial(tail, n_fsdp, n_ctx, n_tp),
        name="tail",
        out_shape=(
            jax.ShapeDtypeStruct((rows, width), HALF),
            jax.ShapeDtypeStruct((rows, width), HALF),
            jax.ShapeDtypeStruct((1, size), FLOAT),
            jax.ShapeDtypeStruct((spread, 3 * chan), HALF),
            jax.ShapeDtypeStruct((chan, spread), HALF),
            jax.ShapeDtypeStruct((units, spread), HALF),
        ),
        in_specs=[vmem] * len(small) + [hbm] * len(large),
        out_specs=[hbm, hbm, vmem, hbm, hbm, hbm],
        scratch_shapes=[
            pltpu.VMEM((n_seq, length, 3 * chan), HALF),
            slots,
            pltpu.VMEM((2 * n_seq, PIECES, length, piece), HALF),
            slots,
            pltpu.VMEM((2, TILE, wide), HALF),
            pltpu.VMEM((2, TILE, wide), HALF),
            *tiles(n_in, TILE, 3 * chan),
            *tiles(n_out, TILE, depth),
            *tiles(units, depth),
            pltpu.VMEM((8, width), FLOAT),
            pltpu.VMEM((n_ctx, 2, n_seq, chan), FLOAT),
            pltpu.VMEM((n_tp, n_seq, length), FLOAT),
            pltpu.VMEM((n_ctx, 1, size), FLOAT),
            pltpu.VMEM((n_fsdp, 1, size), FLOAT),
            pltpu.VMEM((n_seq, length, chan), FLOAT),
            pltpu.SemaphoreType.DMA((6,)),
            pltpu.SemaphoreType.DMA((2, n_seq)),
            pltpu.SemaphoreType.DMA((n_ctx,)),
            pltpu.SemaphoreType.DMA((n_ctx,)),
            pltpu.SemaphoreType.DMA((n_tp,)),
            pltpu.SemaphoreType.DMA((n_tp,)),
            pltpu.SemaphoreType.DMA((n_ctx,)),
            pltpu.SemaphoreType.DMA((n_ctx,)),
            pltpu.SemaphoreType.DMA((n_fsdp,)),
            pltpu.SemaphoreType.DMA((n_fsdp,)),
            pltpu.SemaphoreType.DMA((2,)),
            pltpu.SemaphoreType.DMA((2,)),
            pltpu.SemaphoreType.DMA((2,)),
            pltpu.SemaphoreType.DMA((n_squares, 4)),
            pltpu.SemaphoreType.DMA((n_squares, 4)),
            pltpu.SemaphoreType.DMA((n_squares,)),
        ]
        + [sems] * 4,
        compiler_params=pltpu.CompilerParams(
            collective_id=3, has_side_effects=True, vmem_limit_bytes=63 * MIB
        ),
        cost_estimate=pl.CostEstimate(
            flops=10 * rows * width * units, bytes_accessed=700 * MIB, transcendentals=0
        ),
    )(*small, *large)


def widen_outputs(
    w_in, w_out, w_gate, w_up, w_down, tokens, output, vectors,
    w_in_out, w_out_out, w_glu_out, w_down_out, tokens_out, output_out, one_out, two_out, gate_out, lower_out,
):
    chan = w_in_out.shape[2]
    for gate in range(3):
        w_in_out[gate] = w_in[:, gate * chan : (gate + 1) * chan].astype(FLOAT)
    w_out_out[...] = w_out[...].astype(FLOAT)
    w_glu_out[:, 0, :] = w_gate[...].astype(FLOAT)
    w_glu_out[:, 1, :] = w_up[...].astype(FLOAT)
    w_down_out[...] = w_down[...].astype(FLOAT)
    tokens_out[...] = tokens[...].astype(FLOAT)
    output_out[...] = output[...]

    @pl.when(pl.program_id(0) == 0)
    def _():
        part = one_out.shape[1]
        width = (vectors.shape[1] - 2 * chan) // 2
        begin = lax.axis_index("fsdp") * part
        one_out[...] = vectors[:, span(begin, part, part)]
        two_out[...] = vectors[:, span(width + begin, part, part)]
        gate_out[...] = vectors[:, 2 * width : 2 * width + chan]
        lower_out[...] = vectors[:, 2 * width + chan :]


def run_widen_outputs(w_in, w_out, w_gate, w_up, w_down, tokens, output, vectors):
    steps = 8
    arrays = (w_in, w_out, w_gate, w_up, w_down, tokens, output)

    def spec(array):
        return pl.BlockSpec((array.shape[0] // steps, array.shape[1]), lambda i: (i, 0))

    depth, wide = w_in.shape
    chan = wide // 3
    units = w_gate.shape[1]
    whole = pl.BlockSpec(vectors.shape, lambda i: (0, 0))
    thin = [jax.ShapeDtypeStruct((1, size), FLOAT) for size in (depth, depth, chan, chan)]
    shapes = [
        jax.ShapeDtypeStruct((3, depth, chan), FLOAT),
        jax.ShapeDtypeStruct(w_out.shape, FLOAT),
        jax.ShapeDtypeStruct((depth, 2, units), FLOAT),
        jax.ShapeDtypeStruct(w_down.shape, FLOAT),
        jax.ShapeDtypeStruct(tokens.shape, FLOAT),
        jax.ShapeDtypeStruct(output.shape, HALF),
    ]
    in_specs = [spec(array) for array in arrays] + [whole]
    specs = [
        pl.BlockSpec((3, depth // steps, chan), lambda i: (0, i, 0)),
        spec(w_out),
        pl.BlockSpec((depth // steps, 2, units), lambda i: (i, 0, 0)),
        spec(w_down),
        spec(tokens),
        spec(output),
    ] + [pl.BlockSpec(shape.shape, lambda i: (0, 0)) for shape in thin]
    return pl.pallas_call(
        widen_outputs,
        name="widen_outputs",
        grid=(steps,),
        out_shape=shapes + thin,
        in_specs=in_specs,
        out_specs=specs,
        compiler_params=pltpu.CompilerParams(vmem_limit_bytes=62 * MIB),
    )(*arrays, vectors)


def head(
    n_fsdp, n_ctx, n_tp,
    gains, same, first, last, gate_gain, lower, w_in, tokens, wo_in,
    gated, scale, carry_out, keep, gain_one, gain_two, proj_out, state_out, normed_out, w_out, wo_out,
    staged, w_all, wo_staged, wo_all, normed, proj, state, local, reach, ends, squares, gain_slots, edge_slots,
    load_sem, store_sem, half_send, half_recv, ctx_send, ctx_recv, tp_send, tp_recv,
    gain_send, gain_recv, edge_send, edge_recv,
):
    n_seq, length, chan = state.shape
    rows = n_seq * length
    depth = w_in.shape[1]
    width = w_all.shape[0]
    greet(others("ctx", n_ctx) + others("tp", n_tp) + others("fsdp", n_fsdp))
    core = lax.axis_index("fsdp")
    gate_cols = [slice(gate * chan, (gate + 1) * chan) for gate in range(3)]
    x_load = pltpu.make_async_copy(tokens, normed, load_sem.at[3])
    if n_fsdp == 2:
        w_loads = [
            pltpu.make_async_copy(w_in.at[gate], staged.at[gate], load_sem.at[gate])
            for gate in range(3)
        ]
    else:
        w_loads = [
            pltpu.make_async_copy(w_in.at[gate], w_all.at[:, gate_cols[gate]], load_sem.at[gate])
            for gate in range(3)
        ]
    if n_fsdp == 2:
        wo_load = pltpu.make_async_copy(wo_in, wo_staged, load_sem.at[4])
    else:
        wo_load = pltpu.make_async_copy(wo_in, wo_out, load_sem.at[4])
    for load in w_loads + [x_load, wo_load]:
        load.start()
    gain_slots[core] = gains[...].astype(HALF).astype(FLOAT)
    edge_slots[lax.axis_index("ctx")] = last[...]
    small = shares(gain_slots, "fsdp", n_fsdp, gain_send, gain_recv)
    small += shares(edge_slots, "ctx", n_ctx, edge_send, edge_recv)
    for copy in small:
        copy.start()
    halves_sent = []
    if n_fsdp == 2:
        own = span(core * depth, depth, depth)
        for gate in range(3):
            w_loads[gate].wait()

            def cast(at):
                to = span(core * depth + at.start, at.size, at.size)
                w_all[to, gate_cols[gate]] = staged[gate, at, :].astype(HALF)

            row_blocks(depth, 32, cast)
            place = w_all.at[own, gate_cols[gate]]
            copy = pltpu.make_async_remote_copy(
                src_ref=place,
                dst_ref=place,
                send_sem=half_send.at[gate],
                recv_sem=half_recv.at[gate],
                device_id={"fsdp": 1 - core},
                device_id_type=MESH,
            )
            copy.start()
            halves_sent.append(copy)
    for copy in small:
        copy.wait()
    part = gains.shape[1]
    for place in range(n_fsdp):
        cols = slice(place * part, (place + 1) * part)
        gain_one[:, cols] = gain_slots[place, :1, :]
        gain_two[:, cols] = gain_slots[place, 1:2, :]
    here = lax.axis_index("ctx")
    keep[...] = same[...]
    before = edge_slots[0]
    for place in range(1, n_ctx):
        before = jnp.where(place == here - 1, edge_slots[place], before)
    joins = jnp.where((before == first[...]) & (here > 0), 1.0, 0.0)
    keep[:, :1, :] = joins[:, :1].reshape(n_seq, 1, 1)
    x_load.wait()

    def norm(at):
        value = normed[at, :].astype(FLOAT)
        normed[at, :] = (value * rms_scale(value) * gain_one[...]).astype(HALF)

    row_blocks(rows, 16, norm)
    if n_fsdp == 2:
        size = wo_staged.shape[1]
        own_cols = span(core * size, size, size)
        wo_load.wait()

        def cast_out(at):
            wo_all[at, own_cols] = wo_staged[at, :].astype(HALF)

        row_blocks(chan, 32, cast_out)
        copy = pltpu.make_async_remote_copy(
            src_ref=wo_all.at[:, own_cols],
            dst_ref=wo_all.at[:, own_cols],
            send_sem=half_send.at[3],
            recv_sem=half_recv.at[3],
            device_id={"fsdp": 1 - core},
            device_id_type=MESH,
        )
        copy.start()
        halves_sent.append(copy)
    normed_store = pltpu.make_async_copy(normed, normed_out, store_sem.at[0])
    normed_store.start()
    flat = proj.reshape(3, rows, chan)
    band = rows
    if n_fsdp == 2:
        for gate in range(3):
            @pl.loop(0, rows // band)
            def _(index):
                at = span(index * band, band, band)
                cols = span(core * depth, depth, depth)
                flat[gate, at, :] = dot(normed[at, cols], w_all[own, gate_cols[gate]])

        for gate in range(3):
            halves_sent[gate].wait_recv()

            @pl.loop(0, rows // band)
            def _(index):
                at = span(index * band, band, band)
                other = span((1 - core) * depth, depth, depth)
                flat[gate, at, :] += dot(normed[at, other], w_all[other, gate_cols[gate]])
    else:
        for gate in range(3):
            w_loads[gate].wait()

            @pl.loop(0, rows // band)
            def _(index):
                at = span(index * band, band, band)
                flat[gate, at, :] = dot(normed[at, :], w_all[:, gate_cols[gate]])

    stores = [
        pltpu.make_async_copy(proj, proj_out, store_sem.at[1]),
        pltpu.make_async_copy(w_all, w_out, store_sem.at[2]),
    ]
    for store in stores:
        store.start()
    low = lower[...].reshape(1, 1, chan)
    row = lax.broadcasted_iota(jnp.int32, (n_seq, GROUP, chan), 1)

    def step(index, carry):
        prod, total = carry
        rows = pl.ds(pl.multiple_of(index * GROUP, GROUP), GROUP)
        inp = proj[0, :, rows, :]
        decay = low + (1.0 - low) * jax.nn.sigmoid(proj[1, :, rows, :])
        add = inp * jax.nn.sigmoid(inp) * (1.0 - decay)
        mult = decay * keep[:, rows, :]
        for hop in (1, 2, 4):
            inside = row >= hop
            add = jnp.where(inside, mult * pltpu.roll(add, hop, 1) + add, add)
            mult = jnp.where(inside, mult * pltpu.roll(mult, hop, 1), mult)
        add = add + mult * total
        mult = mult * prod
        local[:, rows, :] = add
        reach[:, rows, :] = mult
        return mult[:, GROUP - 1 :, :], add[:, GROUP - 1 :, :]

    start = (jnp.ones((n_seq, 1, chan), FLOAT), jnp.zeros((n_seq, 1, chan), FLOAT))
    prod, total = lax.fori_loop(0, length // GROUP, step, start)
    ends[here, 0] = prod.reshape(n_seq, chan)
    ends[here, 1] = total.reshape(n_seq, chan)
    share(ends, "ctx", n_ctx, ctx_send, ctx_recv)
    carry = jnp.zeros((n_seq, chan), FLOAT)
    for place in range(n_ctx - 1):
        carry = jnp.where(place < here, ends[place, 1] + ends[place, 0] * carry, carry)
    carry_out[...] = carry
    mine = lax.axis_index("tp")
    for seq in range(n_seq):
        for start in range(0, length, BLOCK):
            rows = slice(start, start + BLOCK)
            value = local[seq, rows, :] + reach[seq, rows, :] * carry[seq : seq + 1]
            state[seq, rows, :] = value
            squares[mine, seq : seq + 1, rows] = lane_sums(value * value)
    state_store = pltpu.make_async_copy(state, state_out, store_sem.at[3])
    state_store.start()
    share(squares, "tp", n_tp, tp_send, tp_recv)
    total = squares[0]
    for place in range(1, n_tp):
        total = total + squares[place]
    rate = lax.rsqrt(total / width + EPS)
    scale[...] = rate
    for seq in range(n_seq):
        for start in range(0, length, BLOCK):
            rows = slice(start, start + BLOCK)
            gate = proj[2, seq, rows, :]
            unit = state[seq, rows, :] * widen(columns(rate[seq : seq + 1, rows]), chan)
            swish = gate * jax.nn.sigmoid(gate)
            gated[seq, rows, :] = (unit * gate_gain[...] * swish).astype(HALF)
    for copy in halves_sent:
        copy.wait_send()
    if n_fsdp == 2:
        halves_sent[3].wait_recv()
        stores.append(pltpu.make_async_copy(wo_all, wo_out, load_sem.at[4]))
        stores[-1].start()
    else:
        stores.append(wo_load)
    for store in stores + [normed_store, state_store]:
        store.wait()


def run_head(
    gains, same, first, last, gate_gain, lower, w_in, tokens, w_out, n_fsdp, n_ctx, n_tp
):
    n_seq, length, _ = same.shape
    rows, width = tokens.shape
    chan = w_in.shape[2]
    shape = (n_seq, length, chan)
    vmem = pl.BlockSpec(memory_space=pltpu.VMEM)
    hbm = pl.BlockSpec(memory_space=pl.ANY)
    staged = w_in.shape if n_fsdp == 2 else (3, 8, BLOCK)
    wo_staged = w_out.shape if n_fsdp == 2 else (8, BLOCK)
    dma = pltpu.SemaphoreType.DMA
    return pl.pallas_call(
        functools.partial(head, n_fsdp, n_ctx, n_tp),
        name="head",
        out_shape=(
            jax.ShapeDtypeStruct(shape, HALF),
            jax.ShapeDtypeStruct((n_seq, length), FLOAT),
            jax.ShapeDtypeStruct((n_seq, chan), FLOAT),
            jax.ShapeDtypeStruct((n_seq, length, 1), FLOAT),
            jax.ShapeDtypeStruct((1, width), FLOAT),
            jax.ShapeDtypeStruct((1, width), FLOAT),
            jax.ShapeDtypeStruct((3, *shape), FLOAT),
            jax.ShapeDtypeStruct(shape, FLOAT),
            jax.ShapeDtypeStruct((rows, width), HALF),
            jax.ShapeDtypeStruct((width, 3 * chan), HALF),
            jax.ShapeDtypeStruct((chan, width), HALF),
        ),
        in_specs=[vmem] * 6 + [hbm] * 3,
        out_specs=[vmem] * 6 + [hbm] * 5,
        scratch_shapes=[
            pltpu.VMEM(staged, FLOAT),
            pltpu.VMEM((width, 3 * chan), HALF),
            pltpu.VMEM(wo_staged, FLOAT),
            pltpu.VMEM((chan, width), HALF),
            pltpu.VMEM((rows, width), HALF),
            pltpu.VMEM((3, *shape), FLOAT),
            pltpu.VMEM(shape, FLOAT),
            pltpu.VMEM(shape, FLOAT),
            pltpu.VMEM(shape, FLOAT),
            pltpu.VMEM((n_ctx, 2, n_seq, chan), FLOAT),
            pltpu.VMEM((n_tp, n_seq, length), FLOAT),
            pltpu.VMEM((n_fsdp, *gains.shape), FLOAT),
            pltpu.VMEM((n_ctx, *last.shape), FLOAT),
            dma((5,)), dma((4,)), dma((4,)), dma((4,)), dma((n_ctx,)), dma((n_ctx,)),
            dma((n_tp,)), dma((n_tp,)), dma((n_fsdp,)), dma((n_fsdp,)), dma((n_ctx,)), dma((n_ctx,)),
        ],
        compiler_params=pltpu.CompilerParams(
            collective_id=0, has_side_effects=True, vmem_limit_bytes=63 * MIB
        ),
    )(gains, same, first, last, gate_gain, lower, w_in, tokens, w_out)


def gather_fsdp(part, dim):
    return lax.all_gather(part, "fsdp", axis=dim, tiled=True)


def local(
    sizes,
    tokens, segment_ids, w_in, w_out, w_glu, w_down, gain_one, gain_two, gate_gain, lower, cotangent,
):
    n_fsdp, n_ctx, n_tp = sizes
    n_seq, length, width = tokens.shape
    rows = n_seq * length
    chan = w_in.shape[2]
    x_half = tokens.reshape(rows, width)
    parts = (w_glu[:, 0].astype(HALF), w_glu[:, 1].astype(HALF), w_down)
    if n_fsdp != 2:
        parts = (*parts[:2], w_down.astype(HALF))
        parts = tuple(gather_fsdp(part, dim) for part, dim in zip(parts, (0, 0, 1)))
        w_in = gather_fsdp(w_in.astype(HALF), 1)
        w_out = gather_fsdp(w_out.astype(HALF), 1)
    gain_gate = gate_gain[None]
    low = lower[None]
    seg = segment_ids.astype(FLOAT)
    same = jnp.pad((seg[:, 1:] == seg[:, :-1]).astype(FLOAT), ((0, 0), (1, 0)))[..., None]
    first, last = (jnp.broadcast_to(seg[:, at], (n_seq, BLOCK)) for at in (slice(0, 1), slice(-1, None)))
    (
        gated, gate_scale, carry, keep, gain_a, gain_b, proj, state, normed, w_in_all, w_out_all
    ) = run_head(
        jnp.stack([gain_one, gain_two]), same, first, last, gain_gate, low, w_in, x_half, w_out,
        n_fsdp, n_ctx, n_tp,
    )
    gated = gated.reshape(rows, chan)
    grad_y_half = cotangent.reshape(rows, width)
    (
        mixed, _, act, _, grad_resid, grad_mixed, grad_gated, grad_w_gate, grad_w_up, w_down_all,
        grad_gain_two,
    ) = run_middle(
        gated, x_half, grad_y_half, gain_b, (w_out_all, *parts), n_fsdp, n_ctx, length
    )
    if n_fsdp == 2:
        grad_w_up = lax.psum(grad_w_up, "ctx")
    grad_tokens, output, vectors, grad_w_in, grad_w_out, grad_w_down = run_tail(
        (keep, gain_gate, low, gate_scale, carry, gain_a, grad_gain_two),
        (
            proj, state, grad_gated.reshape(n_seq, length, chan), w_in_all, w_down_all, act, normed,
            grad_mixed, gated, grad_y_half, grad_resid, x_half, mixed,
        ),
        n_fsdp, n_ctx, n_tp,
    )
    grads = (grad_w_in, grad_w_out, grad_w_gate, grad_w_up, grad_w_down)
    if n_fsdp != 2:
        grads = tuple(
            lax.psum(lax.psum_scatter(value, "fsdp", scatter_dimension=dim, tiled=True), "ctx")
            for value, dim in zip(grads, (0, 1, 0, 0, 1))
        )
    results = run_widen_outputs(*grads, grad_tokens, output, vectors)
    grad_w_in, grad_w_out, grad_w_glu, grad_w_down, grad_tokens, output = results[:6]
    return (
        output.reshape(n_seq, length, width),
        grad_tokens.reshape(n_seq, length, width),
        grad_w_in,
        grad_w_out,
        grad_w_glu,
        grad_w_down,
        *(vector[0] for vector in results[6:]),
    )


def solution(mesh):
    sizes = tuple(mesh.shape[axis] for axis in ("fsdp", "ctx", "tp"))
    return jax.shard_map(
        functools.partial(local, sizes),
        mesh=mesh,
        in_specs=(
            P("fsdp", "ctx", None),
            P("fsdp", "ctx"),
            P(None, "fsdp", "tp"),
            P("tp", "fsdp"),
            P("fsdp", None, "tp"),
            P("tp", "fsdp"),
            P("fsdp"),
            P("fsdp"),
            P("tp"),
            P("tp"),
            P("fsdp", "ctx", None),
        ),
        out_specs=(
            P("fsdp", "ctx", None),
            P("fsdp", "ctx", None),
            P(None, "fsdp", "tp"),
            P("tp", "fsdp"),
            P("fsdp", None, "tp"),
            P("tp", "fsdp"),
            P("fsdp"),
            P("fsdp"),
            P("tp"),
            P("tp"),
        ),
        check_vma=False,
    )
```

```python
import functools

import jax
import jax.numpy as jnp
from jax import lax
from jax.experimental import pallas as pl
from jax.experimental.pallas import tpu as pltpu
from jax.sharding import PartitionSpec as P

EPS = 1e-06
FLOAT = jnp.float32
HALF = jnp.bfloat16
MESH = pl.DeviceIdType.MESH
GROUP = 8
BLOCK = 128
MIB = 1 << 20


def rms_scale(values):
    return lax.rsqrt(jnp.mean(values * values, -1, keepdims=True) + EPS)


def silu_slope(values):
    sig = jax.nn.sigmoid(values)
    return sig * (1.0 + values * (1.0 - sig))


def greet(peers):
    barrier = pltpu.get_barrier_semaphore()
    for peer in peers:
        pl.semaphore_signal(barrier, inc=1, device_id=peer, device_id_type=MESH)
    pl.semaphore_wait(barrier, len(peers))


def others(axis, count):
    mine = lax.axis_index(axis)
    return [{axis: lax.rem(mine + step, count)} for step in range(1, count)]


def shares(slots, axis, count, send, recv):
    mine = lax.axis_index(axis)
    return [
        pltpu.make_async_remote_copy(
            src_ref=slots.at[mine],
            dst_ref=slots.at[mine],
            send_sem=send.at[step],
            recv_sem=recv.at[step],
            device_id=peer,
            device_id_type=MESH,
        )
        for step, peer in enumerate(others(axis, count))
    ]


def share(slots, axis, count, send, recv):
    copies = shares(slots, axis, count, send, recv)
    for copy in copies:
        copy.start()
    for copy in copies:
        copy.wait()


def lane_sums(values):
    part = values[:, :BLOCK]
    for start in range(BLOCK, values.shape[1], BLOCK):
        part = part + values[:, start : start + BLOCK]
    return jnp.sum(part.T, 0, keepdims=True)


def columns(row):
    return jnp.broadcast_to(row, (BLOCK, BLOCK)).T


def widen(values, chan):
    return jnp.concatenate([values] * (chan // BLOCK), -1)


PIECES = 4
TILE = 256
WIDE = 512


def bands(count, size):
    return [(start, min(size, count - start)) for start in range(0, count, size)]


def dot(lhs, rhs):
    return jnp.dot(lhs, rhs, preferred_element_type=FLOAT)


def dot_nt(lhs, rhs):
    return lax.dot_general(lhs, rhs, (((1,), (1,)), ((), ())), preferred_element_type=FLOAT)


class Line:
    def __init__(self, held, cross, total, sems):
        self.held, self.cross, self.total, self.sems = held, cross, total, sems
        place = lax.axis_index("tp")
        self.inner = (place == 1) | (place == 2)
        self.side = place + 1 - 2 * lax.rem(place, 2)
        self.facing = 3 - place

    def slot(self, job, ref):
        slots = ref.shape[0]
        if slots == self.total.shape[0]:
            return job
        return job % slots if isinstance(job, int) else lax.rem(job, slots)

    def copy(self, source, target, send, recv, place):
        return pltpu.make_async_remote_copy(
            src_ref=source,
            dst_ref=target,
            send_sem=send,
            recv_sem=recv,
            device_id={"tp": place},
            device_id_type=MESH,
        )

    def inward(self, job, q):
        send, recv, _, _ = self.sems
        return self.copy(
            self.held.at[self.slot(job, self.held), q], self.total.at[job, q],
            send.at[job, q], recv.at[job, q], self.side,
        )

    def outward(self, job, q):
        send, recv, _, _ = self.sems
        return self.copy(
            self.total.at[job, q], self.total.at[job, q],
            send.at[job, q], recv.at[job, q], self.side,
        )

    def across(self, job, q):
        _, _, send, recv = self.sems
        return self.copy(
            self.held.at[self.slot(job, self.held), q], self.cross.at[self.slot(job, self.cross), q],
            send.at[job, q], recv.at[job, q], self.facing,
        )

    def offer(self, job, q):
        @pl.when(jnp.logical_not(self.inner))
        def _():
            self.inward(job, q).start()

    def forward(self, job, q):
        slot = self.slot(job, self.held)

        @pl.when(self.inner)
        def _():
            self.inward(job, q).wait_recv()
            self.held[slot, q] = self.held[slot, q] + self.total[job, q]
            self.across(job, q).start()

    def close(self, job, q):
        slot, cross_slot = self.slot(job, self.held), self.slot(job, self.cross)

        @pl.when(self.inner)
        def _():
            self.across(job, q).wait_recv()
            self.total[job, q] = self.held[slot, q] + self.cross[cross_slot, q]
            self.outward(job, q).start()

    def tick(self, base, step):
        if step > 0:
            self.close(base, step - 1)
        if step < PIECES:
            ahead = step + 1
            self.forward(base + ahead // PIECES, ahead % PIECES)

    def arrive(self, job):
        @pl.when(jnp.logical_not(self.inner))
        def _():
            @pl.loop(0, PIECES)
            def _(q):
                self.outward(job, q).wait_recv()

    def release(self, job):
        @pl.when(self.inner)
        def _():
            @pl.loop(0, PIECES)
            def _(q):
                self.across(job, q).wait_send()

        @pl.when(jnp.logical_not(self.inner))
        def _():
            @pl.loop(0, PIECES)
            def _(q):
                self.inward(job, q).wait_send()

    def settle(self, job):
        @pl.when(self.inner)
        def _():
            @pl.loop(0, PIECES)
            def _(q):
                self.outward(job, q).wait_send()


def span(start, size, unit):
    return pl.ds(pl.multiple_of(start, unit), size)


def row_blocks(count, size, body):
    @pl.loop(0, count // size)
    def _(index):
        body(pl.ds(pl.multiple_of(index * size, size), size))


def line_peers():
    place = lax.axis_index("tp")
    return [{"tp": place + 1 - 2 * lax.rem(place, 2)}, {"tp": 3 - place}]


def joined(ref, c, rows):
    return jnp.concatenate([ref[c, q, rows, :].astype(FLOAT) for q in range(PIECES)], -1)


def add_to(target, extra, rows):
    target[rows, :] = target[rows, :] + extra[rows, :]


def halves(n_fsdp, store_sem, send_sem, recv_sem, spare, inbox):
    mine = lax.axis_index("fsdp")
    pending = {}

    def send(index, view):
        slot = index % 2
        return pltpu.make_async_remote_copy(
            src_ref=view(spare.at[slot]),
            dst_ref=view(inbox.at[slot]),
            send_sem=send_sem.at[slot],
            recv_sem=recv_sem.at[slot],
            device_id={"fsdp": 1 - mine},
            device_id_type=MESH,
        )

    def item(index, view, compute_other, compute_own, other_place, target):
        slot = index % 2
        if index - 2 in pending:
            pending.pop(index - 2)()
        compute_other(view(spare.at[slot]))
        if n_fsdp == 2:
            copy = send(index, view)
            copy.start()
            pending[index] = lambda: send(index, view).wait_send()
        else:
            def store():
                return pltpu.make_async_copy(view(spare.at[slot]), other_place(), store_sem.at[slot])

            store().start()
            pending[index] = lambda: store().wait()
        compute_own(target)
        if n_fsdp == 2:
            send(index, view).wait_recv()
            extra = view(inbox.at[slot])
            row_blocks(target.shape[0], 32, lambda rows: add_to(target, extra, rows))

    def finish():
        for wait in pending.values():
            wait()

    return item, finish


class Square:
    def __init__(self, index, buffers, at, place, send, recv, store_sem):
        self.buffers, self.at, self.place_of = buffers, at, place
        self.send, self.recv, self.index, self.store_sem = send, recv, index, store_sem

    @property
    def tile(self):
        return self.buffers[0].at[self.at[0]]

    @property
    def half(self):
        return self.buffers[1].at[self.at[1]]

    @property
    def quarter(self):
        return self.buffers[2].at[self.at[2]]

    def geometry(self):
        here = lax.axis_index("ctx")
        low, high = lax.rem(here, 2), here // 2
        near, far = here + 1 - 2 * low, here + 2 - 4 * high
        bits = (low, high) if self.index % 2 == 0 else (high, low)
        peers = (near, far) if self.index % 2 == 0 else (far, near)
        wide, thin = self.half.shape[0], self.quarter.shape[0]
        begin = bits[0] * wide
        return (
            peers,
            span(begin, wide, wide),
            span((1 - bits[0]) * wide, wide, wide),
            span(begin + bits[1] * thin, thin, thin),
            span(begin + (1 - bits[1]) * thin, thin, thin),
        )

    def round(self, number):
        peers, mine, yours, my_part, your_part = self.geometry()
        source, target, peer = (
            (self.tile.at[yours], self.half, 0),
            (self.tile.at[your_part], self.quarter, 1),
            (self.tile.at[my_part], self.place_of().at[my_part], 1),
            (self.place_of().at[mine], self.place_of().at[mine], 0),
        )[number]
        return pltpu.make_async_remote_copy(
            src_ref=source,
            dst_ref=target,
            send_sem=self.send.at[self.index, number],
            recv_sem=self.recv.at[self.index, number],
            device_id={"ctx": peers[peer]},
            device_id_type=MESH,
        )

    def add(self, part, extra):
        target = self.tile.at[part]
        row_blocks(extra.shape[0], 32, lambda rows: add_to(target, extra, rows))

    def store(self):
        return pltpu.make_async_copy(self.tile, self.place_of(), self.store_sem.at[self.index])

    def store_part(self):
        part = self.geometry()[3]
        return pltpu.make_async_copy(
            self.tile.at[part], self.place_of().at[part], self.store_sem.at[self.index]
        )

    def advance(self, number):
        if number > 0:
            self.round(number - 1).wait_recv()
        if number == 1:
            self.add(self.geometry()[1], self.half)
        if number == 2:
            self.add(self.geometry()[3], self.quarter)
            self.store_part().start()
        if number == 3:
            self.store_part().wait()
        if number < 4:
            self.round(number).start()

    def settle(self):
        for number in range(4):
            self.round(number).wait_send()


def fill(target, left, right, first):
    for start, size in bands(target.shape[1], WIDE):
        cols = pl.ds(pl.multiple_of(first + start, BLOCK), size)
        target[:, start : start + size] = dot(left, right[:, cols]).astype(HALF)


def middle(
    n_fsdp, n_ctx, CHUNK,
    gated, tokens, cotangent, gain, wo_part, wg_part, wu_part, wd_part,
    mixed_out, normed_out, act_out, grad_glu_out, grad_resid_out, grad_mixed_out,
    grad_gated_out, w_gate_out, w_up_out, w_down_out, grad_gain_out,
    wo, wg, wu, wd, x_all, dy_all, held, crossed, total, normed, act, grad_glu,
    grad_resid, grad_mixed, grad_gated, gain_total, spare, inbox, half, quarter,
    square_send, square_recv, square_store, weight_sem, weight_send, weight_recv, again_sem,
    own_sem, stage_sem, glu_send, glu_recv, down_send, down_recv,
    load_sem, store_sem, *line_sems,
):
    n_chunks, _, _, piece = held.shape
    units = wd.shape[0]
    width = wd.shape[1]
    peers = line_peers() + others("ctx", n_ctx)
    if n_fsdp == 2:
        peers.append({"fsdp": 1 - lax.axis_index("fsdp")})
    local_parts = [(wo_part, wo)]
    if n_fsdp != 2:
        local_parts += [(wg_part, wg), (wu_part, wu), (wd_part, wd)]
    ready = [
        pltpu.make_async_copy(part, whole, own_sem.at[index])
        for index, (part, whole) in enumerate(local_parts)
    ]
    for copy in ready:
        copy.start()
    greet(peers)
    core = lax.axis_index("fsdp")
    n_bands = units // BLOCK

    def to_sibling(place, send, recv):
        return pltpu.make_async_remote_copy(
            src_ref=place,
            dst_ref=place,
            send_sem=send,
            recv_sem=recv,
            device_id={"fsdp": 1 - core},
            device_id_type=MESH,
        )

    def glu_copies(number):
        part, whole = ((wg_part, wg), (wu_part, wu))[number]
        at = span(core * (width // 2), width // 2, width // 2)
        far = pltpu.make_async_remote_copy(
            src_ref=part,
            dst_ref=whole.at[at],
            send_sem=glu_send.at[number],
            recv_sem=glu_recv.at[number],
            device_id={"fsdp": 1 - core},
            device_id_type=MESH,
        )
        return far, pltpu.make_async_copy(part, whole.at[at], own_sem.at[1 + number])

    def down_stage(index):
        return grad_resid.at[span(lax.rem(index, 2) * BLOCK, BLOCK, BLOCK), : width // 2]

    def down_load(index):
        return pltpu.make_async_copy(
            wd_part.at[span(index * BLOCK, BLOCK, BLOCK)], down_stage(index),
            stage_sem.at[lax.rem(index, 2)],
        )

    def down_copy(index):
        cols = span(core * (width // 2), width // 2, width // 2)
        place = wd.at[span(index * BLOCK, BLOCK, BLOCK), cols]
        return to_sibling(place, down_send.at[index], down_recv.at[index])

    def down_band(index):
        down_load(index).wait()
        cols = span(core * (width // 2), width // 2, width // 2)
        wd[span(index * BLOCK, BLOCK, BLOCK), cols] = down_stage(index)[...].astype(HALF)

        @pl.when(index + 2 < n_bands)
        def _():
            down_load(index + 2).start()

        down_copy(index).start()

    if n_fsdp == 2:
        for first_load in (*glu_copies(0), *glu_copies(1), down_load(0), down_load(1)):
            first_load.start()
    loads = [
        pltpu.make_async_copy(tokens, x_all, load_sem.at[0]),
        pltpu.make_async_copy(cotangent, dy_all, load_sem.at[1]),
    ]
    for load in loads:
        load.start()
    line = Line(held, crossed, total, line_sems)

    def chunk_rows(c):
        return pl.ds(pl.multiple_of(c * CHUNK, CHUNK), CHUNK)

    def stores(c, wanted=None):
        rows = chunk_rows(c)
        pairs = [
            (normed, normed_out.at[rows]),
            (act, act_out.at[rows]),
            (grad_glu.at[0], grad_glu_out.at[0, rows]),
            (grad_glu.at[1], grad_glu_out.at[1, rows]),
            (grad_resid, grad_resid_out.at[rows]),
            (grad_mixed, grad_mixed_out.at[rows]),
            (grad_gated, grad_gated_out.at[rows]),
        ]
        pairs += [
            (total.at[c, q], mixed_out.at[rows, pl.ds(q * piece, piece)]) for q in range(PIECES)
        ]
        return [
            pltpu.make_async_copy(source, target, store_sem.at[index])
            for index, (source, target) in enumerate(pairs)
            if wanted is None or index in wanted
        ]

    FORWARD = (0, 1, 2, 3, 7, 8, 9, 10)
    BACKWARD = (4, 5, 6)

    ready[0].wait()

    @pl.loop(0, n_chunks)
    def _(c):
        lhs = gated[chunk_rows(c), :]

        @pl.loop(0, PIECES)
        def _(q):
            cols = pl.ds(pl.multiple_of(q * piece, piece), piece)
            held[c, q] = dot(lhs, wo[:, cols]).astype(HALF)
            line.offer(c, q)

    for load in loads:
        load.wait()
    def cast_down(part):
        pl.loop(part * n_bands // 4, (part + 1) * n_bands // 4)(down_band)

    for step in range(PIECES + 2):
        if n_fsdp == 2 and step < 4:
            cast_down(step)
        if step == 0:
            line.forward(0, 0)
        else:
            line.tick(0, step - 1)

    w_down_store = pltpu.make_async_copy(wd, w_down_out, again_sem.at[3])

    def weights_here():
        for copy in ready[1:]:
            copy.wait()
        if n_fsdp == 2:
            for copy in (*glu_copies(0), *glu_copies(1)):
                copy.wait()

            @pl.loop(0, n_bands)
            def _(index):
                down_copy(index).wait()

        w_down_store.start()

    @pl.loop(0, n_chunks)
    def _(c):
        line.arrive(c)
        line.tick(c + 1, 0)

        @pl.when(c > 0)
        def _():
            for store in stores(c - 1, FORWARD):
                store.wait()

        def norm(rows):
            at = pl.ds(pl.multiple_of(c * CHUNK + rows.start, 16), rows.size)
            resid = x_all[at, :].astype(FLOAT) + joined(total, c, rows)
            normed[rows, :] = (resid * rms_scale(resid) * gain[...]).astype(HALF)

        row_blocks(CHUNK, 16, norm)
        pl.when(c == 0)(weights_here)

        def unit(cols):
            glu_gate = dot(normed[...], wg[:, cols])
            glu_up = dot(normed[...], wu[:, cols])
            grad_act = dot_nt(dy_all[chunk_rows(c), :], wd[cols, :])
            sig = jax.nn.sigmoid(glu_gate)
            silu = glu_gate * sig
            act[:, cols] = (silu * glu_up).astype(HALF)
            slope = sig * (1.0 + glu_gate * (1.0 - sig))
            grad_glu[0, :, cols] = (grad_act * glu_up * slope).astype(HALF)
            grad_glu[1, :, cols] = (grad_act * silu).astype(HALF)

        for index, (start, size) in enumerate(bands(units, WIDE)):
            unit(slice(start, start + size))
            if index == 0:
                line.tick(c + 1, 1)
        line.tick(c + 1, 2)
        line.release(c)

        @pl.loop(0, PIECES)
        def _(q):
            @pl.when(q == PIECES // 2)
            def _():
                line.tick(c + 1, 3)

            at = pl.ds(pl.multiple_of(q * piece, piece), piece)
            value = dot_nt(grad_glu[0], wg[at, :]) + dot_nt(grad_glu[1], wu[at, :])
            held[c, q] = value.astype(HALF)
            line.offer(n_chunks + c, q)

        line.tick(c + 1, 4)

        for store in stores(c, FORWARD):
            store.start()

    for store in stores(n_chunks - 1, FORWARD):
        store.wait()
    rows = n_chunks * CHUNK
    w_down_store.wait()
    kept = [
        (grad_glu_out.at[0], wg.at[:rows]),
        (grad_glu_out.at[1], wu.at[:rows]),
        (normed_out, wd.at[:rows]),
    ]
    again = [
        pltpu.make_async_copy(source, target, again_sem.at[index])
        for index, (source, target) in enumerate(kept)
    ]
    for copy in again:
        copy.start()
    gain_total[...] = jnp.zeros_like(gain_total)
    item, finish = halves(n_fsdp, weight_sem, weight_send, weight_recv, spare, inbox)
    mine = lax.axis_index("fsdp") if n_fsdp == 2 else 1
    depth = width // 2
    whole = n_fsdp != 2
    per_part = depth // TILE
    squares, plain, turn = [], [], [0]

    def weight_item(index):
        if index >= 2 * per_part:
            return
        part, k = divmod(index, per_part)
        right = (wg, wu)[part].at[:rows]
        out = (w_gate_out, w_up_out)[part]

        def compute(side):
            at = pl.ds(pl.multiple_of(side * depth + k * TILE, TILE), TILE)
            return lambda target: fill(target, wd[:rows, at].T, right, 0)

        at = slice(k * TILE + whole * depth, (k + 1) * TILE + whole * depth)
        square = Square(
            index, ((wg, wu)[part], half, quarter),
            (slice(rows + k * TILE, rows + (k + 1) * TILE), k, k), lambda: out.at[at],
            square_send, square_recv, square_store,
        )
        item(
            index, lambda ref: ref, compute(1 - mine), compute(mine),
            lambda: out.at[k * TILE : (k + 1) * TILE], square.tile,
        )
        if whole or part == 1:
            square.store().start()
            plain.append(square)
        else:
            squares.append([square, 0, turn[0]])

    def pump():
        for square in squares:
            if square[1] < 5 and turn[0] >= square[2] + 3 * square[1]:
                square[0].advance(square[1])
                square[1] += 1
        turn[0] += 1

    def backward(c, between):
        line.arrive(n_chunks + c)
        if c > 0:
            for store in stores(c - 1, BACKWARD):
                store.wait()

        def norm_back(rows):
            at = pl.ds(pl.multiple_of(c * CHUNK + rows.start, 16), rows.size)
            resid = x_all[at, :].astype(FLOAT) + joined(total, c, rows)
            rate = rms_scale(resid)
            grad = joined(total, n_chunks + c, rows)
            by_gain = grad * (resid * rate)
            gain_total[...] += by_gain[:8] + by_gain[8:]
            inner = gain[...] * grad
            mean = jnp.mean(inner * resid, -1, keepdims=True)
            value = dy_all[at, :].astype(FLOAT) + rate * inner - resid * (rate * rate * rate * mean)
            grad_resid[rows, :] = value
            grad_mixed[rows, :] = value.astype(HALF)

        row_blocks(CHUNK, 16, norm_back)
        between()
        for start, size in bands(grad_gated.shape[1], WIDE):
            grad_gated[:, start : start + size] = dot_nt(
                grad_mixed[...], wo[start : start + size, :]
            )
        for store in stores(c, BACKWARD):
            store.start()

    for copy in again:
        copy.wait()
    count = 0
    for c in range(n_chunks):
        if c == n_chunks - 1:
            while count < 2 * per_part:
                weight_item(count)
                count += 1
        if c + 1 == n_chunks:
            backward(c, lambda: None)
            continue

        def between():
            line.tick(n_chunks + c + 1, 0)
            pump()

        backward(c, between)
        for step in range(1, PIECES + 1):
            weight_item(count)
            count += 1
            if c + 2 == n_chunks and step == PIECES - 1:
                line.close(2 * n_chunks - 1, step - 1)
            else:
                line.tick(n_chunks + c + 1, step)
            pump()
    while any(square[1] < 5 for square in squares):
        pump()
    finish()
    for square, _, _ in squares:
        square.settle()
    for square in plain:
        square.store().wait()

    grad_gain_out[...] = jnp.sum(gain_total[...], 0, keepdims=True)
    for store in stores(n_chunks - 1, BACKWARD):
        store.wait()

    @pl.loop(0, n_chunks)
    def _(c):
        line.settle(c)
        line.settle(n_chunks + c)
        line.release(n_chunks + c)


def run_middle(gated, tokens, cotangent, gain, parts, n_fsdp, n_ctx, length):
    rows, chan = gated.shape
    width = tokens.shape[1]
    units = parts[3].shape[0]
    n_chunks = rows // length
    piece = width // PIECES
    vmem = pl.BlockSpec(memory_space=pltpu.VMEM)
    hbm = pl.BlockSpec(memory_space=pl.ANY)
    sems = pltpu.SemaphoreType.DMA((2 * n_chunks, PIECES))
    return pl.pallas_call(
        functools.partial(middle, n_fsdp, n_ctx, length),
        name="middle",
        out_shape=(
            jax.ShapeDtypeStruct((rows, width), HALF),
            jax.ShapeDtypeStruct((rows, width), HALF),
            jax.ShapeDtypeStruct((rows, units), HALF),
            jax.ShapeDtypeStruct((2, rows, units), HALF),
            jax.ShapeDtypeStruct((rows, width), FLOAT),
            jax.ShapeDtypeStruct((rows, width), HALF),
            jax.ShapeDtypeStruct((rows, chan), FLOAT),
            jax.ShapeDtypeStruct((width if n_fsdp != 2 else width // 2, units), HALF),
            jax.ShapeDtypeStruct((width if n_fsdp != 2 else width // 2, units), HALF),
            jax.ShapeDtypeStruct((units, width), HALF),
            jax.ShapeDtypeStruct((1, width), FLOAT),
        ),
        in_specs=[vmem, hbm, hbm, vmem, hbm, hbm, hbm, hbm],
        out_specs=[hbm] * 10 + [vmem],
        scratch_shapes=[
            pltpu.VMEM((chan, width), HALF),
            pltpu.VMEM((width, units), HALF),
            pltpu.VMEM((width, units), HALF),
            pltpu.VMEM((units, width), HALF),
            pltpu.VMEM((rows, width), HALF),
            pltpu.VMEM((rows, width), HALF),
            pltpu.VMEM((n_chunks, PIECES, length, piece), HALF),
            pltpu.VMEM((n_chunks, PIECES, length, piece), HALF),
            pltpu.VMEM((2 * n_chunks, PIECES, length, piece), HALF),
            pltpu.VMEM((length, width), HALF),
            pltpu.VMEM((length, units), HALF),
            pltpu.VMEM((2, length, units), HALF),
            pltpu.VMEM((length, width), FLOAT),
            pltpu.VMEM((length, width), HALF),
            pltpu.VMEM((length, chan), FLOAT),
            pltpu.VMEM((8, width), FLOAT),
            pltpu.VMEM((2, TILE, units), HALF),
            pltpu.VMEM((2, TILE, units), HALF),
            pltpu.VMEM((width // 2 // TILE, TILE // 2, units), HALF),
            pltpu.VMEM((width // 2 // TILE, TILE // 4, units), HALF),
            pltpu.SemaphoreType.DMA((width // 2 // TILE, 4)),
            pltpu.SemaphoreType.DMA((width // 2 // TILE, 4)),
            pltpu.SemaphoreType.DMA((width // TILE,)),
            pltpu.SemaphoreType.DMA((4,)),
            pltpu.SemaphoreType.DMA((2,)),
            pltpu.SemaphoreType.DMA((2,)),
            pltpu.SemaphoreType.DMA((4,)),
            pltpu.SemaphoreType.DMA((4,)),
            pltpu.SemaphoreType.DMA((2,)),
            pltpu.SemaphoreType.DMA((2,)),
            pltpu.SemaphoreType.DMA((2,)),
            pltpu.SemaphoreType.DMA((units // BLOCK,)),
            pltpu.SemaphoreType.DMA((units // BLOCK,)),
            pltpu.SemaphoreType.DMA((2,)),
            pltpu.SemaphoreType.DMA((12,)),
        ]
        + [sems] * 4,
        compiler_params=pltpu.CompilerParams(
            collective_id=2, has_side_effects=True, vmem_limit_bytes=63 * MIB
        ),
        cost_estimate=pl.CostEstimate(
            flops=16 * rows * width * units, bytes_accessed=400 * MIB, transcendentals=0
        ),
    )(gated, tokens, cotangent, gain, *parts)


def scan_cross(gate_all, state, scale, gain, near, grad_proj, gain_out, cross):
    n_seq, length, chan = state.shape
    mine = lax.axis_index("tp")
    gain_total = jnp.zeros((8, chan), FLOAT)
    for seq in range(n_seq):
        for start in range(0, length, BLOCK):
            rows = slice(start, start + BLOCK)
            rate = columns(scale[seq : seq + 1, rows])
            gate = gate_all[seq, rows, :]
            sig = jax.nn.sigmoid(gate)
            swish = gate * sig
            value = state[seq, rows, :]
            into = near[seq, rows, :]
            by_unit = into * value * widen(rate, chan)
            slope = sig * (1.0 + gate * (1.0 - sig))
            grad_proj[seq, rows, 2 * chan :] = (by_unit * gain[...] * slope).astype(HALF)
            gain_total = gain_total + jnp.sum((by_unit * swish).reshape(-1, 8, chan), 0)
            grad_unit = into * swish * gain[...]
            near[seq, rows, :] = grad_unit
            cross[mine, seq : seq + 1, rows] = lane_sums(grad_unit * value)
    gain_out[...] = jnp.sum(gain_total, 0, keepdims=True)


def scan_back(
    n_ctx, n_tp, width, pump,
    proj, keep, lower, state, scale, carry_in, near,
    grad_proj, lower_out,
    reach, rate_wide, cross_wide, ends, cross, ctx_sems,
):
    n_seq, length, chan = state.shape
    low = lower[...].reshape(1, 1, chan)
    total = cross[0]
    for place in range(1, n_tp):
        total = total + cross[place]
    rate = scale[...]
    total = total * (rate * rate * rate) / width
    for seq in range(n_seq):
        for start in range(0, length, BLOCK):
            rows = slice(start, start + BLOCK)
            rate_wide[seq, rows, :] = columns(rate[seq : seq + 1, rows])
            cross_wide[seq, rows, :] = columns(total[seq : seq + 1, rows])

    row = lax.broadcasted_iota(jnp.int32, (n_seq, GROUP, chan), 1)

    def back(index, carry):
        prod, above = carry
        rows = pl.ds(pl.multiple_of((length // GROUP - 1 - index) * GROUP, GROUP), GROUP)
        decay = low + (1.0 - low) * jax.nn.sigmoid(proj[1, :, rows, :])
        mult = decay * keep[:, rows, :]
        direct = (
            widen(rate_wide[:, rows, :], chan) * near[:, rows, :]
            - widen(cross_wide[:, rows, :], chan) * state[:, rows, :]
        )
        add = mult * direct
        for hop in (1, 2, 4):
            inside = row < GROUP - hop
            add = jnp.where(inside, mult * pltpu.roll(add, GROUP - hop, 1) + add, add)
            mult = jnp.where(inside, mult * pltpu.roll(mult, GROUP - hop, 1), mult)
        add = add + mult * above
        mult = mult * prod
        inside = row < GROUP - 1
        near[:, rows, :] = direct + jnp.where(inside, pltpu.roll(add, GROUP - 1, 1), above)
        reach[:, rows, :] = jnp.where(inside, pltpu.roll(mult, GROUP - 1, 1), prod)
        return mult[:, :1, :], add[:, :1, :]

    held = (jnp.ones((n_seq, 1, chan), FLOAT), jnp.zeros((n_seq, 1, chan), FLOAT))
    middle_of = length // GROUP // 2
    held = lax.fori_loop(0, middle_of, back, held)
    pump()
    prod, total = lax.fori_loop(middle_of, length // GROUP, back, held)
    here = lax.axis_index("ctx")
    ends[here, 0] = prod.reshape(n_seq, chan)
    ends[here, 1] = total.reshape(n_seq, chan)
    pump()
    share(ends, "ctx", n_ctx, *ctx_sems)
    carry = jnp.zeros((n_seq, chan), FLOAT)
    for place in range(n_ctx - 1, 0, -1):
        carry = jnp.where(place > here, ends[place, 1] + ends[place, 0] * carry, carry)
    carry = carry.reshape(n_seq, 1, chan)
    wide = 2 * GROUP
    first = lax.broadcasted_iota(jnp.int32, (n_seq, wide, chan), 1) == 0

    def finish(index, held):
        before, low_total = held
        rows = pl.ds(pl.multiple_of(index * wide, wide), wide)
        inp = proj[0, :, rows, :]
        sig = jax.nn.sigmoid(inp)
        silu = inp * sig
        fsig = jax.nn.sigmoid(proj[1, :, rows, :])
        rest = 1.0 - fsig
        decay = low + (1.0 - low) * fsig
        grad_state = near[:, rows, :] + reach[:, rows, :] * carry
        value = state[:, rows, :]
        prev = jnp.where(first, before, pltpu.roll(value, 1, 1))
        grad_decay = grad_state * (prev * keep[:, rows, :] - silu)
        grad_proj[:, rows, :chan] = (
            grad_state * (1.0 - decay) * (sig * (1.0 + inp * (1.0 - sig)))
        ).astype(HALF)
        grad_proj[:, rows, chan : 2 * chan] = (
            grad_decay * (1.0 - low) * fsig * rest
        ).astype(HALF)
        return value[:, wide - 1 :, :], low_total + grad_decay * rest

    held = (carry_in[...].reshape(n_seq, 1, chan), jnp.zeros((n_seq, wide, chan), FLOAT))
    middle_of = length // wide // 2
    held = lax.fori_loop(0, middle_of, finish, held)
    pump()
    _, low_total = lax.fori_loop(middle_of, length // wide, finish, held)
    lower_out[...] = jnp.sum(jnp.sum(low_total, 0), 0, keepdims=True)
    pump()


def tail(
    n_fsdp, n_ctx, n_tp,
    keep, gate_gain, lower, scale, carry_in, gain, gain_two_grad,
    proj, state, grad_gated, w_in, w_down, act, normed, grad_mixed, gated, cotangent,
    grad_resid, tokens, mixed,
    grad_tokens_out, output_out, vectors_out, w_in_out, w_out_out, w_down_out,
    grad_proj, held, crossed, total, spare, inbox,
    in_tile, in_half, in_quarter, out_tile, out_half, out_quarter, down_tile, down_half, down_quarter,
    gain_total, ends, cross, over_ctx, over_fsdp, near,
    load_sem, store_sem, end_send, end_recv, cross_send, cross_recv, ctx_send, ctx_recv,
    fsdp_send, fsdp_recv, part_sem, part_send, part_recv, square_send, square_recv, square_store,
    *line_sems,
):
    n_seq, length, wide = grad_proj.shape
    chan = wide // 3
    rows = n_seq * length
    width = gain.shape[1]
    units = w_down.shape[0]
    piece = width // PIECES
    n_chunks = n_seq
    whole = n_fsdp != 2
    greet(others("ctx", n_ctx) + others("tp", n_tp) + others("fsdp", n_fsdp))
    line = Line(held, crossed, total, line_sems)
    pieces = [(job, q) for job in range(2 * n_chunks) for q in range(PIECES)]
    relay = [(line.forward, spot) for spot in pieces[:2]]
    for index, spot in enumerate(pieces):
        relay.append((line.close, spot))
        relay += [(line.forward, ahead) for ahead in pieces[index + 2 : index + 3]]
    squares = []
    turn = [0]
    SPACE = 4

    def pump():
        while relay:
            action, spot = relay.pop(0)
            action(*spot)
            if action == line.forward:
                break
        for square in squares:
            if square[1] < 5 and turn[0] >= square[2] + SPACE * square[1]:
                square[0].advance(square[1])
                square[1] += 1
        turn[0] += 1

    def start_loads(pairs, first=0):
        copies = [
            pltpu.make_async_copy(source, target, load_sem.at[first + index])
            for index, (source, target) in enumerate(pairs)
        ]
        for copy in copies:
            copy.start()
        return copies

    def chunk_rows(c):
        return pl.ds(c * length, length) if isinstance(c, int) else span(c * length, length, length)

    shape = (n_seq, length, chan)

    crossing = shares(cross, "tp", n_tp, cross_send, cross_recv)

    def down_terms(w_all, act_all):
        copies = start_loads([(w_down, w_all), (act, act_all)], 3)

        def cross_terms(gate_all, state_all):
            for copy in start_loads(
                [(proj.at[2], gate_all), (state, state_all), (grad_gated, near)]
            ):
                copy.wait()
            gain_at = over_ctx.at[lax.axis_index("ctx"), :, 2 * width : 2 * width + chan]
            scan_cross(gate_all, state_all, scale, gate_gain, near, grad_proj, gain_at, cross)

        def down_term(c, first, stop):
            @pl.loop(first, stop)
            def _(q):
                cols = pl.ds(pl.multiple_of(q * piece, piece), piece)
                held[c, q] = dot(act_all[chunk_rows(c), :], w_all[:, cols]).astype(HALF)
                line.offer(c, q)

        for copy in copies:
            copy.wait()
        down_term(0, 0, 2)
        pl.run_scoped(cross_terms, pltpu.VMEM(shape, FLOAT), pltpu.VMEM(shape, FLOAT))
        for copy in crossing:
            copy.start()

        for c in range(n_chunks):
            down_term(c, 0 if c else 2, PIECES)

            if c >= n_chunks // 2:
                pump()

    pl.run_scoped(
        down_terms, pltpu.VMEM((units, width), HALF), pltpu.VMEM((rows, units), HALF)
    )

    for copy in crossing:
        copy.wait()

    def back(proj_all, state_all, reach, rate_wide, cross_wide):
        for copy in start_loads([(proj.at[:2], proj_all), (state, state_all)]):
            copy.wait()
        lower_at = over_ctx.at[lax.axis_index("ctx"), :, 2 * width + chan :]
        scan_back(
            n_ctx, n_tp, width, pump,
            proj_all, keep, lower, state_all, scale, carry_in, near,
            grad_proj, lower_at,
            reach, rate_wide, cross_wide, ends, cross, (end_send, end_recv),
        )

    pl.run_scoped(
        back,
        pltpu.VMEM((2, *shape), FLOAT),
        pltpu.VMEM(shape, FLOAT),
        pltpu.VMEM(shape, FLOAT),
        pltpu.VMEM((n_seq, length, BLOCK), FLOAT),
        pltpu.VMEM((n_seq, length, BLOCK), FLOAT),
    )

    def back_terms(w_all):
        for copy in start_loads([(w_in, w_all)]):
            copy.wait()

        for c in range(n_chunks):
            @pl.loop(0, PIECES)
            def _(q):
                at = pl.ds(pl.multiple_of(q * piece, piece), piece)
                held[n_chunks + c, q] = dot_nt(grad_proj[c], w_all[at, :]).astype(HALF)
                line.offer(n_chunks + c, q)

            if c % 2 == 1:
                pump()

    pl.run_scoped(back_terms, pltpu.VMEM((width, wide), HALF))

    item, finish = halves(n_fsdp, part_sem, part_send, part_recv, spare, inbox)
    mine = 1 if whole else lax.axis_index("fsdp")
    depth = width // 2
    skip = whole * depth
    stores = []

    def weights(act_all, dy_all, normed_all, mixed_all, gated_all):
        copies = start_loads(
            [(act, act_all), (cotangent, dy_all), (normed, normed_all), (grad_mixed, mixed_all),
             (gated, gated_all)]
        )
        count = [0]

        def tile(view, compute, other_place, own_place, buffers, at):
            index = count[0]
            count[0] += 1
            square = Square(
                index, buffers, at, own_place, square_send, square_recv, square_store
            )
            item(index, view, compute(1 - mine), compute(mine), other_place, square.tile)
            if whole:
                square.store().start()
                stores.append(square)
            else:
                squares.append([square, 0, turn[0]])
            pump()

        copies[0].wait()
        copies[1].wait()
        for start, size in bands(units, TILE):
            left = act_all[:, start : start + size].T
            at = slice(start, start + size)

            def compute(side):
                return lambda target: fill(target, left, dy_all, side * depth)

            tile(
                lambda ref, size=size: ref.at[:size, :depth], compute,
                lambda at=at: w_down_out.at[at, :depth], lambda at=at: w_down_out.at[at, skip:],
                (down_tile, down_half, down_quarter),
                [slice(start // cut, (start + size) // cut) for cut in (1, 2, 4)],
            )
        copies[2].wait()
        flat_proj = grad_proj.reshape(rows, wide)
        for k in range(depth // TILE):
            def compute(side):
                at = pl.ds(pl.multiple_of(side * depth + k * TILE, TILE), TILE)
                return lambda target: fill(target, normed_all[:, at].T, flat_proj, 0)

            at = slice(k * TILE, (k + 1) * TILE)
            tile(
                lambda ref: ref, compute,
                lambda at=at: w_in_out.at[at],
                lambda k=k: w_in_out.at[k * TILE + skip : (k + 1) * TILE + skip],
                (in_tile, in_half, in_quarter), (k, k, k),
            )
        copies[3].wait()
        copies[4].wait()
        for k in range(chan // TILE):
            at = slice(k * TILE, (k + 1) * TILE)
            left = gated_all[:, at].T

            def compute(side):
                return lambda target: fill(target, left, mixed_all, side * depth)

            tile(
                lambda ref: ref.at[:, :depth], compute,
                lambda at=at: w_out_out.at[at, :depth], lambda at=at: w_out_out.at[at, skip:],
                (out_tile, out_half, out_quarter), (k, k, k),
            )

    pl.run_scoped(
        weights,
        pltpu.VMEM((rows, units), HALF),
        pltpu.VMEM((rows, width), HALF),
        pltpu.VMEM((rows, width), HALF),
        pltpu.VMEM((rows, width), HALF),
        pltpu.VMEM((rows, chan), HALF),
    )
    finish()

    def ends_of(resid_all, x_all, mixed_all):
        copies = start_loads([(tokens, x_all), (mixed, mixed_all), (grad_resid, resid_all)])
        copies[0].wait()
        copies[1].wait()
        gain_total[...] = jnp.zeros_like(gain_total)

        def token_store(c):
            at = chunk_rows(c)
            return pltpu.make_async_copy(
                x_all.at[at], grad_tokens_out.at[at], store_sem.at[0, c]
            )

        def output_store(c):
            at = chunk_rows(c)
            return pltpu.make_async_copy(mixed_all.at[at], output_out.at[at], store_sem.at[1, c])

        def until(job):
            while (line.close, (job, PIECES - 1)) in relay:
                if relay[0] == (line.close, (job, PIECES - 1)):
                    action, spot = relay.pop(0)
                    action(*spot)
                else:
                    pump()

        for c in range(n_chunks):
            until(c)
            line.arrive(c)

            @pl.loop(0, length // 16)
            def _(index):
                at = pl.ds(pl.multiple_of(c * length + index * 16, 16), 16)
                rows = pl.ds(pl.multiple_of(index * 16, 16), 16)
                value = x_all[at, :].astype(FLOAT) + mixed_all[at, :].astype(FLOAT)
                mixed_all[at, :] = (value + joined(total, c, rows)).astype(HALF)

            output_store(c).start()

        copies[2].wait()
        for c in range(n_chunks):
            until(n_chunks + c)
            line.arrive(n_chunks + c)
            for quarter in range(PIECES):
                pump()

                @pl.loop(0, length // PIECES // 16)
                def _(index):
                    start = quarter * (length // PIECES) + index * 16
                    rows = pl.ds(pl.multiple_of(start, 16), 16)
                    at = pl.ds(pl.multiple_of(c * length + start, 16), 16)
                    value = x_all[at, :].astype(FLOAT)
                    rate = rms_scale(value)
                    grad = joined(total, n_chunks + c, rows)
                    by_gain = grad * (value * rate)
                    gain_total[...] += by_gain[:8] + by_gain[8:]
                    inner = gain[...] * grad
                    mean = jnp.mean(inner * value, -1, keepdims=True)
                    result = resid_all[at, :] + rate * inner - value * (rate * rate * rate * mean)
                    x_all[at, :] = result.astype(HALF)

            token_store(c).start()

        here = lax.axis_index("ctx")
        over_ctx[here, :, :width] = jnp.sum(gain_total[...], 0, keepdims=True)
        over_ctx[here, :, width : 2 * width] = gain_two_grad[...]
        share(over_ctx, "ctx", n_ctx, ctx_send, ctx_recv)
        value = over_ctx[0]
        for place in range(1, n_ctx):
            value = value + over_ctx[place]
        over_fsdp[lax.axis_index("fsdp")] = value
        share(over_fsdp, "fsdp", n_fsdp, fsdp_send, fsdp_recv)
        value = over_fsdp[0]
        for place in range(1, n_fsdp):
            value = value + over_fsdp[place]
        vectors_out[...] = value
        while any(square[1] < 5 for square in squares):
            pump()
        for c in range(n_chunks):
            token_store(c).wait()
            output_store(c).wait()

    pl.run_scoped(
        ends_of,
        pltpu.VMEM((rows, width), FLOAT),
        pltpu.VMEM((rows, width), HALF),
        pltpu.VMEM((rows, width), HALF),
    )
    for square in squares:
        square[0].settle()
    for square in stores:
        square.store().wait()

    @pl.loop(0, 2 * n_chunks)
    def _(job):
        line.settle(job)
        line.release(job)


def run_tail(small, large, n_fsdp, n_ctx, n_tp):
    grad_gated, w_down, tokens = large[2], large[4], large[11]
    n_seq, length, chan = grad_gated.shape
    rows, width = tokens.shape
    units = w_down.shape[0]
    piece = width // PIECES
    size = 2 * width + 2 * chan
    depth = width // 2
    spread = width if n_fsdp != 2 else depth
    vmem = pl.BlockSpec(memory_space=pltpu.VMEM)
    hbm = pl.BlockSpec(memory_space=pl.ANY)
    slots = pltpu.VMEM((2 * n_seq, PIECES, length, piece), HALF)
    sems = pltpu.SemaphoreType.DMA((2 * n_seq, PIECES))
    n_in, n_out = depth // TILE, chan // TILE
    n_squares = n_in + n_out + len(bands(units, TILE))
    wide = max(3 * chan, depth)

    def tiles(*shape):
        return [
            pltpu.VMEM((*shape[:-2], shape[-2] // cut, shape[-1]), HALF) for cut in (1, 2, 4)
        ]

    return pl.pallas_call(
        functools.partial(tail, n_fsdp, n_ctx, n_tp),
        name="tail",
        out_shape=(
            jax.ShapeDtypeStruct((rows, width), HALF),
            jax.ShapeDtypeStruct((rows, width), HALF),
            jax.ShapeDtypeStruct((1, size), FLOAT),
            jax.ShapeDtypeStruct((spread, 3 * chan), HALF),
            jax.ShapeDtypeStruct((chan, spread), HALF),
            jax.ShapeDtypeStruct((units, spread), HALF),
        ),
        in_specs=[vmem] * len(small) + [hbm] * len(large),
        out_specs=[hbm, hbm, vmem, hbm, hbm, hbm],
        scratch_shapes=[
            pltpu.VMEM((n_seq, length, 3 * chan), HALF),
            slots,
            pltpu.VMEM((2 * n_seq, PIECES, length, piece), HALF),
            slots,
            pltpu.VMEM((2, TILE, wide), HALF),
            pltpu.VMEM((2, TILE, wide), HALF),
            *tiles(n_in, TILE, 3 * chan),
            *tiles(n_out, TILE, depth),
            *tiles(units, depth),
            pltpu.VMEM((8, width), FLOAT),
            pltpu.VMEM((n_ctx, 2, n_seq, chan), FLOAT),
            pltpu.VMEM((n_tp, n_seq, length), FLOAT),
            pltpu.VMEM((n_ctx, 1, size), FLOAT),
            pltpu.VMEM((n_fsdp, 1, size), FLOAT),
            pltpu.VMEM((n_seq, length, chan), FLOAT),
            pltpu.SemaphoreType.DMA((6,)),
            pltpu.SemaphoreType.DMA((2, n_seq)),
            pltpu.SemaphoreType.DMA((n_ctx,)),
            pltpu.SemaphoreType.DMA((n_ctx,)),
            pltpu.SemaphoreType.DMA((n_tp,)),
            pltpu.SemaphoreType.DMA((n_tp,)),
            pltpu.SemaphoreType.DMA((n_ctx,)),
            pltpu.SemaphoreType.DMA((n_ctx,)),
            pltpu.SemaphoreType.DMA((n_fsdp,)),
            pltpu.SemaphoreType.DMA((n_fsdp,)),
            pltpu.SemaphoreType.DMA((2,)),
            pltpu.SemaphoreType.DMA((2,)),
            pltpu.SemaphoreType.DMA((2,)),
            pltpu.SemaphoreType.DMA((n_squares, 4)),
            pltpu.SemaphoreType.DMA((n_squares, 4)),
            pltpu.SemaphoreType.DMA((n_squares,)),
        ]
        + [sems] * 4,
        compiler_params=pltpu.CompilerParams(
            collective_id=3, has_side_effects=True, vmem_limit_bytes=63 * MIB
        ),
        cost_estimate=pl.CostEstimate(
            flops=10 * rows * width * units, bytes_accessed=700 * MIB, transcendentals=0
        ),
    )(*small, *large)


def widen_outputs(
    w_in, w_out, w_gate, w_up, w_down, tokens, output, vectors,
    w_in_out, w_out_out, w_glu_out, w_down_out, tokens_out, output_out, one_out, two_out, gate_out, lower_out,
):
    chan = w_in_out.shape[2]
    for gate in range(3):
        w_in_out[gate] = w_in[:, gate * chan : (gate + 1) * chan].astype(FLOAT)
    w_out_out[...] = w_out[...].astype(FLOAT)
    w_glu_out[:, 0, :] = w_gate[...].astype(FLOAT)
    w_glu_out[:, 1, :] = w_up[...].astype(FLOAT)
    w_down_out[...] = w_down[...].astype(FLOAT)
    tokens_out[...] = tokens[...].astype(FLOAT)
    output_out[...] = output[...]

    @pl.when(pl.program_id(0) == 0)
    def _():
        part = one_out.shape[1]
        width = (vectors.shape[1] - 2 * chan) // 2
        begin = lax.axis_index("fsdp") * part
        one_out[...] = vectors[:, span(begin, part, part)]
        two_out[...] = vectors[:, span(width + begin, part, part)]
        gate_out[...] = vectors[:, 2 * width : 2 * width + chan]
        lower_out[...] = vectors[:, 2 * width + chan :]


def run_widen_outputs(w_in, w_out, w_gate, w_up, w_down, tokens, output, vectors):
    steps = 8
    arrays = (w_in, w_out, w_gate, w_up, w_down, tokens, output)

    def spec(array):
        return pl.BlockSpec((array.shape[0] // steps, array.shape[1]), lambda i: (i, 0))

    depth, wide = w_in.shape
    chan = wide // 3
    units = w_gate.shape[1]
    whole = pl.BlockSpec(vectors.shape, lambda i: (0, 0))
    thin = [jax.ShapeDtypeStruct((1, size), FLOAT) for size in (depth, depth, chan, chan)]
    shapes = [
        jax.ShapeDtypeStruct((3, depth, chan), FLOAT),
        jax.ShapeDtypeStruct(w_out.shape, FLOAT),
        jax.ShapeDtypeStruct((depth, 2, units), FLOAT),
        jax.ShapeDtypeStruct(w_down.shape, FLOAT),
        jax.ShapeDtypeStruct(tokens.shape, FLOAT),
        jax.ShapeDtypeStruct(output.shape, HALF),
    ]
    in_specs = [spec(array) for array in arrays] + [whole]
    specs = [
        pl.BlockSpec((3, depth // steps, chan), lambda i: (0, i, 0)),
        spec(w_out),
        pl.BlockSpec((depth // steps, 2, units), lambda i: (i, 0, 0)),
        spec(w_down),
        spec(tokens),
        spec(output),
    ] + [pl.BlockSpec(shape.shape, lambda i: (0, 0)) for shape in thin]
    return pl.pallas_call(
        widen_outputs,
        name="widen_outputs",
        grid=(steps,),
        out_shape=shapes + thin,
        in_specs=in_specs,
        out_specs=specs,
        compiler_params=pltpu.CompilerParams(vmem_limit_bytes=62 * MIB),
    )(*arrays, vectors)


def head(
    n_fsdp, n_ctx, n_tp,
    gains, same, edges, gate_gain, lower, w_in, tokens, wo_in,
    gated, scale, carry_out, keep, gain_one, gain_two, proj_out, state_out, normed_out, w_out, wo_out,
    staged, w_all, wo_staged, wo_all, normed, proj, state, local, reach, ends, squares, gain_slots, edge_slots,
    load_sem, store_sem, half_send, half_recv, ctx_send, ctx_recv, tp_send, tp_recv,
    gain_send, gain_recv, edge_send, edge_recv,
):
    n_seq, length, chan = state.shape
    rows = n_seq * length
    depth = w_in.shape[1]
    width = w_all.shape[0]
    core = lax.axis_index("fsdp")
    gate_cols = [slice(gate * chan, (gate + 1) * chan) for gate in range(3)]
    x_load = pltpu.make_async_copy(tokens, normed, load_sem.at[3])
    if n_fsdp == 2:
        w_loads = [
            pltpu.make_async_copy(w_in.at[gate], staged.at[gate], load_sem.at[gate])
            for gate in range(3)
        ]
    else:
        w_loads = [
            pltpu.make_async_copy(w_in.at[gate], w_all.at[:, gate_cols[gate]], load_sem.at[gate])
            for gate in range(3)
        ]
    if n_fsdp == 2:
        wo_load = pltpu.make_async_copy(wo_in, wo_staged, load_sem.at[4])
    else:
        wo_load = pltpu.make_async_copy(wo_in, wo_out, load_sem.at[4])
    for load in w_loads + [x_load, wo_load]:
        load.start()
    gain_slots[core] = gains[...].astype(HALF).astype(FLOAT)
    edge_slots[lax.axis_index("ctx")] = edges[1]
    greet(others("ctx", n_ctx) + others("tp", n_tp) + others("fsdp", n_fsdp))
    small = shares(gain_slots, "fsdp", n_fsdp, gain_send, gain_recv)
    small += shares(edge_slots, "ctx", n_ctx, edge_send, edge_recv)
    for copy in small:
        copy.start()
    halves_sent = []
    if n_fsdp == 2:
        own = span(core * depth, depth, depth)
        for gate in range(3):
            w_loads[gate].wait()

            def cast(at):
                to = span(core * depth + at.start, at.size, at.size)
                w_all[to, gate_cols[gate]] = staged[gate, at, :].astype(HALF)

            row_blocks(depth, 32, cast)
            place = w_all.at[own, gate_cols[gate]]
            copy = pltpu.make_async_remote_copy(
                src_ref=place,
                dst_ref=place,
                send_sem=half_send.at[gate],
                recv_sem=half_recv.at[gate],
                device_id={"fsdp": 1 - core},
                device_id_type=MESH,
            )
            copy.start()
            halves_sent.append(copy)
    for copy in small:
        copy.wait()
    part = gains.shape[1]
    for place in range(n_fsdp):
        cols = slice(place * part, (place + 1) * part)
        gain_one[:, cols] = gain_slots[place, :1, :]
        gain_two[:, cols] = gain_slots[place, 1:2, :]
    here = lax.axis_index("ctx")
    keep[...] = same[...]
    before = edge_slots[0]
    for place in range(1, n_ctx):
        before = jnp.where(place == here - 1, edge_slots[place], before)
    joins = jnp.where((before == edges[0]) & (here > 0), 1.0, 0.0)
    keep[:, :1, :] = joins[:, :1].reshape(n_seq, 1, 1)
    x_load.wait()

    def norm(at):
        value = normed[at, :].astype(FLOAT)
        normed[at, :] = (value * rms_scale(value) * gain_one[...]).astype(HALF)

    row_blocks(rows, 16, norm)
    if n_fsdp == 2:
        size = wo_staged.shape[1]
        own_cols = span(core * size, size, size)
        wo_load.wait()

        def cast_out(at):
            wo_all[at, own_cols] = wo_staged[at, :].astype(HALF)

        row_blocks(chan, 32, cast_out)
        copy = pltpu.make_async_remote_copy(
            src_ref=wo_all.at[:, own_cols],
            dst_ref=wo_all.at[:, own_cols],
            send_sem=half_send.at[3],
            recv_sem=half_recv.at[3],
            device_id={"fsdp": 1 - core},
            device_id_type=MESH,
        )
        copy.start()
        halves_sent.append(copy)
    normed_store = pltpu.make_async_copy(normed, normed_out, store_sem.at[0])
    normed_store.start()
    flat = proj.reshape(3, rows, chan)
    band = rows
    if n_fsdp == 2:
        for gate in range(3):
            @pl.loop(0, rows // band)
            def _(index):
                at = span(index * band, band, band)
                cols = span(core * depth, depth, depth)
                flat[gate, at, :] = dot(normed[at, cols], w_all[own, gate_cols[gate]])

        for gate in range(3):
            halves_sent[gate].wait_recv()

            @pl.loop(0, rows // band)
            def _(index):
                at = span(index * band, band, band)
                other = span((1 - core) * depth, depth, depth)
                flat[gate, at, :] += dot(normed[at, other], w_all[other, gate_cols[gate]])
    else:
        for gate in range(3):
            w_loads[gate].wait()

            @pl.loop(0, rows // band)
            def _(index):
                at = span(index * band, band, band)
                flat[gate, at, :] = dot(normed[at, :], w_all[:, gate_cols[gate]])

    stores = [
        pltpu.make_async_copy(proj, proj_out, store_sem.at[1]),
        pltpu.make_async_copy(w_all, w_out, store_sem.at[2]),
    ]
    for store in stores:
        store.start()
    low = lower[...].reshape(1, 1, chan)
    row = lax.broadcasted_iota(jnp.int32, (n_seq, GROUP, chan), 1)

    def step(index, carry):
        prod, total = carry
        rows = pl.ds(pl.multiple_of(index * GROUP, GROUP), GROUP)
        inp = proj[0, :, rows, :]
        decay = low + (1.0 - low) * jax.nn.sigmoid(proj[1, :, rows, :])
        add = inp * jax.nn.sigmoid(inp) * (1.0 - decay)
        mult = decay * keep[:, rows, :]
        for hop in (1, 2, 4):
            inside = row >= hop
            add = jnp.where(inside, mult * pltpu.roll(add, hop, 1) + add, add)
            mult = jnp.where(inside, mult * pltpu.roll(mult, hop, 1), mult)
        add = add + mult * total
        mult = mult * prod
        local[:, rows, :] = add
        reach[:, rows, :] = mult
        return mult[:, GROUP - 1 :, :], add[:, GROUP - 1 :, :]

    start = (jnp.ones((n_seq, 1, chan), FLOAT), jnp.zeros((n_seq, 1, chan), FLOAT))
    prod, total = lax.fori_loop(0, length // GROUP, step, start)
    ends[here, 0] = prod.reshape(n_seq, chan)
    ends[here, 1] = total.reshape(n_seq, chan)
    share(ends, "ctx", n_ctx, ctx_send, ctx_recv)
    carry = jnp.zeros((n_seq, chan), FLOAT)
    for place in range(n_ctx - 1):
        carry = jnp.where(place < here, ends[place, 1] + ends[place, 0] * carry, carry)
    carry_out[...] = carry
    mine = lax.axis_index("tp")
    for seq in range(n_seq):
        for start in range(0, length, BLOCK):
            rows = slice(start, start + BLOCK)
            value = local[seq, rows, :] + reach[seq, rows, :] * carry[seq : seq + 1]
            state[seq, rows, :] = value
            squares[mine, seq : seq + 1, rows] = lane_sums(value * value)
    state_store = pltpu.make_async_copy(state, state_out, store_sem.at[3])
    state_store.start()
    share(squares, "tp", n_tp, tp_send, tp_recv)
    total = squares[0]
    for place in range(1, n_tp):
        total = total + squares[place]
    rate = lax.rsqrt(total / width + EPS)
    scale[...] = rate
    for seq in range(n_seq):
        for start in range(0, length, BLOCK):
            rows = slice(start, start + BLOCK)
            gate = proj[2, seq, rows, :]
            unit = state[seq, rows, :] * widen(columns(rate[seq : seq + 1, rows]), chan)
            swish = gate * jax.nn.sigmoid(gate)
            gated[seq, rows, :] = (unit * gate_gain[...] * swish).astype(HALF)
    for copy in halves_sent:
        copy.wait_send()
    if n_fsdp == 2:
        halves_sent[3].wait_recv()
        stores.append(pltpu.make_async_copy(wo_all, wo_out, load_sem.at[4]))
        stores[-1].start()
    else:
        stores.append(wo_load)
    for store in stores + [normed_store, state_store]:
        store.wait()


def run_head(
    gains, same, edges, gate_gain, lower, w_in, tokens, w_out, n_fsdp, n_ctx, n_tp
):
    n_seq, length, _ = same.shape
    rows, width = tokens.shape
    chan = w_in.shape[2]
    shape = (n_seq, length, chan)
    vmem = pl.BlockSpec(memory_space=pltpu.VMEM)
    hbm = pl.BlockSpec(memory_space=pl.ANY)
    staged = w_in.shape if n_fsdp == 2 else (3, 8, BLOCK)
    wo_staged = w_out.shape if n_fsdp == 2 else (8, BLOCK)
    dma = pltpu.SemaphoreType.DMA
    return pl.pallas_call(
        functools.partial(head, n_fsdp, n_ctx, n_tp),
        name="head",
        out_shape=(
            jax.ShapeDtypeStruct(shape, HALF),
            jax.ShapeDtypeStruct((n_seq, length), FLOAT),
            jax.ShapeDtypeStruct((n_seq, chan), FLOAT),
            jax.ShapeDtypeStruct((n_seq, length, 1), FLOAT),
            jax.ShapeDtypeStruct((1, width), FLOAT),
            jax.ShapeDtypeStruct((1, width), FLOAT),
            jax.ShapeDtypeStruct((3, *shape), FLOAT),
            jax.ShapeDtypeStruct(shape, FLOAT),
            jax.ShapeDtypeStruct((rows, width), HALF),
            jax.ShapeDtypeStruct((width, 3 * chan), HALF),
            jax.ShapeDtypeStruct((chan, width), HALF),
        ),
        in_specs=[vmem] * 5 + [hbm] * 3,
        out_specs=[vmem] * 6 + [hbm] * 5,
        scratch_shapes=[
            pltpu.VMEM(staged, FLOAT),
            pltpu.VMEM((width, 3 * chan), HALF),
            pltpu.VMEM(wo_staged, FLOAT),
            pltpu.VMEM((chan, width), HALF),
            pltpu.VMEM((rows, width), HALF),
            pltpu.VMEM((3, *shape), FLOAT),
            pltpu.VMEM(shape, FLOAT),
            pltpu.VMEM(shape, FLOAT),
            pltpu.VMEM(shape, FLOAT),
            pltpu.VMEM((n_ctx, 2, n_seq, chan), FLOAT),
            pltpu.VMEM((n_tp, n_seq, length), FLOAT),
            pltpu.VMEM((n_fsdp, *gains.shape), FLOAT),
            pltpu.VMEM((n_ctx, *edges.shape[1:]), FLOAT),
            dma((5,)), dma((4,)), dma((4,)), dma((4,)), dma((n_ctx,)), dma((n_ctx,)),
            dma((n_tp,)), dma((n_tp,)), dma((n_fsdp,)), dma((n_fsdp,)), dma((n_ctx,)), dma((n_ctx,)),
        ],
        compiler_params=pltpu.CompilerParams(
            collective_id=0, has_side_effects=True, vmem_limit_bytes=63 * MIB
        ),
    )(gains, same, edges, gate_gain, lower, w_in, tokens, w_out)


def gather_fsdp(part, dim):
    return lax.all_gather(part, "fsdp", axis=dim, tiled=True)


def local(
    sizes,
    tokens, segment_ids, w_in, w_out, w_glu, w_down, gain_one, gain_two, gate_gain, lower, cotangent,
):
    n_fsdp, n_ctx, n_tp = sizes
    n_seq, length, width = tokens.shape
    rows = n_seq * length
    chan = w_in.shape[2]
    x_half = tokens.reshape(rows, width)
    parts = (w_glu[:, 0].astype(HALF), w_glu[:, 1].astype(HALF), w_down)
    if n_fsdp != 2:
        parts = (*parts[:2], w_down.astype(HALF))
        parts = tuple(gather_fsdp(part, dim) for part, dim in zip(parts, (0, 0, 1)))
        w_in = gather_fsdp(w_in.astype(HALF), 1)
        w_out = gather_fsdp(w_out.astype(HALF), 1)
    gain_gate = gate_gain[None]
    low = lower[None]
    seg = segment_ids.astype(FLOAT)
    same = jnp.pad((seg[:, 1:] == seg[:, :-1]).astype(FLOAT), ((0, 0), (1, 0)))[..., None]
    edges = jnp.broadcast_to(jnp.stack([seg[:, 0], seg[:, -1]])[..., None], (2, n_seq, BLOCK))
    (
        gated, gate_scale, carry, keep, gain_a, gain_b, proj, state, normed, w_in_all, w_out_all
    ) = run_head(
        jnp.stack([gain_one, gain_two]), same, edges, gain_gate, low, w_in, x_half, w_out,
        n_fsdp, n_ctx, n_tp,
    )
    gated = gated.reshape(rows, chan)
    grad_y_half = cotangent.reshape(rows, width)
    (
        mixed, _, act, _, grad_resid, grad_mixed, grad_gated, grad_w_gate, grad_w_up, w_down_all,
        grad_gain_two,
    ) = run_middle(
        gated, x_half, grad_y_half, gain_b, (w_out_all, *parts), n_fsdp, n_ctx, length
    )
    if n_fsdp == 2:
        grad_w_up = lax.psum(grad_w_up, "ctx")
    grad_tokens, output, vectors, grad_w_in, grad_w_out, grad_w_down = run_tail(
        (keep, gain_gate, low, gate_scale, carry, gain_a, grad_gain_two),
        (
            proj, state, grad_gated.reshape(n_seq, length, chan), w_in_all, w_down_all, act, normed,
            grad_mixed, gated, grad_y_half, grad_resid, x_half, mixed,
        ),
        n_fsdp, n_ctx, n_tp,
    )
    grads = (grad_w_in, grad_w_out, grad_w_gate, grad_w_up, grad_w_down)
    if n_fsdp != 2:
        grads = tuple(
            lax.psum(lax.psum_scatter(value, "fsdp", scatter_dimension=dim, tiled=True), "ctx")
            for value, dim in zip(grads, (0, 1, 0, 0, 1))
        )
    results = run_widen_outputs(*grads, grad_tokens, output, vectors)
    grad_w_in, grad_w_out, grad_w_glu, grad_w_down, grad_tokens, output = results[:6]
    return (
        output.reshape(n_seq, length, width),
        grad_tokens.reshape(n_seq, length, width),
        grad_w_in,
        grad_w_out,
        grad_w_glu,
        grad_w_down,
        *(vector[0] for vector in results[6:]),
    )


def solution(mesh):
    sizes = tuple(mesh.shape[axis] for axis in ("fsdp", "ctx", "tp"))
    return jax.shard_map(
        functools.partial(local, sizes),
        mesh=mesh,
        in_specs=(
            P("fsdp", "ctx", None),
            P("fsdp", "ctx"),
            P(None, "fsdp", "tp"),
            P("tp", "fsdp"),
            P("fsdp", None, "tp"),
            P("tp", "fsdp"),
            P("fsdp"),
            P("fsdp"),
            P("tp"),
            P("tp"),
            P("fsdp", "ctx", None),
        ),
        out_specs=(
            P("fsdp", "ctx", None),
            P("fsdp", "ctx", None),
            P(None, "fsdp", "tp"),
            P("tp", "fsdp"),
            P("fsdp", None, "tp"),
            P("tp", "fsdp"),
            P("fsdp"),
            P("fsdp"),
            P("tp"),
            P("tp"),
        ),
        check_vma=False,
    )
```

```python
import functools

import jax
import jax.numpy as jnp
from jax import lax
from jax.experimental import pallas as pl
from jax.experimental.pallas import tpu as pltpu
from jax.sharding import PartitionSpec as P

EPS = 1e-06
FLOAT = jnp.float32
HALF = jnp.bfloat16
MESH = pl.DeviceIdType.MESH
GROUP = 8
BLOCK = 128
MIB = 1 << 20


def rms_scale(values):
    return lax.rsqrt(jnp.mean(values * values, -1, keepdims=True) + EPS)


def silu_slope(values):
    sig = jax.nn.sigmoid(values)
    return sig * (1.0 + values * (1.0 - sig))


def greet(peers):
    barrier = pltpu.get_barrier_semaphore()
    for peer in peers:
        pl.semaphore_signal(barrier, inc=1, device_id=peer, device_id_type=MESH)
    pl.semaphore_wait(barrier, len(peers))


def others(axis, count):
    mine = lax.axis_index(axis)
    return [{axis: lax.rem(mine + step, count)} for step in range(1, count)]


def shares(slots, axis, count, send, recv):
    mine = lax.axis_index(axis)
    return [
        pltpu.make_async_remote_copy(
            src_ref=slots.at[mine],
            dst_ref=slots.at[mine],
            send_sem=send.at[step],
            recv_sem=recv.at[step],
            device_id=peer,
            device_id_type=MESH,
        )
        for step, peer in enumerate(others(axis, count))
    ]


def share(slots, axis, count, send, recv):
    copies = shares(slots, axis, count, send, recv)
    for copy in copies:
        copy.start()
    for copy in copies:
        copy.wait()


def lane_sums(values):
    part = values[:, :BLOCK]
    for start in range(BLOCK, values.shape[1], BLOCK):
        part = part + values[:, start : start + BLOCK]
    return jnp.sum(part.T, 0, keepdims=True)


def columns(row):
    return jnp.broadcast_to(row, (BLOCK, BLOCK)).T


def widen(values, chan):
    return jnp.concatenate([values] * (chan // BLOCK), -1)


PIECES = 4
TILE = 256
WIDE = 512


def bands(count, size):
    return [(start, min(size, count - start)) for start in range(0, count, size)]


def dot(lhs, rhs):
    return jnp.dot(lhs, rhs, preferred_element_type=FLOAT)


def dot_nt(lhs, rhs):
    return lax.dot_general(lhs, rhs, (((1,), (1,)), ((), ())), preferred_element_type=FLOAT)


class Line:
    def __init__(self, held, cross, total, sems):
        self.held, self.cross, self.total, self.sems = held, cross, total, sems
        place = lax.axis_index("tp")
        self.inner = (place == 1) | (place == 2)
        self.side = place + 1 - 2 * lax.rem(place, 2)
        self.facing = 3 - place

    def slot(self, job, ref):
        slots = ref.shape[0]
        if slots == self.total.shape[0]:
            return job
        return job % slots if isinstance(job, int) else lax.rem(job, slots)

    def copy(self, source, target, send, recv, place):
        return pltpu.make_async_remote_copy(
            src_ref=source,
            dst_ref=target,
            send_sem=send,
            recv_sem=recv,
            device_id={"tp": place},
            device_id_type=MESH,
        )

    def inward(self, job, q):
        send, recv, _, _ = self.sems
        return self.copy(
            self.held.at[self.slot(job, self.held), q], self.total.at[job, q],
            send.at[job, q], recv.at[job, q], self.side,
        )

    def outward(self, job, q):
        send, recv, _, _ = self.sems
        return self.copy(
            self.total.at[job, q], self.total.at[job, q],
            send.at[job, q], recv.at[job, q], self.side,
        )

    def across(self, job, q):
        _, _, send, recv = self.sems
        return self.copy(
            self.held.at[self.slot(job, self.held), q], self.cross.at[self.slot(job, self.cross), q],
            send.at[job, q], recv.at[job, q], self.facing,
        )

    def offer(self, job, q):
        @pl.when(jnp.logical_not(self.inner))
        def _():
            self.inward(job, q).start()

    def forward(self, job, q):
        slot = self.slot(job, self.held)

        @pl.when(self.inner)
        def _():
            self.inward(job, q).wait_recv()
            self.held[slot, q] = self.held[slot, q] + self.total[job, q]
            self.across(job, q).start()

    def close(self, job, q):
        slot, cross_slot = self.slot(job, self.held), self.slot(job, self.cross)

        @pl.when(self.inner)
        def _():
            self.across(job, q).wait_recv()
            self.total[job, q] = self.held[slot, q] + self.cross[cross_slot, q]
            self.outward(job, q).start()

    def tick(self, base, step):
        if step > 0:
            self.close(base, step - 1)
        if step < PIECES:
            ahead = step + 1
            self.forward(base + ahead // PIECES, ahead % PIECES)

    def arrive(self, job):
        @pl.when(jnp.logical_not(self.inner))
        def _():
            @pl.loop(0, PIECES)
            def _(q):
                self.outward(job, q).wait_recv()

    def release(self, job):
        @pl.when(self.inner)
        def _():
            @pl.loop(0, PIECES)
            def _(q):
                self.across(job, q).wait_send()

        @pl.when(jnp.logical_not(self.inner))
        def _():
            @pl.loop(0, PIECES)
            def _(q):
                self.inward(job, q).wait_send()

    def settle(self, job):
        @pl.when(self.inner)
        def _():
            @pl.loop(0, PIECES)
            def _(q):
                self.outward(job, q).wait_send()


def span(start, size, unit):
    return pl.ds(pl.multiple_of(start, unit), size)


def row_blocks(count, size, body):
    @pl.loop(0, count // size)
    def _(index):
        body(pl.ds(pl.multiple_of(index * size, size), size))


def line_peers():
    place = lax.axis_index("tp")
    return [{"tp": place + 1 - 2 * lax.rem(place, 2)}, {"tp": 3 - place}]


def joined(ref, c, rows):
    return jnp.concatenate([ref[c, q, rows, :].astype(FLOAT) for q in range(PIECES)], -1)


def add_to(target, extra, rows):
    target[rows, :] = target[rows, :] + extra[rows, :]


def halves(n_fsdp, store_sem, send_sem, recv_sem, spare, inbox):
    mine = lax.axis_index("fsdp")
    pending = {}

    def send(index, view):
        slot = index % 2
        return pltpu.make_async_remote_copy(
            src_ref=view(spare.at[slot]),
            dst_ref=view(inbox.at[slot]),
            send_sem=send_sem.at[slot],
            recv_sem=recv_sem.at[slot],
            device_id={"fsdp": 1 - mine},
            device_id_type=MESH,
        )

    def item(index, view, compute_other, compute_own, other_place, target):
        slot = index % 2
        if index - 2 in pending:
            pending.pop(index - 2)()
        compute_other(view(spare.at[slot]))
        if n_fsdp == 2:
            copy = send(index, view)
            copy.start()
            pending[index] = lambda: send(index, view).wait_send()
        else:
            def store():
                return pltpu.make_async_copy(view(spare.at[slot]), other_place(), store_sem.at[slot])

            store().start()
            pending[index] = lambda: store().wait()
        compute_own(target)
        if n_fsdp == 2:
            send(index, view).wait_recv()
            extra = view(inbox.at[slot])
            row_blocks(target.shape[0], 32, lambda rows: add_to(target, extra, rows))

    def finish():
        for wait in pending.values():
            wait()

    return item, finish


class Square:
    def __init__(self, index, buffers, at, place, send, recv, store_sem):
        self.buffers, self.at, self.place_of = buffers, at, place
        self.send, self.recv, self.index, self.store_sem = send, recv, index, store_sem

    @property
    def tile(self):
        return self.buffers[0].at[self.at[0]]

    @property
    def half(self):
        return self.buffers[1].at[self.at[1]]

    @property
    def quarter(self):
        return self.buffers[2].at[self.at[2]]

    def geometry(self):
        here = lax.axis_index("ctx")
        low, high = lax.rem(here, 2), here // 2
        near, far = here + 1 - 2 * low, here + 2 - 4 * high
        bits = (low, high) if self.index % 2 == 0 else (high, low)
        peers = (near, far) if self.index % 2 == 0 else (far, near)
        wide, thin = self.half.shape[0], self.quarter.shape[0]
        begin = bits[0] * wide
        return (
            peers,
            span(begin, wide, wide),
            span((1 - bits[0]) * wide, wide, wide),
            span(begin + bits[1] * thin, thin, thin),
            span(begin + (1 - bits[1]) * thin, thin, thin),
        )

    def round(self, number):
        peers, mine, yours, my_part, your_part = self.geometry()
        source, target, peer = (
            (self.tile.at[yours], self.half, 0),
            (self.tile.at[your_part], self.quarter, 1),
            (self.tile.at[my_part], self.place_of().at[my_part], 1),
            (self.place_of().at[mine], self.place_of().at[mine], 0),
        )[number]
        return pltpu.make_async_remote_copy(
            src_ref=source,
            dst_ref=target,
            send_sem=self.send.at[self.index, number],
            recv_sem=self.recv.at[self.index, number],
            device_id={"ctx": peers[peer]},
            device_id_type=MESH,
        )

    def add(self, part, extra):
        target = self.tile.at[part]
        row_blocks(extra.shape[0], 32, lambda rows: add_to(target, extra, rows))

    def store(self):
        return pltpu.make_async_copy(self.tile, self.place_of(), self.store_sem.at[self.index])

    def store_part(self):
        part = self.geometry()[3]
        return pltpu.make_async_copy(
            self.tile.at[part], self.place_of().at[part], self.store_sem.at[self.index]
        )

    def advance(self, number):
        if number > 0:
            self.round(number - 1).wait_recv()
        if number == 1:
            self.add(self.geometry()[1], self.half)
        if number == 2:
            self.add(self.geometry()[3], self.quarter)
            self.store_part().start()
        if number == 3:
            self.store_part().wait()
        if number < 4:
            self.round(number).start()

    def settle(self):
        for number in range(4):
            self.round(number).wait_send()


def fill(target, left, right, first):
    for start, size in bands(target.shape[1], WIDE):
        cols = pl.ds(pl.multiple_of(first + start, BLOCK), size)
        target[:, start : start + size] = dot(left, right[:, cols]).astype(HALF)


def middle(
    n_fsdp, n_ctx, CHUNK,
    gated, tokens, cotangent, gain, wo_part, wg_part, wu_part, wd_part,
    mixed_out, normed_out, act_out, grad_glu_out, grad_resid_out, grad_mixed_out,
    grad_gated_out, w_gate_out, w_up_out, w_down_out, grad_gain_out,
    wo, wg, wu, wd, x_all, dy_all, held, crossed, total, normed, act, grad_glu,
    grad_resid, grad_mixed, grad_gated, gain_total, spare, inbox, half, quarter,
    square_send, square_recv, square_store, weight_sem, weight_send, weight_recv, again_sem,
    own_sem, stage_sem, glu_send, glu_recv, down_send, down_recv,
    load_sem, store_sem, *line_sems,
):
    n_chunks, _, _, piece = held.shape
    units = wd.shape[0]
    width = wd.shape[1]
    peers = line_peers() + others("ctx", n_ctx)
    if n_fsdp == 2:
        peers.append({"fsdp": 1 - lax.axis_index("fsdp")})
    local_parts = [(wo_part, wo)]
    if n_fsdp != 2:
        local_parts += [(wg_part, wg), (wu_part, wu), (wd_part, wd)]
    ready = [
        pltpu.make_async_copy(part, whole, own_sem.at[index])
        for index, (part, whole) in enumerate(local_parts)
    ]
    for copy in ready:
        copy.start()
    greet(peers)
    core = lax.axis_index("fsdp")
    n_bands = units // BLOCK

    def to_sibling(place, send, recv):
        return pltpu.make_async_remote_copy(
            src_ref=place,
            dst_ref=place,
            send_sem=send,
            recv_sem=recv,
            device_id={"fsdp": 1 - core},
            device_id_type=MESH,
        )

    def glu_copies(number):
        part, whole = ((wg_part, wg), (wu_part, wu))[number]
        at = span(core * (width // 2), width // 2, width // 2)
        far = pltpu.make_async_remote_copy(
            src_ref=part,
            dst_ref=whole.at[at],
            send_sem=glu_send.at[number],
            recv_sem=glu_recv.at[number],
            device_id={"fsdp": 1 - core},
            device_id_type=MESH,
        )
        return far, pltpu.make_async_copy(part, whole.at[at], own_sem.at[1 + number])

    def down_stage(index):
        return grad_resid.at[span(lax.rem(index, 2) * BLOCK, BLOCK, BLOCK), : width // 2]

    def down_load(index):
        return pltpu.make_async_copy(
            wd_part.at[span(index * BLOCK, BLOCK, BLOCK)], down_stage(index),
            stage_sem.at[lax.rem(index, 2)],
        )

    def down_copy(index):
        cols = span(core * (width // 2), width // 2, width // 2)
        place = wd.at[span(index * BLOCK, BLOCK, BLOCK), cols]
        return to_sibling(place, down_send.at[index], down_recv.at[index])

    def down_band(index):
        down_load(index).wait()
        cols = span(core * (width // 2), width // 2, width // 2)
        wd[span(index * BLOCK, BLOCK, BLOCK), cols] = down_stage(index)[...].astype(HALF)

        @pl.when(index + 2 < n_bands)
        def _():
            down_load(index + 2).start()

        down_copy(index).start()

    if n_fsdp == 2:
        for first_load in (*glu_copies(0), *glu_copies(1), down_load(0), down_load(1)):
            first_load.start()
    loads = [
        pltpu.make_async_copy(tokens, x_all, load_sem.at[0]),
        pltpu.make_async_copy(cotangent, dy_all, load_sem.at[1]),
    ]
    for load in loads:
        load.start()
    line = Line(held, crossed, total, line_sems)

    def chunk_rows(c):
        return pl.ds(pl.multiple_of(c * CHUNK, CHUNK), CHUNK)

    def stores(c, wanted=None):
        rows = chunk_rows(c)
        pairs = [
            (normed, normed_out.at[rows]),
            (act, act_out.at[rows]),
            (grad_glu.at[0], grad_glu_out.at[0, rows]),
            (grad_glu.at[1], grad_glu_out.at[1, rows]),
            (grad_resid, grad_resid_out.at[rows]),
            (grad_mixed, grad_mixed_out.at[rows]),
            (grad_gated, grad_gated_out.at[rows]),
        ]
        pairs += [
            (total.at[c, q], mixed_out.at[rows, pl.ds(q * piece, piece)]) for q in range(PIECES)
        ]
        return [
            pltpu.make_async_copy(source, target, store_sem.at[index])
            for index, (source, target) in enumerate(pairs)
            if wanted is None or index in wanted
        ]

    FORWARD = (0, 1, 2, 3, 7, 8, 9, 10)
    BACKWARD = (4, 5, 6)

    ready[0].wait()

    @pl.loop(0, n_chunks)
    def _(c):
        lhs = gated[chunk_rows(c), :]

        @pl.loop(0, PIECES)
        def _(q):
            cols = pl.ds(pl.multiple_of(q * piece, piece), piece)
            held[c, q] = dot(lhs, wo[:, cols]).astype(HALF)
            line.offer(c, q)

    for load in loads:
        load.wait()
    def cast_down(part):
        pl.loop(part * n_bands // 4, (part + 1) * n_bands // 4)(down_band)

    for step in range(PIECES + 2):
        if n_fsdp == 2 and step < 4:
            cast_down(step)
        if step == 0:
            line.forward(0, 0)
        else:
            line.tick(0, step - 1)

    w_down_store = pltpu.make_async_copy(wd, w_down_out, again_sem.at[3])

    def weights_here():
        for copy in ready[1:]:
            copy.wait()
        if n_fsdp == 2:
            for copy in (*glu_copies(0), *glu_copies(1)):
                copy.wait()

            @pl.loop(0, n_bands)
            def _(index):
                down_copy(index).wait()

        w_down_store.start()

    @pl.loop(0, n_chunks)
    def _(c):
        line.arrive(c)
        line.tick(c + 1, 0)

        @pl.when(c > 0)
        def _():
            for store in stores(c - 1, FORWARD):
                store.wait()

        def norm(rows):
            at = pl.ds(pl.multiple_of(c * CHUNK + rows.start, 16), rows.size)
            resid = x_all[at, :].astype(FLOAT) + joined(total, c, rows)
            normed[rows, :] = (resid * rms_scale(resid) * gain[...]).astype(HALF)

        row_blocks(CHUNK, 16, norm)
        pl.when(c == 0)(weights_here)

        def unit(cols):
            glu_gate = dot(normed[...], wg[:, cols])
            glu_up = dot(normed[...], wu[:, cols])
            grad_act = dot_nt(dy_all[chunk_rows(c), :], wd[cols, :])
            sig = jax.nn.sigmoid(glu_gate)
            silu = glu_gate * sig
            act[:, cols] = (silu * glu_up).astype(HALF)
            slope = sig * (1.0 + glu_gate * (1.0 - sig))
            grad_glu[0, :, cols] = (grad_act * glu_up * slope).astype(HALF)
            grad_glu[1, :, cols] = (grad_act * silu).astype(HALF)

        for index, (start, size) in enumerate(bands(units, WIDE)):
            unit(slice(start, start + size))
            if index == 0:
                line.tick(c + 1, 1)
        line.tick(c + 1, 2)
        line.release(c)

        @pl.loop(0, PIECES)
        def _(q):
            @pl.when(q == PIECES // 2)
            def _():
                line.tick(c + 1, 3)

            at = pl.ds(pl.multiple_of(q * piece, piece), piece)
            value = dot_nt(grad_glu[0], wg[at, :]) + dot_nt(grad_glu[1], wu[at, :])
            held[c, q] = value.astype(HALF)
            line.offer(n_chunks + c, q)

        line.tick(c + 1, 4)

        for store in stores(c, FORWARD):
            store.start()

    for store in stores(n_chunks - 1, FORWARD):
        store.wait()
    rows = n_chunks * CHUNK
    w_down_store.wait()
    kept = [
        (grad_glu_out.at[0], wg.at[:rows]),
        (grad_glu_out.at[1], wu.at[:rows]),
        (normed_out, wd.at[:rows]),
    ]
    again = [
        pltpu.make_async_copy(source, target, again_sem.at[index])
        for index, (source, target) in enumerate(kept)
    ]
    for copy in again:
        copy.start()
    gain_total[...] = jnp.zeros_like(gain_total)
    item, finish = halves(n_fsdp, weight_sem, weight_send, weight_recv, spare, inbox)
    mine = lax.axis_index("fsdp") if n_fsdp == 2 else 1
    depth = width // 2
    whole = n_fsdp != 2
    per_part = depth // TILE
    squares, plain, turn = [], [], [0]

    def weight_item(index):
        if index >= 2 * per_part:
            return
        part, k = divmod(index, per_part)
        right = (wg, wu)[part].at[:rows]
        out = (w_gate_out, w_up_out)[part]

        def compute(side):
            at = pl.ds(pl.multiple_of(side * depth + k * TILE, TILE), TILE)
            return lambda target: fill(target, wd[:rows, at].T, right, 0)

        at = slice(k * TILE + whole * depth, (k + 1) * TILE + whole * depth)
        square = Square(
            index, ((wg, wu)[part], half, quarter),
            (slice(rows + k * TILE, rows + (k + 1) * TILE), k, k), lambda: out.at[at],
            square_send, square_recv, square_store,
        )
        item(
            index, lambda ref: ref, compute(1 - mine), compute(mine),
            lambda: out.at[k * TILE : (k + 1) * TILE], square.tile,
        )
        if whole or part == 1:
            square.store().start()
            plain.append(square)
        else:
            squares.append([square, 0, turn[0]])

    def pump():
        for square in squares:
            if square[1] < 5 and turn[0] >= square[2] + 3 * square[1]:
                square[0].advance(square[1])
                square[1] += 1
        turn[0] += 1

    def backward(c, between):
        line.arrive(n_chunks + c)
        if c > 0:
            for store in stores(c - 1, BACKWARD):
                store.wait()

        def norm_back(rows):
            at = pl.ds(pl.multiple_of(c * CHUNK + rows.start, 16), rows.size)
            resid = x_all[at, :].astype(FLOAT) + joined(total, c, rows)
            rate = rms_scale(resid)
            grad = joined(total, n_chunks + c, rows)
            by_gain = grad * (resid * rate)
            gain_total[...] += by_gain[:8] + by_gain[8:]
            inner = gain[...] * grad
            mean = jnp.mean(inner * resid, -1, keepdims=True)
            value = dy_all[at, :].astype(FLOAT) + rate * inner - resid * (rate * rate * rate * mean)
            grad_resid[rows, :] = value
            grad_mixed[rows, :] = value.astype(HALF)

        row_blocks(CHUNK, 16, norm_back)
        between()
        for start, size in bands(grad_gated.shape[1], WIDE):
            grad_gated[:, start : start + size] = dot_nt(
                grad_mixed[...], wo[start : start + size, :]
            )
        for store in stores(c, BACKWARD):
            store.start()

    for copy in again:
        copy.wait()
    count = 0
    for c in range(n_chunks):
        if c == n_chunks - 1:
            while count < 2 * per_part:
                weight_item(count)
                count += 1
        if c + 1 == n_chunks:
            backward(c, lambda: None)
            continue

        def between():
            line.tick(n_chunks + c + 1, 0)
            pump()

        backward(c, between)
        for step in range(1, PIECES + 1):
            weight_item(count)
            count += 1
            if c + 2 == n_chunks and step == PIECES - 1:
                line.close(2 * n_chunks - 1, step - 1)
            else:
                line.tick(n_chunks + c + 1, step)
            pump()
    while any(square[1] < 5 for square in squares):
        pump()
    finish()
    for square, _, _ in squares:
        square.settle()
    for square in plain:
        square.store().wait()

    grad_gain_out[...] = jnp.sum(gain_total[...], 0, keepdims=True)
    for store in stores(n_chunks - 1, BACKWARD):
        store.wait()

    @pl.loop(0, n_chunks)
    def _(c):
        line.settle(c)
        line.settle(n_chunks + c)
        line.release(n_chunks + c)


def run_middle(gated, tokens, cotangent, gain, parts, n_fsdp, n_ctx, length):
    rows, chan = gated.shape
    width = tokens.shape[1]
    units = parts[3].shape[0]
    n_chunks = rows // length
    piece = width // PIECES
    vmem = pl.BlockSpec(memory_space=pltpu.VMEM)
    hbm = pl.BlockSpec(memory_space=pl.ANY)
    sems = pltpu.SemaphoreType.DMA((2 * n_chunks, PIECES))
    return pl.pallas_call(
        functools.partial(middle, n_fsdp, n_ctx, length),
        name="middle",
        out_shape=(
            jax.ShapeDtypeStruct((rows, width), HALF),
            jax.ShapeDtypeStruct((rows, width), HALF),
            jax.ShapeDtypeStruct((rows, units), HALF),
            jax.ShapeDtypeStruct((2, rows, units), HALF),
            jax.ShapeDtypeStruct((rows, width), FLOAT),
            jax.ShapeDtypeStruct((rows, width), HALF),
            jax.ShapeDtypeStruct((rows, chan), FLOAT),
            jax.ShapeDtypeStruct((width if n_fsdp != 2 else width // 2, units), HALF),
            jax.ShapeDtypeStruct((width if n_fsdp != 2 else width // 2, units), HALF),
            jax.ShapeDtypeStruct((units, width), HALF),
            jax.ShapeDtypeStruct((1, width), FLOAT),
        ),
        in_specs=[vmem, hbm, hbm, vmem, hbm, hbm, hbm, hbm],
        out_specs=[hbm] * 10 + [vmem],
        scratch_shapes=[
            pltpu.VMEM((chan, width), HALF),
            pltpu.VMEM((width, units), HALF),
            pltpu.VMEM((width, units), HALF),
            pltpu.VMEM((units, width), HALF),
            pltpu.VMEM((rows, width), HALF),
            pltpu.VMEM((rows, width), HALF),
            pltpu.VMEM((n_chunks, PIECES, length, piece), HALF),
            pltpu.VMEM((n_chunks, PIECES, length, piece), HALF),
            pltpu.VMEM((2 * n_chunks, PIECES, length, piece), HALF),
            pltpu.VMEM((length, width), HALF),
            pltpu.VMEM((length, units), HALF),
            pltpu.VMEM((2, length, units), HALF),
            pltpu.VMEM((length, width), FLOAT),
            pltpu.VMEM((length, width), HALF),
            pltpu.VMEM((length, chan), FLOAT),
            pltpu.VMEM((8, width), FLOAT),
            pltpu.VMEM((2, TILE, units), HALF),
            pltpu.VMEM((2, TILE, units), HALF),
            pltpu.VMEM((width // 2 // TILE, TILE // 2, units), HALF),
            pltpu.VMEM((width // 2 // TILE, TILE // 4, units), HALF),
            pltpu.SemaphoreType.DMA((width // 2 // TILE, 4)),
            pltpu.SemaphoreType.DMA((width // 2 // TILE, 4)),
            pltpu.SemaphoreType.DMA((width // TILE,)),
            pltpu.SemaphoreType.DMA((4,)),
            pltpu.SemaphoreType.DMA((2,)),
            pltpu.SemaphoreType.DMA((2,)),
            pltpu.SemaphoreType.DMA((4,)),
            pltpu.SemaphoreType.DMA((4,)),
            pltpu.SemaphoreType.DMA((2,)),
            pltpu.SemaphoreType.DMA((2,)),
            pltpu.SemaphoreType.DMA((2,)),
            pltpu.SemaphoreType.DMA((units // BLOCK,)),
            pltpu.SemaphoreType.DMA((units // BLOCK,)),
            pltpu.SemaphoreType.DMA((2,)),
            pltpu.SemaphoreType.DMA((12,)),
        ]
        + [sems] * 4,
        compiler_params=pltpu.CompilerParams(
            collective_id=2, has_side_effects=True, vmem_limit_bytes=63 * MIB
        ),
        cost_estimate=pl.CostEstimate(
            flops=16 * rows * width * units, bytes_accessed=400 * MIB, transcendentals=0
        ),
    )(gated, tokens, cotangent, gain, *parts)


def scan_cross(gate_all, state, scale, gain, near, grad_proj, gain_out, cross):
    n_seq, length, chan = state.shape
    mine = lax.axis_index("tp")
    gain_total = jnp.zeros((8, chan), FLOAT)
    for seq in range(n_seq):
        for start in range(0, length, BLOCK):
            rows = slice(start, start + BLOCK)
            rate = columns(scale[seq : seq + 1, rows])
            gate = gate_all[seq, rows, :]
            sig = jax.nn.sigmoid(gate)
            swish = gate * sig
            value = state[seq, rows, :]
            into = near[seq, rows, :]
            by_unit = into * value * widen(rate, chan)
            slope = sig * (1.0 + gate * (1.0 - sig))
            grad_proj[seq, rows, 2 * chan :] = (by_unit * gain[...] * slope).astype(HALF)
            gain_total = gain_total + jnp.sum((by_unit * swish).reshape(-1, 8, chan), 0)
            grad_unit = into * swish * gain[...]
            near[seq, rows, :] = grad_unit
            cross[mine, seq : seq + 1, rows] = lane_sums(grad_unit * value)
    gain_out[...] = jnp.sum(gain_total, 0, keepdims=True)


def scan_back(
    n_ctx, n_tp, width, pump,
    proj, keep, lower, state, scale, carry_in, near,
    grad_proj, lower_out,
    reach, rate_wide, cross_wide, ends, cross, ctx_sems,
):
    n_seq, length, chan = state.shape
    low = lower[...].reshape(1, 1, chan)
    total = cross[0]
    for place in range(1, n_tp):
        total = total + cross[place]
    rate = scale[...]
    total = total * (rate * rate * rate) / width
    for seq in range(n_seq):
        for start in range(0, length, BLOCK):
            rows = slice(start, start + BLOCK)
            rate_wide[seq, rows, :] = columns(rate[seq : seq + 1, rows])
            cross_wide[seq, rows, :] = columns(total[seq : seq + 1, rows])

    row = lax.broadcasted_iota(jnp.int32, (n_seq, GROUP, chan), 1)

    def back(index, carry):
        prod, above = carry
        rows = pl.ds(pl.multiple_of((length // GROUP - 1 - index) * GROUP, GROUP), GROUP)
        decay = low + (1.0 - low) * jax.nn.sigmoid(proj[1, :, rows, :])
        mult = decay * keep[:, rows, :]
        direct = (
            widen(rate_wide[:, rows, :], chan) * near[:, rows, :]
            - widen(cross_wide[:, rows, :], chan) * state[:, rows, :]
        )
        add = mult * direct
        for hop in (1, 2, 4):
            inside = row < GROUP - hop
            add = jnp.where(inside, mult * pltpu.roll(add, GROUP - hop, 1) + add, add)
            mult = jnp.where(inside, mult * pltpu.roll(mult, GROUP - hop, 1), mult)
        add = add + mult * above
        mult = mult * prod
        inside = row < GROUP - 1
        near[:, rows, :] = direct + jnp.where(inside, pltpu.roll(add, GROUP - 1, 1), above)
        reach[:, rows, :] = jnp.where(inside, pltpu.roll(mult, GROUP - 1, 1), prod)
        return mult[:, :1, :], add[:, :1, :]

    held = (jnp.ones((n_seq, 1, chan), FLOAT), jnp.zeros((n_seq, 1, chan), FLOAT))
    middle_of = length // GROUP // 2
    held = lax.fori_loop(0, middle_of, back, held)
    pump()
    prod, total = lax.fori_loop(middle_of, length // GROUP, back, held)
    here = lax.axis_index("ctx")
    ends[here, 0] = prod.reshape(n_seq, chan)
    ends[here, 1] = total.reshape(n_seq, chan)
    pump()
    share(ends, "ctx", n_ctx, *ctx_sems)
    carry = jnp.zeros((n_seq, chan), FLOAT)
    for place in range(n_ctx - 1, 0, -1):
        carry = jnp.where(place > here, ends[place, 1] + ends[place, 0] * carry, carry)
    carry = carry.reshape(n_seq, 1, chan)
    wide = 2 * GROUP
    first = lax.broadcasted_iota(jnp.int32, (n_seq, wide, chan), 1) == 0

    def finish(index, held):
        before, low_total = held
        rows = pl.ds(pl.multiple_of(index * wide, wide), wide)
        inp = proj[0, :, rows, :]
        sig = jax.nn.sigmoid(inp)
        silu = inp * sig
        fsig = jax.nn.sigmoid(proj[1, :, rows, :])
        rest = 1.0 - fsig
        decay = low + (1.0 - low) * fsig
        grad_state = near[:, rows, :] + reach[:, rows, :] * carry
        value = state[:, rows, :]
        prev = jnp.where(first, before, pltpu.roll(value, 1, 1))
        grad_decay = grad_state * (prev * keep[:, rows, :] - silu)
        grad_proj[:, rows, :chan] = (
            grad_state * (1.0 - decay) * (sig * (1.0 + inp * (1.0 - sig)))
        ).astype(HALF)
        grad_proj[:, rows, chan : 2 * chan] = (
            grad_decay * (1.0 - low) * fsig * rest
        ).astype(HALF)
        return value[:, wide - 1 :, :], low_total + grad_decay * rest

    held = (carry_in[...].reshape(n_seq, 1, chan), jnp.zeros((n_seq, wide, chan), FLOAT))
    middle_of = length // wide // 2
    held = lax.fori_loop(0, middle_of, finish, held)
    pump()
    _, low_total = lax.fori_loop(middle_of, length // wide, finish, held)
    lower_out[...] = jnp.sum(jnp.sum(low_total, 0), 0, keepdims=True)
    pump()


def tail(
    n_fsdp, n_ctx, n_tp,
    keep, gate_gain, lower, scale, carry_in, gain, gain_two_grad,
    proj, state, grad_gated, w_in, w_down, act, normed, grad_mixed, gated, cotangent,
    grad_resid, tokens, mixed,
    grad_tokens_out, output_out, vectors_out, w_in_out, w_out_out, w_down_out,
    grad_proj, held, crossed, total, spare, inbox,
    in_tile, in_half, in_quarter, out_tile, out_half, out_quarter, down_tile, down_half, down_quarter,
    gain_total, ends, cross, over_ctx, over_fsdp, near,
    load_sem, store_sem, end_send, end_recv, cross_send, cross_recv, ctx_send, ctx_recv,
    fsdp_send, fsdp_recv, part_sem, part_send, part_recv, square_send, square_recv, square_store,
    *line_sems,
):
    n_seq, length, wide = grad_proj.shape
    chan = wide // 3
    rows = n_seq * length
    width = gain.shape[1]
    units = w_down.shape[0]
    piece = width // PIECES
    n_chunks = n_seq
    whole = n_fsdp != 2
    line = Line(held, crossed, total, line_sems)
    pieces = [(job, q) for job in range(2 * n_chunks) for q in range(PIECES)]
    relay = [(line.forward, spot) for spot in pieces[:2]]
    for index, spot in enumerate(pieces):
        relay.append((line.close, spot))
        relay += [(line.forward, ahead) for ahead in pieces[index + 2 : index + 3]]
    squares = []
    turn = [0]
    SPACE = 4

    def pump():
        while relay:
            action, spot = relay.pop(0)
            action(*spot)
            if action == line.forward:
                break
        for square in squares:
            if square[1] < 5 and turn[0] >= square[2] + SPACE * square[1]:
                square[0].advance(square[1])
                square[1] += 1
        turn[0] += 1

    def start_loads(pairs, first=0):
        copies = [
            pltpu.make_async_copy(source, target, load_sem.at[first + index])
            for index, (source, target) in enumerate(pairs)
        ]
        for copy in copies:
            copy.start()
        return copies

    def chunk_rows(c):
        return pl.ds(c * length, length) if isinstance(c, int) else span(c * length, length, length)

    shape = (n_seq, length, chan)

    crossing = shares(cross, "tp", n_tp, cross_send, cross_recv)

    def down_terms(w_all, act_all):
        copies = start_loads([(w_down, w_all), (act, act_all)], 3)
        greet(others("ctx", n_ctx) + others("tp", n_tp) + others("fsdp", n_fsdp))

        def cross_terms(gate_all, state_all):
            for copy in start_loads(
                [(proj.at[2], gate_all), (state, state_all), (grad_gated, near)]
            ):
                copy.wait()
            gain_at = over_ctx.at[lax.axis_index("ctx"), :, 2 * width : 2 * width + chan]
            scan_cross(gate_all, state_all, scale, gate_gain, near, grad_proj, gain_at, cross)

        def down_term(c, first, stop):
            @pl.loop(first, stop)
            def _(q):
                cols = pl.ds(pl.multiple_of(q * piece, piece), piece)
                held[c, q] = dot(act_all[chunk_rows(c), :], w_all[:, cols]).astype(HALF)
                line.offer(c, q)

        for copy in copies:
            copy.wait()
        down_term(0, 0, 2)
        pl.run_scoped(cross_terms, pltpu.VMEM(shape, FLOAT), pltpu.VMEM(shape, FLOAT))
        for copy in crossing:
            copy.start()

        for c in range(n_chunks):
            down_term(c, 0 if c else 2, PIECES)

            if c >= n_chunks // 2:
                pump()

    pl.run_scoped(
        down_terms, pltpu.VMEM((units, width), HALF), pltpu.VMEM((rows, units), HALF)
    )

    for copy in crossing:
        copy.wait()

    def back(proj_all, state_all, reach, rate_wide, cross_wide):
        for copy in start_loads([(proj.at[:2], proj_all), (state, state_all)]):
            copy.wait()
        lower_at = over_ctx.at[lax.axis_index("ctx"), :, 2 * width + chan :]
        scan_back(
            n_ctx, n_tp, width, pump,
            proj_all, keep, lower, state_all, scale, carry_in, near,
            grad_proj, lower_at,
            reach, rate_wide, cross_wide, ends, cross, (end_send, end_recv),
        )

    pl.run_scoped(
        back,
        pltpu.VMEM((2, *shape), FLOAT),
        pltpu.VMEM(shape, FLOAT),
        pltpu.VMEM(shape, FLOAT),
        pltpu.VMEM((n_seq, length, BLOCK), FLOAT),
        pltpu.VMEM((n_seq, length, BLOCK), FLOAT),
    )

    def back_terms(w_all):
        for copy in start_loads([(w_in, w_all)]):
            copy.wait()

        for c in range(n_chunks):
            @pl.loop(0, PIECES)
            def _(q):
                at = pl.ds(pl.multiple_of(q * piece, piece), piece)
                held[n_chunks + c, q] = dot_nt(grad_proj[c], w_all[at, :]).astype(HALF)
                line.offer(n_chunks + c, q)

            if c % 2 == 1:
                pump()

    pl.run_scoped(back_terms, pltpu.VMEM((width, wide), HALF))

    item, finish = halves(n_fsdp, part_sem, part_send, part_recv, spare, inbox)
    mine = 1 if whole else lax.axis_index("fsdp")
    depth = width // 2
    skip = whole * depth
    stores = []

    def weights(act_all, dy_all, normed_all, mixed_all, gated_all):
        copies = start_loads(
            [(act, act_all), (cotangent, dy_all), (normed, normed_all), (grad_mixed, mixed_all),
             (gated, gated_all)]
        )
        count = [0]

        def tile(view, compute, other_place, own_place, buffers, at):
            index = count[0]
            count[0] += 1
            square = Square(
                index, buffers, at, own_place, square_send, square_recv, square_store
            )
            item(index, view, compute(1 - mine), compute(mine), other_place, square.tile)
            if whole:
                square.store().start()
                stores.append(square)
            else:
                squares.append([square, 0, turn[0]])
            pump()

        copies[0].wait()
        copies[1].wait()
        for start, size in bands(units, TILE):
            left = act_all[:, start : start + size].T
            at = slice(start, start + size)

            def compute(side):
                return lambda target: fill(target, left, dy_all, side * depth)

            tile(
                lambda ref, size=size: ref.at[:size, :depth], compute,
                lambda at=at: w_down_out.at[at, :depth], lambda at=at: w_down_out.at[at, skip:],
                (down_tile, down_half, down_quarter),
                [slice(start // cut, (start + size) // cut) for cut in (1, 2, 4)],
            )
        copies[2].wait()
        flat_proj = grad_proj.reshape(rows, wide)
        for k in range(depth // TILE):
            def compute(side):
                at = pl.ds(pl.multiple_of(side * depth + k * TILE, TILE), TILE)
                return lambda target: fill(target, normed_all[:, at].T, flat_proj, 0)

            at = slice(k * TILE, (k + 1) * TILE)
            tile(
                lambda ref: ref, compute,
                lambda at=at: w_in_out.at[at],
                lambda k=k: w_in_out.at[k * TILE + skip : (k + 1) * TILE + skip],
                (in_tile, in_half, in_quarter), (k, k, k),
            )
        copies[3].wait()
        copies[4].wait()
        for k in range(chan // TILE):
            at = slice(k * TILE, (k + 1) * TILE)
            left = gated_all[:, at].T

            def compute(side):
                return lambda target: fill(target, left, mixed_all, side * depth)

            tile(
                lambda ref: ref.at[:, :depth], compute,
                lambda at=at: w_out_out.at[at, :depth], lambda at=at: w_out_out.at[at, skip:],
                (out_tile, out_half, out_quarter), (k, k, k),
            )

    pl.run_scoped(
        weights,
        pltpu.VMEM((rows, units), HALF),
        pltpu.VMEM((rows, width), HALF),
        pltpu.VMEM((rows, width), HALF),
        pltpu.VMEM((rows, width), HALF),
        pltpu.VMEM((rows, chan), HALF),
    )
    finish()

    def ends_of(resid_all, x_all, mixed_all):
        copies = start_loads([(tokens, x_all), (mixed, mixed_all), (grad_resid, resid_all)])
        copies[0].wait()
        copies[1].wait()
        gain_total[...] = jnp.zeros_like(gain_total)

        def token_store(c):
            at = chunk_rows(c)
            return pltpu.make_async_copy(
                x_all.at[at], grad_tokens_out.at[at], store_sem.at[0, c]
            )

        def output_store(c):
            at = chunk_rows(c)
            return pltpu.make_async_copy(mixed_all.at[at], output_out.at[at], store_sem.at[1, c])

        def until(job):
            while (line.close, (job, PIECES - 1)) in relay:
                if relay[0] == (line.close, (job, PIECES - 1)):
                    action, spot = relay.pop(0)
                    action(*spot)
                else:
                    pump()

        for c in range(n_chunks):
            until(c)
            line.arrive(c)

            @pl.loop(0, length // 16)
            def _(index):
                at = pl.ds(pl.multiple_of(c * length + index * 16, 16), 16)
                rows = pl.ds(pl.multiple_of(index * 16, 16), 16)
                value = x_all[at, :].astype(FLOAT) + mixed_all[at, :].astype(FLOAT)
                mixed_all[at, :] = (value + joined(total, c, rows)).astype(HALF)

            output_store(c).start()

        copies[2].wait()
        for c in range(n_chunks):
            until(n_chunks + c)
            line.arrive(n_chunks + c)
            for quarter in range(PIECES):
                pump()

                @pl.loop(0, length // PIECES // 16)
                def _(index):
                    start = quarter * (length // PIECES) + index * 16
                    rows = pl.ds(pl.multiple_of(start, 16), 16)
                    at = pl.ds(pl.multiple_of(c * length + start, 16), 16)
                    value = x_all[at, :].astype(FLOAT)
                    rate = rms_scale(value)
                    grad = joined(total, n_chunks + c, rows)
                    by_gain = grad * (value * rate)
                    gain_total[...] += by_gain[:8] + by_gain[8:]
                    inner = gain[...] * grad
                    mean = jnp.mean(inner * value, -1, keepdims=True)
                    result = resid_all[at, :] + rate * inner - value * (rate * rate * rate * mean)
                    x_all[at, :] = result.astype(HALF)

            token_store(c).start()

        here = lax.axis_index("ctx")
        over_ctx[here, :, :width] = jnp.sum(gain_total[...], 0, keepdims=True)
        over_ctx[here, :, width : 2 * width] = gain_two_grad[...]
        share(over_ctx, "ctx", n_ctx, ctx_send, ctx_recv)
        value = over_ctx[0]
        for place in range(1, n_ctx):
            value = value + over_ctx[place]
        over_fsdp[lax.axis_index("fsdp")] = value
        share(over_fsdp, "fsdp", n_fsdp, fsdp_send, fsdp_recv)
        value = over_fsdp[0]
        for place in range(1, n_fsdp):
            value = value + over_fsdp[place]
        vectors_out[...] = value
        while any(square[1] < 5 for square in squares):
            pump()
        for c in range(n_chunks):
            token_store(c).wait()
            output_store(c).wait()

    pl.run_scoped(
        ends_of,
        pltpu.VMEM((rows, width), FLOAT),
        pltpu.VMEM((rows, width), HALF),
        pltpu.VMEM((rows, width), HALF),
    )
    for square in squares:
        square[0].settle()
    for square in stores:
        square.store().wait()

    @pl.loop(0, 2 * n_chunks)
    def _(job):
        line.settle(job)
        line.release(job)


def run_tail(small, large, n_fsdp, n_ctx, n_tp):
    grad_gated, w_down, tokens = large[2], large[4], large[11]
    n_seq, length, chan = grad_gated.shape
    rows, width = tokens.shape
    units = w_down.shape[0]
    piece = width // PIECES
    size = 2 * width + 2 * chan
    depth = width // 2
    spread = width if n_fsdp != 2 else depth
    vmem = pl.BlockSpec(memory_space=pltpu.VMEM)
    hbm = pl.BlockSpec(memory_space=pl.ANY)
    slots = pltpu.VMEM((2 * n_seq, PIECES, length, piece), HALF)
    sems = pltpu.SemaphoreType.DMA((2 * n_seq, PIECES))
    n_in, n_out = depth // TILE, chan // TILE
    n_squares = n_in + n_out + len(bands(units, TILE))
    wide = max(3 * chan, depth)

    def tiles(*shape):
        return [
            pltpu.VMEM((*shape[:-2], shape[-2] // cut, shape[-1]), HALF) for cut in (1, 2, 4)
        ]

    return pl.pallas_call(
        functools.partial(tail, n_fsdp, n_ctx, n_tp),
        name="tail",
        out_shape=(
            jax.ShapeDtypeStruct((rows, width), HALF),
            jax.ShapeDtypeStruct((rows, width), HALF),
            jax.ShapeDtypeStruct((1, size), FLOAT),
            jax.ShapeDtypeStruct((spread, 3 * chan), HALF),
            jax.ShapeDtypeStruct((chan, spread), HALF),
            jax.ShapeDtypeStruct((units, spread), HALF),
        ),
        in_specs=[vmem] * len(small) + [hbm] * len(large),
        out_specs=[hbm, hbm, vmem, hbm, hbm, hbm],
        scratch_shapes=[
            pltpu.VMEM((n_seq, length, 3 * chan), HALF),
            slots,
            pltpu.VMEM((2 * n_seq, PIECES, length, piece), HALF),
            slots,
            pltpu.VMEM((2, TILE, wide), HALF),
            pltpu.VMEM((2, TILE, wide), HALF),
            *tiles(n_in, TILE, 3 * chan),
            *tiles(n_out, TILE, depth),
            *tiles(units, depth),
            pltpu.VMEM((8, width), FLOAT),
            pltpu.VMEM((n_ctx, 2, n_seq, chan), FLOAT),
            pltpu.VMEM((n_tp, n_seq, length), FLOAT),
            pltpu.VMEM((n_ctx, 1, size), FLOAT),
            pltpu.VMEM((n_fsdp, 1, size), FLOAT),
            pltpu.VMEM((n_seq, length, chan), FLOAT),
            pltpu.SemaphoreType.DMA((6,)),
            pltpu.SemaphoreType.DMA((2, n_seq)),
            pltpu.SemaphoreType.DMA((n_ctx,)),
            pltpu.SemaphoreType.DMA((n_ctx,)),
            pltpu.SemaphoreType.DMA((n_tp,)),
            pltpu.SemaphoreType.DMA((n_tp,)),
            pltpu.SemaphoreType.DMA((n_ctx,)),
            pltpu.SemaphoreType.DMA((n_ctx,)),
            pltpu.SemaphoreType.DMA((n_fsdp,)),
            pltpu.SemaphoreType.DMA((n_fsdp,)),
            pltpu.SemaphoreType.DMA((2,)),
            pltpu.SemaphoreType.DMA((2,)),
            pltpu.SemaphoreType.DMA((2,)),
            pltpu.SemaphoreType.DMA((n_squares, 4)),
            pltpu.SemaphoreType.DMA((n_squares, 4)),
            pltpu.SemaphoreType.DMA((n_squares,)),
        ]
        + [sems] * 4,
        compiler_params=pltpu.CompilerParams(
            collective_id=3, has_side_effects=True, vmem_limit_bytes=63 * MIB
        ),
        cost_estimate=pl.CostEstimate(
            flops=10 * rows * width * units, bytes_accessed=700 * MIB, transcendentals=0
        ),
    )(*small, *large)


def widen_outputs(
    w_in, w_out, w_gate, w_up, w_down, tokens, output, vectors,
    w_in_out, w_out_out, w_glu_out, w_down_out, tokens_out, output_out, one_out, two_out, gate_out, lower_out,
):
    chan = w_in_out.shape[2]
    for gate in range(3):
        w_in_out[gate] = w_in[:, gate * chan : (gate + 1) * chan].astype(FLOAT)
    w_out_out[...] = w_out[...].astype(FLOAT)
    w_glu_out[:, 0, :] = w_gate[...].astype(FLOAT)
    w_glu_out[:, 1, :] = w_up[...].astype(FLOAT)
    w_down_out[...] = w_down[...].astype(FLOAT)
    tokens_out[...] = tokens[...].astype(FLOAT)
    output_out[...] = output[...]

    @pl.when(pl.program_id(0) == 0)
    def _():
        part = one_out.shape[1]
        width = (vectors.shape[1] - 2 * chan) // 2
        begin = lax.axis_index("fsdp") * part
        one_out[...] = vectors[:, span(begin, part, part)]
        two_out[...] = vectors[:, span(width + begin, part, part)]
        gate_out[...] = vectors[:, 2 * width : 2 * width + chan]
        lower_out[...] = vectors[:, 2 * width + chan :]


def run_widen_outputs(w_in, w_out, w_gate, w_up, w_down, tokens, output, vectors):
    steps = 8
    arrays = (w_in, w_out, w_gate, w_up, w_down, tokens, output)

    def spec(array):
        return pl.BlockSpec((array.shape[0] // steps, array.shape[1]), lambda i: (i, 0))

    depth, wide = w_in.shape
    chan = wide // 3
    units = w_gate.shape[1]
    whole = pl.BlockSpec(vectors.shape, lambda i: (0, 0))
    thin = [jax.ShapeDtypeStruct((1, size), FLOAT) for size in (depth, depth, chan, chan)]
    shapes = [
        jax.ShapeDtypeStruct((3, depth, chan), FLOAT),
        jax.ShapeDtypeStruct(w_out.shape, FLOAT),
        jax.ShapeDtypeStruct((depth, 2, units), FLOAT),
        jax.ShapeDtypeStruct(w_down.shape, FLOAT),
        jax.ShapeDtypeStruct(tokens.shape, FLOAT),
        jax.ShapeDtypeStruct(output.shape, HALF),
    ]
    in_specs = [spec(array) for array in arrays] + [whole]
    specs = [
        pl.BlockSpec((3, depth // steps, chan), lambda i: (0, i, 0)),
        spec(w_out),
        pl.BlockSpec((depth // steps, 2, units), lambda i: (i, 0, 0)),
        spec(w_down),
        spec(tokens),
        spec(output),
    ] + [pl.BlockSpec(shape.shape, lambda i: (0, 0)) for shape in thin]
    return pl.pallas_call(
        widen_outputs,
        name="widen_outputs",
        grid=(steps,),
        out_shape=shapes + thin,
        in_specs=in_specs,
        out_specs=specs,
        compiler_params=pltpu.CompilerParams(vmem_limit_bytes=62 * MIB),
    )(*arrays, vectors)


def head(
    n_fsdp, n_ctx, n_tp,
    gains, same, edges, gate_gain, lower, w_in, tokens, wo_in,
    gated, scale, carry_out, keep, gain_one, gain_two, proj_out, state_out, normed_out, w_out, wo_out,
    staged, w_all, wo_staged, wo_all, normed, proj, state, local, reach, ends, squares, gain_slots, edge_slots,
    load_sem, store_sem, half_send, half_recv, ctx_send, ctx_recv, tp_send, tp_recv,
    gain_send, gain_recv, edge_send, edge_recv,
):
    n_seq, length, chan = state.shape
    rows = n_seq * length
    depth = w_in.shape[1]
    width = w_all.shape[0]
    core = lax.axis_index("fsdp")
    gate_cols = [slice(gate * chan, (gate + 1) * chan) for gate in range(3)]
    x_load = pltpu.make_async_copy(tokens, normed, load_sem.at[3])
    if n_fsdp == 2:
        w_loads = [
            pltpu.make_async_copy(w_in.at[gate], staged.at[gate], load_sem.at[gate])
            for gate in range(3)
        ]
    else:
        w_loads = [
            pltpu.make_async_copy(w_in.at[gate], w_all.at[:, gate_cols[gate]], load_sem.at[gate])
            for gate in range(3)
        ]
    if n_fsdp == 2:
        wo_load = pltpu.make_async_copy(wo_in, wo_staged, load_sem.at[4])
    else:
        wo_load = pltpu.make_async_copy(wo_in, wo_out, load_sem.at[4])
    for load in w_loads + [x_load, wo_load]:
        load.start()
    gain_slots[core] = gains[...].astype(HALF).astype(FLOAT)
    edge_slots[lax.axis_index("ctx")] = edges[1]
    greet(others("ctx", n_ctx) + others("tp", n_tp) + others("fsdp", n_fsdp))
    small = shares(gain_slots, "fsdp", n_fsdp, gain_send, gain_recv)
    small += shares(edge_slots, "ctx", n_ctx, edge_send, edge_recv)
    for copy in small:
        copy.start()
    halves_sent = []
    if n_fsdp == 2:
        own = span(core * depth, depth, depth)
        for gate in range(3):
            w_loads[gate].wait()

            def cast(at):
                to = span(core * depth + at.start, at.size, at.size)
                w_all[to, gate_cols[gate]] = staged[gate, at, :].astype(HALF)

            row_blocks(depth, 32, cast)
            place = w_all.at[own, gate_cols[gate]]
            copy = pltpu.make_async_remote_copy(
                src_ref=place,
                dst_ref=place,
                send_sem=half_send.at[gate],
                recv_sem=half_recv.at[gate],
                device_id={"fsdp": 1 - core},
                device_id_type=MESH,
            )
            copy.start()
            halves_sent.append(copy)
    for copy in small:
        copy.wait()
    part = gains.shape[1]
    for place in range(n_fsdp):
        cols = slice(place * part, (place + 1) * part)
        gain_one[:, cols] = gain_slots[place, :1, :]
        gain_two[:, cols] = gain_slots[place, 1:2, :]
    here = lax.axis_index("ctx")
    keep[...] = same[...]
    before = edge_slots[0]
    for place in range(1, n_ctx):
        before = jnp.where(place == here - 1, edge_slots[place], before)
    joins = jnp.where((before == edges[0]) & (here > 0), 1.0, 0.0)
    keep[:, :1, :] = joins[:, :1].reshape(n_seq, 1, 1)
    x_load.wait()

    def norm(at):
        value = normed[at, :].astype(FLOAT)
        normed[at, :] = (value * rms_scale(value) * gain_one[...]).astype(HALF)

    row_blocks(rows, 16, norm)
    if n_fsdp == 2:
        size = wo_staged.shape[1]
        own_cols = span(core * size, size, size)
        wo_load.wait()

        def cast_out(at):
            wo_all[at, own_cols] = wo_staged[at, :].astype(HALF)

        row_blocks(chan, 32, cast_out)
        copy = pltpu.make_async_remote_copy(
            src_ref=wo_all.at[:, own_cols],
            dst_ref=wo_all.at[:, own_cols],
            send_sem=half_send.at[3],
            recv_sem=half_recv.at[3],
            device_id={"fsdp": 1 - core},
            device_id_type=MESH,
        )
        copy.start()
        halves_sent.append(copy)
    normed_store = pltpu.make_async_copy(normed, normed_out, store_sem.at[0])
    normed_store.start()
    flat = proj.reshape(3, rows, chan)
    band = rows
    if n_fsdp == 2:
        for gate in range(3):
            @pl.loop(0, rows // band)
            def _(index):
                at = span(index * band, band, band)
                cols = span(core * depth, depth, depth)
                flat[gate, at, :] = dot(normed[at, cols], w_all[own, gate_cols[gate]])

        for gate in range(3):
            halves_sent[gate].wait_recv()

            @pl.loop(0, rows // band)
            def _(index):
                at = span(index * band, band, band)
                other = span((1 - core) * depth, depth, depth)
                flat[gate, at, :] += dot(normed[at, other], w_all[other, gate_cols[gate]])
    else:
        for gate in range(3):
            w_loads[gate].wait()

            @pl.loop(0, rows // band)
            def _(index):
                at = span(index * band, band, band)
                flat[gate, at, :] = dot(normed[at, :], w_all[:, gate_cols[gate]])

    stores = [
        pltpu.make_async_copy(proj, proj_out, store_sem.at[1]),
        pltpu.make_async_copy(w_all, w_out, store_sem.at[2]),
    ]
    for store in stores:
        store.start()
    low = lower[...].reshape(1, 1, chan)
    row = lax.broadcasted_iota(jnp.int32, (n_seq, GROUP, chan), 1)

    def step(index, carry):
        prod, total = carry
        rows = pl.ds(pl.multiple_of(index * GROUP, GROUP), GROUP)
        inp = proj[0, :, rows, :]
        decay = low + (1.0 - low) * jax.nn.sigmoid(proj[1, :, rows, :])
        add = inp * jax.nn.sigmoid(inp) * (1.0 - decay)
        mult = decay * keep[:, rows, :]
        for hop in (1, 2, 4):
            inside = row >= hop
            add = jnp.where(inside, mult * pltpu.roll(add, hop, 1) + add, add)
            mult = jnp.where(inside, mult * pltpu.roll(mult, hop, 1), mult)
        add = add + mult * total
        mult = mult * prod
        local[:, rows, :] = add
        reach[:, rows, :] = mult
        return mult[:, GROUP - 1 :, :], add[:, GROUP - 1 :, :]

    start = (jnp.ones((n_seq, 1, chan), FLOAT), jnp.zeros((n_seq, 1, chan), FLOAT))
    prod, total = lax.fori_loop(0, length // GROUP, step, start)
    ends[here, 0] = prod.reshape(n_seq, chan)
    ends[here, 1] = total.reshape(n_seq, chan)
    share(ends, "ctx", n_ctx, ctx_send, ctx_recv)
    carry = jnp.zeros((n_seq, chan), FLOAT)
    for place in range(n_ctx - 1):
        carry = jnp.where(place < here, ends[place, 1] + ends[place, 0] * carry, carry)
    carry_out[...] = carry
    mine = lax.axis_index("tp")
    for seq in range(n_seq):
        for start in range(0, length, BLOCK):
            rows = slice(start, start + BLOCK)
            value = local[seq, rows, :] + reach[seq, rows, :] * carry[seq : seq + 1]
            state[seq, rows, :] = value
            squares[mine, seq : seq + 1, rows] = lane_sums(value * value)
    state_store = pltpu.make_async_copy(state, state_out, store_sem.at[3])
    state_store.start()
    share(squares, "tp", n_tp, tp_send, tp_recv)
    total = squares[0]
    for place in range(1, n_tp):
        total = total + squares[place]
    rate = lax.rsqrt(total / width + EPS)
    scale[...] = rate
    for seq in range(n_seq):
        for start in range(0, length, BLOCK):
            rows = slice(start, start + BLOCK)
            gate = proj[2, seq, rows, :]
            unit = state[seq, rows, :] * widen(columns(rate[seq : seq + 1, rows]), chan)
            swish = gate * jax.nn.sigmoid(gate)
            gated[seq, rows, :] = (unit * gate_gain[...] * swish).astype(HALF)
    for copy in halves_sent:
        copy.wait_send()
    if n_fsdp == 2:
        halves_sent[3].wait_recv()
        stores.append(pltpu.make_async_copy(wo_all, wo_out, load_sem.at[4]))
        stores[-1].start()
    else:
        stores.append(wo_load)
    for store in stores + [normed_store, state_store]:
        store.wait()


def run_head(
    gains, same, edges, gate_gain, lower, w_in, tokens, w_out, n_fsdp, n_ctx, n_tp
):
    n_seq, length, _ = same.shape
    rows, width = tokens.shape
    chan = w_in.shape[2]
    shape = (n_seq, length, chan)
    vmem = pl.BlockSpec(memory_space=pltpu.VMEM)
    hbm = pl.BlockSpec(memory_space=pl.ANY)
    staged = w_in.shape if n_fsdp == 2 else (3, 8, BLOCK)
    wo_staged = w_out.shape if n_fsdp == 2 else (8, BLOCK)
    dma = pltpu.SemaphoreType.DMA
    return pl.pallas_call(
        functools.partial(head, n_fsdp, n_ctx, n_tp),
        name="head",
        out_shape=(
            jax.ShapeDtypeStruct(shape, HALF),
            jax.ShapeDtypeStruct((n_seq, length), FLOAT),
            jax.ShapeDtypeStruct((n_seq, chan), FLOAT),
            jax.ShapeDtypeStruct((n_seq, length, 1), FLOAT),
            jax.ShapeDtypeStruct((1, width), FLOAT),
            jax.ShapeDtypeStruct((1, width), FLOAT),
            jax.ShapeDtypeStruct((3, *shape), FLOAT),
            jax.ShapeDtypeStruct(shape, FLOAT),
            jax.ShapeDtypeStruct((rows, width), HALF),
            jax.ShapeDtypeStruct((width, 3 * chan), HALF),
            jax.ShapeDtypeStruct((chan, width), HALF),
        ),
        in_specs=[vmem] * 5 + [hbm] * 3,
        out_specs=[vmem] * 6 + [hbm] * 5,
        scratch_shapes=[
            pltpu.VMEM(staged, FLOAT),
            pltpu.VMEM((width, 3 * chan), HALF),
            pltpu.VMEM(wo_staged, FLOAT),
            pltpu.VMEM((chan, width), HALF),
            pltpu.VMEM((rows, width), HALF),
            pltpu.VMEM((3, *shape), FLOAT),
            pltpu.VMEM(shape, FLOAT),
            pltpu.VMEM(shape, FLOAT),
            pltpu.VMEM(shape, FLOAT),
            pltpu.VMEM((n_ctx, 2, n_seq, chan), FLOAT),
            pltpu.VMEM((n_tp, n_seq, length), FLOAT),
            pltpu.VMEM((n_fsdp, *gains.shape), FLOAT),
            pltpu.VMEM((n_ctx, *edges.shape[1:]), FLOAT),
            dma((5,)), dma((4,)), dma((4,)), dma((4,)), dma((n_ctx,)), dma((n_ctx,)),
            dma((n_tp,)), dma((n_tp,)), dma((n_fsdp,)), dma((n_fsdp,)), dma((n_ctx,)), dma((n_ctx,)),
        ],
        compiler_params=pltpu.CompilerParams(
            collective_id=0, has_side_effects=True, vmem_limit_bytes=63 * MIB
        ),
    )(gains, same, edges, gate_gain, lower, w_in, tokens, w_out)


def gather_fsdp(part, dim):
    return lax.all_gather(part, "fsdp", axis=dim, tiled=True)


def local(
    sizes,
    tokens, segment_ids, w_in, w_out, w_glu, w_down, gain_one, gain_two, gate_gain, lower, cotangent,
):
    n_fsdp, n_ctx, n_tp = sizes
    n_seq, length, width = tokens.shape
    rows = n_seq * length
    chan = w_in.shape[2]
    x_half = tokens.reshape(rows, width)
    parts = (w_glu[:, 0].astype(HALF), w_glu[:, 1].astype(HALF), w_down)
    if n_fsdp != 2:
        parts = (*parts[:2], w_down.astype(HALF))
        parts = tuple(gather_fsdp(part, dim) for part, dim in zip(parts, (0, 0, 1)))
        w_in = gather_fsdp(w_in.astype(HALF), 1)
        w_out = gather_fsdp(w_out.astype(HALF), 1)
    gain_gate = gate_gain[None]
    low = lower[None]
    seg = segment_ids.astype(FLOAT)
    same = jnp.pad((seg[:, 1:] == seg[:, :-1]).astype(FLOAT), ((0, 0), (1, 0)))[..., None]
    edges = jnp.broadcast_to(jnp.stack([seg[:, 0], seg[:, -1]])[..., None], (2, n_seq, BLOCK))
    (
        gated, gate_scale, carry, keep, gain_a, gain_b, proj, state, normed, w_in_all, w_out_all
    ) = run_head(
        jnp.stack([gain_one, gain_two]), same, edges, gain_gate, low, w_in, x_half, w_out,
        n_fsdp, n_ctx, n_tp,
    )
    gated = gated.reshape(rows, chan)
    grad_y_half = cotangent.reshape(rows, width)
    (
        mixed, _, act, _, grad_resid, grad_mixed, grad_gated, grad_w_gate, grad_w_up, w_down_all,
        grad_gain_two,
    ) = run_middle(
        gated, x_half, grad_y_half, gain_b, (w_out_all, *parts), n_fsdp, n_ctx, length
    )
    if n_fsdp == 2:
        grad_w_up = lax.psum(grad_w_up, "ctx")
    grad_tokens, output, vectors, grad_w_in, grad_w_out, grad_w_down = run_tail(
        (keep, gain_gate, low, gate_scale, carry, gain_a, grad_gain_two),
        (
            proj, state, grad_gated.reshape(n_seq, length, chan), w_in_all, w_down_all, act, normed,
            grad_mixed, gated, grad_y_half, grad_resid, x_half, mixed,
        ),
        n_fsdp, n_ctx, n_tp,
    )
    grads = (grad_w_in, grad_w_out, grad_w_gate, grad_w_up, grad_w_down)
    if n_fsdp != 2:
        grads = tuple(
            lax.psum(lax.psum_scatter(value, "fsdp", scatter_dimension=dim, tiled=True), "ctx")
            for value, dim in zip(grads, (0, 1, 0, 0, 1))
        )
    results = run_widen_outputs(*grads, grad_tokens, output, vectors)
    grad_w_in, grad_w_out, grad_w_glu, grad_w_down, grad_tokens, output = results[:6]
    return (
        output.reshape(n_seq, length, width),
        grad_tokens.reshape(n_seq, length, width),
        grad_w_in,
        grad_w_out,
        grad_w_glu,
        grad_w_down,
        *(vector[0] for vector in results[6:]),
    )


def solution(mesh):
    sizes = tuple(mesh.shape[axis] for axis in ("fsdp", "ctx", "tp"))
    return jax.shard_map(
        functools.partial(local, sizes),
        mesh=mesh,
        in_specs=(
            P("fsdp", "ctx", None),
            P("fsdp", "ctx"),
            P(None, "fsdp", "tp"),
            P("tp", "fsdp"),
            P("fsdp", None, "tp"),
            P("tp", "fsdp"),
            P("fsdp"),
            P("fsdp"),
            P("tp"),
            P("tp"),
            P("fsdp", "ctx", None),
        ),
        out_specs=(
            P("fsdp", "ctx", None),
            P("fsdp", "ctx", None),
            P(None, "fsdp", "tp"),
            P("tp", "fsdp"),
            P("fsdp", None, "tp"),
            P("tp", "fsdp"),
            P("fsdp"),
            P("fsdp"),
            P("tp"),
            P("tp"),
        ),
        check_vma=False,
    )
```
